32 devices in a mesh: dp: 8 (over y, x, core), ctx: 4 (over z).
Axes of the slice: x: 2, y: 2, z: 4, core: 2. Of those that a mesh axis runs over, the one named last changes fastest.
Arguments:
- streams: bfloat16 [4, 16, 1024, 1024], P(None, 'dp', 'ctx'), may hold values from -6 to 6
- history: bfloat16 [12, 16, 1024, 1024], P(None, 'dp', 'ctx'), may hold values from -6 to 6
- teacher: bfloat16 [4, 16, 1024, 1024], P(None, 'dp', 'ctx'), may hold values from -18 to 18
- prefix: int32 [16], P('dp'), may hold values from 0 to 1023
- valid_mask: int32 [16, 1024], P('dp', 'ctx'), may hold values from 0 to 1, as said below
- loss_scale: float32 [1], replicated, may hold values from 4194304 to 16777216
- projections: bfloat16 [3, 1024, 1024], P(None, ('dp', 'ctx')), may hold values from -0.1875 to 0.1875
- attention_out: bfloat16 [1024, 1024], P(('dp', 'ctx')), may hold values from -1.5 to 1.5
- up_weight: bfloat16 [1024, 4096], P(('dp', 'ctx')), may hold values from -0.1875 to 0.1875
- down_weight: bfloat16 [4096, 1024], P(('dp', 'ctx')), may hold values from -0.09375 to 0.09375
- mixer_first: bfloat16 [1024, 52], P(('dp', 'ctx')), may hold values from -0.1875 to 0.1875
- mixer_second: float32 [52, 52], replicated, may hold values from -0.875 to 0.875
- mixer_bias: float32 [52], replicated, may hold values from -3 to 3
- gains: bfloat16 [5, 1024], P(None, ('dp', 'ctx')), may hold values from 0.5 to 1.5
Outputs:
- next_streams: bfloat16 [4, 16, 1024, 1024], P(None, 'dp', 'ctx')
- mean_loss: float32 [], replicated
- grad_streams: bfloat16 [4, 16, 1024, 1024], P(None, 'dp', 'ctx')
- grad_history: bfloat16 [12, 16, 1024, 1024], P(None, 'dp', 'ctx')
- grad_projections: float32 [3, 1024, 1024], P(None, ('dp', 'ctx'))
- grad_attention_out: float32 [1024, 1024], P(('dp', 'ctx'))
- grad_up: float32 [1024, 4096], P(('dp', 'ctx'))
- grad_down: float32 [4096, 1024], P(('dp', 'ctx'))
- grad_mixer_first: float32 [1024, 52], P(('dp', 'ctx'))
- grad_mixer_second: float32 [52, 52], replicated
- grad_mixer_bias: float32 [52], replicated
- grad_gains: float32 [5, 1024], P(None, ('dp', 'ctx'))
The draws below stay inside these ranges and needn't reach their ends.
Inputs may be any that keep to these rules, and one draw needn't show every extreme that they name: `valid_mask`: the first token of every sequence is valid.
All inputs are finite; a program needn't handle non-finite values.
Results may differ from the reference program's by a relative error of at most 0.015.
Values may be sent and summed in bfloat16 or wider, within the bound.
A program may use at most 168 MiB of HBM per device.

```python
import math
import jax
import jax.numpy as jnp
from jax import lax

D = 1024
FF = 4096
HEADS = 16
HEAD_DIM = 64
ROT = 16
NOUT = 13
NPREV = 12
MIXW = 52
SEQ_LEN = 1024
SEQS = 16


def draw_valid_mask(key, part):
    sequence_rank = jnp.arange(SEQS, dtype=jnp.int32)[:, None]
    position_rank = jnp.arange(SEQ_LEN, dtype=jnp.int32)[None, :]
    along_level = 25 + 75 * position_rank // SEQ_LEN
    across_level = 40 + 60 * sequence_rank // max(SEQS - 1, 1)
    threshold = along_level * across_level
    ticket = jax.random.randint(key, (SEQS, SEQ_LEN), 0, 10000, dtype=jnp.int32)
    chosen = (ticket < threshold) | (position_rank == 0)
    return chosen.astype(jnp.int32)


def set_ends(drawn, key, low, high):
    longest = drawn.shape.index(max(drawn.shape))
    spots = []
    for shift in (0, 1):
        where = [jax.random.randint(jax.random.fold_in(key, axis), (), 0, length) for axis, length in enumerate(drawn.shape)]
        where[longest] = (where[longest] + shift) % drawn.shape[longest]
        spots.append(tuple(where))
    return drawn.at[spots[0]].set(low).at[spots[1]].set(high)


def block_scale(key, shape, cuts, least, largest):
    factor_of = 1.0
    for position, shards_of in cuts:
        draws = jax.random.uniform(jax.random.fold_in(jax.random.fold_in(key, 6), position), (shards_of,), jnp.float32, least / len(cuts), largest / len(cuts))
        factor_of = factor_of * jnp.repeat(jnp.exp(draws), shape[position] // shards_of).reshape((-1,) + (1,) * (len(shape) - 1 - position))
    return factor_of


def centred(stream_key, extent, spread, reach, cuts=(), held_as=jnp.bfloat16):
    drawn = spread * jax.random.normal(stream_key, extent, jnp.float32)
    if cuts:
        drawn = drawn * block_scale(stream_key, extent, cuts, -0.22, 0.18)
    return jnp.clip(drawn, -reach, reach).astype(held_as)


def setup_inputs(seed: int = 0) -> dict:
    splits = jax.random.split(jax.random.key(seed), 15)
    streams = centred(splits[0], (4, SEQS, SEQ_LEN, D), 1.0, 6.0, ((1, 8), (2, 4)))
    history = centred(splits[1], (NPREV, SEQS, SEQ_LEN, D), 1.0, 6.0, ((1, 8), (2, 4)))
    teacher = centred(splits[2], (4, SEQS, SEQ_LEN, D), 3.0, 18.0, ((1, 8), (2, 4)))
    prefix = set_ends(jax.random.randint(splits[3], (SEQS,), 0, SEQ_LEN), jax.random.fold_in(splits[3], 1), 0, SEQ_LEN - 1).astype(jnp.int32)
    valid_mask = draw_valid_mask(jax.random.fold_in(splits[14], 71), 0)
    loss_scale = jnp.clip(jnp.exp(jax.random.uniform(splits[5], (1,), jnp.float32, math.log(4194304), math.log(16777216))), 4194304, 16777216)
    projections = centred(splits[6], (3, D, D), D ** -0.5, 0.1875, ((1, 32),))
    attention_out = centred(splits[7], (D, D), (D // 64) ** -0.5, 1.5, ((0, 32),))
    up_weight = centred(splits[8], (D, FF), D ** -0.5, 0.1875, ((0, 32),))
    down_weight = centred(splits[9], (FF, D), FF ** -0.5, 0.09375, ((0, 32),))
    mixer_first = centred(splits[10], (D, MIXW), D ** -0.5, 0.1875, ((0, 32),))
    mixer_second = centred(splits[11], (MIXW, MIXW), MIXW ** -0.5, 0.875, (), jnp.float32)
    mixer_bias = centred(splits[12], (MIXW,), 0.5, 3.0, (), jnp.float32)
    gains = jnp.clip(1.0 + 0.1 * jax.random.normal(splits[13], (5, D), jnp.float32), 0.5, 1.5).astype(jnp.bfloat16)
    return {"streams": streams, "history": history, "teacher": teacher, "prefix": prefix, "valid_mask": valid_mask, "loss_scale": loss_scale, "projections": projections, "attention_out": attention_out, "up_weight": up_weight, "down_weight": down_weight, "mixer_first": mixer_first, "mixer_second": mixer_second, "mixer_bias": mixer_bias, "gains": gains}


@jax.custom_vjp
def low(v):
    return lax.optimization_barrier(v.astype(jnp.bfloat16)).astype(jnp.float32)

@jax.custom_vjp
def low_back(v):
    return v

def low_keep(v):
    return (low(v), None)

def low_pass(kept, grad):
    return (grad,)

def back_keep(v):
    return (v, None)

def back_low(kept, grad):
    return (low(grad),)
low.defvjp(low_keep, low_pass)
low_back.defvjp(back_keep, back_low)
highest = lax.Precision.HIGHEST
epsilon = 1e-05

def layer_norm(values, gain_row):
    centered = values - lax.optimization_barrier(jnp.mean(values, axis=-1, keepdims=True))
    return centered * lax.rsqrt(lax.optimization_barrier(jnp.mean(centered * centered, axis=-1, keepdims=True)) + epsilon) * gain_row

def rms_norm(values, gain_row):
    return values * lax.rsqrt(lax.optimization_barrier(jnp.mean(values * values, axis=-1, keepdims=True)) + epsilon) * gain_row

def rotary_tables(positions):
    frequency_steps = jnp.arange(ROT // 2).astype(positions.dtype)
    inverse = jnp.exp(frequency_steps * (-2.0 * math.log(10000.0) / ROT))
    angles = positions[:, None] * inverse[None, :]
    return (jnp.cos(angles)[:, None, :], jnp.sin(angles)[:, None, :])

def rotate(values, cosine_table, sine_table, direction):
    row_count = values.shape[0]
    shaped = values.reshape(row_count, HEADS, HEAD_DIM)
    half_rot = ROT // 2
    first_half = shaped[:, :, :half_rot]
    second_half = shaped[:, :, half_rot:ROT]
    remainder = shaped[:, :, ROT:]
    turned_first = first_half * cosine_table - direction * second_half * sine_table
    turned_second = second_half * cosine_table + direction * first_half * sine_table
    return jnp.concatenate([turned_first, turned_second, remainder], axis=-1).reshape(row_count, -1)

def gelu_exact(values):
    return jax.nn.gelu(values, approximate=False)

def sequence_forward(weight_set, stream_seq, history_seq, teacher_seq, prefix_len, valid_row, token_total, scale_value):
    projections, attention_out, up_weight, down_weight, mixer_first, mixer_second, mixer_bias, gains = weight_set
    length = stream_seq.shape[1]
    position_ids = jnp.arange(length, dtype=jnp.int32)
    cosine_table, sine_table = rotary_tables(position_ids.astype(jnp.float32))
    normed = low(layer_norm(stream_seq[:3], gains[:3, None, :]))
    projected = low_back(jnp.einsum('std,sde->ste', normed, projections, precision=highest))
    queries = low(rotate(projected[0], cosine_table, sine_table, 1.0)).reshape(length, HEADS, HEAD_DIM)
    keys = low(rotate(projected[1], cosine_table, sine_table, 1.0)).reshape(length, HEADS, HEAD_DIM)
    values = low(projected[2]).reshape(length, HEADS, HEAD_DIM)
    scores = low_back(jnp.einsum('qhd,khd->hqk', queries, keys, precision=highest) * HEAD_DIM ** (-0.5))
    allowed = (position_ids[None, :] <= position_ids[:, None]) | (position_ids[None, :] < prefix_len)
    scores = jnp.where(allowed[None], scores, -1e+30)
    probs = low(jax.nn.softmax(scores, axis=-1))
    heads = low(low_back(jnp.einsum('hqk,khd->qhd', probs, values, precision=highest).reshape(length, D)))
    hidden = stream_seq[3] + low_back(jnp.dot(heads, attention_out, precision=highest))
    normed_mlp = low(layer_norm(hidden, gains[3]))
    upper = low_back(jnp.dot(normed_mlp, up_weight, precision=highest))
    activated = low(gelu_exact(upper))
    layer_out = hidden + low_back(jnp.dot(activated, down_weight, precision=highest))
    normed_mix = low(rms_norm(layer_out, gains[4]))
    mix_hidden = low_back(jnp.dot(normed_mix, mixer_first, precision=highest))
    coeff = jnp.dot(gelu_exact(mix_hidden), mixer_second, precision=highest) + mixer_bias
    outputs_all = jnp.concatenate([history_seq, layer_out[None]], axis=0)
    next_seq = jnp.einsum('tsj,jtd->std', coeff.reshape(length, 4, NOUT), outputs_all, precision=highest)
    difference = next_seq - teacher_seq
    part_loss = jnp.sum(lax.optimization_barrier(jnp.sum(difference * difference, axis=(0, 2))) * valid_row) / (4.0 * D * token_total)
    return (part_loss * scale_value, (next_seq, part_loss))

def reference(streams, history, teacher, prefix, valid_mask, loss_scale, projections, attention_out, up_weight, down_weight, mixer_first, mixer_second, mixer_bias, gains):
    weight_set = (projections.astype(jnp.float32), attention_out.astype(jnp.float32), up_weight.astype(jnp.float32), down_weight.astype(jnp.float32), mixer_first.astype(jnp.float32), mixer_second.astype(jnp.float32), mixer_bias.astype(jnp.float32), gains.astype(jnp.float32))
    valid_float = valid_mask.astype(jnp.float32)
    token_total = jnp.sum(valid_float)
    scale_value = loss_scale[0].astype(jnp.float32)
    zero_grads = jax.tree.map(jnp.zeros_like, weight_set)

    def one_sequence(totals, inputs_seq):
        grads_sum, loss_sum = totals
        stream_seq, history_seq, teacher_seq, prefix_len, valid_row = inputs_seq

        def forward(weights_now, streams_now, history_now):
            return sequence_forward(weights_now, streams_now, history_now, teacher_seq, prefix_len, valid_row, token_total, scale_value)
        primal, pullback, aux_pair = jax.vjp(forward, weight_set, stream_seq.astype(jnp.float32), history_seq.astype(jnp.float32), has_aux=True)
        next_seq, part_loss = aux_pair
        grad_weights, grad_stream, grad_hist = pullback(jnp.ones_like(primal))
        grads_sum = jax.tree.map(jnp.add, grads_sum, grad_weights)
        return ((grads_sum, loss_sum + part_loss), (next_seq.astype(jnp.bfloat16), grad_stream.astype(jnp.bfloat16), grad_hist.astype(jnp.bfloat16)))
    scanned = (jnp.swapaxes(streams, 0, 1), jnp.swapaxes(history, 0, 1), jnp.swapaxes(teacher, 0, 1).astype(jnp.float32), prefix, valid_float)
    (grads_sum, loss_sum), (next_all, grad_stream_all, grad_hist_all) = lax.scan(one_sequence, (zero_grads, jnp.zeros((), jnp.float32)), scanned)
    return (jnp.swapaxes(next_all, 0, 1), loss_sum, jnp.swapaxes(grad_stream_all, 0, 1), jnp.swapaxes(grad_hist_all, 0, 1), grads_sum[0], grads_sum[1], grads_sum[2], grads_sum[3], grads_sum[4], grads_sum[5], grads_sum[6], grads_sum[7])
```

```python
import functools
import math

import jax
import jax.numpy as jnp
from jax import lax
from jax.experimental import pallas as pl
from jax.experimental.pallas import tpu as pltpu
from jax.sharding import PartitionSpec as P

HEADS = 16
HEAD_DIM = 64
ROT = 16
AXES = ("dp", "ctx")

highest = lax.Precision.HIGHEST
epsilon = 1e-05
f32 = jnp.float32
bf16 = jnp.bfloat16
VMEM_BYTES = 60 * 1024 * 1024


def dot_nn(a, b, precision=None):
    return lax.dot_general(
        a, b, (((1,), (0,)), ((), ())), precision=precision, preferred_element_type=f32
    )


def dot_nt(a, b, precision=None):
    return lax.dot_general(
        a, b, (((1,), (1,)), ((), ())), precision=precision, preferred_element_type=f32
    )


def dot_tn(a, b, precision=None):
    return lax.dot_general(
        a, b, (((0,), (0,)), ((), ())), precision=precision, preferred_element_type=f32
    )


def normal_cdf(v):
    z = jnp.abs(v) * math.sqrt(0.5)
    t = 1.0 / (1.0 + 0.39 * z)
    bell = jnp.exp(-0.5 * v * v)
    poly = -0.22760540438261295
    for c in (
        0.8869388009365644,
        -0.6358388689155755,
        0.649907738051149,
        0.09125094908545259,
        0.23534677935551734,
    ):
        poly = poly * t + c
    half_tail = (0.5 * poly) * t * bell
    return jnp.where(v < 0.0, half_tail, 1.0 - half_tail), bell


def gelu_pair(v):
    cdf, bell = normal_cdf(v)
    return v * cdf, cdf + v * bell * (1.0 / math.sqrt(2.0 * math.pi))


def vmem(block=None, index_map=None):
    if block is None:
        return pl.BlockSpec(memory_space=pltpu.VMEM)
    return pl.BlockSpec(block, index_map)


def params(**kw):
    return pltpu.CompilerParams(vmem_limit_bytes=VMEM_BYTES, **kw)


def norm_body(ids, r0, r1, r2, r3, gain_ref, out_ref):
    mine = ids[2]
    rows = r0.shape[1]
    for k, r in enumerate((r0, r1, r2, r3)):
        block = jnp.bitwise_xor(mine, k)
        for s in range(3):
            gain = gain_ref[s : s + 1, :].astype(f32)

            def body(i, _, r=r, s=s, gain=gain, block=block):
                at = pl.ds(pl.multiple_of(i * 16, 16), 16)
                x = r[s, at, :].astype(f32)
                x = x - jnp.mean(x, axis=-1, keepdims=True)
                scale = lax.rsqrt(jnp.mean(x * x, axis=-1, keepdims=True) + epsilon)
                out_ref[s, block, at, :] = (x * scale * gain).astype(bf16)
                return 0

            lax.fori_loop(0, rows // 16, body, 0)


def turn(x, cosine, sine_up, sine_down):
    return (
        x * cosine + pltpu.roll(x, ROT // 2, 1) * sine_up + pltpu.roll(x, 128 - ROT // 2, 1) * sine_down
    )


def allowed_limit(base, rows, prefix, axis):
    shape = (rows, 1) if axis == 0 else (1, rows)
    position = base + lax.broadcasted_iota(jnp.int32, shape, axis)
    return jnp.maximum(position, prefix - 1)


def attention_forward_body(
    ids, own_ref, other_ref, wq_ref, wk_ref, wv_ref, cos_ref, up_ref, down_ref,
    heads_ref, lse_ref, q_ref, k_ref, v_ref,
):
    half = ids[1]
    prefix = ids[3]
    blocks, _, piece, width = q_ref.shape
    length = blocks * 2 * piece
    for part, source in ((0, own_ref), (1, other_ref)):
        place = jnp.bitwise_xor(half, part)
        for s, w_ref, out_ref in ((0, wq_ref, q_ref), (1, wk_ref, k_ref), (2, wv_ref, v_ref)):
            x = source[s].reshape(blocks * piece, -1)
            y = dot_nn(x, w_ref[0])
            if s < 2:
                cosine = cos_ref[:, place].reshape(blocks * piece, 128)
                sine_up = up_ref[:, place].reshape(blocks * piece, 128)
                sine_down = down_ref[:, place].reshape(blocks * piece, 128)
                y = jnp.concatenate(
                    [
                        turn(y[:, i : i + 128], cosine, sine_up, sine_down)
                        for i in range(0, width, 128)
                    ],
                    axis=1,
                )
            y = y.astype(bf16)
            if s == 0:
                y = y * jnp.asarray(HEAD_DIM**-0.5, bf16)
            out_ref[:, place] = y.reshape(blocks, piece, width)

    rows = 2 * piece
    lane = lax.broadcasted_iota(jnp.int32, (rows, 128), 1)
    key_index = lax.broadcasted_iota(jnp.int32, (rows, length), 1)

    def block_body(block, _):
        limit = allowed_limit(block * rows, rows, prefix, 0)
        allowed = key_index <= limit
        lse_all = jnp.zeros((rows, 8), f32)
        lse_lane = lax.broadcasted_iota(jnp.int32, (rows, 8), 1)
        for pair in range(width // 128):
            at = slice(pair * 128, pair * 128 + 128)
            queries = q_ref[block, :, :, at].reshape(rows, 128)
            keys = k_ref[:, :, :, at].reshape(length, 128)
            values = v_ref[:, :, :, at].reshape(length, 128)
            results = []
            for h in range(2):
                chosen = (lane < 64) if h == 0 else (lane >= 64)
                scores = dot_nt(jnp.where(chosen, queries, jnp.zeros_like(queries)), keys)
                scores = jnp.where(allowed, scores, -1e30)
                top = jnp.max(scores, axis=-1, keepdims=True)
                weights = jnp.exp(scores - top)
                total = jnp.sum(weights, axis=-1, keepdims=True)
                results.append(dot_nn(weights.astype(bf16), values) / total)
                lse_all = jnp.where(lse_lane == pair * 2 + h, top + jnp.log(total), lse_all)
            heads_ref[block, :, at] = jnp.where(lane < 64, results[0], results[1]).astype(bf16)
        lse_ref[block] = lse_all
        return 0

    lax.fori_loop(0, blocks, block_body, 0)


def mlp_forward_body(
    ids, h0, h1, h2, h3, res_ref, out_w_ref, gain_ref, up_ref, down_ref,
    hidden_ref, normed_ref, active_ref, slope_ref, layer_ref,
):
    step = pl.program_id(0)
    seqs, rows, width = res_ref.shape[1:]

    @pl.when(step == 0)
    def _():
        hidden_ref[...] = res_ref[0].astype(f32)
        for k, piece in enumerate((h0, h1, h2, h3)):
            code = jnp.bitwise_xor(ids[0], k)
            features = piece.shape[-1]
            at = pl.ds(pl.multiple_of(lax.rem(code, 2) * features, features), features)
            seq = lax.div(code, 2)
            hidden_ref[seq] += dot_nn(piece[...], out_w_ref[at, :])
        gain = gain_ref[3:4, :].astype(f32)
        for j in range(seqs):
            x = hidden_ref[j]
            layer_ref[j] = x
            x = x - jnp.mean(x, axis=-1, keepdims=True)
            scale = lax.rsqrt(jnp.mean(x * x, axis=-1, keepdims=True) + epsilon)
            normed_ref[j] = (x * scale * gain).astype(bf16)

    upper = dot_nn(normed_ref[...].reshape(seqs * rows, width), up_ref[...])
    active, slope = gelu_pair(upper)
    active = active.astype(bf16)
    active_ref[...] = active
    slope_ref[...] = slope.astype(bf16)
    layer_ref[...] += dot_nn(active, down_ref[...]).reshape(seqs, rows, width)


def mixer_body(
    scal_ref, layer_ref, hist_ref, teacher_ref, valid_ref, gain_ref, first_ref, second_ref, bias_ref,
    next_ref, ghist_ref, glayer_ref, gfirst_ref, gsecond_ref, stats_ref, ggain_ref,
    coef_ref, part_ref, gnext_ref,
):
    step = pl.program_id(0)
    past, rows, width = hist_ref.shape
    streams = teacher_ref.shape[0]
    outs = past + 1
    span = first_ref.shape[0]

    @pl.when(step == 0)
    def _():
        gfirst_ref[...] = jnp.zeros_like(gfirst_ref)
        gsecond_ref[...] = jnp.zeros_like(gsecond_ref)
        stats_ref[...] = jnp.zeros_like(stats_ref)
        ggain_ref[...] = jnp.zeros_like(ggain_ref)

    factor = scal_ref[0]
    x = layer_ref[...]
    scale = lax.rsqrt(jnp.mean(x * x, axis=-1, keepdims=True) + epsilon)
    gain = gain_ref[4:5, :].astype(f32)
    normed = (x * scale * gain).astype(bf16)
    mix_hidden = dot_nt(normed, first_ref[...])
    mix_active, mix_slope = gelu_pair(mix_hidden)
    coeff = dot_nn(mix_active, second_ref[...], highest) + bias_ref[...]
    for c in range(streams * outs):
        coef_ref[c] = jnp.broadcast_to(coeff[:, c : c + 1], (rows, 128))
    part_ref[...] = jnp.zeros_like(part_ref)

    chunk = 16
    lanes = 512

    def rows_body(i, loss_rows):
        at = pl.ds(pl.multiple_of(i * chunk, chunk), chunk)
        valid = jnp.broadcast_to(valid_ref[at, :], (chunk, 128))

        def read(j, lane_at):
            return layer_ref[at, lane_at] if j == past else hist_ref[j, at, lane_at].astype(f32)

        for l0 in range(0, width, 256):
            lane_at = slice(l0, l0 + 256)
            sums = [jnp.zeros((chunk, 256), f32) for _ in range(streams)]
            for j in range(outs):
                value = read(j, lane_at)
                for s in range(streams):
                    c = coef_ref[s * outs + j, at, :]
                    sums[s] = sums[s] + jnp.concatenate([c, c], axis=1) * value
            both = jnp.concatenate([valid, valid], axis=1)
            for s in range(streams):
                next_ref[s, at, lane_at] = sums[s].astype(bf16)
                difference = sums[s] - teacher_ref[s, at, lane_at].astype(f32)
                weighted = both * difference
                gnext_ref[s, at, lane_at] = factor * weighted
                square = weighted * difference
                loss_rows = loss_rows + square[:, :128] + square[:, 128:]
        for l0 in range(0, width, lanes):
            lane_at = slice(l0, l0 + lanes)
            for j in range(outs):
                value = read(j, lane_at)
                total = jnp.zeros((chunk, lanes), f32)
                for s in range(streams):
                    grad = gnext_ref[s, at, lane_at]
                    c = coef_ref[s * outs + j, at, :]
                    total = total + jnp.concatenate([c] * (lanes // 128), axis=1) * grad
                    product = grad * value
                    folded = product[:, :128]
                    for q in range(128, lanes, 128):
                        folded = folded + product[:, q : q + 128]
                    part_ref[s * outs + j, at, :] += folded
                if j == past:
                    glayer_ref[at, lane_at] = total
                else:
                    ghist_ref[j, at, lane_at] = total.astype(bf16)
        return loss_rows

    loss_rows = lax.fori_loop(0, rows // chunk, rows_body, jnp.zeros((chunk, 128), f32))
    lane = lax.broadcasted_iota(jnp.int32, (rows, span), 1)
    grad_coeff = jnp.zeros((rows, span), f32)
    for c in range(streams * outs):
        grad_coeff = jnp.where(lane == c, jnp.sum(part_ref[c], axis=-1, keepdims=True), grad_coeff)
    gsecond_ref[...] += dot_tn(mix_active, grad_coeff, highest)
    stats_ref[0:1, :] += jnp.sum(grad_coeff, axis=0, keepdims=True)
    stats_ref[1:2, :] += jnp.broadcast_to(jnp.sum(loss_rows), (1, span))
    grad_active = dot_nt(grad_coeff, second_ref[...], highest)
    grad_mix = (grad_active * mix_slope).astype(bf16)
    gfirst_ref[...] += dot_tn(grad_mix, normed)
    grad_normed = dot_nn(grad_mix, first_ref[...])
    x = layer_ref[...]
    ggain_ref[...] += jnp.sum(grad_normed * (x * scale), axis=0, keepdims=True)
    inner = grad_normed * gain
    mean = jnp.mean(inner * x, axis=-1, keepdims=True)
    glayer_ref[...] += scale * inner - x * (scale * scale * scale * mean)


def norm_back(x, grad, gain):
    centered = x - jnp.mean(x, axis=-1, keepdims=True)
    scale = lax.rsqrt(jnp.mean(centered * centered, axis=-1, keepdims=True) + epsilon)
    unit = centered * scale
    grad_gain = jnp.sum(grad * unit, axis=0, keepdims=True)
    inner = grad * gain
    inner = (
        inner
        - jnp.mean(inner, axis=-1, keepdims=True)
        - unit * jnp.mean(inner * unit, axis=-1, keepdims=True)
    )
    return scale * inner, grad_gain


def mlp_backward_body(
    ids, glayer_ref, active_ref, slope_ref, normed_ref, up_ref, down_ref,
    hidden_ref, h0, h1, h2, h3, out_w_ref, gain_ref,
    gdown_ref, gup_ref, gres_ref, g0, g1, g2, g3, gout_ref, ggain_ref,
    low_ref, sum_ref, normed_t_ref, gout_sum_ref,
):
    step = pl.program_id(0)
    seqs, rows, width = hidden_ref.shape
    tokens = seqs * rows

    @pl.when(step == 0)
    def _():
        low_ref[...] = glayer_ref[...].astype(bf16)
        sum_ref[...] = jnp.zeros_like(sum_ref)
        normed_t_ref[...] = normed_ref[...].reshape(tokens, width).T

    grad = low_ref[...].reshape(tokens, width)
    grad_active = dot_nt(grad, down_ref[...])
    grad_upper = (grad_active * slope_ref[...].astype(f32)).astype(bf16)
    gdown_ref[...] = dot_tn(active_ref[...], grad).astype(bf16)
    gup_ref[...] = dot_nn(normed_t_ref[...], grad_upper).astype(bf16)
    sum_ref[...] += dot_nt(grad_upper, up_ref[...]).reshape(seqs, rows, width)

    @pl.when(step == pl.num_programs(0) - 1)
    def _():
        gain = gain_ref[3:4, :].astype(f32)
        ggain = jnp.zeros((1, width), f32)
        for j in range(seqs):
            back, part = norm_back(hidden_ref[j], sum_ref[j], gain)
            ggain = ggain + part
            gres_ref[j] = (glayer_ref[j] + back).astype(bf16)
        ggain_ref[...] = ggain
        gout_sum_ref[...] = jnp.zeros_like(gout_sum_ref)
        for k, (piece, out) in enumerate(((h0, g0), (h1, g1), (h2, g2), (h3, g3))):
            code = jnp.bitwise_xor(ids[0], k)
            features = piece.shape[-1]
            at = pl.ds(pl.multiple_of(lax.rem(code, 2) * features, features), features)
            low = gres_ref[lax.div(code, 2)]
            out[...] = dot_nt(low, out_w_ref[at, :]).astype(bf16)
            gout_sum_ref[at, :] += dot_tn(piece[...], low)
        gout_ref[...] = gout_sum_ref[...].astype(bf16)


def attention_backward_body(
    ids, q_ref, k_ref, v_ref, heads_ref, lse_ref, g0, g1, g2, g3, cos_ref, up_ref, down_ref,
    own_ref, send_ref,
    dk_ref, dv_ref, kt_ref, turn_ref,
):
    half = ids[1]
    mine = ids[2]
    prefix = ids[3]
    pair = pl.program_id(0)
    blocks, _, piece, lanes = q_ref.shape
    rows = 2 * piece
    length = blocks * rows
    dk_ref[...] = jnp.zeros_like(dk_ref)
    dv_ref[...] = jnp.zeros_like(dv_ref)
    keys = k_ref[...].reshape(length, lanes)
    values = v_ref[...].reshape(length, lanes)
    kt_ref[...] = keys.T
    lane = lax.broadcasted_iota(jnp.int32, (rows, lanes), 1)
    key_index = lax.broadcasted_iota(jnp.int32, (length, rows), 0)
    choose = (
        lax.broadcasted_iota(jnp.int32, (8, lanes), 1) // 64
        == lax.broadcasted_iota(jnp.int32, (8, lanes), 0)
    ).astype(f32)

    def give(s, x):
        turn_ref[...] = x.astype(bf16).reshape(blocks, 2, piece, lanes)
        own_ref[s] = turn_ref[:, half]
        send_ref[s] = turn_ref[:, 1 - half]

    def back(x, block):
        if block is None:
            parts = [r[...].reshape(length, lanes) for r in (cos_ref, up_ref, down_ref)]
        else:
            parts = [r[block].reshape(rows, lanes) for r in (cos_ref, up_ref, down_ref)]
        return (
            x * parts[0]
            - pltpu.roll(x, ROT // 2, 1) * parts[1]
            - pltpu.roll(x, 128 - ROT // 2, 1) * parts[2]
        )

    for k, g in enumerate((g0, g1, g2, g3)):
        block = jnp.bitwise_xor(mine, k)
        queries = q_ref[block].reshape(rows, lanes)
        grads = g[...]
        inner_rows = dot_nt(choose, grads.astype(f32) * heads_ref[block].astype(f32), highest)
        limit = allowed_limit(block * rows, rows, prefix, 1)
        allowed = key_index <= limit
        dqt = []
        for h in range(2):
            chosen = (lane < 64) if h == 0 else (lane >= 64)
            q_h = jnp.where(chosen, queries, jnp.zeros_like(queries))
            g_h = jnp.where(chosen, grads, jnp.zeros_like(grads))
            scores = dot_nt(keys, q_h)
            probs = jnp.where(allowed, jnp.exp(scores - lse_ref[pair * 2 + h, block]), 0.0)
            grad_probs = dot_nt(values, g_h)
            grad_scores = (probs * (grad_probs - inner_rows[h : h + 1, :])).astype(bf16)
            dv_ref[...] += dot_nn(probs.astype(bf16), g_h)
            dk_ref[...] += dot_nn(grad_scores, q_h)
            dqt.append(dot_nn(kt_ref[...], grad_scores)[h * 64 : h * 64 + 64, :])
        dq = jnp.concatenate(dqt, axis=0).T * (HEAD_DIM**-0.5)
        low = back(dq, block).astype(bf16)
        turn_ref[0] = low.reshape(2, piece, lanes)
        own_ref[0, block] = turn_ref[0, half]
        send_ref[0, block] = turn_ref[0, 1 - half]
    give(1, back(dk_ref[...], None))
    give(2, dv_ref[...])


def projection_backward_body(
    ids, n_own_ref, n_other_ref, d_own_ref, d_send_ref, d_recv_ref, w_own_ref, w_other_ref,
    r0, r1, r2, r3, gain_ref,
    gproj_ref, o0, o1, o2, o3, ggain_ref,
):
    mine = ids[2]
    s = pl.program_id(0)
    _, blocks, piece, width = n_own_ref.shape
    rows = blocks * piece
    d_own = d_own_ref[...].reshape(rows, -1)
    grad = dot_tn(n_own_ref[...].reshape(rows, width), d_own)
    grad = grad + dot_tn(n_other_ref[...].reshape(rows, width), d_send_ref[...].reshape(rows, -1))
    gproj_ref[...] = grad.astype(bf16)[None]
    gain = gain_ref[pl.ds(s, 1), :].astype(f32)
    total = jnp.zeros((1, width), f32)
    for k, (r, o) in enumerate(((r0, o0), (r1, o1), (r2, o2), (r3, o3))):
        block = jnp.bitwise_xor(mine, k)
        grad_normed = dot_nt(d_own_ref[0, block], w_own_ref[0]) + dot_nt(
            d_recv_ref[0, block], w_other_ref[0]
        )
        back, part = norm_back(r[0].astype(f32), grad_normed, gain)
        o[0] = back.astype(bf16)
        total = total + part
    ggain_ref[0] = total


def swap(x, bit, count):
    return lax.ppermute(x, AXES, [(i, i ^ bit) for i in range(count)])


def add_all(x, count):
    bit = 1
    while bit < count:
        x = x + swap(x, bit, count)
        bit *= 2
    return x


def gather_all(x, me, count):
    x = x[None]
    bit = 1
    while bit < count:
        other = swap(x, bit, count)
        low = (me & bit) == 0
        x = jnp.concatenate([jnp.where(low, x, other), jnp.where(low, other, x)], axis=0)
        bit *= 2
    return x


def scatter_sum(x, steps, me, count):
    gone = []
    for bit, axis in steps:
        at = axis - sum(1 for g in gone if g < axis)
        mine = jnp.where((me & bit) == 0, 0, 1)
        keep = lax.dynamic_index_in_dim(x, mine, at, keepdims=False)
        send = lax.dynamic_index_in_dim(x, 1 - mine, at, keepdims=False)
        x = keep + swap(send, bit, count)
        gone.append(axis)
    return x


def rotary_lanes(length, piece):
    lane = jnp.arange(128, dtype=jnp.int32) % HEAD_DIM
    step = (lane % (ROT // 2)).astype(f32)
    inverse = jnp.exp(step * (-2.0 * math.log(10000.0) / ROT))
    angles = jnp.arange(length, dtype=jnp.int32).astype(f32)[:, None] * inverse[None, :]
    cosine = jnp.where(lane < ROT, jnp.cos(angles), 1.0)
    sine = jnp.sin(angles)
    up = jnp.where((lane >= ROT // 2) & (lane < ROT), sine, 0.0)
    down = jnp.where(lane < ROT // 2, -sine, 0.0)
    return [t.reshape(-1, 2, piece, 128) for t in (cosine, up, down)]


def local_fast(
    streams, history, teacher, prefix, valid_mask, loss_scale, projections, attention_out,
    up_weight, down_weight, mixer_first, mixer_second, mixer_bias, gains,
):
    lines = lax.axis_size("ctx")
    count = lax.axis_size("dp") * lines
    place = lax.axis_index("ctx")
    group = lax.axis_index("dp")
    me = group * lines + place
    half = group % 2
    mine = 2 * (place % 2) + half
    seqs, rows, width = streams.shape[1:]
    tokens = seqs * rows
    piece = rows // 2
    length = rows * lines
    features = width // 2
    hidden_units = down_weight.shape[0] * count
    past = history.shape[0]
    count_of_streams = teacher.shape[0]
    mixw = mixer_bias.shape[0]
    span = 64

    def out_perm(k):
        pairs = []
        for i in range(count):
            pair, core, z = i // (2 * lines), (i // lines) % 2, i % lines
            code = z ^ k
            pairs.append((i, (pair * 2 + code % 2) * lines + 2 * core + code // 2))
        return pairs

    def send_out(x, k):
        return lax.ppermute(x, AXES, out_perm(k))

    def send_back(x, k):
        return lax.ppermute(x, AXES, [(b, a) for a, b in out_perm(k)])

    by_code = streams.reshape(streams.shape[0], 2 * seqs, piece, width)
    received = [
        send_out(
            lax.dynamic_slice(by_code, (0, place ^ k, 0, 0), (3, 1, piece, width)).reshape(
                3, piece, width
            ),
            k,
        )
        for k in range(4)
    ]
    both_prefix = swap(prefix, lines, count)
    source_half = place // 2
    prefix_pair = jnp.where(source_half == half, prefix, both_prefix)
    my_prefix = jnp.where(place % 2 == 0, prefix_pair[0], prefix_pair[1])
    ids = jnp.stack([place, half, mine, my_prefix]).astype(jnp.int32)

    small = gather_all(jnp.concatenate([gains, mixer_first.T], axis=0), me, count)
    small = small.transpose(1, 0, 2).reshape(-1, width)
    gain_full = jnp.pad(small[:5], ((0, 3), (0, 0))).astype(f32)
    first_t = jnp.pad(small[5:], ((0, span - mixw), (0, 0)))
    second = jnp.pad(mixer_second, ((0, span - mixw), (0, span - mixw)))
    bias = jnp.pad(mixer_bias, (0, span - mixw))[None]
    valid = valid_mask.astype(f32).reshape(tokens, 1)
    token_total = add_all(jnp.sum(valid).reshape(1), count)
    factor = loss_scale * 2.0 / (4.0 * width * token_total)

    proj_full = lax.all_gather(projections, AXES, axis=1, tiled=True)
    out_full = lax.all_gather(attention_out, AXES, axis=0, tiled=True)
    up_full = lax.all_gather(up_weight, AXES, axis=0, tiled=True)
    down_full = lax.all_gather(down_weight, AXES, axis=0, tiled=True)

    smem = pl.BlockSpec(memory_space=pltpu.SMEM)
    piece_shape = (3, lines, piece, width)
    normed_own = pl.pallas_call(
        norm_body,
        in_specs=[smem] + [vmem()] * 5,
        out_specs=vmem(),
        out_shape=jax.ShapeDtypeStruct(piece_shape, bf16),
        compiler_params=params(),
        name="stream_norm",
    )(ids, *received, gain_full)
    normed_other = swap(normed_own, lines, count)

    tables = rotary_lanes(length, piece)
    wide = jax.ShapeDtypeStruct((lines, 2, piece, features), bf16)

    def weight_spec(s):
        return pl.BlockSpec((1, width, features), lambda i, ids: (s, 0, ids[1]))

    def whole(shape):
        return pl.BlockSpec(shape, lambda i, ids: (0,) * len(shape))

    heads_seq, lse, queries, keys, values = pl.pallas_call(
        attention_forward_body,
        grid_spec=pltpu.PrefetchScalarGridSpec(
            num_scalar_prefetch=1,
            grid=(1,),
            in_specs=[whole(piece_shape), whole(piece_shape)]
            + [weight_spec(s) for s in range(3)]
            + [whole((lines, 2, piece, 128))] * 3,
            out_specs=[whole((lines, rows, features)), whole((lines, rows, 8))]
            + [whole((lines, 2, piece, features))] * 3,
        ),
        out_shape=[
            jax.ShapeDtypeStruct((lines, rows, features), bf16),
            jax.ShapeDtypeStruct((lines, rows, 8), f32),
            wide,
            wide,
            wide,
        ],
        compiler_params=params(),
        name="attention_forward",
    )(ids, normed_own, normed_other, proj_full, proj_full, proj_full, *tables)

    heads = [
        send_back(lax.dynamic_index_in_dim(heads_seq, mine ^ k, 0, keepdims=False), k)
        for k in range(4)
    ]

    tile = 512
    tiles = hidden_units // tile
    token_shape = (seqs, rows, width)

    def fixed(shape, index=None):
        index = index or (0,) * len(shape)
        return pl.BlockSpec(shape, lambda i, *_: index)

    hidden, normed_mlp, active, slope, layer_out = pl.pallas_call(
        mlp_forward_body,
        grid_spec=pltpu.PrefetchScalarGridSpec(
            num_scalar_prefetch=1,
            grid=(tiles,),
            in_specs=[fixed((rows, features))] * 4
            + [
                fixed((1,) + token_shape, (3, 0, 0, 0)),
                fixed((width, width)),
                fixed((8, width)),
                pl.BlockSpec((width, tile), lambda i, *_: (0, i)),
                pl.BlockSpec((tile, width), lambda i, *_: (i, 0)),
            ],
            out_specs=[
                fixed(token_shape),
                fixed(token_shape),
                pl.BlockSpec((tokens, tile), lambda i, *_: (0, i)),
                pl.BlockSpec((tokens, tile), lambda i, *_: (0, i)),
                fixed(token_shape),
            ],
        ),
        out_shape=[
            jax.ShapeDtypeStruct(token_shape, f32),
            jax.ShapeDtypeStruct(token_shape, bf16),
            jax.ShapeDtypeStruct((tokens, hidden_units), bf16),
            jax.ShapeDtypeStruct((tokens, hidden_units), bf16),
            jax.ShapeDtypeStruct(token_shape, f32),
        ],
        compiler_params=params(),
        name="mlp_forward",
    )(ids, *heads, streams, out_full, gain_full, up_full, down_full)

    block = 64
    next_streams, grad_history, grad_layer, g_first, g_second, stats, g_gain_mix = pl.pallas_call(
        mixer_body,
        grid=(tokens // block,),
        in_specs=[
            smem,
            pl.BlockSpec((block, width), lambda i: (i, 0)),
            pl.BlockSpec((past, block, width), lambda i: (0, i, 0)),
            pl.BlockSpec((count_of_streams, block, width), lambda i: (0, i, 0)),
            pl.BlockSpec((block, 1), lambda i: (i, 0)),
            fixed((8, width)),
            fixed((span, width)),
            fixed((span, span)),
            fixed((1, span)),
        ],
        out_specs=[
            pl.BlockSpec((count_of_streams, block, width), lambda i: (0, i, 0)),
            pl.BlockSpec((past, block, width), lambda i: (0, i, 0)),
            pl.BlockSpec((block, width), lambda i: (i, 0)),
            fixed((span, width)),
            fixed((span, span)),
            fixed((8, span)),
            fixed((1, width)),
        ],
        out_shape=[
            jax.ShapeDtypeStruct((count_of_streams, tokens, width), bf16),
            jax.ShapeDtypeStruct((past, tokens, width), bf16),
            jax.ShapeDtypeStruct((tokens, width), f32),
            jax.ShapeDtypeStruct((span, width), f32),
            jax.ShapeDtypeStruct((span, span), f32),
            jax.ShapeDtypeStruct((8, span), f32),
            jax.ShapeDtypeStruct((1, width), f32),
        ],
        scratch_shapes=[
            pltpu.VMEM((mixw, block, 128), f32),
            pltpu.VMEM((mixw, block, 128), f32),
            pltpu.VMEM((count_of_streams, block, width), f32),
        ],
        compiler_params=params(),
        name="mixer",
    )(
        factor,
        layer_out.reshape(tokens, width),
        history.reshape(past, tokens, width),
        teacher.reshape(count_of_streams, tokens, width),
        valid,
        gain_full,
        first_t,
        second,
        bias,
    )

    g_down, g_up, g_streams, gh0, gh1, gh2, gh3, g_out, g_gain_mlp = pl.pallas_call(
        mlp_backward_body,
        grid_spec=pltpu.PrefetchScalarGridSpec(
            num_scalar_prefetch=1,
            grid=(tiles,),
            in_specs=[
                fixed(token_shape),
                pl.BlockSpec((tokens, tile), lambda i, *_: (0, i)),
                pl.BlockSpec((tokens, tile), lambda i, *_: (0, i)),
                fixed(token_shape),
                pl.BlockSpec((width, tile), lambda i, *_: (0, i)),
                pl.BlockSpec((tile, width), lambda i, *_: (i, 0)),
                fixed(token_shape),
            ]
            + [fixed((rows, features))] * 4
            + [fixed((width, width)), fixed((8, width))],
            out_specs=[
                pl.BlockSpec((tile, width), lambda i, *_: (i, 0)),
                pl.BlockSpec((width, tile), lambda i, *_: (0, i)),
                pl.BlockSpec((None,) + token_shape, lambda i, *_: (3, 0, 0, 0)),
            ]
            + [fixed((rows, features))] * 4
            + [fixed((width, width)), fixed((1, width))],
            scratch_shapes=[
                pltpu.VMEM(token_shape, bf16),
                pltpu.VMEM(token_shape, f32),
                pltpu.VMEM((width, tokens), bf16),
                pltpu.VMEM((width, width), f32),
            ],
        ),
        out_shape=[
            jax.ShapeDtypeStruct((hidden_units, width), bf16),
            jax.ShapeDtypeStruct((width, hidden_units), bf16),
            jax.ShapeDtypeStruct(streams.shape, bf16),
        ]
        + [jax.ShapeDtypeStruct((rows, features), bf16)] * 4
        + [
            jax.ShapeDtypeStruct((width, width), bf16),
            jax.ShapeDtypeStruct((1, width), f32),
        ],
        compiler_params=params(),
        name="mlp_backward",
    )(
        ids, grad_layer.reshape(token_shape), active, slope, normed_mlp, up_full, down_full,
        hidden, *heads, out_full, gain_full,
    )

    sum_down = lax.psum_scatter(g_down, AXES, scatter_dimension=0, tiled=True).astype(f32)
    sum_up = lax.psum_scatter(g_up, AXES, scatter_dimension=0, tiled=True).astype(f32)
    sum_out = lax.psum_scatter(g_out, AXES, scatter_dimension=0, tiled=True).astype(f32)

    def scatter_columns(x):
        bits = count.bit_length() - 1
        x = x.reshape(x.shape[0], count, -1).transpose(1, 0, 2)
        x = x.reshape((2,) * bits + x.shape[1:])
        order = [(1 << (bits - 1 - axis), axis) for axis in range(bits)]
        return scatter_sum(x, order, me, count)

    g_head_rows = [send_out(g, k) for k, g in enumerate((gh0, gh1, gh2, gh3))]

    pairs = features // 128

    def pair_spec(shape):
        return pl.BlockSpec(shape + (128,), lambda i, *_: (0,) * len(shape) + (i,))

    d_own, d_send = pl.pallas_call(
        attention_backward_body,
        grid_spec=pltpu.PrefetchScalarGridSpec(
            num_scalar_prefetch=1,
            grid=(pairs,),
            in_specs=[pair_spec((lines, 2, piece))] * 3
            + [pair_spec((lines, rows)), fixed((8, lines, 1, rows))]
            + [pair_spec((rows,))] * 4
            + [fixed((lines, 2, piece, 128))] * 3,
            out_specs=[pair_spec((3, lines, piece))] * 2,
            scratch_shapes=[
                pltpu.VMEM((length, 128), f32),
                pltpu.VMEM((length, 128), f32),
                pltpu.VMEM((128, length), bf16),
                pltpu.VMEM((lines, 2, piece, 128), bf16),
            ],
        ),
        out_shape=[jax.ShapeDtypeStruct((3, lines, piece, features), bf16)] * 2,
        compiler_params=params(),
        name="attention_backward",
    )(
        ids, queries, keys, values, heads_seq,
        lse.reshape(length, 8).T.reshape(8, lines, 1, rows), *g_head_rows, *tables,
    )
    d_recv = swap(d_send, lines, count)

    def stream_spec(shape):
        return pl.BlockSpec((1,) + shape, lambda s, *_: (s,) + (0,) * len(shape))

    back_piece = (piece, width)
    g_proj, b0, b1, b2, b3, g_gain_three = pl.pallas_call(
        projection_backward_body,
        grid_spec=pltpu.PrefetchScalarGridSpec(
            num_scalar_prefetch=1,
            grid=(3,),
            in_specs=[stream_spec((lines, piece, width))] * 2
            + [stream_spec((lines, piece, features))] * 3
            + [
                pl.BlockSpec((1, width, features), lambda s, ids: (s, 0, ids[1])),
                pl.BlockSpec((1, width, features), lambda s, ids: (s, 0, 1 - ids[1])),
            ]
            + [stream_spec(back_piece)] * 4
            + [fixed((8, width))],
            out_specs=[stream_spec((width, features))]
            + [stream_spec(back_piece)] * 4
            + [stream_spec((1, width))],
        ),
        out_shape=[jax.ShapeDtypeStruct((3, width, features), bf16)]
        + [jax.ShapeDtypeStruct((3,) + back_piece, bf16)] * 4
        + [jax.ShapeDtypeStruct((3, 1, width), f32)],
        compiler_params=params(),
        name="projection_backward",
    )(
        ids, normed_own, normed_other, d_own, d_send, d_recv, proj_full, proj_full,
        *received, gain_full,
    )

    grad_streams = g_streams.reshape(streams.shape[0], 2 * seqs, piece, width)
    for k, b in enumerate((b0, b1, b2, b3)):
        grad_streams = lax.dynamic_update_slice(
            grad_streams, send_back(b, k)[:, None], (0, place ^ k, 0, 0)
        )
    grad_streams = grad_streams.reshape(streams.shape)

    shard = projections.shape[1]
    bits = count.bit_length() - 1
    core_axis = bits - lines.bit_length()
    cut = g_proj.reshape((3,) + (2,) * bits + (shard, features))
    steps = [(1 << (bits - 1 - axis), axis + 1) for axis in range(bits) if axis != core_axis]
    quarter = features // 2
    parts = []
    for n in range(2):
        order = steps if n == 0 else [steps[1], steps[0]] + steps[2:]
        parts.append(
            scatter_sum(cut[..., n * quarter : (n + 1) * quarter], order, me, count)
        )
    total = jnp.concatenate(parts, axis=-1)
    kept = lax.dynamic_index_in_dim(total, half, 1, keepdims=False)
    sent = swap(lax.dynamic_index_in_dim(total, 1 - half, 1, keepdims=False), lines, count)
    low = half == 0
    grad_projections = jnp.concatenate(
        [jnp.where(low, kept, sent), jnp.where(low, sent, kept)], axis=-1
    ).astype(f32)

    early = scatter_columns(
        jnp.concatenate([g_first[:mixw], g_gain_mlp, g_gain_mix], axis=0)
    )
    late = scatter_columns(g_gain_three.reshape(3, width))
    grad_first = early[:mixw].T
    grad_gains = jnp.concatenate([late, early[mixw:]], axis=0)
    totals = add_all(jnp.concatenate([g_second, stats], axis=0), count)
    grad_second = totals[:mixw, :mixw]
    grad_bias = totals[span, :mixw]
    mean_loss = totals[span + 1, 0] / (4.0 * width * token_total[0])
    return (
        next_streams.reshape(teacher.shape),
        mean_loss,
        grad_streams,
        grad_history.reshape(history.shape),
        grad_projections,
        sum_out,
        sum_up,
        sum_down,
        grad_first,
        grad_second,
        grad_bias,
        grad_gains,
    )


def layer_norm(values, gain_row):
    centered = values - jnp.mean(values, axis=-1, keepdims=True)
    return (
        centered
        * lax.rsqrt(jnp.mean(centered * centered, axis=-1, keepdims=True) + epsilon)
        * gain_row
    )


def rms_norm(values, gain_row):
    return (
        values * lax.rsqrt(jnp.mean(values * values, axis=-1, keepdims=True) + epsilon) * gain_row
    )


def gelu_exact(values):
    return jax.nn.gelu(values, approximate=False)


def rotary_tables(positions):
    frequency_steps = jnp.arange(ROT // 2).astype(positions.dtype)
    inverse = jnp.exp(frequency_steps * (-2.0 * math.log(10000.0) / ROT))
    angles = positions[:, None] * inverse[None, :]
    return (jnp.cos(angles)[:, None, :], jnp.sin(angles)[:, None, :])


def rotate(values, cosine_table, sine_table, direction):
    row_count = values.shape[0]
    shaped = values.reshape(row_count, HEADS, HEAD_DIM)
    half_rot = ROT // 2
    first_half = shaped[:, :, :half_rot]
    second_half = shaped[:, :, half_rot:ROT]
    remainder = shaped[:, :, ROT:]
    turned_first = first_half * cosine_table - direction * second_half * sine_table
    turned_second = second_half * cosine_table + direction * first_half * sine_table
    return jnp.concatenate([turned_first, turned_second, remainder], axis=-1).reshape(row_count, -1)


def masked_scores(query_heads, key_heads, query_index, key_index, prefix_len):
    scores = jnp.einsum(
        "qhd,khd->hqk", query_heads, key_heads, preferred_element_type=jnp.float32
    ) * HEAD_DIM ** (-0.5)
    allowed = (key_index[None, :] <= query_index[:, None]) | (key_index[None, :] < prefix_len)
    return jnp.where(allowed[None], scores, -1e30)


def local_plain(
    streams,
    history,
    teacher,
    prefix,
    valid_mask,
    loss_scale,
    projections,
    attention_out,
    up_weight,
    down_weight,
    mixer_first,
    mixer_second,
    mixer_bias,
    gains,
):
    micro_count = streams.shape[1]
    row_count = streams.shape[2]
    model_width = streams.shape[3]
    length = row_count * lax.axis_size("ctx")
    query_index = lax.axis_index("ctx") * row_count + jnp.arange(row_count, dtype=jnp.int32)
    key_index = jnp.arange(length, dtype=jnp.int32)
    cosine_table, sine_table = rotary_tables(query_index.astype(jnp.float32))
    score_scale = HEAD_DIM ** (-0.5)
    valid_float = valid_mask.astype(jnp.float32)
    token_total = lax.psum(jnp.sum(valid_float), ("dp", "ctx"))
    factor = loss_scale[0] * 2.0 / (4.0 * model_width * token_total)

    def one_batch(totals, number):
        (
            kept_projections,
            kept_attention,
            kept_gains,
            kept_up,
            kept_down,
            kept_first,
            kept_second,
            kept_bias,
            kept_loss,
        ) = totals
        stream_block = lax.dynamic_index_in_dim(streams, number, 1, keepdims=False)
        past_outputs = lax.dynamic_index_in_dim(history, number, 1, keepdims=False)
        target = lax.dynamic_index_in_dim(teacher, number, 1, keepdims=False).astype(jnp.float32)
        prefix_len = lax.dynamic_index_in_dim(prefix, number, 0, keepdims=False)
        valid_row = lax.dynamic_index_in_dim(valid_float, number, 0, keepdims=False)
        proj_full, out_full, gain_low, up_full, down_full, first_full = (
            lax.all_gather(projections, ("dp", "ctx"), axis=1, tiled=True),
            lax.all_gather(attention_out, ("dp", "ctx"), axis=0, tiled=True),
            lax.all_gather(gains, ("dp", "ctx"), axis=1, tiled=True),
            lax.all_gather(up_weight, ("dp", "ctx"), axis=0, tiled=True),
            lax.all_gather(down_weight, ("dp", "ctx"), axis=0, tiled=True),
            lax.all_gather(mixer_first, ("dp", "ctx"), axis=0, tiled=True),
        )
        gain_full = gain_low.astype(jnp.float32)
        inputs = stream_block.astype(jnp.float32)
        gain_three = gain_full[:3, None, :]
        normed_low = layer_norm(inputs[:3], gain_three).astype(jnp.bfloat16)
        projected = jnp.einsum(
            "std,sde->ste", normed_low, proj_full, preferred_element_type=jnp.float32
        )
        query_heads = (
            rotate(projected[0], cosine_table, sine_table, 1.0)
            .astype(jnp.bfloat16)
            .reshape(row_count, HEADS, HEAD_DIM)
        )
        key_low = rotate(projected[1], cosine_table, sine_table, 1.0).astype(jnp.bfloat16)
        value_low = projected[2].astype(jnp.bfloat16)
        all_keys, all_values = (
            lax.all_gather(key_low, "ctx", axis=0, tiled=True),
            lax.all_gather(value_low, "ctx", axis=0, tiled=True),
        )
        key_heads = all_keys.reshape(length, HEADS, HEAD_DIM)
        value_heads = all_values.reshape(length, HEADS, HEAD_DIM)
        scores = masked_scores(query_heads, key_heads, query_index, key_index, prefix_len)
        row_max = jnp.max(scores, axis=-1, keepdims=True)
        log_total = row_max + jnp.log(jnp.sum(jnp.exp(scores - row_max), axis=-1, keepdims=True))
        probs_low = jnp.exp(scores - log_total).astype(jnp.bfloat16)
        heads_low = (
            jnp.einsum("hqk,khd->qhd", probs_low, value_heads, preferred_element_type=jnp.float32)
            .reshape(row_count, model_width)
            .astype(jnp.bfloat16)
        )
        hidden = inputs[3] + jnp.dot(heads_low, out_full, preferred_element_type=jnp.float32)
        normed_mlp = layer_norm(hidden, gain_full[3]).astype(jnp.bfloat16)
        upper = jnp.dot(normed_mlp, up_full, preferred_element_type=jnp.float32)
        activated = gelu_exact(upper).astype(jnp.bfloat16)
        layer_out = hidden + jnp.dot(activated, down_full, preferred_element_type=jnp.float32)
        normed_mix = rms_norm(layer_out, gain_full[4]).astype(jnp.bfloat16)
        mix_hidden = jnp.dot(normed_mix, first_full, preferred_element_type=jnp.float32)
        mix_active = gelu_exact(mix_hidden)
        coeff = jnp.dot(mix_active, mixer_second, precision=highest) + mixer_bias
        coeff_grid = coeff.reshape(row_count, 4, -1)
        outputs_all = jnp.concatenate([past_outputs.astype(jnp.float32), layer_out[None]], axis=0)
        next_block = jnp.einsum("tsj,jtd->std", coeff_grid, outputs_all, precision=highest)
        difference = next_block - target
        loss_part = jnp.sum(jnp.sum(difference * difference, axis=(0, 2)) * valid_row) / (
            4.0 * model_width * token_total
        )
        grad_next = factor * valid_row[None, :, None] * difference
        grad_coeff = jnp.einsum("std,jtd->tsj", grad_next, outputs_all, precision=highest).reshape(
            row_count, -1
        )
        grad_outputs = jnp.einsum("tsj,std->jtd", coeff_grid, grad_next, precision=highest)
        grad_past = grad_outputs[:-1].astype(jnp.bfloat16)
        grad_second = jnp.dot(mix_active.T, grad_coeff, precision=highest)
        grad_bias = jnp.sum(grad_coeff, axis=0)
        grad_active = jnp.dot(grad_coeff, mixer_second.T, precision=highest)
        gelu_mix_back = jax.vjp(gelu_exact, mix_hidden)[1]
        grad_mix = gelu_mix_back(grad_active)[0].astype(jnp.bfloat16)
        grad_first = jnp.einsum(
            "td,tm->dm", normed_mix, grad_mix, preferred_element_type=jnp.float32
        )
        grad_normed_mix = jnp.einsum(
            "tm,dm->td", grad_mix, first_full, preferred_element_type=jnp.float32
        )
        rms_back = jax.vjp(rms_norm, layer_out, gain_full[4])[1]
        grad_layer_mix, grad_gain_mix = rms_back(grad_normed_mix)
        grad_layer = grad_outputs[-1] + grad_layer_mix
        grad_branch = grad_layer.astype(jnp.bfloat16)
        grad_down = jnp.einsum(
            "tf,td->fd", activated, grad_branch, preferred_element_type=jnp.float32
        )
        grad_active_up = jnp.einsum(
            "td,fd->tf", grad_branch, down_full, preferred_element_type=jnp.float32
        )
        gelu_up_back = jax.vjp(gelu_exact, upper)[1]
        grad_upper = gelu_up_back(grad_active_up)[0].astype(jnp.bfloat16)
        grad_up = jnp.einsum(
            "td,tf->df", normed_mlp, grad_upper, preferred_element_type=jnp.float32
        )
        grad_normed_mlp = jnp.einsum(
            "tf,df->td", grad_upper, up_full, preferred_element_type=jnp.float32
        )
        down_shard, first_shard, up_shard = (
            lax.psum_scatter(grad_down, ("dp", "ctx"), scatter_dimension=0, tiled=True),
            lax.psum_scatter(grad_first, ("dp", "ctx"), scatter_dimension=0, tiled=True),
            lax.psum_scatter(grad_up, ("dp", "ctx"), scatter_dimension=0, tiled=True),
        )
        down_next = kept_down + down_shard
        norm_mlp_back = jax.vjp(layer_norm, hidden, gain_full[3])[1]
        grad_hidden_mlp, grad_gain_mlp = norm_mlp_back(grad_normed_mlp)
        grad_hidden = grad_layer + grad_hidden_mlp
        grad_attn = grad_hidden.astype(jnp.bfloat16)
        grad_attention = jnp.einsum(
            "td,te->de", heads_low, grad_attn, preferred_element_type=jnp.float32
        )
        grad_heads = jnp.einsum(
            "te,de->td", grad_attn, out_full, preferred_element_type=jnp.float32
        ).astype(jnp.bfloat16)
        grad_head_grid = grad_heads.reshape(row_count, HEADS, HEAD_DIM)
        scores_again = masked_scores(query_heads, key_heads, query_index, key_index, prefix_len)
        probs_exact = jnp.exp(scores_again - log_total)
        probs_again = probs_exact.astype(jnp.bfloat16)
        grad_probs = jnp.einsum(
            "qhd,khd->hqk", grad_head_grid, value_heads, preferred_element_type=jnp.float32
        )
        row_inner = jnp.sum(probs_exact * grad_probs, axis=-1, keepdims=True)
        grad_scores = (probs_exact * (grad_probs - row_inner)).astype(jnp.bfloat16)
        grad_queries = (
            jnp.einsum(
                "hqk,khd->qhd", grad_scores, key_heads, preferred_element_type=jnp.float32
            ).reshape(row_count, model_width)
            * score_scale
        )
        grad_key_part = (
            jnp.einsum("hqk,qhd->khd", grad_scores, query_heads, preferred_element_type=jnp.float32)
            * score_scale
        )
        grad_value_part = jnp.einsum(
            "hqk,qhd->khd", probs_again, grad_head_grid, preferred_element_type=jnp.float32
        )
        key_grads = lax.psum_scatter(
            jnp.concatenate(
                [
                    grad_key_part.reshape(row_count * lax.axis_size("ctx"), -1),
                    grad_value_part.reshape(row_count * lax.axis_size("ctx"), -1),
                ],
                axis=-1,
            ).astype(jnp.bfloat16),
            "ctx",
            scatter_dimension=0,
            tiled=True,
        ).astype(jnp.float32)
        grad_query_low = rotate(grad_queries, cosine_table, sine_table, -1.0).astype(jnp.bfloat16)
        grad_key_low = rotate(key_grads[:, :model_width], cosine_table, sine_table, -1.0).astype(
            jnp.bfloat16
        )
        grad_value_low = key_grads[:, model_width:].astype(jnp.bfloat16)
        grad_projected = jnp.stack([grad_query_low, grad_key_low, grad_value_low])
        grad_proj = jnp.einsum(
            "std,ste->sde", normed_low, grad_projected, preferred_element_type=jnp.float32
        )
        grad_normed = jnp.einsum(
            "ste,sde->std", grad_projected, proj_full, preferred_element_type=jnp.float32
        )
        norm_three_back = jax.vjp(layer_norm, inputs[:3], gain_three)[1]
        grad_inputs_three, grad_gain_three = norm_three_back(grad_normed)
        grad_gain_all = jnp.concatenate(
            [grad_gain_three.reshape(3, -1), grad_gain_mlp[None], grad_gain_mix[None]], axis=0
        )
        proj_shard, attention_shard, gain_shard = (
            lax.psum_scatter(grad_proj, ("dp", "ctx"), scatter_dimension=1, tiled=True),
            lax.psum_scatter(grad_attention, ("dp", "ctx"), scatter_dimension=0, tiled=True),
            lax.psum_scatter(grad_gain_all, ("dp", "ctx"), scatter_dimension=1, tiled=True),
        )
        grad_block = jnp.concatenate([grad_inputs_three, grad_hidden[None]], axis=0).astype(
            jnp.bfloat16
        )
        new_totals = (
            kept_projections + proj_shard,
            kept_attention + attention_shard,
            kept_gains + gain_shard,
            kept_up + up_shard,
            down_next,
            kept_first + first_shard,
            kept_second + grad_second,
            kept_bias + grad_bias,
            kept_loss + loss_part,
        )
        return (new_totals, (next_block.astype(jnp.bfloat16), grad_block, grad_past))

    down_start = jnp.zeros(down_weight.shape, jnp.float32)
    start_totals = (
        jnp.zeros(projections.shape, jnp.float32),
        jnp.zeros(attention_out.shape, jnp.float32),
        jnp.zeros(gains.shape, jnp.float32),
        jnp.zeros(up_weight.shape, jnp.float32),
        down_start,
        jnp.zeros(mixer_first.shape, jnp.float32),
        jnp.zeros(mixer_second.shape, jnp.float32),
        jnp.zeros(mixer_bias.shape, jnp.float32),
        jnp.zeros((), jnp.float32),
    )
    final_totals, stacked = lax.scan(
        one_batch, start_totals, jnp.arange(micro_count, dtype=jnp.int32)
    )
    (
        sum_projections,
        sum_attention,
        sum_gains,
        sum_up,
        sum_down,
        sum_first,
        sum_second,
        sum_bias,
        sum_loss,
    ) = final_totals
    grad_second_all, grad_bias_all, loss_all = lax.psum(
        (sum_second, sum_bias, sum_loss), ("dp", "ctx")
    )
    next_streams = jnp.moveaxis(stacked[0], 0, 1)
    grad_streams = jnp.moveaxis(stacked[1], 0, 1)
    grad_history = jnp.moveaxis(stacked[2], 0, 1)
    return (
        next_streams,
        loss_all,
        grad_streams,
        grad_history,
        sum_projections,
        sum_attention,
        sum_up,
        sum_down,
        sum_first,
        grad_second_all,
        grad_bias_all,
        sum_gains,
    )


def fits(mesh):
    return mesh.shape["ctx"] == 4 and mesh.shape["dp"] % 2 == 0


def solution(mesh):
    specs = dict(
        in_specs=(
            P(None, "dp", "ctx", None),
            P(None, "dp", "ctx", None),
            P(None, "dp", "ctx", None),
            P("dp"),
            P("dp", "ctx"),
            P(),
            P(None, ("dp", "ctx"), None),
            P(("dp", "ctx"), None),
            P(("dp", "ctx"), None),
            P(("dp", "ctx"), None),
            P(("dp", "ctx"), None),
            P(),
            P(),
            P(None, ("dp", "ctx")),
        ),
        out_specs=(
            P(None, "dp", "ctx", None),
            P(),
            P(None, "dp", "ctx", None),
            P(None, "dp", "ctx", None),
            P(None, ("dp", "ctx"), None),
            P(("dp", "ctx"), None),
            P(("dp", "ctx"), None),
            P(("dp", "ctx"), None),
            P(("dp", "ctx"), None),
            P(),
            P(),
            P(None, ("dp", "ctx")),
        ),
        check_vma=False,
    )

    def chosen(*arrays):
        fast = fits(mesh) and arrays[0].shape[1] == 2 * mesh.shape["dp"]
        return jax.shard_map(local_fast if fast else local_plain, mesh=mesh, **specs)(*arrays)

    return chosen
```

```python
import functools
import math

import jax
import jax.numpy as jnp
from jax import lax
from jax.experimental import pallas as pl
from jax.experimental.pallas import tpu as pltpu
from jax.sharding import PartitionSpec as P

HEADS = 16
HEAD_DIM = 64
ROT = 16
AXES = ("dp", "ctx")

highest = lax.Precision.HIGHEST
epsilon = 1e-05
f32 = jnp.float32
bf16 = jnp.bfloat16
VMEM_BYTES = 60 * 1024 * 1024


def dot_nn(a, b, precision=None):
    return lax.dot_general(
        a, b, (((1,), (0,)), ((), ())), precision=precision, preferred_element_type=f32
    )


def dot_nt(a, b, precision=None):
    return lax.dot_general(
        a, b, (((1,), (1,)), ((), ())), precision=precision, preferred_element_type=f32
    )


def dot_tn(a, b, precision=None):
    return lax.dot_general(
        a, b, (((0,), (0,)), ((), ())), precision=precision, preferred_element_type=f32
    )


def normal_cdf(v):
    z = jnp.abs(v) * math.sqrt(0.5)
    t = 1.0 / (1.0 + 0.39 * z)
    bell = jnp.exp(-0.5 * v * v)
    poly = -0.22760540438261295
    for c in (
        0.8869388009365644,
        -0.6358388689155755,
        0.649907738051149,
        0.09125094908545259,
        0.23534677935551734,
    ):
        poly = poly * t + c
    half_tail = (0.5 * poly) * t * bell
    return jnp.where(v < 0.0, half_tail, 1.0 - half_tail), bell


def gelu_pair(v):
    cdf, bell = normal_cdf(v)
    return v * cdf, cdf + v * bell * (1.0 / math.sqrt(2.0 * math.pi))


def vmem(block=None, index_map=None):
    if block is None:
        return pl.BlockSpec(memory_space=pltpu.VMEM)
    return pl.BlockSpec(block, index_map)


def params(**kw):
    return pltpu.CompilerParams(vmem_limit_bytes=VMEM_BYTES, **kw)


Z_ORDER = (0, 2, 1, 3)


def place_rows(me, ref, base_bits, out_ref):
    rows = ref.shape[-2]
    for b, base in enumerate(base_bits):
        for q, z in enumerate(Z_ORDER):
            device = jnp.bitwise_xor(me, base | z)
            at = pl.ds(pl.multiple_of(device * rows, rows), rows)
            out_ref[at, :] = ref[b * 4 + q]


def place_rows_of_projection(me, s, ref, out_ref):
    rows = ref.shape[-2]
    for xy in range(4):
        for q, z in enumerate(Z_ORDER):
            for core in range(2):
                device = jnp.bitwise_xor(me, 8 * (xy // 2) + 16 * (xy % 2) + 4 * core + z)
                at = pl.ds(pl.multiple_of(device * rows, rows), rows)
                out_ref[at, :] = ref[xy * 4 + q, core, s]


def place_tile(me, step, ups, downs, up_ref, down_ref):
    for p, ref in enumerate(ups):
        base = 8 * (p % 2) + 4 * (p // 2)
        place_rows(me, ref, (base, base + 16), up_ref)
    place = lax.rem(me, 4)
    for p, ref in enumerate(downs):

        @pl.when(lax.div(step, 2) == p)
        def _(ref=ref):
            rows = ref.shape[1]
            for q, z in enumerate(Z_ORDER):
                at = pl.ds(pl.multiple_of(jnp.bitwise_xor(place, z) * rows, rows), rows)
                down_ref[at, :] = ref[q]


def place_output_weight(me, refs, out_ref):
    for p, ref in enumerate(refs):
        base = 16 * (p % 2) + 4 * (p // 2)
        place_rows(me, ref, (base, base + 8), out_ref)


class Place:
    def __init__(self):
        self.group = lax.axis_index("dp")
        self.z = lax.axis_index("ctx")
        self.core = lax.rem(self.group, 2)
        self.x = lax.rem(lax.div(self.group, 2), 2)
        self.y = lax.div(self.group, 4)
        self.z_low = lax.rem(self.z, 2)
        self.z_high = lax.div(self.z, 2)

    def across(self, axis):
        if axis == "core":
            return (self.group + 1 - 2 * self.core, self.z)
        if axis == "x":
            return (self.group + 2 - 4 * self.x, self.z)
        if axis == "y":
            return (self.group + 4 - 8 * self.y, self.z)
        if axis == "zl":
            return (self.group, self.z + 1 - 2 * self.z_low)
        return (self.group, self.z + 2 - 4 * self.z_high)

    def code(self, k):
        return flip(self.z_high, k // 2), flip(self.z_low, k % 2)

    def block(self, k):
        return flip(self.z_low, k // 2) * 2 + flip(self.core, k % 2)

    def out_to(self, k):
        seq, half = self.code(k)
        return (self.group - self.core + half, 2 * self.core + seq)

    def out_is_self(self, k):
        group, z = self.out_to(k)
        return jnp.logical_and(group == self.group, z == self.z)

    def back_to(self, k):
        return (self.group - self.core + self.z_high, self.block(k))

    def back_is_self(self, k):
        group, z = self.back_to(k)
        return jnp.logical_and(group == self.group, z == self.z)

    def meet(self, names, line):
        barrier = pltpu.get_barrier_semaphore()
        others = [self.across(name) for name in names]
        if line:
            for step in range(1, 8):
                place = self.core * 4 + self.z + step
                others.append(
                    (self.group - self.core + lax.rem(lax.div(place, 4), 2), lax.rem(place, 4))
                )
        for other in others:
            pl.semaphore_signal(barrier, inc=1, device_id=other, device_id_type=pl.DeviceIdType.MESH)
        pl.semaphore_wait(barrier, len(others))


def flip(bit, by):
    return 1 - bit if by else bit


class Sends:
    def __init__(self, send_sems, recv_sems):
        self.send_sems, self.recv_sems, self.used, self.open = send_sems, recv_sems, 0, []

    def make(self, source, target, device):
        n = self.used
        self.used += 1
        return pltpu.make_async_remote_copy(
            src_ref=source,
            dst_ref=target,
            send_sem=self.send_sems.at[n],
            recv_sem=self.recv_sems.at[n],
            device_id=device,
            device_id_type=pl.DeviceIdType.MESH,
        )

    def start(self, source, target, device):
        copy = self.make(source, target, device)
        copy.start()
        self.open.append((copy, None))
        return copy

    def start_or_keep(self, source, target, device, stays):
        copy = self.make(source, target, device)
        kept = pltpu.make_async_copy(source, target, self.recv_sems.at[self.used - 1])

        @pl.when(stays)
        def _():
            kept.start()

        @pl.when(jnp.logical_not(stays))
        def _():
            copy.start()

        self.open.append((copy, stays))
        return copy

    def finish(self):
        for copy, stays in self.open:
            if stays is None:
                copy.wait_send()
            else:

                @pl.when(jnp.logical_not(stays))
                def _(copy=copy):
                    copy.wait_send()


def front_body(
    streams_ref, proj_in, up_in, down_in, out_in, small_in, count_in,
    received_ref, own_ref, other_ref, proj_ref, up_ref, down_ref, small_ref, count_ref,
    small_got, count_got, local_sems, send_sems, recv_sems,
):
    here = Place()
    sends = Sends(send_sems, recv_sems)
    features = proj_ref.shape[-1]
    units = down_in.shape[0]
    here.meet(("x", "y"), True)

    def columns(which):
        return proj_in.at[:, :, pl.ds(pl.multiple_of(which * features, features), features)]

    proj_core = sends.start(columns(1 - here.core), proj_ref.at[0, 1], here.across("core"))
    locals_ = [
        pltpu.make_async_copy(columns(here.core), proj_ref.at[0, 0], local_sems.at[0]),
        pltpu.make_async_copy(up_in, up_ref.at[0], local_sems.at[1]),
        pltpu.make_async_copy(down_in, down_ref.at[0, pl.ds(0, units)], local_sems.at[2]),
        pltpu.make_async_copy(
            out_in, down_ref.at[0, pl.ds(units, out_in.shape[0])], local_sems.at[3]
        ),
    ]
    for copy in locals_:
        copy.start()

    small_ref[...] = small_in[...]
    count_ref[...] = count_in[...]
    small_steps = []

    def small_start(axis):
        n = len(small_steps)
        small_steps.append(
            (
                n,
                sends.start(small_ref, small_got.at[n], here.across(axis)),
                sends.start(count_ref, count_got.at[n], here.across(axis)),
            )
        )

    def small_end():
        n, a, b = small_steps[-1]
        a.wait()
        b.wait()
        small_ref[...] += small_got[n]
        count_ref[...] += count_got[n]
        sends.open = [o for o in sends.open if o[0] is not a and o[0] is not b]

    def widen(ref, n, axis):
        return sends.start(ref.at[pl.ds(0, n)], ref.at[pl.ds(n, n)], here.across(axis))

    def stream(s):
        copies = []
        for k in range(4):
            seq, half = here.code(k)
            copies.append(
                sends.start_or_keep(
                    streams_ref.at[s, 2 * seq + half],
                    received_ref.at[k, s],
                    here.out_to(k),
                    here.out_is_self(k),
                )
            )
        return copies

    small_start("core")
    small_end()
    small_start("x")
    for copy in locals_:
        copy.wait()
    proj_core.wait_recv()
    proj_zh = widen(proj_ref, 1, "zh")
    small_end()
    small_start("y")
    small_end()
    small_start("zl")
    up_zh = widen(up_ref, 1, "zh")
    small_end()
    small_start("zh")
    down_zh = widen(down_ref, 1, "zh")
    rows = {}
    rows[1] = stream(1)
    proj_zh.wait_recv()
    proj_zl = widen(proj_ref, 2, "zl")
    small_end()
    up_zh.wait_recv()
    up_zl = widen(up_ref, 2, "zl")
    down_zh.wait_recv()
    down_zl = widen(down_ref, 2, "zl")
    rows[2] = stream(2)
    proj_zl.wait_recv()
    proj_y = widen(proj_ref, 4, "y")
    rows[0] = stream(0)
    up_zl.wait_recv()
    up_y = widen(up_ref, 4, "y")
    down_zl.wait_recv()
    down_x = widen(down_ref, 4, "x")
    proj_y.wait_recv()
    proj_x = widen(proj_ref, 8, "x")

    chunk = 32
    arrivals = []
    for s in (1, 2, 0):
        gain = small_ref[s : s + 1, :].astype(f32)
        for k, copy in enumerate(rows[s]):
            copy.wait_recv()
            block = here.block(k)

            def body(i, _, s=s, k=k, gain=gain, block=block):
                at = pl.ds(pl.multiple_of(i * chunk, chunk), chunk)
                x = received_ref[k, s, at, :].astype(f32)
                x = x - jnp.mean(x, axis=-1, keepdims=True)
                scale = lax.rsqrt(jnp.mean(x * x, axis=-1, keepdims=True) + epsilon)
                own_ref[s, block, at, :] = (x * scale * gain).astype(bf16)
                return 0

            lax.fori_loop(0, received_ref.shape[2] // chunk, body, 0, unroll=2)
        arrivals.append(sends.start(own_ref.at[s], other_ref.at[s], here.across("core")))
    for copy in [proj_x, up_y, down_x] + arrivals:
        copy.wait_recv()
    sends.finish()


def turn(x, cosine, sine_up, sine_down):
    return (
        x * cosine + pltpu.roll(x, ROT // 2, 1) * sine_up + pltpu.roll(x, 128 - ROT // 2, 1) * sine_down
    )


def allowed_limit(base, rows, prefix, axis):
    shape = (rows, 1) if axis == 0 else (1, rows)
    position = base + lax.broadcasted_iota(jnp.int32, shape, axis)
    return jnp.maximum(position, prefix - 1)


def attention_forward_body(
    ids, own_ref, other_ref, proj_ref, cos_ref, up_ref, down_ref,
    heads_ref, lse_ref, q_ref, k_ref, v_ref,
    weight_ref,
):
    half = ids[1]
    prefix = ids[3]
    blocks, _, piece, width = q_ref.shape
    length = blocks * 2 * piece
    for s in range(3):
        place_rows_of_projection(ids[4], s, proj_ref, weight_ref.at[s])
    for part, source in ((0, own_ref), (1, other_ref)):
        place = jnp.bitwise_xor(half, part)
        for s, out_ref in ((0, q_ref), (1, k_ref), (2, v_ref)):
            x = source[s].reshape(blocks * piece, -1)
            y = dot_nn(x, weight_ref[s])
            if s < 2:
                cosine = cos_ref[:, place].reshape(blocks * piece, 128)
                sine_up = up_ref[:, place].reshape(blocks * piece, 128)
                sine_down = down_ref[:, place].reshape(blocks * piece, 128)
                y = jnp.concatenate(
                    [
                        turn(y[:, i : i + 128], cosine, sine_up, sine_down)
                        for i in range(0, width, 128)
                    ],
                    axis=1,
                )
            y = y.astype(bf16)
            if s == 0:
                y = y * jnp.asarray(HEAD_DIM**-0.5, bf16)
            out_ref[:, place] = y.reshape(blocks, piece, width)

    rows = 2 * piece
    lane = lax.broadcasted_iota(jnp.int32, (rows, 128), 1)
    key_index = lax.broadcasted_iota(jnp.int32, (rows, length), 1)

    def block_body(block, _):
        limit = allowed_limit(block * rows, rows, prefix, 0)
        allowed = key_index <= limit
        lse_all = jnp.zeros((rows, 8), f32)
        lse_lane = lax.broadcasted_iota(jnp.int32, (rows, 8), 1)
        for pair in range(width // 128):
            at = slice(pair * 128, pair * 128 + 128)
            queries = q_ref[block, :, :, at].reshape(rows, 128)
            keys = k_ref[:, :, :, at].reshape(length, 128)
            values = v_ref[:, :, :, at].reshape(length, 128)
            results = []
            for h in range(2):
                chosen = (lane < 64) if h == 0 else (lane >= 64)
                scores = dot_nt(jnp.where(chosen, queries, jnp.zeros_like(queries)), keys)
                scores = jnp.where(allowed, scores, -1e30)
                top = jnp.max(scores, axis=-1, keepdims=True)
                weights = jnp.exp(scores - top)
                total = jnp.sum(weights, axis=-1, keepdims=True)
                results.append(dot_nn(weights.astype(bf16), values) / total)
                lse_all = jnp.where(lse_lane == pair * 2 + h, top + jnp.log(total), lse_all)
            heads_ref[block, :, at] = jnp.where(lane < 64, results[0], results[1]).astype(bf16)
        lse_ref[block] = lse_all
        return 0

    lax.fori_loop(0, blocks, block_body, 0)


def mlp_forward_body(
    ids, h0, h1, h2, h3, res_ref, gain_ref, u0, u1, u2, u3, d0, d1, d2, d3, w0, w1, w2, w3,
    hidden_ref, normed_ref, active_ref, slope_ref, layer_ref,
    out_w_ref, up_ref, down_ref,
):
    step = pl.program_id(0)
    seqs, rows, width = res_ref.shape[1:]
    me = ids[4]

    @pl.when(step == 0)
    def _():
        place_output_weight(me, (w0, w1, w2, w3), out_w_ref)
        hidden_ref[...] = res_ref[0].astype(f32)
        for k, piece in enumerate((h0, h1, h2, h3)):
            code = jnp.bitwise_xor(ids[0], k)
            features = piece.shape[-1]
            at = pl.ds(pl.multiple_of(lax.rem(code, 2) * features, features), features)
            seq = lax.div(code, 2)
            hidden_ref[seq] += dot_nn(piece[...], out_w_ref[at, :])
        gain = gain_ref[3:4, :].astype(f32)
        for j in range(seqs):
            x = hidden_ref[j]
            layer_ref[j] = x
            x = x - jnp.mean(x, axis=-1, keepdims=True)
            scale = lax.rsqrt(jnp.mean(x * x, axis=-1, keepdims=True) + epsilon)
            normed_ref[j] = (x * scale * gain).astype(bf16)

    place_tile(me, step, (u0, u1, u2, u3), (d0, d1, d2, d3), up_ref, down_ref)
    upper = dot_nn(normed_ref[...].reshape(seqs * rows, width), up_ref[...])
    active, slope = gelu_pair(upper)
    active = active.astype(bf16)
    active_ref[...] = active
    slope_ref[...] = slope.astype(bf16)
    layer_ref[...] += dot_nn(active, down_ref[...]).reshape(seqs, rows, width)


def mixer_body(
    scal_ref, layer_ref, hist_ref, teacher_ref, valid_ref, gain_ref, first_ref, second_ref, bias_ref,
    next_ref, ghist_ref, glayer_ref, gfirst_ref, gsecond_ref, stats_ref, ggain_ref,
    coef_ref, part_ref, gnext_ref,
):
    step = pl.program_id(0)
    past, rows, width = hist_ref.shape
    streams = teacher_ref.shape[0]
    outs = past + 1
    span = first_ref.shape[0]

    @pl.when(step == 0)
    def _():
        gfirst_ref[...] = jnp.zeros_like(gfirst_ref)
        gsecond_ref[...] = jnp.zeros_like(gsecond_ref)
        stats_ref[...] = jnp.zeros_like(stats_ref)
        ggain_ref[...] = jnp.zeros_like(ggain_ref)

    factor = scal_ref[0]
    x = layer_ref[...]
    scale = lax.rsqrt(jnp.mean(x * x, axis=-1, keepdims=True) + epsilon)
    gain = gain_ref[4:5, :].astype(f32)
    normed = (x * scale * gain).astype(bf16)
    mix_hidden = dot_nt(normed, first_ref[...])
    mix_active, mix_slope = gelu_pair(mix_hidden)
    coeff = dot_nn(mix_active, second_ref[...], highest) + bias_ref[...]
    for c in range(streams * outs):
        coef_ref[c] = jnp.broadcast_to(coeff[:, c : c + 1], (rows, 128))
    part_ref[...] = jnp.zeros_like(part_ref)

    chunk = 16
    lanes = 512

    def rows_body(i, loss_rows):
        at = pl.ds(pl.multiple_of(i * chunk, chunk), chunk)
        valid = jnp.broadcast_to(valid_ref[at, :], (chunk, 128))

        def read(j, lane_at):
            return layer_ref[at, lane_at] if j == past else hist_ref[j, at, lane_at].astype(f32)

        for l0 in range(0, width, 256):
            lane_at = slice(l0, l0 + 256)
            sums = [jnp.zeros((chunk, 256), f32) for _ in range(streams)]
            for j in range(outs):
                value = read(j, lane_at)
                for s in range(streams):
                    c = coef_ref[s * outs + j, at, :]
                    sums[s] = sums[s] + jnp.concatenate([c, c], axis=1) * value
            both = jnp.concatenate([valid, valid], axis=1)
            for s in range(streams):
                next_ref[s, at, lane_at] = sums[s].astype(bf16)
                difference = sums[s] - teacher_ref[s, at, lane_at].astype(f32)
                weighted = both * difference
                gnext_ref[s, at, lane_at] = factor * weighted
                square = weighted * difference
                loss_rows = loss_rows + square[:, :128] + square[:, 128:]
        for l0 in range(0, width, lanes):
            lane_at = slice(l0, l0 + lanes)
            for j in range(outs):
                value = read(j, lane_at)
                total = jnp.zeros((chunk, lanes), f32)
                for s in range(streams):
                    grad = gnext_ref[s, at, lane_at]
                    c = coef_ref[s * outs + j, at, :]
                    total = total + jnp.concatenate([c] * (lanes // 128), axis=1) * grad
                    product = grad * value
                    folded = product[:, :128]
                    for q in range(128, lanes, 128):
                        folded = folded + product[:, q : q + 128]
                    part_ref[s * outs + j, at, :] += folded
                if j == past:
                    glayer_ref[at, lane_at] = total
                else:
                    ghist_ref[j, at, lane_at] = total.astype(bf16)
        return loss_rows

    loss_rows = lax.fori_loop(0, rows // chunk, rows_body, jnp.zeros((chunk, 128), f32))
    lane = lax.broadcasted_iota(jnp.int32, (rows, span), 1)
    grad_coeff = jnp.zeros((rows, span), f32)
    for c in range(streams * outs):
        grad_coeff = jnp.where(lane == c, jnp.sum(part_ref[c], axis=-1, keepdims=True), grad_coeff)
    gsecond_ref[...] += dot_tn(mix_active, grad_coeff, highest)
    stats_ref[0:1, :] += jnp.sum(grad_coeff, axis=0, keepdims=True)
    stats_ref[1:2, :] += jnp.broadcast_to(jnp.sum(loss_rows), (1, span))
    grad_active = dot_nt(grad_coeff, second_ref[...], highest)
    grad_mix = (grad_active * mix_slope).astype(bf16)
    gfirst_ref[...] += dot_tn(grad_mix, normed)
    grad_normed = dot_nn(grad_mix, first_ref[...])
    x = layer_ref[...]
    ggain_ref[...] += jnp.sum(grad_normed * (x * scale), axis=0, keepdims=True)
    inner = grad_normed * gain
    mean = jnp.mean(inner * x, axis=-1, keepdims=True)
    glayer_ref[...] += scale * inner - x * (scale * scale * scale * mean)


def norm_back(x, grad, gain):
    centered = x - jnp.mean(x, axis=-1, keepdims=True)
    scale = lax.rsqrt(jnp.mean(centered * centered, axis=-1, keepdims=True) + epsilon)
    unit = centered * scale
    grad_gain = jnp.sum(grad * unit, axis=0, keepdims=True)
    inner = grad * gain
    inner = (
        inner
        - jnp.mean(inner, axis=-1, keepdims=True)
        - unit * jnp.mean(inner * unit, axis=-1, keepdims=True)
    )
    return scale * inner, grad_gain


def mlp_backward_body(
    ids, glayer_ref, active_ref, slope_ref, normed_ref, u0, u1, u2, u3, d0, d1, d2, d3,
    gu0, gu1, gu2, gu3, gd0, gd1, gd2, gd3, sum_ref,
    low_ref, normed_t_ref, up_ref, down_ref, tile_ref,
):
    step = pl.program_id(0)
    seqs, rows, width = glayer_ref.shape
    tokens = seqs * rows
    me = ids[4]
    place = lax.rem(me, 4)

    @pl.when(step == 0)
    def _():
        low_ref[...] = glayer_ref[...].astype(bf16)
        sum_ref[...] = jnp.zeros_like(sum_ref)
        normed_t_ref[...] = normed_ref[...].reshape(tokens, width).T

    place_tile(me, step, (u0, u1, u2, u3), (d0, d1, d2, d3), up_ref, down_ref)
    grad = low_ref[...].reshape(tokens, width)
    grad_active = dot_nt(grad, down_ref[...])
    grad_upper = (grad_active * slope_ref[...].astype(f32)).astype(bf16)
    sum_ref[...] += dot_nt(grad_upper, up_ref[...]).reshape(seqs, rows, width)
    down_ref[...] = dot_tn(active_ref[...], grad).astype(bf16)
    for p, ref in enumerate((gd0, gd1, gd2, gd3)):

        @pl.when(lax.div(step, 2) == p)
        def _(ref=ref):
            block_rows = ref.shape[1]
            for q, z in enumerate(Z_ORDER):
                at = pl.multiple_of(jnp.bitwise_xor(place, z) * block_rows, block_rows)
                ref[q] = down_ref[pl.ds(at, block_rows), :]

    tile_ref[...] = dot_nn(normed_t_ref[...], grad_upper).astype(bf16)
    for p, ref in enumerate((gu0, gu1, gu2, gu3)):
        base = 8 * (p % 2) + 4 * (p // 2)
        take_rows(me, tile_ref, (base, base + 16), ref)


def take_rows(me, from_ref, base_bits, ref):
    rows = ref.shape[-2]
    for b, base in enumerate(base_bits):
        for q, z in enumerate(Z_ORDER):
            device = jnp.bitwise_xor(me, base | z)
            ref[b * 4 + q] = from_ref[pl.ds(pl.multiple_of(device * rows, rows), rows), :]


def hidden_backward_body(
    ids, glayer_ref, sum_ref, hidden_ref, h0, h1, h2, h3, gain_ref, w0, w1, w2, w3,
    gres_ref, g0, g1, g2, g3, go0, go1, go2, go3, ggain_ref,
    out_w_ref, gout_ref,
):
    seqs, rows, width = hidden_ref.shape
    me = ids[4]
    place_output_weight(me, (w0, w1, w2, w3), out_w_ref)
    gain = gain_ref[3:4, :].astype(f32)
    ggain = jnp.zeros((1, width), f32)
    for j in range(seqs):
        back, part = norm_back(hidden_ref[j], sum_ref[j], gain)
        ggain = ggain + part
        gres_ref[j] = (glayer_ref[j] + back).astype(bf16)
    ggain_ref[...] = ggain
    gout_ref[...] = jnp.zeros_like(gout_ref)
    for k, (piece, out) in enumerate(((h0, g0), (h1, g1), (h2, g2), (h3, g3))):
        code = jnp.bitwise_xor(ids[0], k)
        features = piece.shape[-1]
        at = pl.ds(pl.multiple_of(lax.rem(code, 2) * features, features), features)
        low = gres_ref[lax.div(code, 2)]
        out[...] = dot_nt(low, out_w_ref[at, :]).astype(bf16)
        gout_ref[at, :] += dot_tn(piece[...], low)
    out_w_ref[...] = gout_ref[...].astype(bf16)
    for p, ref in enumerate((go0, go1, go2, go3)):
        base = 16 * (p % 2) + 4 * (p // 2)
        take_rows(me, out_w_ref, (base, base + 8), ref)


def attention_backward_body(
    ids, q_ref, k_ref, v_ref, heads_ref, lse_ref, g0, g1, g2, g3, cos_ref, up_ref, down_ref,
    own_ref, send_ref,
    dk_ref, dv_ref, kt_ref, turn_ref,
):
    half = ids[1]
    mine = ids[2]
    prefix = ids[3]
    pair = pl.program_id(0)
    blocks, _, piece, lanes = q_ref.shape
    rows = 2 * piece
    length = blocks * rows
    dk_ref[...] = jnp.zeros_like(dk_ref)
    dv_ref[...] = jnp.zeros_like(dv_ref)
    keys = k_ref[...].reshape(length, lanes)
    values = v_ref[...].reshape(length, lanes)
    kt_ref[...] = keys.T
    lane = lax.broadcasted_iota(jnp.int32, (rows, lanes), 1)
    key_index = lax.broadcasted_iota(jnp.int32, (length, rows), 0)
    choose = (
        lax.div(lax.broadcasted_iota(jnp.int32, (8, lanes), 1), 64)
        == lax.broadcasted_iota(jnp.int32, (8, lanes), 0)
    ).astype(f32)

    def give(s, x):
        turn_ref[...] = x.astype(bf16).reshape(blocks, 2, piece, lanes)
        own_ref[s] = turn_ref[:, half]
        send_ref[s] = turn_ref[:, 1 - half]

    def back(x, block):
        if block is None:
            parts = [r[...].reshape(length, lanes) for r in (cos_ref, up_ref, down_ref)]
        else:
            parts = [r[block].reshape(rows, lanes) for r in (cos_ref, up_ref, down_ref)]
        return (
            x * parts[0]
            - pltpu.roll(x, ROT // 2, 1) * parts[1]
            - pltpu.roll(x, 128 - ROT // 2, 1) * parts[2]
        )

    for k, g in enumerate((g0, g1, g2, g3)):
        block = jnp.bitwise_xor(mine, k)
        queries = q_ref[block].reshape(rows, lanes)
        grads = g[...]
        inner_rows = dot_nt(choose, grads.astype(f32) * heads_ref[block].astype(f32), highest)
        limit = allowed_limit(block * rows, rows, prefix, 1)
        allowed = key_index <= limit
        dqt = []
        for h in range(2):
            chosen = (lane < 64) if h == 0 else (lane >= 64)
            q_h = jnp.where(chosen, queries, jnp.zeros_like(queries))
            g_h = jnp.where(chosen, grads, jnp.zeros_like(grads))
            scores = dot_nt(keys, q_h)
            probs = jnp.where(allowed, jnp.exp(scores - lse_ref[pair * 2 + h, block]), 0.0)
            grad_probs = dot_nt(values, g_h)
            grad_scores = (probs * (grad_probs - inner_rows[h : h + 1, :])).astype(bf16)
            dv_ref[...] += dot_nn(probs.astype(bf16), g_h)
            dk_ref[...] += dot_nn(grad_scores, q_h)
            dqt.append(dot_nn(kt_ref[...], grad_scores)[h * 64 : h * 64 + 64, :])
        dq = jnp.concatenate(dqt, axis=0).T * (HEAD_DIM**-0.5)
        low = back(dq, block).astype(bf16)
        turn_ref[0] = low.reshape(2, piece, lanes)
        own_ref[0, block] = turn_ref[0, half]
        send_ref[0, block] = turn_ref[0, 1 - half]
    give(1, back(dk_ref[...], None))
    give(2, dv_ref[...])


def projection_backward_body(
    ids, n_own_ref, n_other_ref, d_own_ref, d_send_ref, d_recv_ref, proj_ref, far_ref,
    received_ref, gain_ref,
    gp0, gp1, o0, o1, o2, o3, ggain_ref,
    w_own_ref, w_other_ref, grad_ref,
):
    mine = ids[2]
    me = ids[4]
    s = pl.program_id(0)
    _, blocks, piece, width = n_own_ref.shape
    rows = blocks * piece
    place_rows_of_projection(me, 0, proj_ref, w_own_ref)
    place_rows_of_projection(jnp.bitwise_xor(me, 4), 0, far_ref, w_other_ref)
    d_own = d_own_ref[...].reshape(rows, -1)
    grad = dot_tn(n_own_ref[...].reshape(rows, width), d_own)
    grad = grad + dot_tn(n_other_ref[...].reshape(rows, width), d_send_ref[...].reshape(rows, -1))
    grad_ref[...] = grad.astype(bf16)
    for x, ref in enumerate((gp0, gp1)):
        shard = ref.shape[-2]
        for y in range(2):
            for q, z in enumerate(Z_ORDER):
                for core in range(2):
                    device = jnp.bitwise_xor(me, 16 * y + 8 * x + 4 * core + z)
                    at = pl.ds(pl.multiple_of(device * shard, shard), shard)
                    ref[y * 4 + q, core, 0] = grad_ref[at, :]
    gain = gain_ref[pl.ds(s, 1), :].astype(f32)
    total = jnp.zeros((1, width), f32)
    for k, o in enumerate((o0, o1, o2, o3)):
        block = jnp.bitwise_xor(mine, k)
        grad_normed = dot_nt(d_own_ref[0, block], w_own_ref[...]) + dot_nt(
            d_recv_ref[0, block], w_other_ref[...]
        )
        back, part = norm_back(received_ref[k, 0].astype(f32), grad_normed, gain)
        o[0] = back.astype(bf16)
        total = total + part
    ggain_ref[0] = total


def swap(x, bit, count):
    return lax.ppermute(x, AXES, [(i, i ^ bit) for i in range(count)])


def add_all(x, count):
    bit = 1
    while bit < count:
        x = x + swap(x, bit, count)
        bit *= 2
    return x


def scatter_sum(x, steps, me, count):
    gone = []
    for bit, axis in steps:
        at = axis - sum(1 for g in gone if g < axis)
        mine = jnp.where((me & bit) == 0, 0, 1)
        keep = lax.dynamic_index_in_dim(x, mine, at, keepdims=False)
        send = lax.dynamic_index_in_dim(x, 1 - mine, at, keepdims=False)
        x = keep + swap(send, bit, count)
        gone.append(axis)
    return x


def rotary_lanes(length, piece):
    lane = jnp.arange(128, dtype=jnp.int32) % HEAD_DIM
    step = (lane % (ROT // 2)).astype(f32)
    inverse = jnp.exp(step * (-2.0 * math.log(10000.0) / ROT))
    angles = jnp.arange(length, dtype=jnp.int32).astype(f32)[:, None] * inverse[None, :]
    cosine = jnp.where(lane < ROT, jnp.cos(angles), 1.0)
    sine = jnp.sin(angles)
    up = jnp.where((lane >= ROT // 2) & (lane < ROT), sine, 0.0)
    down = jnp.where(lane < ROT // 2, -sine, 0.0)
    return [t.reshape(-1, 2, piece, 128) for t in (cosine, up, down)]


def local_fast(
    streams, history, teacher, prefix, valid_mask, loss_scale, projections, attention_out,
    up_weight, down_weight, mixer_first, mixer_second, mixer_bias, gains,
):
    lines = lax.axis_size("ctx")
    count = lax.axis_size("dp") * lines
    place = lax.axis_index("ctx")
    group = lax.axis_index("dp")
    me = group * lines + place
    half = group % 2
    mine = 2 * (place % 2) + half
    seqs, rows, width = streams.shape[1:]
    tokens = seqs * rows
    piece = rows // 2
    length = rows * lines
    features = width // 2
    hidden_units = down_weight.shape[0] * count
    past = history.shape[0]
    count_of_streams = teacher.shape[0]
    mixw = mixer_bias.shape[0]
    span = 64

    def out_perm(k):
        pairs = []
        for i in range(count):
            pair, core, z = i // (2 * lines), (i // lines) % 2, i % lines
            code = z ^ k
            pairs.append((i, (pair * 2 + code % 2) * lines + 2 * core + code // 2))
        return pairs

    def send_out(x, k):
        return lax.ppermute(x, AXES, out_perm(k))

    def send_back(x, k):
        return lax.ppermute(x, AXES, [(b, a) for a, b in out_perm(k)])

    both_prefix = swap(prefix, lines, count)
    source_half = place // 2
    prefix_pair = jnp.where(source_half == half, prefix, both_prefix)
    my_prefix = jnp.where(place % 2 == 0, prefix_pair[0], prefix_pair[1])
    ids = jnp.stack([place, half, mine, my_prefix, me]).astype(jnp.int32)

    second = jnp.pad(mixer_second, ((0, span - mixw), (0, span - mixw)))
    bias = jnp.pad(mixer_bias, (0, span - mixw))[None]
    valid = valid_mask.astype(f32).reshape(tokens, 1)
    core = lines
    column, row = core * 2, core * 4
    shard = width // count
    unit_shard = hidden_units // count

    small = jnp.concatenate([gains, jnp.zeros((3, shard), bf16), mixer_first.T], axis=0)
    small = jnp.pad(small, ((0, span + 8 - small.shape[0]), (0, 0)))
    lane_place = jnp.arange(width, dtype=jnp.int32) // shard
    small = jnp.where(lane_place == me, jnp.tile(small, (1, count)), jnp.zeros((), bf16))
    counted = jnp.full((8, 128), jnp.sum(valid), f32)

    smem = pl.BlockSpec(memory_space=pltpu.SMEM)
    anywhere = pl.BlockSpec(memory_space=pl.ANY)
    piece_shape = (3, lines, piece, width)
    proj_shape = (count // 2, 2, 3, shard, features)
    received, normed_own, normed_other, proj, up_part, down_part, small, counted = pl.pallas_call(
        front_body,
        in_specs=[anywhere] + [vmem()] * 6,
        out_specs=[vmem()] * 3 + [anywhere] * 3 + [vmem()] * 2,
        out_shape=[
            jax.ShapeDtypeStruct((4, 3, piece, width), bf16),
            jax.ShapeDtypeStruct(piece_shape, bf16),
            jax.ShapeDtypeStruct(piece_shape, bf16),
            jax.ShapeDtypeStruct(proj_shape, bf16),
            jax.ShapeDtypeStruct((8, shard, hidden_units), bf16),
            jax.ShapeDtypeStruct((8, unit_shard + shard, width), bf16),
            jax.ShapeDtypeStruct((span + 8, width), bf16),
            jax.ShapeDtypeStruct((8, 128), f32),
        ],
        scratch_shapes=[
            pltpu.VMEM((5, span + 8, width), bf16),
            pltpu.VMEM((5, 8, 128), f32),
            pltpu.SemaphoreType.DMA((4,)),
            pltpu.SemaphoreType.DMA((48,)),
            pltpu.SemaphoreType.DMA((48,)),
        ],
        compiler_params=params(collective_id=0, has_side_effects=True),
        name="front",
    )(
        streams.reshape(streams.shape[0], 2 * seqs, piece, width),
        projections, up_weight, down_weight, attention_out, small, counted,
    )
    gain_full = small[:8].astype(f32)
    first_t = small[8:]
    token_total = counted[0, :1]
    factor = loss_scale * 2.0 / (4.0 * width * token_total)
    ups = [up_part, swap(up_part, column, count)]
    ups += [swap(u, core, count) for u in ups]
    downs = [down_part, swap(down_part, row, count)]
    downs += [swap(u, core, count) for u in downs]
    proj_other = swap(proj, core, count)

    tables = rotary_lanes(length, piece)
    wide = jax.ShapeDtypeStruct((lines, 2, piece, features), bf16)

    def whole(shape):
        return pl.BlockSpec(shape, lambda i, ids: (0,) * len(shape))

    heads_seq, lse, queries, keys, values = pl.pallas_call(
        attention_forward_body,
        grid_spec=pltpu.PrefetchScalarGridSpec(
            num_scalar_prefetch=1,
            grid=(1,),
            in_specs=[whole(piece_shape), whole(piece_shape)]
            + [whole(proj.shape)]
            + [whole((lines, 2, piece, 128))] * 3,
            out_specs=[whole((lines, rows, features)), whole((lines, rows, 8))]
            + [whole((lines, 2, piece, features))] * 3,
            scratch_shapes=[pltpu.VMEM((3, width, features), bf16)],
        ),
        out_shape=[
            jax.ShapeDtypeStruct((lines, rows, features), bf16),
            jax.ShapeDtypeStruct((lines, rows, 8), f32),
            wide,
            wide,
            wide,
        ],
        compiler_params=params(),
        name="attention_forward",
    )(ids, normed_own, normed_other, proj, *tables)

    heads = [
        send_back(lax.dynamic_index_in_dim(heads_seq, mine ^ k, 0, keepdims=False), k)
        for k in range(4)
    ]

    tile = 512
    tiles = hidden_units // tile
    token_shape = (seqs, rows, width)

    def fixed(shape, index=None):
        index = index or (0,) * len(shape)
        return pl.BlockSpec(shape, lambda i, *_: index)

    def up_column(i, ids):
        distance = lax.rem(lax.div(i, 2), 2) * 4 + lax.rem(i, 2) * 2 + lax.div(i, 4)
        return (0, 0, jnp.bitwise_xor(lax.div(ids[4], 4), distance))

    def down_block(p):
        return lambda i, *_: (jnp.clip(i - 2 * p, 0, 1), 0, 0)

    tile_specs = [pl.BlockSpec((8, shard, tile), up_column)] * 4
    tile_specs += [pl.BlockSpec((4, unit_shard, width), down_block(p)) for p in range(4)]
    out_weight_specs = [
        pl.BlockSpec((8, shard, width), lambda i, *_: (0, unit_shard // shard, 0))
    ] * 4

    hidden, normed_mlp, active, slope, layer_out = pl.pallas_call(
        mlp_forward_body,
        grid_spec=pltpu.PrefetchScalarGridSpec(
            num_scalar_prefetch=1,
            grid=(tiles,),
            in_specs=[fixed((rows, features))] * 4
            + [
                fixed((1,) + token_shape, (3, 0, 0, 0)),
                fixed((8, width)),
            ]
            + tile_specs
            + out_weight_specs,
            out_specs=[
                fixed(token_shape),
                fixed(token_shape),
                pl.BlockSpec((tokens, tile), lambda i, *_: (0, i)),
                pl.BlockSpec((tokens, tile), lambda i, *_: (0, i)),
                fixed(token_shape),
            ],
            scratch_shapes=[
                pltpu.VMEM((width, width), bf16),
                pltpu.VMEM((width, tile), bf16),
                pltpu.VMEM((tile, width), bf16),
            ],
        ),
        out_shape=[
            jax.ShapeDtypeStruct(token_shape, f32),
            jax.ShapeDtypeStruct(token_shape, bf16),
            jax.ShapeDtypeStruct((tokens, hidden_units), bf16),
            jax.ShapeDtypeStruct((tokens, hidden_units), bf16),
            jax.ShapeDtypeStruct(token_shape, f32),
        ],
        compiler_params=params(),
        name="mlp_forward",
    )(ids, *heads, streams, gain_full, *ups, *downs, *downs)

    block = 64
    next_streams, grad_history, grad_layer, g_first, g_second, stats, g_gain_mix = pl.pallas_call(
        mixer_body,
        grid=(tokens // block,),
        in_specs=[
            smem,
            pl.BlockSpec((block, width), lambda i: (i, 0)),
            pl.BlockSpec((past, block, width), lambda i: (0, i, 0)),
            pl.BlockSpec((count_of_streams, block, width), lambda i: (0, i, 0)),
            pl.BlockSpec((block, 1), lambda i: (i, 0)),
            fixed((8, width)),
            fixed((span, width)),
            fixed((span, span)),
            fixed((1, span)),
        ],
        out_specs=[
            pl.BlockSpec((count_of_streams, block, width), lambda i: (0, i, 0)),
            pl.BlockSpec((past, block, width), lambda i: (0, i, 0)),
            pl.BlockSpec((block, width), lambda i: (i, 0)),
            fixed((span, width)),
            fixed((span, span)),
            fixed((8, span)),
            fixed((1, width)),
        ],
        out_shape=[
            jax.ShapeDtypeStruct((count_of_streams, tokens, width), bf16),
            jax.ShapeDtypeStruct((past, tokens, width), bf16),
            jax.ShapeDtypeStruct((tokens, width), f32),
            jax.ShapeDtypeStruct((span, width), f32),
            jax.ShapeDtypeStruct((span, span), f32),
            jax.ShapeDtypeStruct((8, span), f32),
            jax.ShapeDtypeStruct((1, width), f32),
        ],
        scratch_shapes=[
            pltpu.VMEM((mixw, block, 128), f32),
            pltpu.VMEM((mixw, block, 128), f32),
            pltpu.VMEM((count_of_streams, block, width), f32),
        ],
        compiler_params=params(),
        name="mixer",
    )(
        factor,
        layer_out.reshape(tokens, width),
        history.reshape(past, tokens, width),
        teacher.reshape(count_of_streams, tokens, width),
        valid,
        gain_full,
        first_t,
        second,
        bias,
    )

    *g_ups, gd0, gd1, gd2, gd3, g_normed = pl.pallas_call(
        mlp_backward_body,
        grid_spec=pltpu.PrefetchScalarGridSpec(
            num_scalar_prefetch=1,
            grid=(tiles,),
            in_specs=[
                fixed(token_shape),
                pl.BlockSpec((tokens, tile), lambda i, *_: (0, i)),
                pl.BlockSpec((tokens, tile), lambda i, *_: (0, i)),
                fixed(token_shape),
            ]
            + tile_specs,
            out_specs=tile_specs + [fixed(token_shape)],
            scratch_shapes=[
                pltpu.VMEM(token_shape, bf16),
                pltpu.VMEM((width, tokens), bf16),
                pltpu.VMEM((width, tile), bf16),
                pltpu.VMEM((tile, width), bf16),
                pltpu.VMEM((width, tile), bf16),
            ],
        ),
        out_shape=[jax.ShapeDtypeStruct((8, shard, hidden_units), bf16)] * 4
        + [jax.ShapeDtypeStruct((8, unit_shard, width), bf16)] * 4
        + [jax.ShapeDtypeStruct(token_shape, f32)],
        compiler_params=params(),
        name="mlp_backward",
    )(ids, grad_layer.reshape(token_shape), active, slope, normed_mlp, *ups, *downs)
    g_downs = [gd0, gd1, gd2, gd3]

    hidden_results = pl.pallas_call(
        hidden_backward_body,
        grid_spec=pltpu.PrefetchScalarGridSpec(
            num_scalar_prefetch=1,
            grid=(1,),
            in_specs=[fixed(token_shape)] * 3
            + [fixed((rows, features))] * 4
            + [fixed((8, width))]
            + out_weight_specs,
            out_specs=[pl.BlockSpec((None,) + token_shape, lambda i, *_: (3, 0, 0, 0))]
            + [fixed((rows, features))] * 4
            + [fixed((8, shard, width))] * 4
            + [fixed((1, width))],
            scratch_shapes=[pltpu.VMEM((width, width), bf16), pltpu.VMEM((width, width), f32)],
        ),
        out_shape=[jax.ShapeDtypeStruct(streams.shape, bf16)]
        + [jax.ShapeDtypeStruct((rows, features), bf16)] * 4
        + [jax.ShapeDtypeStruct((8, shard, width), bf16)] * 4
        + [jax.ShapeDtypeStruct((1, width), f32)],
        compiler_params=params(),
        name="hidden_backward",
    )(ids, grad_layer.reshape(token_shape), g_normed, hidden, *heads, gain_full, *downs)
    g_streams, gh0, gh1, gh2, gh3, go0, go1, go2, go3, g_gain_mlp = hidden_results

    def fold(x, bit):
        n = x.shape[0] // 2
        return x[:n] + swap(x[n:], bit, count)

    def last_fold(x, bit):
        return x[0].astype(f32) + swap(x[1], bit, count).astype(f32)

    up_pair = [g_ups[n] + swap(g_ups[n + 2], core, count) for n in range(2)]
    up_sum = up_pair[0] + swap(up_pair[1], column, count)
    up_sum = fold(fold(up_sum, row), 1)
    sum_up = last_fold(up_sum, 2)
    g_outs = [go0, go1, go2, go3]
    down_pair = [
        jnp.concatenate(
            [g[n] + swap(g[n + 2], core, count) for g in (g_downs, g_outs)], axis=1
        )
        for n in range(2)
    ]
    down_sum = down_pair[0] + swap(down_pair[1], row, count)
    down_sum = fold(fold(down_sum, column), 1)
    down_sum = last_fold(down_sum, 2)
    sum_down, sum_out = down_sum[:unit_shard], down_sum[unit_shard:]

    def scatter_columns(x):
        bits = count.bit_length() - 1
        x = x.reshape(x.shape[0], count, -1).transpose(1, 0, 2)
        x = x.reshape((2,) * bits + x.shape[1:])
        order = [(1 << (bits - 1 - axis), axis) for axis in range(bits)]
        return scatter_sum(x, order, me, count)

    g_head_rows = [send_out(g, k) for k, g in enumerate((gh0, gh1, gh2, gh3))]

    pairs = features // 128

    def pair_spec(shape):
        return pl.BlockSpec(shape + (128,), lambda i, *_: (0,) * len(shape) + (i,))

    d_own, d_send = pl.pallas_call(
        attention_backward_body,
        grid_spec=pltpu.PrefetchScalarGridSpec(
            num_scalar_prefetch=1,
            grid=(pairs,),
            in_specs=[pair_spec((lines, 2, piece))] * 3
            + [pair_spec((lines, rows)), fixed((8, lines, 1, rows))]
            + [pair_spec((rows,))] * 4
            + [fixed((lines, 2, piece, 128))] * 3,
            out_specs=[pair_spec((3, lines, piece))] * 2,
            scratch_shapes=[
                pltpu.VMEM((length, 128), f32),
                pltpu.VMEM((length, 128), f32),
                pltpu.VMEM((128, length), bf16),
                pltpu.VMEM((lines, 2, piece, 128), bf16),
            ],
        ),
        out_shape=[jax.ShapeDtypeStruct((3, lines, piece, features), bf16)] * 2,
        compiler_params=params(),
        name="attention_backward",
    )(
        ids, queries, keys, values, heads_seq,
        lse.reshape(length, 8).T.reshape(8, lines, 1, rows), *g_head_rows, *tables,
    )
    d_recv = swap(d_send, lines, count)

    def stream_spec(shape):
        return pl.BlockSpec((1,) + shape, lambda s, *_: (s,) + (0,) * len(shape))

    back_piece = (piece, width)
    weight_spec = pl.BlockSpec((count // 2, 2, 1, shard, features), lambda s, *_: (0, 0, s, 0, 0))
    half_spec = pl.BlockSpec((count // 4, 2, 1, shard, features), lambda s, *_: (0, 0, s, 0, 0))
    gp0, gp1, b0, b1, b2, b3, g_gain_three = pl.pallas_call(
        projection_backward_body,
        grid_spec=pltpu.PrefetchScalarGridSpec(
            num_scalar_prefetch=1,
            grid=(3,),
            in_specs=[stream_spec((lines, piece, width))] * 2
            + [stream_spec((lines, piece, features))] * 3
            + [weight_spec] * 2
            + [pl.BlockSpec((4, 1) + back_piece, lambda s, *_: (0, s, 0, 0))]
            + [fixed((8, width))],
            out_specs=[half_spec] * 2
            + [stream_spec(back_piece)] * 4
            + [stream_spec((1, width))],
            scratch_shapes=[pltpu.VMEM((width, features), bf16)] * 3,
        ),
        out_shape=[jax.ShapeDtypeStruct((8, 2, 3, shard, features), bf16)] * 2
        + [jax.ShapeDtypeStruct((3,) + back_piece, bf16)] * 4
        + [jax.ShapeDtypeStruct((3, 1, width), f32)],
        compiler_params=params(),
        name="projection_backward",
    )(
        ids, normed_own, normed_other, d_own, d_send, d_recv, proj, proj_other,
        received, gain_full,
    )

    grad_streams = g_streams.reshape(streams.shape[0], 2 * seqs, piece, width)
    for k, b in enumerate((b0, b1, b2, b3)):
        grad_streams = lax.dynamic_update_slice(
            grad_streams, send_back(b, k)[:, None], (0, place ^ k, 0, 0)
        )
    grad_streams = grad_streams.reshape(streams.shape)

    proj_sum = gp0 + swap(gp1, column, count)
    proj_sum = fold(fold(fold(proj_sum, row), 1), 2)[0]
    kept, sent = proj_sum[0], swap(proj_sum[1], core, count)
    low = half == 0
    grad_projections = jnp.concatenate(
        [jnp.where(low, kept, sent), jnp.where(low, sent, kept)], axis=-1
    ).astype(f32)

    early = scatter_columns(
        jnp.concatenate([g_first[:mixw], g_gain_mlp, g_gain_mix], axis=0)
    )
    late = scatter_columns(g_gain_three.reshape(3, width))
    grad_first = early[:mixw].T
    grad_gains = jnp.concatenate([late, early[mixw:]], axis=0)
    totals = add_all(jnp.concatenate([g_second, stats], axis=0), count)
    grad_second = totals[:mixw, :mixw]
    grad_bias = totals[span, :mixw]
    mean_loss = totals[span + 1, 0] / (4.0 * width * token_total[0])
    return (
        next_streams.reshape(teacher.shape),
        mean_loss,
        grad_streams,
        grad_history.reshape(history.shape),
        grad_projections,
        sum_out,
        sum_up,
        sum_down,
        grad_first,
        grad_second,
        grad_bias,
        grad_gains,
    )


def layer_norm(values, gain_row):
    centered = values - jnp.mean(values, axis=-1, keepdims=True)
    return (
        centered
        * lax.rsqrt(jnp.mean(centered * centered, axis=-1, keepdims=True) + epsilon)
        * gain_row
    )


def rms_norm(values, gain_row):
    return (
        values * lax.rsqrt(jnp.mean(values * values, axis=-1, keepdims=True) + epsilon) * gain_row
    )


def gelu_exact(values):
    return jax.nn.gelu(values, approximate=False)


def rotary_tables(positions):
    frequency_steps = jnp.arange(ROT // 2).astype(positions.dtype)
    inverse = jnp.exp(frequency_steps * (-2.0 * math.log(10000.0) / ROT))
    angles = positions[:, None] * inverse[None, :]
    return (jnp.cos(angles)[:, None, :], jnp.sin(angles)[:, None, :])


def rotate(values, cosine_table, sine_table, direction):
    row_count = values.shape[0]
    shaped = values.reshape(row_count, HEADS, HEAD_DIM)
    half_rot = ROT // 2
    first_half = shaped[:, :, :half_rot]
    second_half = shaped[:, :, half_rot:ROT]
    remainder = shaped[:, :, ROT:]
    turned_first = first_half * cosine_table - direction * second_half * sine_table
    turned_second = second_half * cosine_table + direction * first_half * sine_table
    return jnp.concatenate([turned_first, turned_second, remainder], axis=-1).reshape(row_count, -1)


def masked_scores(query_heads, key_heads, query_index, key_index, prefix_len):
    scores = jnp.einsum(
        "qhd,khd->hqk", query_heads, key_heads, preferred_element_type=jnp.float32
    ) * HEAD_DIM ** (-0.5)
    allowed = (key_index[None, :] <= query_index[:, None]) | (key_index[None, :] < prefix_len)
    return jnp.where(allowed[None], scores, -1e30)


def local_plain(
    streams,
    history,
    teacher,
    prefix,
    valid_mask,
    loss_scale,
    projections,
    attention_out,
    up_weight,
    down_weight,
    mixer_first,
    mixer_second,
    mixer_bias,
    gains,
):
    micro_count = streams.shape[1]
    row_count = streams.shape[2]
    model_width = streams.shape[3]
    length = row_count * lax.axis_size("ctx")
    query_index = lax.axis_index("ctx") * row_count + jnp.arange(row_count, dtype=jnp.int32)
    key_index = jnp.arange(length, dtype=jnp.int32)
    cosine_table, sine_table = rotary_tables(query_index.astype(jnp.float32))
    score_scale = HEAD_DIM ** (-0.5)
    valid_float = valid_mask.astype(jnp.float32)
    token_total = lax.psum(jnp.sum(valid_float), ("dp", "ctx"))
    factor = loss_scale[0] * 2.0 / (4.0 * model_width * token_total)

    def one_batch(totals, number):
        (
            kept_projections,
            kept_attention,
            kept_gains,
            kept_up,
            kept_down,
            kept_first,
            kept_second,
            kept_bias,
            kept_loss,
        ) = totals
        stream_block = lax.dynamic_index_in_dim(streams, number, 1, keepdims=False)
        past_outputs = lax.dynamic_index_in_dim(history, number, 1, keepdims=False)
        target = lax.dynamic_index_in_dim(teacher, number, 1, keepdims=False).astype(jnp.float32)
        prefix_len = lax.dynamic_index_in_dim(prefix, number, 0, keepdims=False)
        valid_row = lax.dynamic_index_in_dim(valid_float, number, 0, keepdims=False)
        proj_full, out_full, gain_low, up_full, down_full, first_full = (
            lax.all_gather(projections, ("dp", "ctx"), axis=1, tiled=True),
            lax.all_gather(attention_out, ("dp", "ctx"), axis=0, tiled=True),
            lax.all_gather(gains, ("dp", "ctx"), axis=1, tiled=True),
            lax.all_gather(up_weight, ("dp", "ctx"), axis=0, tiled=True),
            lax.all_gather(down_weight, ("dp", "ctx"), axis=0, tiled=True),
            lax.all_gather(mixer_first, ("dp", "ctx"), axis=0, tiled=True),
        )
        gain_full = gain_low.astype(jnp.float32)
        inputs = stream_block.astype(jnp.float32)
        gain_three = gain_full[:3, None, :]
        normed_low = layer_norm(inputs[:3], gain_three).astype(jnp.bfloat16)
        projected = jnp.einsum(
            "std,sde->ste", normed_low, proj_full, preferred_element_type=jnp.float32
        )
        query_heads = (
            rotate(projected[0], cosine_table, sine_table, 1.0)
            .astype(jnp.bfloat16)
            .reshape(row_count, HEADS, HEAD_DIM)
        )
        key_low = rotate(projected[1], cosine_table, sine_table, 1.0).astype(jnp.bfloat16)
        value_low = projected[2].astype(jnp.bfloat16)
        all_keys, all_values = (
            lax.all_gather(key_low, "ctx", axis=0, tiled=True),
            lax.all_gather(value_low, "ctx", axis=0, tiled=True),
        )
        key_heads = all_keys.reshape(length, HEADS, HEAD_DIM)
        value_heads = all_values.reshape(length, HEADS, HEAD_DIM)
        scores = masked_scores(query_heads, key_heads, query_index, key_index, prefix_len)
        row_max = jnp.max(scores, axis=-1, keepdims=True)
        log_total = row_max + jnp.log(jnp.sum(jnp.exp(scores - row_max), axis=-1, keepdims=True))
        probs_low = jnp.exp(scores - log_total).astype(jnp.bfloat16)
        heads_low = (
            jnp.einsum("hqk,khd->qhd", probs_low, value_heads, preferred_element_type=jnp.float32)
            .reshape(row_count, model_width)
            .astype(jnp.bfloat16)
        )
        hidden = inputs[3] + jnp.dot(heads_low, out_full, preferred_element_type=jnp.float32)
        normed_mlp = layer_norm(hidden, gain_full[3]).astype(jnp.bfloat16)
        upper = jnp.dot(normed_mlp, up_full, preferred_element_type=jnp.float32)
        activated = gelu_exact(upper).astype(jnp.bfloat16)
        layer_out = hidden + jnp.dot(activated, down_full, preferred_element_type=jnp.float32)
        normed_mix = rms_norm(layer_out, gain_full[4]).astype(jnp.bfloat16)
        mix_hidden = jnp.dot(normed_mix, first_full, preferred_element_type=jnp.float32)
        mix_active = gelu_exact(mix_hidden)
        coeff = jnp.dot(mix_active, mixer_second, precision=highest) + mixer_bias
        coeff_grid = coeff.reshape(row_count, 4, -1)
        outputs_all = jnp.concatenate([past_outputs.astype(jnp.float32), layer_out[None]], axis=0)
        next_block = jnp.einsum("tsj,jtd->std", coeff_grid, outputs_all, precision=highest)
        difference = next_block - target
        loss_part = jnp.sum(jnp.sum(difference * difference, axis=(0, 2)) * valid_row) / (
            4.0 * model_width * token_total
        )
        grad_next = factor * valid_row[None, :, None] * difference
        grad_coeff = jnp.einsum("std,jtd->tsj", grad_next, outputs_all, precision=highest).reshape(
            row_count, -1
        )
        grad_outputs = jnp.einsum("tsj,std->jtd", coeff_grid, grad_next, precision=highest)
        grad_past = grad_outputs[:-1].astype(jnp.bfloat16)
        grad_second = jnp.dot(mix_active.T, grad_coeff, precision=highest)
        grad_bias = jnp.sum(grad_coeff, axis=0)
        grad_active = jnp.dot(grad_coeff, mixer_second.T, precision=highest)
        gelu_mix_back = jax.vjp(gelu_exact, mix_hidden)[1]
        grad_mix = gelu_mix_back(grad_active)[0].astype(jnp.bfloat16)
        grad_first = jnp.einsum(
            "td,tm->dm", normed_mix, grad_mix, preferred_element_type=jnp.float32
        )
        grad_normed_mix = jnp.einsum(
            "tm,dm->td", grad_mix, first_full, preferred_element_type=jnp.float32
        )
        rms_back = jax.vjp(rms_norm, layer_out, gain_full[4])[1]
        grad_layer_mix, grad_gain_mix = rms_back(grad_normed_mix)
        grad_layer = grad_outputs[-1] + grad_layer_mix
        grad_branch = grad_layer.astype(jnp.bfloat16)
        grad_down = jnp.einsum(
            "tf,td->fd", activated, grad_branch, preferred_element_type=jnp.float32
        )
        grad_active_up = jnp.einsum(
            "td,fd->tf", grad_branch, down_full, preferred_element_type=jnp.float32
        )
        gelu_up_back = jax.vjp(gelu_exact, upper)[1]
        grad_upper = gelu_up_back(grad_active_up)[0].astype(jnp.bfloat16)
        grad_up = jnp.einsum(
            "td,tf->df", normed_mlp, grad_upper, preferred_element_type=jnp.float32
        )
        grad_normed_mlp = jnp.einsum(
            "tf,df->td", grad_upper, up_full, preferred_element_type=jnp.float32
        )
        down_shard, first_shard, up_shard = (
            lax.psum_scatter(grad_down, ("dp", "ctx"), scatter_dimension=0, tiled=True),
            lax.psum_scatter(grad_first, ("dp", "ctx"), scatter_dimension=0, tiled=True),
            lax.psum_scatter(grad_up, ("dp", "ctx"), scatter_dimension=0, tiled=True),
        )
        down_next = kept_down + down_shard
        norm_mlp_back = jax.vjp(layer_norm, hidden, gain_full[3])[1]
        grad_hidden_mlp, grad_gain_mlp = norm_mlp_back(grad_normed_mlp)
        grad_hidden = grad_layer + grad_hidden_mlp
        grad_attn = grad_hidden.astype(jnp.bfloat16)
        grad_attention = jnp.einsum(
            "td,te->de", heads_low, grad_attn, preferred_element_type=jnp.float32
        )
        grad_heads = jnp.einsum(
            "te,de->td", grad_attn, out_full, preferred_element_type=jnp.float32
        ).astype(jnp.bfloat16)
        grad_head_grid = grad_heads.reshape(row_count, HEADS, HEAD_DIM)
        scores_again = masked_scores(query_heads, key_heads, query_index, key_index, prefix_len)
        probs_exact = jnp.exp(scores_again - log_total)
        probs_again = probs_exact.astype(jnp.bfloat16)
        grad_probs = jnp.einsum(
            "qhd,khd->hqk", grad_head_grid, value_heads, preferred_element_type=jnp.float32
        )
        row_inner = jnp.sum(probs_exact * grad_probs, axis=-1, keepdims=True)
        grad_scores = (probs_exact * (grad_probs - row_inner)).astype(jnp.bfloat16)
        grad_queries = (
            jnp.einsum(
                "hqk,khd->qhd", grad_scores, key_heads, preferred_element_type=jnp.float32
            ).reshape(row_count, model_width)
            * score_scale
        )
        grad_key_part = (
            jnp.einsum("hqk,qhd->khd", grad_scores, query_heads, preferred_element_type=jnp.float32)
            * score_scale
        )
        grad_value_part = jnp.einsum(
            "hqk,qhd->khd", probs_again, grad_head_grid, preferred_element_type=jnp.float32
        )
        key_grads = lax.psum_scatter(
            jnp.concatenate(
                [
                    grad_key_part.reshape(row_count * lax.axis_size("ctx"), -1),
                    grad_value_part.reshape(row_count * lax.axis_size("ctx"), -1),
                ],
                axis=-1,
            ).astype(jnp.bfloat16),
            "ctx",
            scatter_dimension=0,
            tiled=True,
        ).astype(jnp.float32)
        grad_query_low = rotate(grad_queries, cosine_table, sine_table, -1.0).astype(jnp.bfloat16)
        grad_key_low = rotate(key_grads[:, :model_width], cosine_table, sine_table, -1.0).astype(
            jnp.bfloat16
        )
        grad_value_low = key_grads[:, model_width:].astype(jnp.bfloat16)
        grad_projected = jnp.stack([grad_query_low, grad_key_low, grad_value_low])
        grad_proj = jnp.einsum(
            "std,ste->sde", normed_low, grad_projected, preferred_element_type=jnp.float32
        )
        grad_normed = jnp.einsum(
            "ste,sde->std", grad_projected, proj_full, preferred_element_type=jnp.float32
        )
        norm_three_back = jax.vjp(layer_norm, inputs[:3], gain_three)[1]
        grad_inputs_three, grad_gain_three = norm_three_back(grad_normed)
        grad_gain_all = jnp.concatenate(
            [grad_gain_three.reshape(3, -1), grad_gain_mlp[None], grad_gain_mix[None]], axis=0
        )
        proj_shard, attention_shard, gain_shard = (
            lax.psum_scatter(grad_proj, ("dp", "ctx"), scatter_dimension=1, tiled=True),
            lax.psum_scatter(grad_attention, ("dp", "ctx"), scatter_dimension=0, tiled=True),
            lax.psum_scatter(grad_gain_all, ("dp", "ctx"), scatter_dimension=1, tiled=True),
        )
        grad_block = jnp.concatenate([grad_inputs_three, grad_hidden[None]], axis=0).astype(
            jnp.bfloat16
        )
        new_totals = (
            kept_projections + proj_shard,
            kept_attention + attention_shard,
            kept_gains + gain_shard,
            kept_up + up_shard,
            down_next,
            kept_first + first_shard,
            kept_second + grad_second,
            kept_bias + grad_bias,
            kept_loss + loss_part,
        )
        return (new_totals, (next_block.astype(jnp.bfloat16), grad_block, grad_past))

    down_start = jnp.zeros(down_weight.shape, jnp.float32)
    start_totals = (
        jnp.zeros(projections.shape, jnp.float32),
        jnp.zeros(attention_out.shape, jnp.float32),
        jnp.zeros(gains.shape, jnp.float32),
        jnp.zeros(up_weight.shape, jnp.float32),
        down_start,
        jnp.zeros(mixer_first.shape, jnp.float32),
        jnp.zeros(mixer_second.shape, jnp.float32),
        jnp.zeros(mixer_bias.shape, jnp.float32),
        jnp.zeros((), jnp.float32),
    )
    final_totals, stacked = lax.scan(
        one_batch, start_totals, jnp.arange(micro_count, dtype=jnp.int32)
    )
    (
        sum_projections,
        sum_attention,
        sum_gains,
        sum_up,
        sum_down,
        sum_first,
        sum_second,
        sum_bias,
        sum_loss,
    ) = final_totals
    grad_second_all, grad_bias_all, loss_all = lax.psum(
        (sum_second, sum_bias, sum_loss), ("dp", "ctx")
    )
    next_streams = jnp.moveaxis(stacked[0], 0, 1)
    grad_streams = jnp.moveaxis(stacked[1], 0, 1)
    grad_history = jnp.moveaxis(stacked[2], 0, 1)
    return (
        next_streams,
        loss_all,
        grad_streams,
        grad_history,
        sum_projections,
        sum_attention,
        sum_up,
        sum_down,
        sum_first,
        grad_second_all,
        grad_bias_all,
        sum_gains,
    )


def fits(mesh):
    return mesh.shape["ctx"] == 4 and mesh.shape["dp"] == 8


def solution(mesh):
    specs = dict(
        in_specs=(
            P(None, "dp", "ctx", None),
            P(None, "dp", "ctx", None),
            P(None, "dp", "ctx", None),
            P("dp"),
            P("dp", "ctx"),
            P(),
            P(None, ("dp", "ctx"), None),
            P(("dp", "ctx"), None),
            P(("dp", "ctx"), None),
            P(("dp", "ctx"), None),
            P(("dp", "ctx"), None),
            P(),
            P(),
            P(None, ("dp", "ctx")),
        ),
        out_specs=(
            P(None, "dp", "ctx", None),
            P(),
            P(None, "dp", "ctx", None),
            P(None, "dp", "ctx", None),
            P(None, ("dp", "ctx"), None),
            P(("dp", "ctx"), None),
            P(("dp", "ctx"), None),
            P(("dp", "ctx"), None),
            P(("dp", "ctx"), None),
            P(),
            P(),
            P(None, ("dp", "ctx")),
        ),
        check_vma=False,
    )

    def chosen(*arrays):
        fast = fits(mesh) and arrays[0].shape[1] == 2 * mesh.shape["dp"]
        return jax.shard_map(local_fast if fast else local_plain, mesh=mesh, **specs)(*arrays)

    return chosen
```

```python
import functools
import math

import jax
import jax.numpy as jnp
from jax import lax
from jax.experimental import pallas as pl
from jax.experimental.pallas import tpu as pltpu
from jax.sharding import PartitionSpec as P

HEADS = 16
HEAD_DIM = 64
ROT = 16
AXES = ("dp", "ctx")

highest = lax.Precision.HIGHEST
epsilon = 1e-05
f32 = jnp.float32
bf16 = jnp.bfloat16
VMEM_BYTES = 60 * 1024 * 1024


def dot_nn(a, b, precision=None):
    return lax.dot_general(
        a, b, (((1,), (0,)), ((), ())), precision=precision, preferred_element_type=f32
    )


def dot_nt(a, b, precision=None):
    return lax.dot_general(
        a, b, (((1,), (1,)), ((), ())), precision=precision, preferred_element_type=f32
    )


def dot_tn(a, b, precision=None):
    return lax.dot_general(
        a, b, (((0,), (0,)), ((), ())), precision=precision, preferred_element_type=f32
    )


def normal_cdf(v):
    z = jnp.abs(v) * math.sqrt(0.5)
    t = 1.0 / (1.0 + 0.39 * z)
    bell = jnp.exp(-0.5 * v * v)
    poly = -0.22760540438261295
    for c in (
        0.8869388009365644,
        -0.6358388689155755,
        0.649907738051149,
        0.09125094908545259,
        0.23534677935551734,
    ):
        poly = poly * t + c
    half_tail = (0.5 * poly) * t * bell
    return jnp.where(v < 0.0, half_tail, 1.0 - half_tail), bell


def gelu_pair(v):
    cdf, bell = normal_cdf(v)
    return v * cdf, cdf + v * bell * (1.0 / math.sqrt(2.0 * math.pi))


def vmem(block=None, index_map=None):
    if block is None:
        return pl.BlockSpec(memory_space=pltpu.VMEM)
    return pl.BlockSpec(block, index_map)


def params(**kw):
    return pltpu.CompilerParams(vmem_limit_bytes=VMEM_BYTES, **kw)


Z_ORDER = (0, 2, 1, 3)


UP_BITS = (8, 16)
DOWN_BITS = (16, 8)


def gathered_from(me, place, outer):
    distance = 4 * (place // 16) + outer[0] * (place // 8 % 2) + outer[1] * (place // 4 % 2)
    return jnp.bitwise_xor(me, distance + Z_ORDER[place % 4])


def place_rows(me, ref, outer, out_ref):
    rows = ref.shape[-2]
    for place in range(ref.shape[0]):
        device = gathered_from(me, place, outer)
        out_ref[pl.ds(pl.multiple_of(device * rows, rows), rows), :] = ref[place]


def take_rows(me, from_ref, outer, refs):
    rows = refs[0].shape[-2]
    each_has = refs[0].shape[0]
    for place in range(each_has * len(refs)):
        device = gathered_from(me, place, outer)
        refs[place // each_has][place % each_has] = from_ref[
            pl.ds(pl.multiple_of(device * rows, rows), rows), :
        ]


def place_of_projection(me, place):
    distance = 8 * (place // 16) + 16 * (place // 8 % 2) + 4 * (place % 2)
    return jnp.bitwise_xor(me, distance + Z_ORDER[place // 2 % 4])


def place_rows_of_projection(me, ref, out_ref):
    rows = ref.shape[-2]
    for place in range(2 * ref.shape[0]):
        device = place_of_projection(me, place)
        out_ref[pl.ds(pl.multiple_of(device * rows, rows), rows), :] = ref[place // 2, place % 2, 0]


def place_tile(me, all_up_ref, some_down_ref, up_ref, down_ref):
    place_rows(me, all_up_ref, UP_BITS, up_ref)
    rows = some_down_ref.shape[1]
    for q, z in enumerate(Z_ORDER):
        at = pl.multiple_of(jnp.bitwise_xor(lax.rem(me, 4), z) * rows, rows)
        down_ref[pl.ds(at, rows), :] = some_down_ref[q]


def turn(x, cosine, sine_up, sine_down):
    return (
        x * cosine + pltpu.roll(x, ROT // 2, 1) * sine_up + pltpu.roll(x, 128 - ROT // 2, 1) * sine_down
    )


def allowed_limit(base, rows, prefix, axis):
    shape = (rows, 1) if axis == 0 else (1, rows)
    position = base + lax.broadcasted_iota(jnp.int32, shape, axis)
    return jnp.maximum(position, prefix - 1)


def flip(bit, by):
    return bit + by - 2 * bit * by


class Place:
    def __init__(self):
        self.group = lax.axis_index("dp")
        self.z = lax.axis_index("ctx")
        self.core = lax.rem(self.group, 2)
        self.x = lax.rem(lax.div(self.group, 2), 2)
        self.y = lax.div(self.group, 4)
        self.z_low = lax.rem(self.z, 2)
        self.z_high = lax.div(self.z, 2)

    def across(self, axis):
        if axis == "core":
            return (self.group + 1 - 2 * self.core, self.z)
        if axis == "x":
            return (self.group + 2 - 4 * self.x, self.z)
        if axis == "y":
            return (self.group + 4 - 8 * self.y, self.z)
        if axis == "zl":
            return (self.group, self.z + 1 - 2 * self.z_low)
        return (self.group, self.z + 2 - 4 * self.z_high)

    def device(self, y, x, core, z):
        pair = flip(self.y, y) * 4 + flip(self.x, x) * 2 + flip(self.core, core)
        return pair * 4 + flip(self.z_high, z // 2) * 2 + flip(self.z_low, z % 2)

    def code(self, k):
        return flip(self.z_high, lax.div(k, 2)), flip(self.z_low, lax.rem(k, 2))

    def block(self, k):
        return flip(self.z_low, lax.div(k, 2)) * 2 + flip(self.core, lax.rem(k, 2))

    def out_to(self, k):
        seq, half = self.code(k)
        return (self.group - self.core + half, 2 * self.core + seq)

    def back_to(self, k):
        return (self.group - self.core + self.z_high, self.block(k))

    def is_self(self, device):
        return jnp.logical_and(device[0] == self.group, device[1] == self.z)

    def meet(self, names):
        barrier = pltpu.get_barrier_semaphore()
        others = [self.across(name) for name in names]
        for step in range(1, 8):
            place = self.core * 4 + self.z + step
            others.append(
                (self.group - self.core + lax.rem(lax.div(place, 4), 2), lax.rem(place, 4))
            )
        for other in others:
            pl.semaphore_signal(barrier, inc=1, device_id=other, device_id_type=pl.DeviceIdType.MESH)
        pl.semaphore_wait(barrier, len(others))


class Sends:
    def __init__(self, here, send_sems, recv_sems):
        self.here, self.send_sems, self.recv_sems = here, send_sems, recv_sems
        self.used, self.open = 0, []

    def make(self, n, source, target, device):
        return pltpu.make_async_remote_copy(
            src_ref=source,
            dst_ref=target,
            send_sem=self.send_sems.at[n],
            recv_sem=self.recv_sems.at[n],
            device_id=device,
            device_id_type=pl.DeviceIdType.MESH,
        )

    def start(self, source, target, device):
        copy = self.make(self.used, source, target, device)
        self.used += 1
        copy.start()
        self.open.append(copy)
        return copy

    def four(self, source, target, device):
        base = self.used
        self.used += 4

        def copy(k):
            return self.make(base + k, source(k), target(k), device(k))

        def start(k):
            stays = self.here.is_self(device(k))

            @pl.when(stays)
            def _():
                pltpu.make_async_copy(source(k), target(k), self.recv_sems.at[base + k]).start()

            @pl.when(jnp.logical_not(stays))
            def _():
                copy(k).start()

        def sent(k):
            @pl.when(jnp.logical_not(self.here.is_self(device(k))))
            def _():
                copy(k).wait_send()

        def came(k):
            copy(k).wait_recv()

        return start, sent, came

    def finish(self):
        for copy in self.open:
            copy.wait_send()


def each(n, body):
    def step(i, _):
        body(i)
        return 0

    lax.fori_loop(0, n, step, 0)


class Gathers:
    def __init__(self, here, sends, refs):
        self.here, self.sends, self.refs = here, sends, refs
        self.coming = {name: [] for name in refs}

    def settle(self, name, first=0, count=1 << 20):
        left = []
        for at, n, copy in self.coming[name]:
            if at < first + count and first < at + n:
                copy.wait_recv()
            else:
                left.append((at, n, copy))
        self.coming[name] = left

    def move(self, name, axis, first, count, to):
        self.settle(name, first, count)
        ref = self.refs[name]
        copy = self.sends.start(
            ref.at[pl.ds(first, count)], ref.at[pl.ds(to, count)], self.here.across(axis)
        )
        self.coming[name].append((to, count, copy))

    def follow(self, plan):
        for name, axis, first, count, to in plan:
            self.move(name, axis, first, count, to)


def key_positions(length, blocks, axis):
    shape = (length, 1) if axis == 0 else (1, length)
    i = lax.broadcasted_iota(jnp.int32, shape, axis)
    piece = length // (2 * blocks)
    return (
        lax.rem(lax.div(i, piece), blocks) * (2 * piece)
        + lax.div(i, length // 2) * piece
        + lax.rem(i, piece)
    )


PLAN_AFTER_ROWS_1 = (("proj", "zl", 0, 2, 2),)
PLAN_AFTER_SMALL = (("up", "zl", 0, 2, 2), ("down", "zl", 0, 2, 2))
PLAN_AFTER_ROWS_2 = (("proj", "y", 0, 4, 4), ("proj", "x", 0, 4, 8))
PLAN_AFTER_ROWS_0 = (
    ("up", "y", 0, 4, 4),
    ("down", "x", 0, 4, 4),
    ("up", "x", 0, 4, 8),
    ("down", "y", 0, 4, 8),
    ("proj", "x", 4, 4, 12),
)
PLAN_AFTER_NORM_1 = (("up", "x", 4, 4, 12), ("down", "y", 4, 4, 12))
PLAN_AFTER_NORM_2 = (("up", "core", 0, 8, 16), ("down", "core", 0, 8, 16))
PLAN_AFTER_HEADS = (
    ("up", "core", 8, 4, 24),
    ("down", "core", 8, 4, 24),
    ("up", "core", 12, 4, 28),
    ("down", "core", 12, 4, 28),
)


def front_body(
    prefix_ref, streams_ref, proj_in, up_in, down_in, out_in, small_in, count_in, cos_ref, rise_ref, fall_ref,
    received_out, normed_out, proj_out, far_out, up_ref, down_ref, small_ref, count_ref,
    q_out, k_out, v_out, heads_out, lse_ref, got_ref,
    received_ref, normed_ref, proj_ref, weight_ref, q_ref, k_ref, v_ref, heads_ref,
    small_got, count_got, local_sems, send_sems, recv_sems,
):
    here = Place()
    sends = Sends(here, send_sems, recv_sems)
    gathers = Gathers(here, sends, {"proj": proj_ref, "up": up_ref, "down": down_ref})
    features = proj_ref.shape[-1]
    units = down_in.shape[0]
    kept = []

    def keep(source, target):
        copy = pltpu.make_async_copy(source, target, local_sems.at[len(kept)])
        kept.append(copy)
        copy.start()
        return copy

    def columns(which):
        return proj_in.at[:, :, pl.ds(pl.multiple_of(which * features, features), features)]

    small_ref[...] = small_in[...]
    count_ref[...] = count_in[...]
    here.meet(("x", "y"))
    small_steps = []

    def small_start(axis):
        n = len(small_steps)
        device = here.across(axis)
        small_steps.append(
            (
                sends.start(small_ref, small_got.at[n], device),
                sends.start(count_ref, count_got.at[n], device),
            )
        )

    def small_end():
        n = len(small_steps) - 1
        for copy in small_steps[n]:
            copy.wait()
        sends.open = [c for c in sends.open if not any(c is s for s in small_steps[n])]
        small_ref[...] += small_got[n]
        count_ref[...] += count_got[n]

    def stream(s):
        def source(k):
            seq, half = here.code(k)
            return streams_ref.at[s, 2 * seq + half]

        steps = sends.four(source, lambda k: received_ref.at[s, k], here.out_to)
        each(4, steps[0])
        return steps

    chunk = 32

    def norm(s, steps):
        gain = small_ref[s : s + 1, :].astype(f32)

        def step(k):
            steps[2](k)
            block = here.block(k)

            def body(i, _):
                at = pl.ds(pl.multiple_of(i * chunk, chunk), chunk)
                x = received_ref[s, k, at, :].astype(f32)
                x = x - jnp.mean(x, axis=-1, keepdims=True)
                scale = lax.rsqrt(jnp.mean(x * x, axis=-1, keepdims=True) + epsilon)
                normed_ref[s, here.core, block, at, :] = (x * scale * gain).astype(bf16)
                return 0

            lax.fori_loop(0, received_ref.shape[2] // chunk, body, 0, unroll=2)

        each(4, step)
        keep(received_ref.at[s], received_out.at[s])
        keep(normed_ref.at[s, here.core], normed_out.at[s, here.core])
        return sends.start(
            normed_ref.at[s, here.core], normed_ref.at[s, here.core], here.across("core")
        )

    small_start("zl")
    gathers.coming["proj"].append(
        (0, 1, sends.start(columns(1 - here.core), proj_ref.at[0, 1], here.across("core")))
    )
    own = [
        keep(columns(here.core), proj_ref.at[0, 0]),
        keep(up_in, up_ref.at[0]),
        keep(down_in, down_ref.at[0, pl.ds(0, units)]),
        keep(out_in, down_ref.at[0, pl.ds(units, out_in.shape[0])]),
    ]
    for copy in own:
        copy.wait()
    gathers.move("proj", "zh", 0, 1, 1)
    small_end()
    small_start("zh")
    gathers.move("up", "zh", 0, 1, 1)
    small_end()
    small_start("x")
    gathers.move("down", "zh", 0, 1, 1)
    rows_1 = stream(1)
    small_end()
    small_start("y")
    gathers.follow(PLAN_AFTER_ROWS_1)
    small_end()
    small_start("core")
    small_end()
    gathers.follow(PLAN_AFTER_SMALL)
    rows_2 = stream(2)
    gathers.follow(PLAN_AFTER_ROWS_2)
    rows_0 = stream(0)
    gathers.follow(PLAN_AFTER_ROWS_0)
    others = [norm(1, rows_1)]
    gathers.follow(PLAN_AFTER_NORM_1)
    others.append(norm(2, rows_2))
    gathers.settle("proj")
    far = sends.start(proj_ref, far_out, here.across("core"))
    keep(proj_ref, proj_out)

    def assemble(s):
        rows = proj_ref.shape[-2]
        for x in range(2):
            for y in range(2):
                for q, z in enumerate(Z_ORDER):
                    for core in range(2):
                        device = here.device(y, x, core, z)
                        at = pl.ds(pl.multiple_of(device * rows, rows), rows)
                        weight_ref[s, at, :] = proj_ref[(x * 2 + y) * 4 + q, core, s]

    each(3, assemble)
    gathers.follow(PLAN_AFTER_NORM_2)

    _, blocks, piece, width = q_ref.shape
    half_rows = blocks * piece
    length = 2 * half_rows

    def project(s, out_ref):
        def step(half):
            y = dot_nn(normed_ref[s, half].reshape(half_rows, -1), weight_ref[s])
            if s < 2:
                tables = [r[half].reshape(half_rows, 128) for r in (cos_ref, rise_ref, fall_ref)]
                y = jnp.concatenate(
                    [turn(y[:, i : i + 128], *tables) for i in range(0, width, 128)], axis=1
                )
            y = y.astype(bf16)
            if s == 0:
                y = y * jnp.asarray(HEAD_DIM**-0.5, bf16)
            out_ref[half] = y.reshape(blocks, piece, width)

        each(2, step)

    for copy, s in zip(others, (1, 2)):
        copy.wait_recv()
        keep(normed_ref.at[s, 1 - here.core], normed_out.at[s, 1 - here.core])
    project(1, k_ref)
    keep(k_ref, k_out)
    project(2, v_ref)
    keep(v_ref, v_out)
    last = norm(0, rows_0)
    last.wait_recv()
    keep(normed_ref.at[0, 1 - here.core], normed_out.at[0, 1 - here.core])
    project(0, q_ref)
    keep(q_ref, q_out)

    rows = 2 * piece
    lane = lax.broadcasted_iota(jnp.int32, (rows, 128), 1)
    key_index = key_positions(length, blocks, 1)
    heads_steps = sends.four(
        lambda k: heads_ref.at[here.block(k)], lambda k: got_ref.at[k], here.back_to
    )

    def block_body(k):
        block = here.block(k)
        allowed = key_index <= allowed_limit(block * rows, rows, prefix_ref[0], 0)
        lse_all = jnp.zeros((rows, 8), f32)
        lse_lane = lax.broadcasted_iota(jnp.int32, (rows, 8), 1)
        for pair in range(width // 128):
            at = slice(pair * 128, pair * 128 + 128)
            queries = q_ref[:, block, :, at].reshape(rows, 128)
            keys = k_ref[:, :, :, at].reshape(length, 128)
            values = v_ref[:, :, :, at].reshape(length, 128)
            results = []
            for h in range(2):
                chosen = (lane < 64) if h == 0 else (lane >= 64)
                scores = dot_nt(jnp.where(chosen, queries, jnp.zeros_like(queries)), keys)
                scores = jnp.where(allowed, scores, -1e30)
                top = jnp.max(scores, axis=-1, keepdims=True)
                weights = jnp.exp(scores - top)
                total = jnp.sum(weights, axis=-1, keepdims=True)
                results.append(dot_nn(weights.astype(bf16), values) / total)
                lse_all = jnp.where(lse_lane == pair * 2 + h, top + jnp.log(total), lse_all)
            heads_ref[block, :, at] = jnp.where(lane < 64, results[0], results[1]).astype(bf16)
        lse_ref[block] = lse_all
        heads_steps[0](k)

    each(4, block_body)
    keep(heads_ref, heads_out)
    gathers.follow(PLAN_AFTER_HEADS)
    each(4, heads_steps[2])
    for name in ("up", "down"):
        gathers.settle(name)
    far.wait_recv()
    for steps in (rows_1, rows_2, rows_0, heads_steps):
        each(4, steps[1])
    sends.finish()
    for copy in kept[len(own) :]:
        copy.wait()


def mlp_forward_body(
    ids, heads_ref, res_ref, gain_ref, all_up_ref, some_down_ref, gathered_out_ref,
    hidden_ref, normed_ref, active_ref, slope_ref, layer_ref,
    out_w_ref, up_ref, down_ref,
):
    step = pl.program_id(0)
    seqs, rows, width = res_ref.shape[1:]
    me = ids[4]

    @pl.when(step == 0)
    def _():
        place_rows(me, gathered_out_ref, DOWN_BITS, out_w_ref)
        hidden_ref[...] = res_ref[0].astype(f32)
        for k in range(heads_ref.shape[0]):
            code = jnp.bitwise_xor(ids[0], k)
            features = heads_ref.shape[-1]
            at = pl.ds(pl.multiple_of(lax.rem(code, 2) * features, features), features)
            hidden_ref[lax.div(code, 2)] += dot_nn(heads_ref[k], out_w_ref[at, :])
        gain = gain_ref[3:4, :].astype(f32)
        for j in range(seqs):
            x = hidden_ref[j]
            layer_ref[j] = x
            x = x - jnp.mean(x, axis=-1, keepdims=True)
            scale = lax.rsqrt(jnp.mean(x * x, axis=-1, keepdims=True) + epsilon)
            normed_ref[j] = (x * scale * gain).astype(bf16)

    place_tile(me, all_up_ref, some_down_ref, up_ref, down_ref)
    upper = dot_nn(normed_ref[...].reshape(seqs * rows, width), up_ref[...])
    active, slope = gelu_pair(upper)
    active = active.astype(bf16)
    active_ref[...] = active
    slope_ref[...] = slope.astype(bf16)
    layer_ref[...] += dot_nn(active, down_ref[...]).reshape(seqs, rows, width)


def mixer_body(
    scal_ref, layer_ref, hist_ref, teacher_ref, valid_ref, gain_ref, first_ref, second_ref, bias_ref,
    next_ref, ghist_ref, glayer_ref, gfirst_ref, gsecond_ref, stats_ref, ggain_ref,
    coef_ref, part_ref, gnext_ref,
):
    step = pl.program_id(0)
    past, rows, width = hist_ref.shape
    streams = teacher_ref.shape[0]
    outs = past + 1
    span = first_ref.shape[0]

    @pl.when(step == 0)
    def _():
        gfirst_ref[...] = jnp.zeros_like(gfirst_ref)
        gsecond_ref[...] = jnp.zeros_like(gsecond_ref)
        stats_ref[...] = jnp.zeros_like(stats_ref)
        ggain_ref[...] = jnp.zeros_like(ggain_ref)

    factor = scal_ref[0]
    x = layer_ref[...]
    scale = lax.rsqrt(jnp.mean(x * x, axis=-1, keepdims=True) + epsilon)
    gain = gain_ref[4:5, :].astype(f32)
    normed = (x * scale * gain).astype(bf16)
    mix_hidden = dot_nt(normed, first_ref[...])
    mix_active, mix_slope = gelu_pair(mix_hidden)
    coeff = dot_nn(mix_active, second_ref[...], highest) + bias_ref[...]
    for c in range(streams * outs):
        coef_ref[c] = jnp.broadcast_to(coeff[:, c : c + 1], (rows, 128))
    part_ref[...] = jnp.zeros_like(part_ref)

    chunk = 16
    lanes = 512

    def rows_body(i, loss_rows):
        at = pl.ds(pl.multiple_of(i * chunk, chunk), chunk)
        valid = jnp.broadcast_to(valid_ref[at, :], (chunk, 128))

        def read(j, lane_at):
            return layer_ref[at, lane_at] if j == past else hist_ref[j, at, lane_at].astype(f32)

        for l0 in range(0, width, 256):
            lane_at = slice(l0, l0 + 256)
            sums = [jnp.zeros((chunk, 256), f32) for _ in range(streams)]
            for j in range(outs):
                value = read(j, lane_at)
                for s in range(streams):
                    c = coef_ref[s * outs + j, at, :]
                    sums[s] = sums[s] + jnp.concatenate([c, c], axis=1) * value
            both = jnp.concatenate([valid, valid], axis=1)
            for s in range(streams):
                next_ref[s, at, lane_at] = sums[s].astype(bf16)
                difference = sums[s] - teacher_ref[s, at, lane_at].astype(f32)
                weighted = both * difference
                gnext_ref[s, at, lane_at] = factor * weighted
                square = weighted * difference
                loss_rows = loss_rows + square[:, :128] + square[:, 128:]
        for l0 in range(0, width, lanes):
            lane_at = slice(l0, l0 + lanes)
            for j in range(outs):
                value = read(j, lane_at)
                total = jnp.zeros((chunk, lanes), f32)
                for s in range(streams):
                    grad = gnext_ref[s, at, lane_at]
                    c = coef_ref[s * outs + j, at, :]
                    total = total + jnp.concatenate([c] * (lanes // 128), axis=1) * grad
                    product = grad * value
                    folded = product[:, :128]
                    for q in range(128, lanes, 128):
                        folded = folded + product[:, q : q + 128]
                    part_ref[s * outs + j, at, :] += folded
                if j == past:
                    glayer_ref[at, lane_at] = total
                else:
                    ghist_ref[j, at, lane_at] = total.astype(bf16)
        return loss_rows

    loss_rows = lax.fori_loop(0, rows // chunk, rows_body, jnp.zeros((chunk, 128), f32))
    lane = lax.broadcasted_iota(jnp.int32, (rows, span), 1)
    grad_coeff = jnp.zeros((rows, span), f32)
    for c in range(streams * outs):
        grad_coeff = jnp.where(lane == c, jnp.sum(part_ref[c], axis=-1, keepdims=True), grad_coeff)
    gsecond_ref[...] += dot_tn(mix_active, grad_coeff, highest)
    stats_ref[0:1, :] += jnp.sum(grad_coeff, axis=0, keepdims=True)
    stats_ref[1:2, :] += jnp.broadcast_to(jnp.sum(loss_rows), (1, span))
    grad_active = dot_nt(grad_coeff, second_ref[...], highest)
    grad_mix = (grad_active * mix_slope).astype(bf16)
    gfirst_ref[...] += dot_tn(grad_mix, normed)
    grad_normed = dot_nn(grad_mix, first_ref[...])
    x = layer_ref[...]
    ggain_ref[...] += jnp.sum(grad_normed * (x * scale), axis=0, keepdims=True)
    inner = grad_normed * gain
    mean = jnp.mean(inner * x, axis=-1, keepdims=True)
    glayer_ref[...] += scale * inner - x * (scale * scale * scale * mean)


def norm_back(x, grad, gain):
    centered = x - jnp.mean(x, axis=-1, keepdims=True)
    scale = lax.rsqrt(jnp.mean(centered * centered, axis=-1, keepdims=True) + epsilon)
    unit = centered * scale
    grad_gain = jnp.sum(grad * unit, axis=0, keepdims=True)
    inner = grad * gain
    inner = (
        inner
        - jnp.mean(inner, axis=-1, keepdims=True)
        - unit * jnp.mean(inner * unit, axis=-1, keepdims=True)
    )
    return scale * inner, grad_gain


def mlp_backward_body(
    ids, glayer_ref, active_ref, slope_ref, normed_ref, all_up_ref, some_down_ref,
    gu0, gu1, gu2, gu3, gd0, gd1, gd2, gd3, sum_ref,
    low_ref, normed_t_ref, up_ref, down_ref, tile_ref,
):
    step = pl.program_id(0)
    seqs, rows, width = glayer_ref.shape
    tokens = seqs * rows
    me = ids[4]
    place = lax.rem(me, 4)

    @pl.when(step == 0)
    def _():
        low_ref[...] = glayer_ref[...].astype(bf16)
        sum_ref[...] = jnp.zeros_like(sum_ref)
        normed_t_ref[...] = normed_ref[...].reshape(tokens, width).T

    place_tile(me, all_up_ref, some_down_ref, up_ref, down_ref)
    grad = low_ref[...].reshape(tokens, width)
    grad_active = dot_nt(grad, down_ref[...])
    grad_upper = (grad_active * slope_ref[...].astype(f32)).astype(bf16)
    sum_ref[...] += dot_nt(grad_upper, up_ref[...]).reshape(seqs, rows, width)
    down_ref[...] = dot_tn(active_ref[...], grad).astype(bf16)
    for p, ref in enumerate((gd0, gd1, gd2, gd3)):

        @pl.when(lax.div(step, 2) == p)
        def _(ref=ref):
            block_rows = ref.shape[1]
            for q, z in enumerate(Z_ORDER):
                at = pl.multiple_of(jnp.bitwise_xor(place, z) * block_rows, block_rows)
                ref[q] = down_ref[pl.ds(at, block_rows), :]

    tile_ref[...] = dot_nn(normed_t_ref[...], grad_upper).astype(bf16)
    take_rows(me, tile_ref, UP_BITS, (gu0, gu1, gu2, gu3))


def hidden_backward_body(
    ids, glayer_ref, sum_ref, hidden_ref, heads_ref, gain_ref, gathered_out_ref,
    gres_ref, g0, g1, g2, g3, go0, go1, go2, go3, ggain_ref,
    out_w_ref, gout_ref,
):
    seqs, rows, width = hidden_ref.shape
    me = ids[4]
    place_rows(me, gathered_out_ref, DOWN_BITS, out_w_ref)
    gain = gain_ref[3:4, :].astype(f32)
    ggain = jnp.zeros((1, width), f32)
    for j in range(seqs):
        back, part = norm_back(hidden_ref[j], sum_ref[j], gain)
        ggain = ggain + part
        gres_ref[j] = (glayer_ref[j] + back).astype(bf16)
    ggain_ref[...] = ggain
    gout_ref[...] = jnp.zeros_like(gout_ref)
    for k, out in enumerate((g0, g1, g2, g3)):
        code = jnp.bitwise_xor(ids[0], k)
        features = out.shape[-1]
        at = pl.ds(pl.multiple_of(lax.rem(code, 2) * features, features), features)
        low = gres_ref[lax.div(code, 2)]
        out[...] = dot_nt(low, out_w_ref[at, :]).astype(bf16)
        gout_ref[at, :] += dot_tn(heads_ref[k], low)
    out_w_ref[...] = gout_ref[...].astype(bf16)
    take_rows(me, out_w_ref, DOWN_BITS, (go0, go1, go2, go3))


def attention_backward_body(
    ids, q_ref, k_ref, v_ref, heads_ref, lse_ref, g0, g1, g2, g3, cos_ref, up_ref, down_ref,
    own_ref, send_ref,
    dk_ref, dv_ref, kt_ref, turn_ref,
):
    half = ids[1]
    mine = ids[2]
    prefix = ids[3]
    pair = pl.program_id(0)
    _, blocks, piece, lanes = q_ref.shape
    rows = 2 * piece
    length = blocks * rows
    dk_ref[...] = jnp.zeros_like(dk_ref)
    dv_ref[...] = jnp.zeros_like(dv_ref)
    keys = k_ref[...].reshape(length, lanes)
    values = v_ref[...].reshape(length, lanes)
    kt_ref[...] = keys.T
    lane = lax.broadcasted_iota(jnp.int32, (rows, lanes), 1)
    key_index = key_positions(length, blocks, 0)
    choose = (
        lax.div(lax.broadcasted_iota(jnp.int32, (8, lanes), 1), 64)
        == lax.broadcasted_iota(jnp.int32, (8, lanes), 0)
    ).astype(f32)

    def give(s, x):
        turn_ref[...] = x.astype(bf16).reshape(2, blocks, piece, lanes)
        own_ref[s] = turn_ref[half]
        send_ref[s] = turn_ref[1 - half]

    def back(x, block):
        if block is None:
            parts = [r[...].reshape(length, lanes) for r in (cos_ref, up_ref, down_ref)]
        else:
            parts = [r[:, block].reshape(rows, lanes) for r in (cos_ref, up_ref, down_ref)]
        return (
            x * parts[0]
            - pltpu.roll(x, ROT // 2, 1) * parts[1]
            - pltpu.roll(x, 128 - ROT // 2, 1) * parts[2]
        )

    for k, g in enumerate((g0, g1, g2, g3)):
        block = jnp.bitwise_xor(mine, k)
        queries = q_ref[:, block].reshape(rows, lanes)
        grads = g[...]
        inner_rows = dot_nt(choose, grads.astype(f32) * heads_ref[block].astype(f32), highest)
        limit = allowed_limit(block * rows, rows, prefix, 1)
        allowed = key_index <= limit
        dqt = []
        for h in range(2):
            chosen = (lane < 64) if h == 0 else (lane >= 64)
            q_h = jnp.where(chosen, queries, jnp.zeros_like(queries))
            g_h = jnp.where(chosen, grads, jnp.zeros_like(grads))
            scores = dot_nt(keys, q_h)
            probs = jnp.where(allowed, jnp.exp(scores - lse_ref[pair * 2 + h, block]), 0.0)
            grad_probs = dot_nt(values, g_h)
            grad_scores = (probs * (grad_probs - inner_rows[h : h + 1, :])).astype(bf16)
            dv_ref[...] += dot_nn(probs.astype(bf16), g_h)
            dk_ref[...] += dot_nn(grad_scores, q_h)
            dqt.append(dot_nn(kt_ref[...], grad_scores)[h * 64 : h * 64 + 64, :])
        dq = jnp.concatenate(dqt, axis=0).T * (HEAD_DIM**-0.5)
        low = back(dq, block).astype(bf16)
        turn_ref[:, 0] = low.reshape(2, piece, lanes)
        own_ref[0, block] = turn_ref[half, 0]
        send_ref[0, block] = turn_ref[1 - half, 0]
    give(1, back(dk_ref[...], None))
    give(2, dv_ref[...])


def projection_backward_body(
    ids, normed_ref, d_own_ref, d_send_ref, d_recv_ref, proj_ref, far_ref,
    received_ref, gain_ref,
    gp0, gp1, o0, o1, o2, o3, ggain_ref,
    w_own_ref, w_other_ref, grad_ref,
):
    mine = ids[2]
    me = ids[4]
    s = pl.program_id(0)
    _, _, blocks, piece, width = normed_ref.shape
    half = ids[1]
    rows = blocks * piece
    place_rows_of_projection(me, proj_ref, w_own_ref)
    place_rows_of_projection(jnp.bitwise_xor(me, 4), far_ref, w_other_ref)
    d_own = d_own_ref[...].reshape(rows, -1)
    grad = dot_tn(normed_ref[0, half].reshape(rows, width), d_own)
    grad = grad + dot_tn(
        normed_ref[0, 1 - half].reshape(rows, width), d_send_ref[...].reshape(rows, -1)
    )
    grad_ref[...] = grad.astype(bf16)
    for place in range(32):
        device = place_of_projection(me, place)
        ref = (gp0, gp1)[place // 16]
        shard = ref.shape[-2]
        at = pl.ds(pl.multiple_of(device * shard, shard), shard)
        ref[place % 16 // 2, place % 2, 0] = grad_ref[at, :]
    gain = gain_ref[pl.ds(s, 1), :].astype(f32)
    total = jnp.zeros((1, width), f32)
    for k, o in enumerate((o0, o1, o2, o3)):
        block = jnp.bitwise_xor(mine, k)
        grad_normed = dot_nt(d_own_ref[0, block], w_own_ref[...]) + dot_nt(
            d_recv_ref[0, block], w_other_ref[...]
        )
        back, part = norm_back(received_ref[0, k].astype(f32), grad_normed, gain)
        o[0] = back.astype(bf16)
        total = total + part
    ggain_ref[0] = total


def swap(x, bit, count):
    return lax.ppermute(x, AXES, [(i, i ^ bit) for i in range(count)])


def add_all(x, count):
    bit = 1
    while bit < count:
        x = x + swap(x, bit, count)
        bit *= 2
    return x


def scatter_sum(x, steps, me, count):
    gone = []
    for bit, axis in steps:
        at = axis - sum(1 for g in gone if g < axis)
        mine = jnp.where((me & bit) == 0, 0, 1)
        keep = lax.dynamic_index_in_dim(x, mine, at, keepdims=False)
        send = lax.dynamic_index_in_dim(x, 1 - mine, at, keepdims=False)
        x = keep + swap(send, bit, count)
        gone.append(axis)
    return x


def rotary_lanes(length, piece):
    lane = jnp.arange(128, dtype=jnp.int32) % HEAD_DIM
    step = (lane % (ROT // 2)).astype(f32)
    inverse = jnp.exp(step * (-2.0 * math.log(10000.0) / ROT))
    angles = jnp.arange(length, dtype=jnp.int32).astype(f32)[:, None] * inverse[None, :]
    cosine = jnp.where(lane < ROT, jnp.cos(angles), 1.0)
    sine = jnp.sin(angles)
    up = jnp.where((lane >= ROT // 2) & (lane < ROT), sine, 0.0)
    down = jnp.where(lane < ROT // 2, -sine, 0.0)
    return [
        t.reshape(-1, 2, piece, 128).transpose(1, 0, 2, 3) for t in (cosine, up, down)
    ]


def local_fast(
    streams, history, teacher, prefix, valid_mask, loss_scale, projections, attention_out,
    up_weight, down_weight, mixer_first, mixer_second, mixer_bias, gains,
):
    lines = lax.axis_size("ctx")
    count = lax.axis_size("dp") * lines
    place = lax.axis_index("ctx")
    group = lax.axis_index("dp")
    me = group * lines + place
    half = group % 2
    mine = 2 * (place % 2) + half
    seqs, rows, width = streams.shape[1:]
    tokens = seqs * rows
    piece = rows // 2
    length = rows * lines
    features = width // 2
    hidden_units = down_weight.shape[0] * count
    past = history.shape[0]
    count_of_streams = teacher.shape[0]
    mixw = mixer_bias.shape[0]
    span = 64

    def out_perm(k):
        pairs = []
        for i in range(count):
            pair, core, z = i // (2 * lines), (i // lines) % 2, i % lines
            code = z ^ k
            pairs.append((i, (pair * 2 + code % 2) * lines + 2 * core + code // 2))
        return pairs

    def send_out(x, k):
        return lax.ppermute(x, AXES, out_perm(k))

    def send_back(x, k):
        return lax.ppermute(x, AXES, [(b, a) for a, b in out_perm(k)])

    both_prefix = swap(prefix, lines, count)
    source_half = place // 2
    prefix_pair = jnp.where(source_half == half, prefix, both_prefix)
    my_prefix = jnp.where(place % 2 == 0, prefix_pair[0], prefix_pair[1])
    ids = jnp.stack([place, half, mine, my_prefix, me]).astype(jnp.int32)

    second = jnp.pad(mixer_second, ((0, span - mixw), (0, span - mixw)))
    bias = jnp.pad(mixer_bias, (0, span - mixw))[None]
    valid = valid_mask.astype(f32).reshape(tokens, 1)
    core = lines
    column, row = core * 2, core * 4
    shard = width // count
    unit_shard = hidden_units // count

    small = jnp.concatenate([gains, jnp.zeros((3, shard), bf16), mixer_first.T], axis=0)
    small = jnp.pad(small, ((0, span + 8 - small.shape[0]), (0, 0)))
    lane_place = jnp.arange(width, dtype=jnp.int32) // shard
    small = jnp.where(lane_place == me, jnp.tile(small, (1, count)), jnp.zeros((), bf16))
    counted = jnp.full((8, 128), jnp.sum(valid), f32)

    smem = pl.BlockSpec(memory_space=pltpu.SMEM)
    anywhere = pl.BlockSpec(memory_space=pl.ANY)
    proj_shape = (count // 2, 2, 3, shard, features)
    tables = rotary_lanes(length, piece)
    row_shape = (3, 4, piece, width)
    normed_shape = (3, 2, lines, piece, width)
    wide_shape = (2, lines, piece, features)
    heads_shape = (lines, rows, features)

    def array(shape, dtype=bf16):
        return jax.ShapeDtypeStruct(shape, dtype)

    (
        received, normed, proj, proj_other, up_all, down_all, small, counted,
        queries, keys, values, heads_seq, lse, heads,
    ) = pl.pallas_call(
        front_body,
        in_specs=[smem, anywhere] + [vmem()] * 9,
        out_specs=[anywhere] * 6 + [vmem()] * 2 + [anywhere] * 4 + [vmem(), anywhere],
        out_shape=[
            array(row_shape),
            array(normed_shape),
            array(proj_shape),
            array(proj_shape),
            array((count, shard, hidden_units)),
            array((count, unit_shard + shard, width)),
            array((span + 8, width)),
            array((8, 128), f32),
            array(wide_shape),
            array(wide_shape),
            array(wide_shape),
            array(heads_shape),
            array((lines, rows, 8), f32),
            array((4, rows, features)),
        ],
        scratch_shapes=[
            pltpu.VMEM(row_shape, bf16),
            pltpu.VMEM(normed_shape, bf16),
            pltpu.VMEM(proj_shape, bf16),
            pltpu.VMEM((3, width, features), bf16),
            pltpu.VMEM(wide_shape, bf16),
            pltpu.VMEM(wide_shape, bf16),
            pltpu.VMEM(wide_shape, bf16),
            pltpu.VMEM(heads_shape, bf16),
            pltpu.VMEM((5, span + 8, width), bf16),
            pltpu.VMEM((5, 8, 128), f32),
            pltpu.SemaphoreType.DMA((24,)),
            pltpu.SemaphoreType.DMA((64,)),
            pltpu.SemaphoreType.DMA((64,)),
        ],
        compiler_params=params(collective_id=0, has_side_effects=True),
        name="front",
    )(
        my_prefix.reshape(1),
        streams.reshape(streams.shape[0], 2 * seqs, piece, width),
        projections, up_weight, down_weight, attention_out, small, counted, *tables,
    )
    gain_full = small[:8].astype(f32)
    first_t = small[8:]
    token_total = counted[0, :1]
    factor = loss_scale * 2.0 / (4.0 * width * token_total)

    tile = 512
    tiles = hidden_units // tile
    token_shape = (seqs, rows, width)

    def fixed(shape, index=None):
        index = index or (0,) * len(shape)
        return pl.BlockSpec(shape, lambda i, *_: index)

    def up_column(i, ids):
        distance = lax.rem(lax.div(i, 2), 2) * 4 + lax.rem(i, 2) * 2 + lax.div(i, 4)
        return (0, 0, jnp.bitwise_xor(lax.div(ids[4], 4), distance))

    def down_block(p):
        return lambda i, *_: (jnp.clip(i - 2 * p, 0, 1), 0, 0)

    weight_specs = [
        pl.BlockSpec((count, shard, tile), up_column),
        pl.BlockSpec((4, unit_shard, width), lambda i, *_: (i, 0, 0)),
    ]
    out_weight_spec = pl.BlockSpec(
        (count, shard, width), lambda i, *_: (0, unit_shard // shard, 0)
    )
    tile_specs = [pl.BlockSpec((8, shard, tile), up_column)] * 4
    tile_specs += [pl.BlockSpec((4, unit_shard, width), down_block(p)) for p in range(4)]

    hidden, normed_mlp, active, slope, layer_out = pl.pallas_call(
        mlp_forward_body,
        grid_spec=pltpu.PrefetchScalarGridSpec(
            num_scalar_prefetch=1,
            grid=(tiles,),
            in_specs=[
                fixed((4, rows, features)),
                fixed((1,) + token_shape, (3, 0, 0, 0)),
                fixed((8, width)),
            ]
            + weight_specs
            + [out_weight_spec],
            out_specs=[
                fixed(token_shape),
                fixed(token_shape),
                pl.BlockSpec((tokens, tile), lambda i, *_: (0, i)),
                pl.BlockSpec((tokens, tile), lambda i, *_: (0, i)),
                fixed(token_shape),
            ],
            scratch_shapes=[
                pltpu.VMEM((width, width), bf16),
                pltpu.VMEM((width, tile), bf16),
                pltpu.VMEM((tile, width), bf16),
            ],
        ),
        out_shape=[
            jax.ShapeDtypeStruct(token_shape, f32),
            jax.ShapeDtypeStruct(token_shape, bf16),
            jax.ShapeDtypeStruct((tokens, hidden_units), bf16),
            jax.ShapeDtypeStruct((tokens, hidden_units), bf16),
            jax.ShapeDtypeStruct(token_shape, f32),
        ],
        compiler_params=params(),
        name="mlp_forward",
    )(ids, heads, streams, gain_full, up_all, down_all, down_all)

    block = 64
    next_streams, grad_history, grad_layer, g_first, g_second, stats, g_gain_mix = pl.pallas_call(
        mixer_body,
        grid=(tokens // block,),
        in_specs=[
            smem,
            pl.BlockSpec((block, width), lambda i: (i, 0)),
            pl.BlockSpec((past, block, width), lambda i: (0, i, 0)),
            pl.BlockSpec((count_of_streams, block, width), lambda i: (0, i, 0)),
            pl.BlockSpec((block, 1), lambda i: (i, 0)),
            fixed((8, width)),
            fixed((span, width)),
            fixed((span, span)),
            fixed((1, span)),
        ],
        out_specs=[
            pl.BlockSpec((count_of_streams, block, width), lambda i: (0, i, 0)),
            pl.BlockSpec((past, block, width), lambda i: (0, i, 0)),
            pl.BlockSpec((block, width), lambda i: (i, 0)),
            fixed((span, width)),
            fixed((span, span)),
            fixed((8, span)),
            fixed((1, width)),
        ],
        out_shape=[
            jax.ShapeDtypeStruct((count_of_streams, tokens, width), bf16),
            jax.ShapeDtypeStruct((past, tokens, width), bf16),
            jax.ShapeDtypeStruct((tokens, width), f32),
            jax.ShapeDtypeStruct((span, width), f32),
            jax.ShapeDtypeStruct((span, span), f32),
            jax.ShapeDtypeStruct((8, span), f32),
            jax.ShapeDtypeStruct((1, width), f32),
        ],
        scratch_shapes=[
            pltpu.VMEM((mixw, block, 128), f32),
            pltpu.VMEM((mixw, block, 128), f32),
            pltpu.VMEM((count_of_streams, block, width), f32),
        ],
        compiler_params=params(),
        name="mixer",
    )(
        factor,
        layer_out.reshape(tokens, width),
        history.reshape(past, tokens, width),
        teacher.reshape(count_of_streams, tokens, width),
        valid,
        gain_full,
        first_t,
        second,
        bias,
    )

    *g_ups, gd0, gd1, gd2, gd3, g_normed = pl.pallas_call(
        mlp_backward_body,
        grid_spec=pltpu.PrefetchScalarGridSpec(
            num_scalar_prefetch=1,
            grid=(tiles,),
            in_specs=[
                fixed(token_shape),
                pl.BlockSpec((tokens, tile), lambda i, *_: (0, i)),
                pl.BlockSpec((tokens, tile), lambda i, *_: (0, i)),
                fixed(token_shape),
            ]
            + weight_specs,
            out_specs=tile_specs + [fixed(token_shape)],
            scratch_shapes=[
                pltpu.VMEM(token_shape, bf16),
                pltpu.VMEM((width, tokens), bf16),
                pltpu.VMEM((width, tile), bf16),
                pltpu.VMEM((tile, width), bf16),
                pltpu.VMEM((width, tile), bf16),
            ],
        ),
        out_shape=[jax.ShapeDtypeStruct((8, shard, hidden_units), bf16)] * 4
        + [jax.ShapeDtypeStruct((8, unit_shard, width), bf16)] * 4
        + [jax.ShapeDtypeStruct(token_shape, f32)],
        compiler_params=params(),
        name="mlp_backward",
    )(ids, grad_layer.reshape(token_shape), active, slope, normed_mlp, up_all, down_all)
    g_downs = [gd0, gd1, gd2, gd3]

    hidden_results = pl.pallas_call(
        hidden_backward_body,
        grid_spec=pltpu.PrefetchScalarGridSpec(
            num_scalar_prefetch=1,
            grid=(1,),
            in_specs=[fixed(token_shape)] * 3
            + [fixed((4, rows, features)), fixed((8, width)), out_weight_spec],
            out_specs=[pl.BlockSpec((None,) + token_shape, lambda i, *_: (3, 0, 0, 0))]
            + [fixed((rows, features))] * 4
            + [fixed((8, shard, width))] * 4
            + [fixed((1, width))],
            scratch_shapes=[pltpu.VMEM((width, width), bf16), pltpu.VMEM((width, width), f32)],
        ),
        out_shape=[jax.ShapeDtypeStruct(streams.shape, bf16)]
        + [jax.ShapeDtypeStruct((rows, features), bf16)] * 4
        + [jax.ShapeDtypeStruct((8, shard, width), bf16)] * 4
        + [jax.ShapeDtypeStruct((1, width), f32)],
        compiler_params=params(),
        name="hidden_backward",
    )(ids, grad_layer.reshape(token_shape), g_normed, hidden, heads, gain_full, down_all)
    g_streams, gh0, gh1, gh2, gh3, go0, go1, go2, go3, g_gain_mlp = hidden_results

    def fold(x, bit):
        n = x.shape[0] // 2
        return x[:n] + swap(x[n:], bit, count)

    def last_fold(x, bit):
        return x[0].astype(f32) + swap(x[1], bit, count).astype(f32)

    up_pair = [g_ups[n] + swap(g_ups[n + 2], core, count) for n in range(2)]
    up_sum = up_pair[0] + swap(up_pair[1], column, count)
    up_sum = fold(fold(up_sum, row), 1)
    sum_up = last_fold(up_sum, 2)
    g_outs = [go0, go1, go2, go3]
    down_pair = [
        jnp.concatenate(
            [g[n] + swap(g[n + 2], core, count) for g in (g_downs, g_outs)], axis=1
        )
        for n in range(2)
    ]
    down_sum = down_pair[0] + swap(down_pair[1], row, count)
    down_sum = fold(fold(down_sum, column), 1)
    down_sum = last_fold(down_sum, 2)
    sum_down, sum_out = down_sum[:unit_shard], down_sum[unit_shard:]

    def scatter_columns(x):
        bits = count.bit_length() - 1
        x = x.reshape(x.shape[0], count, -1).transpose(1, 0, 2)
        x = x.reshape((2,) * bits + x.shape[1:])
        order = [(1 << (bits - 1 - axis), axis) for axis in range(bits)]
        return scatter_sum(x, order, me, count)

    g_head_rows = [send_out(g, k) for k, g in enumerate((gh0, gh1, gh2, gh3))]

    pairs = features // 128

    def pair_spec(shape):
        return pl.BlockSpec(shape + (128,), lambda i, *_: (0,) * len(shape) + (i,))

    d_own, d_send = pl.pallas_call(
        attention_backward_body,
        grid_spec=pltpu.PrefetchScalarGridSpec(
            num_scalar_prefetch=1,
            grid=(pairs,),
            in_specs=[pair_spec((2, lines, piece))] * 3
            + [pair_spec((lines, rows)), fixed((8, lines, 1, rows))]
            + [pair_spec((rows,))] * 4
            + [fixed((2, lines, piece, 128))] * 3,
            out_specs=[pair_spec((3, lines, piece))] * 2,
            scratch_shapes=[
                pltpu.VMEM((length, 128), f32),
                pltpu.VMEM((length, 128), f32),
                pltpu.VMEM((128, length), bf16),
                pltpu.VMEM((2, lines, piece, 128), bf16),
            ],
        ),
        out_shape=[jax.ShapeDtypeStruct((3, lines, piece, features), bf16)] * 2,
        compiler_params=params(),
        name="attention_backward",
    )(
        ids, queries, keys, values, heads_seq,
        lse.reshape(length, 8).T.reshape(8, lines, 1, rows), *g_head_rows, *tables,
    )
    d_recv = swap(d_send, lines, count)

    def stream_spec(shape):
        return pl.BlockSpec((1,) + shape, lambda s, *_: (s,) + (0,) * len(shape))

    back_piece = (piece, width)
    weight_spec = pl.BlockSpec((count // 2, 2, 1, shard, features), lambda s, *_: (0, 0, s, 0, 0))
    half_spec = pl.BlockSpec((count // 4, 2, 1, shard, features), lambda s, *_: (0, 0, s, 0, 0))
    gp0, gp1, b0, b1, b2, b3, g_gain_three = pl.pallas_call(
        projection_backward_body,
        grid_spec=pltpu.PrefetchScalarGridSpec(
            num_scalar_prefetch=1,
            grid=(3,),
            in_specs=[stream_spec((2, lines, piece, width))]
            + [stream_spec((lines, piece, features))] * 3
            + [weight_spec] * 2
            + [stream_spec((4,) + back_piece)]
            + [fixed((8, width))],
            out_specs=[half_spec] * 2
            + [stream_spec(back_piece)] * 4
            + [stream_spec((1, width))],
            scratch_shapes=[pltpu.VMEM((width, features), bf16)] * 3,
        ),
        out_shape=[jax.ShapeDtypeStruct((8, 2, 3, shard, features), bf16)] * 2
        + [jax.ShapeDtypeStruct((3,) + back_piece, bf16)] * 4
        + [jax.ShapeDtypeStruct((3, 1, width), f32)],
        compiler_params=params(),
        name="projection_backward",
    )(
        ids, normed, d_own, d_send, d_recv, proj, proj_other,
        received, gain_full,
    )

    grad_streams = g_streams.reshape(streams.shape[0], 2 * seqs, piece, width)
    for k, b in enumerate((b0, b1, b2, b3)):
        grad_streams = lax.dynamic_update_slice(
            grad_streams, send_back(b, k)[:, None], (0, place ^ k, 0, 0)
        )
    grad_streams = grad_streams.reshape(streams.shape)

    proj_sum = gp0 + swap(gp1, column, count)
    proj_sum = fold(fold(fold(proj_sum, row), 1), 2)[0]
    kept, sent = proj_sum[0], swap(proj_sum[1], core, count)
    low = half == 0
    grad_projections = jnp.concatenate(
        [jnp.where(low, kept, sent), jnp.where(low, sent, kept)], axis=-1
    ).astype(f32)

    early = scatter_columns(
        jnp.concatenate([g_first[:mixw], g_gain_mlp, g_gain_mix], axis=0)
    )
    late = scatter_columns(g_gain_three.reshape(3, width))
    grad_first = early[:mixw].T
    grad_gains = jnp.concatenate([late, early[mixw:]], axis=0)
    totals = add_all(jnp.concatenate([g_second, stats], axis=0), count)
    grad_second = totals[:mixw, :mixw]
    grad_bias = totals[span, :mixw]
    mean_loss = totals[span + 1, 0] / (4.0 * width * token_total[0])
    return (
        next_streams.reshape(teacher.shape),
        mean_loss,
        grad_streams,
        grad_history.reshape(history.shape),
        grad_projections,
        sum_out,
        sum_up,
        sum_down,
        grad_first,
        grad_second,
        grad_bias,
        grad_gains,
    )


def layer_norm(values, gain_row):
    centered = values - jnp.mean(values, axis=-1, keepdims=True)
    return (
        centered
        * lax.rsqrt(jnp.mean(centered * centered, axis=-1, keepdims=True) + epsilon)
        * gain_row
    )


def rms_norm(values, gain_row):
    return (
        values * lax.rsqrt(jnp.mean(values * values, axis=-1, keepdims=True) + epsilon) * gain_row
    )


def gelu_exact(values):
    return jax.nn.gelu(values, approximate=False)


def rotary_tables(positions):
    frequency_steps = jnp.arange(ROT // 2).astype(positions.dtype)
    inverse = jnp.exp(frequency_steps * (-2.0 * math.log(10000.0) / ROT))
    angles = positions[:, None] * inverse[None, :]
    return (jnp.cos(angles)[:, None, :], jnp.sin(angles)[:, None, :])


def rotate(values, cosine_table, sine_table, direction):
    row_count = values.shape[0]
    shaped = values.reshape(row_count, HEADS, HEAD_DIM)
    half_rot = ROT // 2
    first_half = shaped[:, :, :half_rot]
    second_half = shaped[:, :, half_rot:ROT]
    remainder = shaped[:, :, ROT:]
    turned_first = first_half * cosine_table - direction * second_half * sine_table
    turned_second = second_half * cosine_table + direction * first_half * sine_table
    return jnp.concatenate([turned_first, turned_second, remainder], axis=-1).reshape(row_count, -1)


def masked_scores(query_heads, key_heads, query_index, key_index, prefix_len):
    scores = jnp.einsum(
        "qhd,khd->hqk", query_heads, key_heads, preferred_element_type=jnp.float32
    ) * HEAD_DIM ** (-0.5)
    allowed = (key_index[None, :] <= query_index[:, None]) | (key_index[None, :] < prefix_len)
    return jnp.where(allowed[None], scores, -1e30)


def local_plain(
    streams,
    history,
    teacher,
    prefix,
    valid_mask,
    loss_scale,
    projections,
    attention_out,
    up_weight,
    down_weight,
    mixer_first,
    mixer_second,
    mixer_bias,
    gains,
):
    micro_count = streams.shape[1]
    row_count = streams.shape[2]
    model_width = streams.shape[3]
    length = row_count * lax.axis_size("ctx")
    query_index = lax.axis_index("ctx") * row_count + jnp.arange(row_count, dtype=jnp.int32)
    key_index = jnp.arange(length, dtype=jnp.int32)
    cosine_table, sine_table = rotary_tables(query_index.astype(jnp.float32))
    score_scale = HEAD_DIM ** (-0.5)
    valid_float = valid_mask.astype(jnp.float32)
    token_total = lax.psum(jnp.sum(valid_float), ("dp", "ctx"))
    factor = loss_scale[0] * 2.0 / (4.0 * model_width * token_total)

    def one_batch(totals, number):
        (
            kept_projections,
            kept_attention,
            kept_gains,
            kept_up,
            kept_down,
            kept_first,
            kept_second,
            kept_bias,
            kept_loss,
        ) = totals
        stream_block = lax.dynamic_index_in_dim(streams, number, 1, keepdims=False)
        past_outputs = lax.dynamic_index_in_dim(history, number, 1, keepdims=False)
        target = lax.dynamic_index_in_dim(teacher, number, 1, keepdims=False).astype(jnp.float32)
        prefix_len = lax.dynamic_index_in_dim(prefix, number, 0, keepdims=False)
        valid_row = lax.dynamic_index_in_dim(valid_float, number, 0, keepdims=False)
        proj_full, out_full, gain_low, up_full, down_full, first_full = (
            lax.all_gather(projections, ("dp", "ctx"), axis=1, tiled=True),
            lax.all_gather(attention_out, ("dp", "ctx"), axis=0, tiled=True),
            lax.all_gather(gains, ("dp", "ctx"), axis=1, tiled=True),
            lax.all_gather(up_weight, ("dp", "ctx"), axis=0, tiled=True),
            lax.all_gather(down_weight, ("dp", "ctx"), axis=0, tiled=True),
            lax.all_gather(mixer_first, ("dp", "ctx"), axis=0, tiled=True),
        )
        gain_full = gain_low.astype(jnp.float32)
        inputs = stream_block.astype(jnp.float32)
        gain_three = gain_full[:3, None, :]
        normed_low = layer_norm(inputs[:3], gain_three).astype(jnp.bfloat16)
        projected = jnp.einsum(
            "std,sde->ste", normed_low, proj_full, preferred_element_type=jnp.float32
        )
        query_heads = (
            rotate(projected[0], cosine_table, sine_table, 1.0)
            .astype(jnp.bfloat16)
            .reshape(row_count, HEADS, HEAD_DIM)
        )
        key_low = rotate(projected[1], cosine_table, sine_table, 1.0).astype(jnp.bfloat16)
        value_low = projected[2].astype(jnp.bfloat16)
        all_keys, all_values = (
            lax.all_gather(key_low, "ctx", axis=0, tiled=True),
            lax.all_gather(value_low, "ctx", axis=0, tiled=True),
        )
        key_heads = all_keys.reshape(length, HEADS, HEAD_DIM)
        value_heads = all_values.reshape(length, HEADS, HEAD_DIM)
        scores = masked_scores(query_heads, key_heads, query_index, key_index, prefix_len)
        row_max = jnp.max(scores, axis=-1, keepdims=True)
        log_total = row_max + jnp.log(jnp.sum(jnp.exp(scores - row_max), axis=-1, keepdims=True))
        probs_low = jnp.exp(scores - log_total).astype(jnp.bfloat16)
        heads_low = (
            jnp.einsum("hqk,khd->qhd", probs_low, value_heads, preferred_element_type=jnp.float32)
            .reshape(row_count, model_width)
            .astype(jnp.bfloat16)
        )
        hidden = inputs[3] + jnp.dot(heads_low, out_full, preferred_element_type=jnp.float32)
        normed_mlp = layer_norm(hidden, gain_full[3]).astype(jnp.bfloat16)
        upper = jnp.dot(normed_mlp, up_full, preferred_element_type=jnp.float32)
        activated = gelu_exact(upper).astype(jnp.bfloat16)
        layer_out = hidden + jnp.dot(activated, down_full, preferred_element_type=jnp.float32)
        normed_mix = rms_norm(layer_out, gain_full[4]).astype(jnp.bfloat16)
        mix_hidden = jnp.dot(normed_mix, first_full, preferred_element_type=jnp.float32)
        mix_active = gelu_exact(mix_hidden)
        coeff = jnp.dot(mix_active, mixer_second, precision=highest) + mixer_bias
        coeff_grid = coeff.reshape(row_count, 4, -1)
        outputs_all = jnp.concatenate([past_outputs.astype(jnp.float32), layer_out[None]], axis=0)
        next_block = jnp.einsum("tsj,jtd->std", coeff_grid, outputs_all, precision=highest)
        difference = next_block - target
        loss_part = jnp.sum(jnp.sum(difference * difference, axis=(0, 2)) * valid_row) / (
            4.0 * model_width * token_total
        )
        grad_next = factor * valid_row[None, :, None] * difference
        grad_coeff = jnp.einsum("std,jtd->tsj", grad_next, outputs_all, precision=highest).reshape(
            row_count, -1
        )
        grad_outputs = jnp.einsum("tsj,std->jtd", coeff_grid, grad_next, precision=highest)
        grad_past = grad_outputs[:-1].astype(jnp.bfloat16)
        grad_second = jnp.dot(mix_active.T, grad_coeff, precision=highest)
        grad_bias = jnp.sum(grad_coeff, axis=0)
        grad_active = jnp.dot(grad_coeff, mixer_second.T, precision=highest)
        gelu_mix_back = jax.vjp(gelu_exact, mix_hidden)[1]
        grad_mix = gelu_mix_back(grad_active)[0].astype(jnp.bfloat16)
        grad_first = jnp.einsum(
            "td,tm->dm", normed_mix, grad_mix, preferred_element_type=jnp.float32
        )
        grad_normed_mix = jnp.einsum(
            "tm,dm->td", grad_mix, first_full, preferred_element_type=jnp.float32
        )
        rms_back = jax.vjp(rms_norm, layer_out, gain_full[4])[1]
        grad_layer_mix, grad_gain_mix = rms_back(grad_normed_mix)
        grad_layer = grad_outputs[-1] + grad_layer_mix
        grad_branch = grad_layer.astype(jnp.bfloat16)
        grad_down = jnp.einsum(
            "tf,td->fd", activated, grad_branch, preferred_element_type=jnp.float32
        )
        grad_active_up = jnp.einsum(
            "td,fd->tf", grad_branch, down_full, preferred_element_type=jnp.float32
        )
        gelu_up_back = jax.vjp(gelu_exact, upper)[1]
        grad_upper = gelu_up_back(grad_active_up)[0].astype(jnp.bfloat16)
        grad_up = jnp.einsum(
            "td,tf->df", normed_mlp, grad_upper, preferred_element_type=jnp.float32
        )
        grad_normed_mlp = jnp.einsum(
            "tf,df->td", grad_upper, up_full, preferred_element_type=jnp.float32
        )
        down_shard, first_shard, up_shard = (
            lax.psum_scatter(grad_down, ("dp", "ctx"), scatter_dimension=0, tiled=True),
            lax.psum_scatter(grad_first, ("dp", "ctx"), scatter_dimension=0, tiled=True),
            lax.psum_scatter(grad_up, ("dp", "ctx"), scatter_dimension=0, tiled=True),
        )
        down_next = kept_down + down_shard
        norm_mlp_back = jax.vjp(layer_norm, hidden, gain_full[3])[1]
        grad_hidden_mlp, grad_gain_mlp = norm_mlp_back(grad_normed_mlp)
        grad_hidden = grad_layer + grad_hidden_mlp
        grad_attn = grad_hidden.astype(jnp.bfloat16)
        grad_attention = jnp.einsum(
            "td,te->de", heads_low, grad_attn, preferred_element_type=jnp.float32
        )
        grad_heads = jnp.einsum(
            "te,de->td", grad_attn, out_full, preferred_element_type=jnp.float32
        ).astype(jnp.bfloat16)
        grad_head_grid = grad_heads.reshape(row_count, HEADS, HEAD_DIM)
        scores_again = masked_scores(query_heads, key_heads, query_index, key_index, prefix_len)
        probs_exact = jnp.exp(scores_again - log_total)
        probs_again = probs_exact.astype(jnp.bfloat16)
        grad_probs = jnp.einsum(
            "qhd,khd->hqk", grad_head_grid, value_heads, preferred_element_type=jnp.float32
        )
        row_inner = jnp.sum(probs_exact * grad_probs, axis=-1, keepdims=True)
        grad_scores = (probs_exact * (grad_probs - row_inner)).astype(jnp.bfloat16)
        grad_queries = (
            jnp.einsum(
                "hqk,khd->qhd", grad_scores, key_heads, preferred_element_type=jnp.float32
            ).reshape(row_count, model_width)
            * score_scale
        )
        grad_key_part = (
            jnp.einsum("hqk,qhd->khd", grad_scores, query_heads, preferred_element_type=jnp.float32)
            * score_scale
        )
        grad_value_part = jnp.einsum(
            "hqk,qhd->khd", probs_again, grad_head_grid, preferred_element_type=jnp.float32
        )
        key_grads = lax.psum_scatter(
            jnp.concatenate(
                [
                    grad_key_part.reshape(row_count * lax.axis_size("ctx"), -1),
                    grad_value_part.reshape(row_count * lax.axis_size("ctx"), -1),
                ],
                axis=-1,
            ).astype(jnp.bfloat16),
            "ctx",
            scatter_dimension=0,
            tiled=True,
        ).astype(jnp.float32)
        grad_query_low = rotate(grad_queries, cosine_table, sine_table, -1.0).astype(jnp.bfloat16)
        grad_key_low = rotate(key_grads[:, :model_width], cosine_table, sine_table, -1.0).astype(
            jnp.bfloat16
        )
        grad_value_low = key_grads[:, model_width:].astype(jnp.bfloat16)
        grad_projected = jnp.stack([grad_query_low, grad_key_low, grad_value_low])
        grad_proj = jnp.einsum(
            "std,ste->sde", normed_low, grad_projected, preferred_element_type=jnp.float32
        )
        grad_normed = jnp.einsum(
            "ste,sde->std", grad_projected, proj_full, preferred_element_type=jnp.float32
        )
        norm_three_back = jax.vjp(layer_norm, inputs[:3], gain_three)[1]
        grad_inputs_three, grad_gain_three = norm_three_back(grad_normed)
        grad_gain_all = jnp.concatenate(
            [grad_gain_three.reshape(3, -1), grad_gain_mlp[None], grad_gain_mix[None]], axis=0
        )
        proj_shard, attention_shard, gain_shard = (
            lax.psum_scatter(grad_proj, ("dp", "ctx"), scatter_dimension=1, tiled=True),
            lax.psum_scatter(grad_attention, ("dp", "ctx"), scatter_dimension=0, tiled=True),
            lax.psum_scatter(grad_gain_all, ("dp", "ctx"), scatter_dimension=1, tiled=True),
        )
        grad_block = jnp.concatenate([grad_inputs_three, grad_hidden[None]], axis=0).astype(
            jnp.bfloat16
        )
        new_totals = (
            kept_projections + proj_shard,
            kept_attention + attention_shard,
            kept_gains + gain_shard,
            kept_up + up_shard,
            down_next,
            kept_first + first_shard,
            kept_second + grad_second,
            kept_bias + grad_bias,
            kept_loss + loss_part,
        )
        return (new_totals, (next_block.astype(jnp.bfloat16), grad_block, grad_past))

    down_start = jnp.zeros(down_weight.shape, jnp.float32)
    start_totals = (
        jnp.zeros(projections.shape, jnp.float32),
        jnp.zeros(attention_out.shape, jnp.float32),
        jnp.zeros(gains.shape, jnp.float32),
        jnp.zeros(up_weight.shape, jnp.float32),
        down_start,
        jnp.zeros(mixer_first.shape, jnp.float32),
        jnp.zeros(mixer_second.shape, jnp.float32),
        jnp.zeros(mixer_bias.shape, jnp.float32),
        jnp.zeros((), jnp.float32),
    )
    final_totals, stacked = lax.scan(
        one_batch, start_totals, jnp.arange(micro_count, dtype=jnp.int32)
    )
    (
        sum_projections,
        sum_attention,
        sum_gains,
        sum_up,
        sum_down,
        sum_first,
        sum_second,
        sum_bias,
        sum_loss,
    ) = final_totals
    grad_second_all, grad_bias_all, loss_all = lax.psum(
        (sum_second, sum_bias, sum_loss), ("dp", "ctx")
    )
    next_streams = jnp.moveaxis(stacked[0], 0, 1)
    grad_streams = jnp.moveaxis(stacked[1], 0, 1)
    grad_history = jnp.moveaxis(stacked[2], 0, 1)
    return (
        next_streams,
        loss_all,
        grad_streams,
        grad_history,
        sum_projections,
        sum_attention,
        sum_up,
        sum_down,
        sum_first,
        grad_second_all,
        grad_bias_all,
        sum_gains,
    )


def fits(mesh):
    return mesh.shape["ctx"] == 4 and mesh.shape["dp"] == 8


def solution(mesh):
    specs = dict(
        in_specs=(
            P(None, "dp", "ctx", None),
            P(None, "dp", "ctx", None),
            P(None, "dp", "ctx", None),
            P("dp"),
            P("dp", "ctx"),
            P(),
            P(None, ("dp", "ctx"), None),
            P(("dp", "ctx"), None),
            P(("dp", "ctx"), None),
            P(("dp", "ctx"), None),
            P(("dp", "ctx"), None),
            P(),
            P(),
            P(None, ("dp", "ctx")),
        ),
        out_specs=(
            P(None, "dp", "ctx", None),
            P(),
            P(None, "dp", "ctx", None),
            P(None, "dp", "ctx", None),
            P(None, ("dp", "ctx"), None),
            P(("dp", "ctx"), None),
            P(("dp", "ctx"), None),
            P(("dp", "ctx"), None),
            P(("dp", "ctx"), None),
            P(),
            P(),
            P(None, ("dp", "ctx")),
        ),
        check_vma=False,
    )

    def chosen(*arrays):
        fast = fits(mesh) and arrays[0].shape[1] == 2 * mesh.shape["dp"]
        return jax.shard_map(local_fast if fast else local_plain, mesh=mesh, **specs)(*arrays)

    return chosen
```

```python
import functools
import math

import jax
import jax.numpy as jnp
from jax import lax
from jax.experimental import pallas as pl
from jax.experimental.pallas import tpu as pltpu
from jax.sharding import PartitionSpec as P

HEADS = 16
HEAD_DIM = 64
ROT = 16
AXES = ("dp", "ctx")

highest = lax.Precision.HIGHEST
epsilon = 1e-05
f32 = jnp.float32
bf16 = jnp.bfloat16
VMEM_BYTES = 60 * 1024 * 1024


def dot_nn(a, b, precision=None):
    return lax.dot_general(
        a, b, (((1,), (0,)), ((), ())), precision=precision, preferred_element_type=f32
    )


def dot_nt(a, b, precision=None):
    return lax.dot_general(
        a, b, (((1,), (1,)), ((), ())), precision=precision, preferred_element_type=f32
    )


def dot_tn(a, b, precision=None):
    return lax.dot_general(
        a, b, (((0,), (0,)), ((), ())), precision=precision, preferred_element_type=f32
    )


def normal_cdf(v):
    z = jnp.abs(v) * math.sqrt(0.5)
    t = 1.0 / (1.0 + 0.39 * z)
    bell = jnp.exp(-0.5 * v * v)
    poly = -0.22760540438261295
    for c in (
        0.8869388009365644,
        -0.6358388689155755,
        0.649907738051149,
        0.09125094908545259,
        0.23534677935551734,
    ):
        poly = poly * t + c
    half_tail = (0.5 * poly) * t * bell
    return jnp.where(v < 0.0, half_tail, 1.0 - half_tail), bell


def gelu_pair(v):
    cdf, bell = normal_cdf(v)
    return v * cdf, cdf + v * bell * (1.0 / math.sqrt(2.0 * math.pi))


def vmem(block=None, index_map=None):
    if block is None:
        return pl.BlockSpec(memory_space=pltpu.VMEM)
    return pl.BlockSpec(block, index_map)


def params(**kw):
    return pltpu.CompilerParams(vmem_limit_bytes=VMEM_BYTES, **kw)


Z_ORDER = (0, 2, 1, 3)


UP_BITS = (8, 16)
DOWN_BITS = (16, 8)


def gathered_from(me, place, outer):
    distance = 4 * (place // 16) + outer[0] * (place // 8 % 2) + outer[1] * (place // 4 % 2)
    return jnp.bitwise_xor(me, distance + Z_ORDER[place % 4])


def place_rows(me, ref, outer, out_ref):
    rows = ref.shape[-2]
    for place in range(ref.shape[0]):
        device = gathered_from(me, place, outer)
        out_ref[pl.ds(pl.multiple_of(device * rows, rows), rows), :] = ref[place]


def take_rows(me, from_ref, outer, refs):
    rows = refs[0].shape[-2]
    each_has = refs[0].shape[0]
    for place in range(each_has * len(refs)):
        device = gathered_from(me, place, outer)
        refs[place // each_has][place % each_has] = from_ref[
            pl.ds(pl.multiple_of(device * rows, rows), rows), :
        ]


def place_tile(me, all_up_ref, some_down_ref, up_ref, down_ref):
    place_rows(me, all_up_ref, UP_BITS, up_ref)
    rows = some_down_ref.shape[1]
    for q, z in enumerate(Z_ORDER):
        at = pl.multiple_of(jnp.bitwise_xor(lax.rem(me, 4), z) * rows, rows)
        down_ref[pl.ds(at, rows), :] = some_down_ref[q]


def turn(x, cosine, sine_up, sine_down):
    return (
        x * cosine + pltpu.roll(x, ROT // 2, 1) * sine_up + pltpu.roll(x, 128 - ROT // 2, 1) * sine_down
    )


def allowed_limit(base, rows, prefix, axis):
    shape = (rows, 1) if axis == 0 else (1, rows)
    position = base + lax.broadcasted_iota(jnp.int32, shape, axis)
    return jnp.maximum(position, prefix - 1)


def flip(bit, by):
    return bit + by - 2 * bit * by


class Place:
    def __init__(self):
        self.group = lax.axis_index("dp")
        self.z = lax.axis_index("ctx")
        self.core = lax.rem(self.group, 2)
        self.x = lax.rem(lax.div(self.group, 2), 2)
        self.y = lax.div(self.group, 4)
        self.z_low = lax.rem(self.z, 2)
        self.z_high = lax.div(self.z, 2)

    def across(self, axis):
        if axis == "core":
            return (self.group + 1 - 2 * self.core, self.z)
        if axis == "x":
            return (self.group + 2 - 4 * self.x, self.z)
        if axis == "y":
            return (self.group + 4 - 8 * self.y, self.z)
        if axis == "zl":
            return (self.group, self.z + 1 - 2 * self.z_low)
        return (self.group, self.z + 2 - 4 * self.z_high)

    def device(self, y, x, core, z):
        pair = flip(self.y, y) * 4 + flip(self.x, x) * 2 + flip(self.core, core)
        return pair * 4 + flip(self.z_high, z // 2) * 2 + flip(self.z_low, z % 2)

    def code(self, k):
        return flip(self.z_high, lax.div(k, 2)), flip(self.z_low, lax.rem(k, 2))

    def block(self, k):
        return flip(self.z_low, lax.div(k, 2)) * 2 + flip(self.core, lax.rem(k, 2))

    def out_to(self, k):
        seq, half = self.code(k)
        return (self.group - self.core + half, 2 * self.core + seq)

    def back_to(self, k):
        return (self.group - self.core + self.z_high, self.block(k))

    def is_self(self, device):
        return jnp.logical_and(device[0] == self.group, device[1] == self.z)

    def meet(self, names):
        barrier = pltpu.get_barrier_semaphore()
        others = [self.across(name) for name in names]
        for step in range(1, 8):
            place = self.core * 4 + self.z + step
            others.append(
                (self.group - self.core + lax.rem(lax.div(place, 4), 2), lax.rem(place, 4))
            )
        for other in others:
            pl.semaphore_signal(barrier, inc=1, device_id=other, device_id_type=pl.DeviceIdType.MESH)
        pl.semaphore_wait(barrier, len(others))


class Sends:
    def __init__(self, here, send_sems, recv_sems):
        self.here, self.send_sems, self.recv_sems = here, send_sems, recv_sems
        self.used, self.open = 0, []

    def make(self, n, source, target, device):
        return pltpu.make_async_remote_copy(
            src_ref=source,
            dst_ref=target,
            send_sem=self.send_sems.at[n],
            recv_sem=self.recv_sems.at[n],
            device_id=device,
            device_id_type=pl.DeviceIdType.MESH,
        )

    def start(self, source, target, device):
        copy = self.make(self.used, source, target, device)
        self.used += 1
        copy.start()
        self.open.append(copy)
        return copy

    def four(self, source, target, device):
        base = self.used
        self.used += 4

        def copy(k):
            return self.make(base + k, source(k), target(k), device(k))

        def start(k):
            stays = self.here.is_self(device(k))

            @pl.when(stays)
            def _():
                pltpu.make_async_copy(source(k), target(k), self.recv_sems.at[base + k]).start()

            @pl.when(jnp.logical_not(stays))
            def _():
                copy(k).start()

        def sent(k):
            @pl.when(jnp.logical_not(self.here.is_self(device(k))))
            def _():
                copy(k).wait_send()

        def came(k):
            copy(k).wait_recv()

        return start, sent, came

    def finish(self):
        for copy in self.open:
            copy.wait_send()


def each(n, body):
    def step(i, _):
        body(i)
        return 0

    lax.fori_loop(0, n, step, 0)


class Gathers:
    def __init__(self, here, sends, refs):
        self.here, self.sends, self.refs = here, sends, refs
        self.coming = {name: [] for name in refs}

    def settle(self, name, first=0, count=1 << 20):
        left = []
        for at, n, copy in self.coming[name]:
            if at < first + count and first < at + n:
                copy.wait_recv()
            else:
                left.append((at, n, copy))
        self.coming[name] = left

    def move(self, name, axis, first, count, to):
        self.settle(name, first, count)
        ref = self.refs[name]
        copy = self.sends.start(
            ref.at[pl.ds(first, count)], ref.at[pl.ds(to, count)], self.here.across(axis)
        )
        self.coming[name].append((to, count, copy))


def key_positions(length, blocks, axis):
    shape = (length, 1) if axis == 0 else (1, length)
    i = lax.broadcasted_iota(jnp.int32, shape, axis)
    piece = length // (2 * blocks)
    return (
        lax.rem(lax.div(i, piece), blocks) * (2 * piece)
        + lax.div(i, length // 2) * piece
        + lax.rem(i, piece)
    )


FRONT_PLAN = (
    ("start", "zl"),
    ("move", "proj", "zh", 0, 1, 1),
    ("move", "proj", "zl", 0, 1, 2),
    ("add",),
    ("start", "zh"),
    ("move", "up", "zh", 0, 1, 1),
    ("move", "up", "zl", 0, 1, 2),
    ("move", "down", "zh", 0, 1, 1),
    ("move", "down", "zl", 0, 1, 2),
    ("add",),
    ("start", "x"),
    ("move", "proj", "y", 0, 1, 4),
    ("move", "proj", "x", 0, 1, 8),
    ("move", "up", "y", 0, 1, 4),
    ("move", "down", "x", 0, 1, 4),
    ("move", "up", "x", 0, 1, 8),
    ("move", "down", "y", 0, 1, 8),
    ("rows", 1),
    ("add",),
    ("start", "y"),
    ("move", "proj", "zl", 1, 1, 3),
    ("move", "proj", "y", 1, 1, 5),
    ("move", "proj", "x", 1, 1, 9),
    ("add",),
    ("start", "core"),
    ("move", "proj", "x", 4, 1, 12),
    ("move", "up", "zl", 1, 1, 3),
    ("move", "down", "zl", 1, 1, 3),
    ("add",),
    ("rows", 2),
    ("move", "up", "y", 1, 1, 5),
    ("move", "down", "x", 1, 1, 5),
    ("move", "up", "x", 1, 1, 9),
    ("move", "down", "y", 1, 1, 9),
    ("rows", 0),
    ("move", "proj", "y", 2, 2, 6),
    ("move", "proj", "x", 2, 2, 10),
    ("move", "proj", "x", 5, 1, 13),
    ("move", "up", "x", 4, 1, 12),
    ("move", "down", "y", 4, 1, 12),
    ("move", "up", "y", 2, 2, 6),
    ("move", "down", "x", 2, 2, 6),
    ("norm", 1),
    ("move", "proj", "x", 6, 2, 14),
    ("move", "up", "x", 2, 2, 10),
    ("move", "down", "y", 2, 2, 10),
    ("move", "up", "x", 5, 1, 13),
    ("move", "down", "y", 5, 1, 13),
    ("norm", 2),
    ("move", "up", "x", 6, 2, 14),
    ("move", "down", "y", 6, 2, 14),
    ("move", "up", "core", 0, 8, 16),
    ("move", "down", "core", 0, 8, 16),
    ("assemble",),
    ("project", 1),
    ("project", 2),
    ("norm", 0),
    ("project", 0),
    ("move", "up", "core", 8, 4, 24),
    ("move", "down", "core", 8, 4, 24),
    ("attend",),
    ("move", "up", "core", 12, 4, 28),
    ("move", "down", "core", 12, 4, 28),
)


def front_body(
    prefix_in, streams_ref, proj_in, up_in, down_in, out_in, gains_in, first_in, valid_in, cos_ref, rise_ref, fall_ref,
    received_out, normed_out, weight_out, far_out, up_ref, down_ref, small_ref, first_ref, prefix_ref,
    q_out, k_out, v_out, heads_out, lse_ref, got_ref,
    received_ref, normed_ref, proj_ref, weight_ref, q_ref, k_ref, v_ref, heads_ref,
    small_got, first_got, prefix_own, prefix_got, local_sems, send_sems, recv_sems,
):
    here = Place()
    sends = Sends(here, send_sems, recv_sems)
    gathers = Gathers(here, sends, {"proj": proj_ref, "up": up_ref, "down": down_ref})
    features = proj_ref.shape[-1]
    units = down_in.shape[0]
    kept = []

    def keep(source, target):
        copy = pltpu.make_async_copy(source, target, local_sems.at[len(kept)])
        kept.append(copy)
        copy.start()
        return copy

    def columns(which):
        return proj_in.at[:, :, pl.ds(pl.multiple_of(which * features, features), features)]

    shard = gains_in.shape[1]
    lanes = small_ref.shape[1]
    column = lax.broadcasted_iota(jnp.int32, (shard, lanes), 1)
    row = lax.broadcasted_iota(jnp.int32, (shard, lanes), 0)
    chosen = (column == row + here.device(0, 0, 0, 0) * shard).astype(bf16)
    count = jnp.sum(valid_in[...].astype(f32))
    small_ref[...] = jnp.zeros_like(small_ref)
    small_ref[0:5, :] = dot_nn(gains_in[...], chosen)
    small_ref[7:8, :] = jnp.full((1, lanes), 1.0, f32) * count
    first_ref[...] = jnp.zeros_like(first_ref)
    first_ref[0 : first_in.shape[1], :] = dot_tn(first_in[...], chosen).astype(bf16)
    second_row = lax.broadcasted_iota(jnp.int32, prefix_own.shape, 0) == 1
    prefix_own[...] = jnp.where(second_row, prefix_in[1], prefix_in[0])
    here.meet(("x", "y"))
    small_steps = []

    def small_start(axis):
        n = len(small_steps)
        device = here.across(axis)
        small_steps.append(
            (
                sends.start(small_ref, small_got.at[n], device),
                sends.start(first_ref, first_got.at[n], device),
            )
        )

    def small_end():
        n = len(small_steps) - 1
        for copy in small_steps[n]:
            copy.wait()
        sends.open = [c for c in sends.open if not any(c is s for s in small_steps[n])]
        small_ref[...] += small_got[n]
        first_ref[...] += first_got[n]

    def stream(s):
        def source(k):
            seq, half = here.code(k)
            return streams_ref.at[s, 2 * seq + half]

        steps = sends.four(source, lambda k: received_ref.at[s, k], here.out_to)
        each(4, steps[0])
        return steps

    chunk = 32

    def norm(s, steps):
        gain = small_ref[s : s + 1, :].astype(f32)

        def step(k):
            steps[2](k)
            block = here.block(k)

            def body(i, _):
                at = pl.ds(pl.multiple_of(i * chunk, chunk), chunk)
                x = received_ref[s, k, at, :].astype(f32)
                x = x - jnp.mean(x, axis=-1, keepdims=True)
                scale = lax.rsqrt(jnp.mean(x * x, axis=-1, keepdims=True) + epsilon)
                normed_ref[s, here.core, block, at, :] = (x * scale * gain).astype(bf16)
                return 0

            lax.fori_loop(0, received_ref.shape[2] // chunk, body, 0, unroll=2)

        each(4, step)
        keep(received_ref.at[s], received_out.at[s])
        keep(normed_ref.at[s, here.core], normed_out.at[s, here.core])
        return sends.start(
            normed_ref.at[s, here.core], normed_ref.at[s, here.core], here.across("core")
        )

    prefix_send = sends.start(prefix_own, prefix_got, here.across("core"))
    gathers.coming["proj"].append(
        (0, 1, sends.start(columns(1 - here.core), proj_ref.at[0, 1], here.across("core")))
    )
    own = [
        keep(columns(here.core), proj_ref.at[0, 0]),
        keep(up_in, up_ref.at[0]),
        keep(down_in, down_ref.at[0, pl.ds(0, units)]),
        keep(out_in, down_ref.at[0, pl.ds(units, out_in.shape[0])]),
    ]
    for copy in own:
        copy.wait()
    prefix_send.wait_recv()
    prefixes = jnp.where(here.z_high == here.core, prefix_own[...], prefix_got[...])
    prefix_ref[...] = jnp.broadcast_to(
        jnp.where(here.z_low == 0, prefixes[0:1], prefixes[1:2]), prefix_ref.shape
    )
    def assemble(s):
        rows = proj_ref.shape[-2]
        for x in range(2):
            for y in range(2):
                for q, z in enumerate(Z_ORDER):
                    for core in range(2):
                        device = here.device(y, x, core, z)
                        at = pl.ds(pl.multiple_of(device * rows, rows), rows)
                        weight_ref[s, at, :] = proj_ref[(x * 2 + y) * 4 + q, core, s]


    _, blocks, piece, width = q_ref.shape
    half_rows = blocks * piece
    length = 2 * half_rows

    def project(s, out_ref):
        def step(half):
            y = dot_nn(normed_ref[s, half].reshape(half_rows, -1), weight_ref[s])
            if s < 2:
                tables = [r[half].reshape(half_rows, 128) for r in (cos_ref, rise_ref, fall_ref)]
                y = jnp.concatenate(
                    [turn(y[:, i : i + 128], *tables) for i in range(0, width, 128)], axis=1
                )
            y = y.astype(bf16)
            if s == 0:
                y = y * jnp.asarray(HEAD_DIM**-0.5, bf16)
            out_ref[half] = y.reshape(blocks, piece, width)

        each(2, step)

    rows = 2 * piece
    lane = lax.broadcasted_iota(jnp.int32, (rows, 128), 1)
    key_index = key_positions(length, blocks, 1)
    heads_steps = sends.four(
        lambda k: heads_ref.at[here.block(k)], lambda k: got_ref.at[k], here.back_to
    )

    def block_body(k):
        block = here.block(k)
        allowed = key_index <= allowed_limit(block * rows, rows, prefix_ref[0:1, 0:1], 0)
        lse_all = jnp.zeros((rows, 128), f32)
        for pair in range(width // 128):
            at = slice(pair * 128, pair * 128 + 128)
            queries = q_ref[:, block, :, at].reshape(rows, 128)
            keys = k_ref[:, :, :, at].reshape(length, 128)
            values = v_ref[:, :, :, at].reshape(length, 128)
            results = []
            for h in range(2):
                chosen = (lane < 64) if h == 0 else (lane >= 64)
                scores = dot_nt(jnp.where(chosen, queries, jnp.zeros_like(queries)), keys)
                scores = jnp.where(allowed, scores, -1e30)
                top = jnp.max(scores, axis=-1, keepdims=True)
                weights = jnp.exp(scores - top)
                total = jnp.sum(weights, axis=-1, keepdims=True)
                results.append(dot_nn(weights.astype(bf16), values) / total)
                lse_all = jnp.where(lane == pair * 2 + h, top + jnp.log(total), lse_all)
            heads_ref[block, :, at] = jnp.where(lane < 64, results[0], results[1]).astype(bf16)
        lse_ref[block] = lse_all.T[0:8]
        heads_steps[0](k)


    rows_steps, others, far = {}, {}, []
    for step in FRONT_PLAN:
        kind = step[0]
        if kind == "start":
            small_start(step[1])
        elif kind == "add":
            small_end()
        elif kind == "rows":
            rows_steps[step[1]] = stream(step[1])
        elif kind == "move":
            gathers.move(*step[1:])
        elif kind == "norm":
            others[step[1]] = norm(step[1], rows_steps[step[1]])
        elif kind == "assemble":
            gathers.settle("proj")
            each(3, assemble)
            far.append(sends.start(weight_ref, far_out, here.across("core")))
            keep(weight_ref, weight_out)
        elif kind == "project":
            s = step[1]
            others[s].wait_recv()
            keep(normed_ref.at[s, 1 - here.core], normed_out.at[s, 1 - here.core])
            ref, out = ((q_ref, q_out), (k_ref, k_out), (v_ref, v_out))[s]
            project(s, ref)
            keep(ref, out)
        else:
            each(4, block_body)
            keep(heads_ref, heads_out)
    each(4, heads_steps[2])
    for name in ("up", "down"):
        gathers.settle(name)
    far[0].wait_recv()
    for steps in list(rows_steps.values()) + [heads_steps]:
        each(4, steps[1])
    sends.finish()
    for copy in kept[len(own) :]:
        copy.wait()


def mlp_forward_body(
    ids, heads_ref, res_ref, gain_ref, all_up_ref, some_down_ref, gathered_out_ref,
    hidden_ref, normed_ref, active_ref, slope_ref, layer_ref,
    out_w_ref, up_ref, down_ref,
):
    step = pl.program_id(0)
    seqs, rows, width = res_ref.shape[1:]
    me = ids[4]

    @pl.when(step == 0)
    def _():
        place_rows(me, gathered_out_ref, DOWN_BITS, out_w_ref)
        hidden_ref[...] = res_ref[0].astype(f32)
        for k in range(heads_ref.shape[0]):
            code = jnp.bitwise_xor(ids[0], k)
            features = heads_ref.shape[-1]
            at = pl.ds(pl.multiple_of(lax.rem(code, 2) * features, features), features)
            hidden_ref[lax.div(code, 2)] += dot_nn(heads_ref[k], out_w_ref[at, :])
        gain = gain_ref[3:4, :].astype(f32)
        for j in range(seqs):
            x = hidden_ref[j]
            layer_ref[j] = x
            x = x - jnp.mean(x, axis=-1, keepdims=True)
            scale = lax.rsqrt(jnp.mean(x * x, axis=-1, keepdims=True) + epsilon)
            normed_ref[j] = (x * scale * gain).astype(bf16)

    place_tile(me, all_up_ref, some_down_ref, up_ref, down_ref)
    upper = dot_nn(normed_ref[...].reshape(seqs * rows, width), up_ref[...])
    active, slope = gelu_pair(upper)
    active = active.astype(bf16)
    active_ref[...] = active
    slope_ref[...] = slope.astype(bf16)
    layer_ref[...] += dot_nn(active, down_ref[...]).reshape(seqs, rows, width)


def mixer_body(
    scal_ref, layer_ref, hist_ref, teacher_ref, valid_in, gain_ref, first_ref, second_in, bias_in,
    next_ref, ghist_ref, glayer_ref, gfirst_ref, gsecond_ref, stats_ref, ggain_ref,
    coef_ref, part_ref, gnext_ref, valid_ref, second_ref, bias_ref,
):
    step = pl.program_id(0)
    past, rows, width = hist_ref.shape
    streams = teacher_ref.shape[0]
    outs = past + 1
    span = first_ref.shape[0]

    @pl.when(step == 0)
    def _():
        gfirst_ref[...] = jnp.zeros_like(gfirst_ref)
        gsecond_ref[...] = jnp.zeros_like(gsecond_ref)
        stats_ref[...] = jnp.zeros_like(stats_ref)
        ggain_ref[...] = jnp.zeros_like(ggain_ref)
        second_ref[...] = jnp.zeros_like(second_ref)
        second_ref[0 : second_in.shape[0], 0 : second_in.shape[1]] = second_in[...]
        bias_ref[...] = jnp.zeros_like(bias_ref)
        bias_ref[:, 0 : bias_in.shape[1]] = bias_in[...]

    factor = scal_ref[0] * 2.0 / (4.0 * width * gain_ref[7:8, 0:128])
    diagonal = lax.broadcasted_iota(jnp.int32, (rows, rows), 0) == lax.broadcasted_iota(
        jnp.int32, (rows, rows), 1
    )
    valid_row = jnp.broadcast_to(valid_in[0].astype(f32), (rows, rows))
    valid_ref[...] = jnp.sum(jnp.where(diagonal, valid_row, 0.0), axis=1, keepdims=True)
    x = layer_ref[...]
    scale = lax.rsqrt(jnp.mean(x * x, axis=-1, keepdims=True) + epsilon)
    gain = gain_ref[4:5, :].astype(f32)
    normed = (x * scale * gain).astype(bf16)
    mix_hidden = dot_nt(normed, first_ref[...])
    mix_active, mix_slope = gelu_pair(mix_hidden)
    coeff = dot_nn(mix_active, second_ref[...], highest) + bias_ref[...]
    for c in range(streams * outs):
        coef_ref[c] = jnp.broadcast_to(coeff[:, c : c + 1], (rows, 128))
    part_ref[...] = jnp.zeros_like(part_ref)

    chunk = 16
    lanes = 512

    def rows_body(i, loss_rows):
        at = pl.ds(pl.multiple_of(i * chunk, chunk), chunk)
        valid = jnp.broadcast_to(valid_ref[at, :], (chunk, 128))

        def read(j, lane_at):
            return layer_ref[at, lane_at] if j == past else hist_ref[j, at, lane_at].astype(f32)

        for l0 in range(0, width, 256):
            lane_at = slice(l0, l0 + 256)
            sums = [jnp.zeros((chunk, 256), f32) for _ in range(streams)]
            for j in range(outs):
                value = read(j, lane_at)
                for s in range(streams):
                    c = coef_ref[s * outs + j, at, :]
                    sums[s] = sums[s] + jnp.concatenate([c, c], axis=1) * value
            both = jnp.concatenate([valid, valid], axis=1)
            for s in range(streams):
                next_ref[s, at, lane_at] = sums[s].astype(bf16)
                difference = sums[s] - teacher_ref[s, at, lane_at].astype(f32)
                weighted = both * difference
                gnext_ref[s, at, lane_at] = jnp.concatenate([factor, factor], axis=1) * weighted
                square = weighted * difference
                loss_rows = loss_rows + square[:, :128] + square[:, 128:]
        for l0 in range(0, width, lanes):
            lane_at = slice(l0, l0 + lanes)
            for j in range(outs):
                value = read(j, lane_at)
                total = jnp.zeros((chunk, lanes), f32)
                for s in range(streams):
                    grad = gnext_ref[s, at, lane_at]
                    c = coef_ref[s * outs + j, at, :]
                    total = total + jnp.concatenate([c] * (lanes // 128), axis=1) * grad
                    product = grad * value
                    folded = product[:, :128]
                    for q in range(128, lanes, 128):
                        folded = folded + product[:, q : q + 128]
                    part_ref[s * outs + j, at, :] += folded
                if j == past:
                    glayer_ref[at, lane_at] = total
                else:
                    ghist_ref[j, at, lane_at] = total.astype(bf16)
        return loss_rows

    loss_rows = lax.fori_loop(0, rows // chunk, rows_body, jnp.zeros((chunk, 128), f32))
    lane = lax.broadcasted_iota(jnp.int32, (rows, span), 1)
    grad_coeff = jnp.zeros((rows, span), f32)
    for c in range(streams * outs):
        grad_coeff = jnp.where(lane == c, jnp.sum(part_ref[c], axis=-1, keepdims=True), grad_coeff)
    gsecond_ref[...] += dot_tn(mix_active, grad_coeff, highest)
    stats_ref[0:1, :] += jnp.sum(grad_coeff, axis=0, keepdims=True)
    stats_ref[1:2, :] += jnp.broadcast_to(jnp.sum(loss_rows), (1, span))
    grad_active = dot_nt(grad_coeff, second_ref[...], highest)
    grad_mix = (grad_active * mix_slope).astype(bf16)
    gfirst_ref[...] += dot_tn(grad_mix, normed)
    grad_normed = dot_nn(grad_mix, first_ref[...])
    x = layer_ref[...]
    ggain_ref[...] += jnp.sum(grad_normed * (x * scale), axis=0, keepdims=True)
    inner = grad_normed * gain
    mean = jnp.mean(inner * x, axis=-1, keepdims=True)
    glayer_ref[...] += scale * inner - x * (scale * scale * scale * mean)


def norm_back(x, grad, gain):
    centered = x - jnp.mean(x, axis=-1, keepdims=True)
    scale = lax.rsqrt(jnp.mean(centered * centered, axis=-1, keepdims=True) + epsilon)
    unit = centered * scale
    grad_gain = jnp.sum(grad * unit, axis=0, keepdims=True)
    inner = grad * gain
    inner = (
        inner
        - jnp.mean(inner, axis=-1, keepdims=True)
        - unit * jnp.mean(inner * unit, axis=-1, keepdims=True)
    )
    return scale * inner, grad_gain


def mlp_backward_body(
    ids, glayer_ref, active_ref, slope_ref, normed_ref, all_up_ref, some_down_ref,
    gu0, gu1, gu2, gu3, gd0, gd1, gd2, gd3, sum_ref,
    low_ref, normed_t_ref, up_ref, down_ref, tile_ref,
):
    step = pl.program_id(0)
    seqs, rows, width = glayer_ref.shape
    tokens = seqs * rows
    me = ids[4]
    place = lax.rem(me, 4)

    @pl.when(step == 0)
    def _():
        low_ref[...] = glayer_ref[...].astype(bf16)
        sum_ref[...] = jnp.zeros_like(sum_ref)
        normed_t_ref[...] = normed_ref[...].reshape(tokens, width).T

    place_tile(me, all_up_ref, some_down_ref, up_ref, down_ref)
    grad = low_ref[...].reshape(tokens, width)
    grad_active = dot_nt(grad, down_ref[...])
    grad_upper = (grad_active * slope_ref[...].astype(f32)).astype(bf16)
    sum_ref[...] += dot_nt(grad_upper, up_ref[...]).reshape(seqs, rows, width)
    down_ref[...] = dot_tn(active_ref[...], grad).astype(bf16)
    for p, ref in enumerate((gd0, gd1, gd2, gd3)):

        @pl.when(lax.div(step, 2) == p)
        def _(ref=ref):
            block_rows = ref.shape[1]
            for q, z in enumerate(Z_ORDER):
                at = pl.multiple_of(jnp.bitwise_xor(place, z) * block_rows, block_rows)
                ref[q] = down_ref[pl.ds(at, block_rows), :]

    tile_ref[...] = dot_nn(normed_t_ref[...], grad_upper).astype(bf16)
    take_rows(me, tile_ref, UP_BITS, (gu0, gu1, gu2, gu3))


def hidden_backward_body(
    ids, glayer_ref, sum_ref, hidden_ref, heads_ref, gain_ref, gathered_out_ref,
    gres_ref, g0, g1, g2, g3, go0, go1, go2, go3, ggain_ref,
    out_w_ref, gout_ref,
):
    seqs, rows, width = hidden_ref.shape
    me = ids[4]
    place_rows(me, gathered_out_ref, DOWN_BITS, out_w_ref)
    gain = gain_ref[3:4, :].astype(f32)
    ggain = jnp.zeros((1, width), f32)
    for j in range(seqs):
        back, part = norm_back(hidden_ref[j], sum_ref[j], gain)
        ggain = ggain + part
        gres_ref[j] = (glayer_ref[j] + back).astype(bf16)
    ggain_ref[...] = ggain
    gout_ref[...] = jnp.zeros_like(gout_ref)
    for k, out in enumerate((g0, g1, g2, g3)):
        code = jnp.bitwise_xor(ids[0], k)
        features = out.shape[-1]
        at = pl.ds(pl.multiple_of(lax.rem(code, 2) * features, features), features)
        low = gres_ref[lax.div(code, 2)]
        out[...] = dot_nt(low, out_w_ref[at, :]).astype(bf16)
        gout_ref[at, :] += dot_tn(heads_ref[k], low)
    out_w_ref[...] = gout_ref[...].astype(bf16)
    take_rows(me, out_w_ref, DOWN_BITS, (go0, go1, go2, go3))


def back_body(
    prefix_ref, q_in, k_in, v_in, heads_in, lse_ref, cos_ref, rise_ref, fall_ref,
    normed_in, received_in, weight_in, far_in, gain_ref, gfirst_in, gmlp_in, gmix_in, gsecond_in, stats_in, res_in,
    gh0, gh1, gh2, gh3, gu0, gu1, gu2, gu3, gd0, gd1, gd2, gd3, go0, go1, go2, go3,
    gstreams_ref, gproj_ref, gup_ref, gdown_ref, gout_ref, early_ref, tiny_ref, late_ref,
    q_ref, k_ref, v_ref, heads_ref, g_ref, d_ref, d_got, dk_ref, dv_ref, kt_ref,
    normed_ref, received_ref, weight_ref, gn_ref, b_ref, grad_ref,
    up_keep, down_keep, up_sum, up_a, up_b, up_c, up_d, down_sum, down_a, down_b, down_c, down_d,
    proj_sum, proj_a, proj_b, proj_c, proj_d, proj_e, early_got, tiny_got, late_got,
    local_sems, send_sems, recv_sems,
):
    here = Place()
    sends = Sends(here, send_sems, recv_sems)
    used = []

    def load(source, target):
        copy = pltpu.make_async_copy(source, target, local_sems.at[len(used)])
        used.append(copy)
        copy.start()
        return copy

    def send(source, target, axis):
        return sends.start(source, target, here.across(axis))

    def add(into, first, source, count, start=0):
        def body(i):
            into[first + i] = into[first + i] + source[start + i]

        each(count, body)

    span = gfirst_in.shape[0]
    early_ref[0:span, :] = gfirst_in[...]
    early_ref[span:, :] = jnp.zeros((8, early_ref.shape[1]), f32)
    early_ref[span : span + 1, :] = gmlp_in[...]
    early_ref[span + 1 : span + 2, :] = gmix_in[...]
    tiny_ref[0:span, :] = gsecond_in[...]
    tiny_ref[span:, :] = stats_in[...]
    here.meet(("x", "y"))

    def ring(*refs):
        stages = []

        def start(axis):
            n = len(stages)
            stages.append([send(value, got.at[n], axis) for value, got in refs])

        def end():
            n = len(stages) - 1
            for copy in stages[n]:
                copy.wait()
            sends.open = [c for c in sends.open if not any(c is s for s in stages[n])]
            for value, got in refs:
                value[...] += got[n]

        return start, end

    early_start, early_end = ring((early_ref, early_got), (tiny_ref, tiny_got))
    late_start, late_end = ring((late_ref, late_got))

    early_start("core")
    gs = (gh0, gh1, gh2, gh3)
    base = sends.used
    sends.used += 4
    exchange = []
    for n, g in enumerate(gs):
        device = here.out_to(n)
        stays = here.is_self(device)
        copy = sends.make(base + n, g, g_ref.at[n], device)
        own = pltpu.make_async_copy(g, g_ref.at[n], recv_sems.at[base + n])

        @pl.when(stays)
        def _(own=own):
            own.start()

        @pl.when(jnp.logical_not(stays))
        def _(copy=copy):
            copy.start()

        exchange.append((copy, stays))
    units = gd0.shape[1]
    shard = go0.shape[1]

    def down_parts(ref, first, count):
        return (
            ref.at[pl.ds(first, count), pl.ds(0, units)],
            ref.at[pl.ds(first, count), pl.ds(units, shard)],
        )

    up_come, down_come = {}, {}
    for n, u, d, o in ((1, gu3, gd3, go3), (0, gu2, gd2, go2)):
        up_come[n] = [send(u, up_sum.at[pl.ds(8 * n, 8)], "core")]
        to_d, to_o = down_parts(down_sum, 8 * n, 8)
        down_come[n] = [send(d, to_d, "core"), send(o, to_o, "core")]
    attention_loads = [
        load(a, b)
        for a, b in ((q_in, q_ref), (k_in, k_ref), (v_in, v_ref), (heads_in, heads_ref))
    ]

    def load_stream(s, slot):
        return [
            load(normed_in.at[s], normed_ref.at[slot]),
            load(received_in.at[s], received_ref.at[slot]),
            load(weight_in.at[s], weight_ref.at[slot, 0]),
            load(far_in.at[s], weight_ref.at[slot, 1]),
        ]

    own_up = {1: gu1, 0: gu0}
    own_down = {1: (gd1, go1), 0: (gd0, go0)}

    def load_up(n, half):
        return [load(own_up[n].at[pl.ds(4 * half, 4)], up_keep)]

    def load_down(n, half):
        d, o = own_down[n]
        to_d, to_o = down_parts(down_keep, 0, 4)
        at = pl.ds(4 * half, 4)
        return [load(d.at[at], to_d), load(o.at[at], to_o)]

    early_end()
    early_start("x")
    order = ((1, 1), (1, 0), (0, 1), (0, 0))
    up_load, down_load = load_up(*order[0]), load_down(*order[0])
    up_hops, down_hops = {}, {}
    for i, (n, half) in enumerate(order):
        first = 8 * n + 4 * half
        for come, copies, total, kept in (
            (up_come, up_load, up_sum, up_keep),
            (down_come, down_load, down_sum, down_keep),
        ):
            for copy in come.pop(n, []):
                copy.wait_recv()
            for copy in copies:
                copy.wait()
            add(total, first, kept, 4)
            if total is up_sum:
                if n == 1:
                    up_hops[half] = send(
                        up_sum.at[pl.ds(first, 4)], up_a.at[pl.ds(4 * half, 4)], "x"
                    )
                if i < 3:
                    up_load = load_up(*order[i + 1])
            else:
                if n == 1:
                    down_hops[half] = send(
                        down_sum.at[pl.ds(first, 4)], down_a.at[pl.ds(4 * half, 4)], "y"
                    )
                if i < 3:
                    down_load = load_down(*order[i + 1])
        if i == 0:
            early_end()
            early_start("y")
    streams_loads = {2: load_stream(2, 0), 1: load_stream(1, 1)}
    res_copy = load(res_in, gstreams_ref.at[3])

    _, blocks, piece, width = q_ref.shape
    rows = 2 * piece
    half_rows = blocks * piece
    length = 2 * half_rows
    lane = lax.broadcasted_iota(jnp.int32, (rows, 128), 1)
    key_index = key_positions(length, blocks, 0)
    choose = (
        lax.div(lax.broadcasted_iota(jnp.int32, (8, 128), 1), 64)
        == lax.broadcasted_iota(jnp.int32, (8, 128), 0)
    ).astype(f32)

    def unturn(x, tables):
        return (
            x * tables[0]
            - pltpu.roll(x, ROT // 2, 1) * tables[1]
            - pltpu.roll(x, 128 - ROT // 2, 1) * tables[2]
        )

    rotary = (cos_ref, rise_ref, fall_ref)
    for copy in attention_loads:
        copy.wait()
    for copy, _ in exchange:
        copy.wait_recv()

    later = {}

    def hook_1():
        up_hops[1].wait_recv()
        add(up_sum, 4, up_a, 4, 4)
        later["up_y"] = send(up_sum.at[pl.ds(4, 4)], up_b, "y")
        early_end()
        early_start("zl")

    def hook_2():
        down_hops[1].wait_recv()
        add(down_sum, 4, down_a, 4, 4)
        later["down_x"] = send(down_sum.at[pl.ds(4, 4)], down_b, "x")
        early_end()
        early_start("zh")

    def one_pair(pair):
        at = pl.ds(pl.multiple_of(pair * 128, 128), 128)
        dk_ref[...] = jnp.zeros_like(dk_ref)
        dv_ref[...] = jnp.zeros_like(dv_ref)
        keys = k_ref[:, :, :, at].reshape(length, 128)
        values = v_ref[:, :, :, at].reshape(length, 128)
        kt_ref[...] = keys.T

        def one_block(k):
            block = here.block(k)
            queries = q_ref[:, block, :, at].reshape(rows, 128)
            grads = g_ref[k, :, at]
            inner_rows = dot_nt(
                choose, grads.astype(f32) * heads_ref[block, :, at].astype(f32), highest
            )
            allowed = key_index <= allowed_limit(block * rows, rows, prefix_ref[0:1, 0:1], 1)
            dqt = []
            for h in range(2):
                chosen = (lane < 64) if h == 0 else (lane >= 64)
                q_h = jnp.where(chosen, queries, jnp.zeros_like(queries))
                g_h = jnp.where(chosen, grads, jnp.zeros_like(grads))
                scores = dot_nt(keys, q_h)
                probs = jnp.where(allowed, jnp.exp(scores - lse_ref[block, pl.ds(pair * 2 + h, 1), :]), 0.0)
                grad_probs = dot_nt(values, g_h)
                grad_scores = (probs * (grad_probs - inner_rows[h : h + 1, :])).astype(bf16)
                dv_ref[...] += dot_nn(probs.astype(bf16), g_h)
                dk_ref[...] += dot_nn(grad_scores, q_h)
                dqt.append(dot_nn(kt_ref[...], grad_scores)[h * 64 : h * 64 + 64, :])
            dq = jnp.concatenate(dqt, axis=0).T * (HEAD_DIM**-0.5)
            dq = unturn(dq, [r[:, block].reshape(rows, 128) for r in rotary])
            d_ref[0, :, block, :, at] = dq.astype(bf16).reshape(2, piece, 128)

        each(4, one_block)
        dk = unturn(dk_ref[...], [r[...].reshape(length, 128) for r in rotary])
        d_ref[1, :, :, :, at] = dk.astype(bf16).reshape(2, blocks, piece, 128)
        d_ref[2, :, :, :, at] = dv_ref[...].astype(bf16).reshape(2, blocks, piece, 128)

    each(2, one_pair)
    hook_1()
    each(1, lambda i: one_pair(i + 2))
    hook_2()
    each(1, lambda i: one_pair(i + 3))

    far_half = 1 - here.core
    d_hops = {s: send(d_ref.at[s, far_half], d_got.at[s], "core") for s in (2, 1, 0)}
    early_end()
    late_ref[...] = jnp.zeros_like(late_ref)
    back = {}

    def mine():
        return here.z_low * 2 + here.core

    def one_stream(s, slot):
        for copy in streams_loads[s]:
            copy.wait()
        d_hops[s].wait_recv()
        near = d_ref[s, here.core].reshape(half_rows, width)
        gn = dot_nt(near, weight_ref[slot, 0])
        gn = gn + dot_nt(d_got[s].reshape(half_rows, width), weight_ref[slot, 1])
        gn_ref[...] = gn.reshape(gn_ref.shape)
        gain = gain_ref[s : s + 1, :]

        def step(k):
            block = here.block(k)
            grad, part = norm_back(received_ref[slot, k].astype(f32), gn_ref[block], gain)
            b_ref[s, k] = grad.astype(bf16)
            late_ref[s : s + 1, :] += part

        each(4, step)

    def send_stream(s):
        steps = sends.four(
            lambda k: b_ref.at[s, k], lambda k: gstreams_ref.at[s, mine()], here.back_to
        )
        each(4, steps[0])
        back[s] = steps

    def project_back(s, slot):
        grad = dot_tn(
            normed_ref[slot, 0].reshape(half_rows, -1), d_ref[s, 0].reshape(half_rows, width)
        )
        grad = grad + dot_tn(
            normed_ref[slot, 1].reshape(half_rows, -1), d_ref[s, 1].reshape(half_rows, width)
        )
        grad_ref[...] = grad.astype(bf16)
        for x in range(2):
            for y in range(2):
                for q, z in enumerate(Z_ORDER):
                    for core in range(2):
                        at = pl.multiple_of(here.device(y, x, core, z) * shard, shard)
                        proj_sum[(x * 2 + y) * 4 + q, core, s] = grad_ref[pl.ds(at, shard), :]

    one_stream(2, 0)
    send_stream(2)
    project_back(2, 0)
    streams_loads[0] = load_stream(0, 0)
    one_stream(1, 1)
    send_stream(1)
    project_back(1, 1)
    one_stream(0, 0)
    project_back(0, 0)
    proj_hops = {}
    for half in (1, 0):
        proj_hops[half] = send(
            proj_sum.at[pl.ds(8 + 4 * half, 4)], proj_a.at[pl.ds(4 * half, 4)], "x"
        )
    late_start("core")
    up_hops[0].wait_recv()
    add(up_sum, 0, up_a, 4)
    down_hops[0].wait_recv()
    add(down_sum, 0, down_a, 4)
    late_end()
    late_start("y")
    later["up_y"].wait_recv()
    add(up_sum, 0, up_b, 4)
    up_zl = send(up_sum.at[pl.ds(2, 2)], up_c, "zl")
    later["down_x"].wait_recv()
    add(down_sum, 0, down_b, 4)
    down_zl = send(down_sum.at[pl.ds(2, 2)], down_c, "zl")
    late_end()
    late_start("zl")
    send_stream(0)
    proj_hops[1].wait_recv()
    add(proj_sum, 4, proj_a, 4, 4)
    proj_y = send(proj_sum.at[pl.ds(4, 4)], proj_b, "y")
    proj_hops[0].wait_recv()
    add(proj_sum, 0, proj_a, 4)
    up_zl.wait_recv()
    add(up_sum, 0, up_c, 2)
    up_zh = send(up_sum.at[pl.ds(1, 1)], up_d, "zh")
    down_zl.wait_recv()
    add(down_sum, 0, down_c, 2)
    down_zh = send(down_sum.at[pl.ds(1, 1)], down_d, "zh")
    late_end()
    late_start("zh")
    proj_y.wait_recv()
    add(proj_sum, 0, proj_b, 4)
    proj_zl = send(proj_sum.at[pl.ds(2, 2)], proj_c, "zl")
    up_zh.wait_recv()
    gup_ref[...] = up_sum[0].astype(f32) + up_d[0].astype(f32)
    down_zh.wait_recv()
    down = down_sum[0].astype(f32) + down_d[0].astype(f32)
    gdown_ref[...] = down[:units]
    gout_ref[...] = down[units:]
    late_end()
    late_start("x")
    proj_zl.wait_recv()
    add(proj_sum, 0, proj_c, 2)
    proj_zh = send(proj_sum.at[pl.ds(1, 1)], proj_d, "zh")
    late_end()
    proj_zh.wait_recv()
    add(proj_sum, 0, proj_d, 1)
    proj_core = send(proj_sum.at[0, 1], proj_e, "core")
    for which, source in ((here.core, proj_sum.at[0, 0]), (1 - here.core, proj_e)):
        if source is proj_e:
            proj_core.wait_recv()
        at = pl.ds(pl.multiple_of(which * width, width), width)
        gproj_ref[:, :, at] = source[...].astype(f32)
    for s in range(3):
        each(4, back[s][2])
        each(4, back[s][1])
    for copy, stays in exchange:

        @pl.when(jnp.logical_not(stays))
        def _(copy=copy):
            copy.wait_send()

    res_copy.wait()
    sends.finish()


def finish_body(
    me_ref, streams_ref, proj_ref, up_ref, down_ref, out_ref, early_ref, tiny_ref, late_ref, small_ref,
    streams_out, proj_out, up_out, down_out, out_out, first_out, second_out, bias_out, gains_out, loss_out,
):
    streams_out[...] = streams_ref[...]

    @pl.when(pl.program_id(0) == 0)
    def _():
        for source, target in (
            (proj_ref, proj_out),
            (up_ref, up_out),
            (down_ref, down_out),
            (out_ref, out_out),
        ):
            target[...] = source[...]
        shard, mixw = first_out.shape
        width = early_ref.shape[1]
        span = tiny_ref.shape[1]
        column = lax.broadcasted_iota(jnp.int32, (shard, width), 1)
        row = lax.broadcasted_iota(jnp.int32, (shard, width), 0)
        chosen = (column == row + me_ref[0] * shard).astype(f32)
        first_out[...] = dot_nt(chosen, early_ref[...], highest)[:, 0:mixw]
        gains_out[0:3, :] = dot_nt(late_ref[...], chosen, highest)[0:3]
        gains_out[3:5, :] = dot_nt(early_ref[span : span + 8, :], chosen, highest)[0:2]
        second_out[...] = tiny_ref[0:mixw, 0:mixw]
        bias_out[...] = tiny_ref[span : span + 1, 0:mixw]
        loss_out[...] = tiny_ref[span + 1 : span + 2, 0:1] / (4.0 * width * small_ref[7:8, 0:1])


def rotary_lanes(length, piece):
    lane = jnp.arange(128, dtype=jnp.int32) % HEAD_DIM
    step = (lane % (ROT // 2)).astype(f32)
    inverse = jnp.exp(step * (-2.0 * math.log(10000.0) / ROT))
    angles = jnp.arange(length, dtype=jnp.int32).astype(f32)[:, None] * inverse[None, :]
    cosine = jnp.where(lane < ROT, jnp.cos(angles), 1.0)
    sine = jnp.sin(angles)
    up = jnp.where((lane >= ROT // 2) & (lane < ROT), sine, 0.0)
    down = jnp.where(lane < ROT // 2, -sine, 0.0)
    return [
        t.reshape(-1, 2, piece, 128).transpose(1, 0, 2, 3) for t in (cosine, up, down)
    ]


def local_fast(
    streams, history, teacher, prefix, valid_mask, loss_scale, projections, attention_out,
    up_weight, down_weight, mixer_first, mixer_second, mixer_bias, gains,
):
    lines = lax.axis_size("ctx")
    count = lax.axis_size("dp") * lines
    place = lax.axis_index("ctx")
    group = lax.axis_index("dp")
    me = group * lines + place
    half = group % 2
    mine = 2 * (place % 2) + half
    seqs, rows, width = streams.shape[1:]
    tokens = seqs * rows
    piece = rows // 2
    length = rows * lines
    features = width // 2
    hidden_units = down_weight.shape[0] * count
    past = history.shape[0]
    count_of_streams = teacher.shape[0]
    mixw = mixer_bias.shape[0]
    span = 64

    ids = jnp.stack([place, half, mine, mine, me]).astype(jnp.int32)
    shard = width // count
    unit_shard = hidden_units // count

    smem = pl.BlockSpec(memory_space=pltpu.SMEM)
    anywhere = pl.BlockSpec(memory_space=pl.ANY)
    proj_shape = (count // 2, 2, 3, shard, features)
    tables = rotary_lanes(length, piece)
    row_shape = (3, 4, piece, width)
    normed_shape = (3, 2, lines, piece, width)
    wide_shape = (2, lines, piece, features)
    heads_shape = (lines, rows, features)

    def array(shape, dtype=bf16):
        return jax.ShapeDtypeStruct(shape, dtype)

    (
        received, normed, proj, proj_other, up_all, down_all, small, first_t, prefix_rows,
        queries, keys, values, heads_seq, lse, heads,
    ) = pl.pallas_call(
        front_body,
        in_specs=[smem, anywhere] + [vmem()] * 10,
        out_specs=[anywhere] * 6 + [vmem()] * 3 + [anywhere] * 4 + [vmem(), anywhere],
        out_shape=[
            array(row_shape),
            array(normed_shape),
            array((3, width, features)),
            array((3, width, features)),
            array((count, shard, hidden_units)),
            array((count, unit_shard + shard, width)),
            array((8, width), f32),
            array((span, width)),
            array((8, 128), jnp.int32),
            array(wide_shape),
            array(wide_shape),
            array(wide_shape),
            array(heads_shape),
            array((lines, 8, rows), f32),
            array((4, rows, features)),
        ],
        scratch_shapes=[
            pltpu.VMEM(row_shape, bf16),
            pltpu.VMEM(normed_shape, bf16),
            pltpu.VMEM(proj_shape, bf16),
            pltpu.VMEM((3, width, features), bf16),
            pltpu.VMEM(wide_shape, bf16),
            pltpu.VMEM(wide_shape, bf16),
            pltpu.VMEM(wide_shape, bf16),
            pltpu.VMEM(heads_shape, bf16),
            pltpu.VMEM((5, 8, width), f32),
            pltpu.VMEM((5, span, width), bf16),
            pltpu.VMEM((8, 128), jnp.int32),
            pltpu.VMEM((8, 128), jnp.int32),
            pltpu.SemaphoreType.DMA((24,)),
            pltpu.SemaphoreType.DMA((112,)),
            pltpu.SemaphoreType.DMA((112,)),
        ],
        compiler_params=params(collective_id=0, has_side_effects=True),
        name="front",
    )(
        prefix,
        streams.reshape(streams.shape[0], 2 * seqs, piece, width),
        projections, up_weight, down_weight, attention_out, gains, mixer_first, valid_mask, *tables,
    )
    gain_full = small
    tile = 512
    tiles = hidden_units // tile
    token_shape = (seqs, rows, width)

    def fixed(shape, index=None):
        index = index or (0,) * len(shape)
        return pl.BlockSpec(shape, lambda i, *_: index)

    def up_column(i, ids):
        distance = lax.rem(lax.div(i, 2), 2) * 4 + lax.rem(i, 2) * 2 + lax.div(i, 4)
        return (0, 0, jnp.bitwise_xor(lax.div(ids[4], 4), distance))

    def down_block(p):
        return lambda i, *_: (jnp.clip(i - 2 * p, 0, 1), 0, 0)

    weight_specs = [
        pl.BlockSpec((count, shard, tile), up_column),
        pl.BlockSpec((4, unit_shard, width), lambda i, *_: (i, 0, 0)),
    ]
    out_weight_spec = pl.BlockSpec(
        (count, shard, width), lambda i, *_: (0, unit_shard // shard, 0)
    )
    tile_specs = [pl.BlockSpec((8, shard, tile), up_column)] * 4
    tile_specs += [pl.BlockSpec((4, unit_shard, width), down_block(p)) for p in range(4)]

    hidden, normed_mlp, active, slope, layer_out = pl.pallas_call(
        mlp_forward_body,
        grid_spec=pltpu.PrefetchScalarGridSpec(
            num_scalar_prefetch=1,
            grid=(tiles,),
            in_specs=[
                fixed((4, rows, features)),
                fixed((1,) + token_shape, (3, 0, 0, 0)),
                fixed((8, width)),
            ]
            + weight_specs
            + [out_weight_spec],
            out_specs=[
                fixed(token_shape),
                fixed(token_shape),
                pl.BlockSpec((tokens, tile), lambda i, *_: (0, i)),
                pl.BlockSpec((tokens, tile), lambda i, *_: (0, i)),
                fixed(token_shape),
            ],
            scratch_shapes=[
                pltpu.VMEM((width, width), bf16),
                pltpu.VMEM((width, tile), bf16),
                pltpu.VMEM((tile, width), bf16),
            ],
        ),
        out_shape=[
            jax.ShapeDtypeStruct(token_shape, f32),
            jax.ShapeDtypeStruct(token_shape, bf16),
            jax.ShapeDtypeStruct((tokens, hidden_units), bf16),
            jax.ShapeDtypeStruct((tokens, hidden_units), bf16),
            jax.ShapeDtypeStruct(token_shape, f32),
        ],
        compiler_params=params(),
        name="mlp_forward",
    )(ids, heads, streams, gain_full, up_all, down_all, down_all)

    block = 64
    next_streams, grad_history, grad_layer, g_first, g_second, stats, g_gain_mix = pl.pallas_call(
        mixer_body,
        grid=(tokens // block,),
        in_specs=[
            smem,
            pl.BlockSpec((block, width), lambda i: (i, 0)),
            pl.BlockSpec((past, block, width), lambda i: (0, i, 0)),
            pl.BlockSpec((count_of_streams, block, width), lambda i: (0, i, 0)),
            pl.BlockSpec((1, 1, block), lambda i: (i, 0, 0)),
            fixed((8, width)),
            fixed((span, width)),
            fixed((mixw, mixw)),
            fixed((1, mixw)),
        ],
        out_specs=[
            pl.BlockSpec((count_of_streams, block, width), lambda i: (0, i, 0)),
            pl.BlockSpec((past, block, width), lambda i: (0, i, 0)),
            pl.BlockSpec((block, width), lambda i: (i, 0)),
            fixed((span, width)),
            fixed((span, span)),
            fixed((8, span)),
            fixed((1, width)),
        ],
        out_shape=[
            jax.ShapeDtypeStruct((count_of_streams, tokens, width), bf16),
            jax.ShapeDtypeStruct((past, tokens, width), bf16),
            jax.ShapeDtypeStruct((tokens, width), f32),
            jax.ShapeDtypeStruct((span, width), f32),
            jax.ShapeDtypeStruct((span, span), f32),
            jax.ShapeDtypeStruct((8, span), f32),
            jax.ShapeDtypeStruct((1, width), f32),
        ],
        scratch_shapes=[
            pltpu.VMEM((mixw, block, 128), f32),
            pltpu.VMEM((mixw, block, 128), f32),
            pltpu.VMEM((count_of_streams, block, width), f32),
            pltpu.VMEM((block, 1), f32),
            pltpu.VMEM((span, span), f32),
            pltpu.VMEM((1, span), f32),
        ],
        compiler_params=params(),
        name="mixer",
    )(
        loss_scale,
        layer_out.reshape(tokens, width),
        history.reshape(past, tokens, width),
        teacher.reshape(count_of_streams, tokens, width),
        valid_mask.reshape(-1, 1, block),
        gain_full,
        first_t,
        mixer_second,
        mixer_bias.reshape(1, mixw),
    )

    *g_ups, gd0, gd1, gd2, gd3, g_normed = pl.pallas_call(
        mlp_backward_body,
        grid_spec=pltpu.PrefetchScalarGridSpec(
            num_scalar_prefetch=1,
            grid=(tiles,),
            in_specs=[
                fixed(token_shape),
                pl.BlockSpec((tokens, tile), lambda i, *_: (0, i)),
                pl.BlockSpec((tokens, tile), lambda i, *_: (0, i)),
                fixed(token_shape),
            ]
            + weight_specs,
            out_specs=tile_specs + [fixed(token_shape)],
            scratch_shapes=[
                pltpu.VMEM(token_shape, bf16),
                pltpu.VMEM((width, tokens), bf16),
                pltpu.VMEM((width, tile), bf16),
                pltpu.VMEM((tile, width), bf16),
                pltpu.VMEM((width, tile), bf16),
            ],
        ),
        out_shape=[jax.ShapeDtypeStruct((8, shard, hidden_units), bf16)] * 4
        + [jax.ShapeDtypeStruct((8, unit_shard, width), bf16)] * 4
        + [jax.ShapeDtypeStruct(token_shape, f32)],
        compiler_params=params(),
        name="mlp_backward",
    )(ids, grad_layer.reshape(token_shape), active, slope, normed_mlp, up_all, down_all)
    g_downs = [gd0, gd1, gd2, gd3]

    hidden_results = pl.pallas_call(
        hidden_backward_body,
        grid_spec=pltpu.PrefetchScalarGridSpec(
            num_scalar_prefetch=1,
            grid=(1,),
            in_specs=[fixed(token_shape)] * 3
            + [fixed((4, rows, features)), fixed((8, width)), out_weight_spec],
            out_specs=[fixed(token_shape)]
            + [fixed((rows, features))] * 4
            + [fixed((8, shard, width))] * 4
            + [fixed((1, width))],
            scratch_shapes=[pltpu.VMEM((width, width), bf16), pltpu.VMEM((width, width), f32)],
        ),
        out_shape=[jax.ShapeDtypeStruct(token_shape, bf16)]
        + [jax.ShapeDtypeStruct((rows, features), bf16)] * 4
        + [jax.ShapeDtypeStruct((8, shard, width), bf16)] * 4
        + [jax.ShapeDtypeStruct((1, width), f32)],
        compiler_params=params(),
        name="hidden_backward",
    )(ids, grad_layer.reshape(token_shape), g_normed, hidden, heads, gain_full, down_all)
    g_res, gh0, gh1, gh2, gh3, go0, go1, go2, go3, g_gain_mlp = hidden_results

    down_block_shape = (unit_shard + shard, width)
    slot_shape = (2, lines, piece, width)

    def buffer(shape, dtype=bf16):
        return pltpu.VMEM(shape, dtype)

    grad_streams, grad_projections, sum_up, sum_down, sum_out, early, tiny, late = pl.pallas_call(
        back_body,
        in_specs=[vmem()]
        + [anywhere] * 4
        + [vmem()] * 4
        + [anywhere] * 4
        + [vmem()] * 6
        + [anywhere] * 17,
        out_specs=[anywhere] + [vmem()] * 7,
        out_shape=[
            array((streams.shape[0], 2 * seqs, piece, width)),
            array((3, shard, width), f32),
            array((shard, hidden_units), f32),
            array((unit_shard, width), f32),
            array((shard, width), f32),
            array((span + 8, width), f32),
            array((span + 8, span), f32),
            array((8, width), f32),
        ],
        scratch_shapes=[
            buffer(wide_shape),
            buffer(wide_shape),
            buffer(wide_shape),
            buffer(heads_shape),
            buffer((4, rows, features)),
            buffer((3,) + wide_shape),
            buffer((3,) + wide_shape[1:]),
            buffer((length, 128), f32),
            buffer((length, 128), f32),
            buffer((128, length)),
            buffer((2,) + slot_shape),
            buffer((2,) + row_shape[1:]),
            buffer((2, 2, width, features)),
            buffer((lines, piece, width), f32),
            buffer(row_shape),
            buffer((width, features)),
            buffer((4, shard, hidden_units)),
            buffer((4,) + down_block_shape),
            buffer((16, shard, hidden_units)),
            buffer((8, shard, hidden_units)),
            buffer((4, shard, hidden_units)),
            buffer((2, shard, hidden_units)),
            buffer((1, shard, hidden_units)),
            buffer((16,) + down_block_shape),
            buffer((8,) + down_block_shape),
            buffer((4,) + down_block_shape),
            buffer((2,) + down_block_shape),
            buffer((1,) + down_block_shape),
            buffer(proj_shape),
            buffer((8,) + proj_shape[1:]),
            buffer((4,) + proj_shape[1:]),
            buffer((2,) + proj_shape[1:]),
            buffer((1,) + proj_shape[1:]),
            buffer(proj_shape[2:]),
            buffer((5, span + 8, width), f32),
            buffer((5, span + 8, span), f32),
            buffer((5, 8, width), f32),
            pltpu.SemaphoreType.DMA((40,)),
            pltpu.SemaphoreType.DMA((64,)),
            pltpu.SemaphoreType.DMA((64,)),
        ],
        compiler_params=pltpu.CompilerParams(
            vmem_limit_bytes=63 * 1024 * 1024, collective_id=1, has_side_effects=True
        ),
        name="back",
    )(
        prefix_rows,
        queries, keys, values, heads_seq,
        lse,
        *tables,
        normed, received, proj, proj_other, gain_full, g_first, g_gain_mlp, g_gain_mix, g_second, stats,
        g_res.reshape(2 * seqs, piece, width),
        gh0, gh1, gh2, gh3, *g_ups, *g_downs, go0, go1, go2, go3,
    )
    quarters = 2 * seqs
    stream_block = pl.BlockSpec((1, quarters // 2, piece, width), lambda i: (i // 2, i % 2, 0, 0))
    whole_shapes = [
        ((3, shard, width), f32),
        ((shard, hidden_units), f32),
        ((unit_shard, width), f32),
        ((shard, width), f32),
    ]
    small_shapes = [((shard, mixw), f32), ((mixw, mixw), f32), ((1, mixw), f32), ((5, shard), f32), ((1, 1), f32)]
    (
        grad_streams, grad_projections, sum_up, sum_down, sum_out,
        grad_first, grad_second, grad_bias, grad_gains, mean_loss,
    ) = pl.pallas_call(
        finish_body,
        grid=(2 * streams.shape[0],),
        in_specs=[smem, stream_block]
        + [fixed(s) for s, _ in whole_shapes]
        + [fixed((span + 8, width)), fixed((span + 8, span)), fixed((8, width)), fixed((8, width))],
        out_specs=[stream_block] + [fixed(s) for s, _ in whole_shapes + small_shapes],
        out_shape=[array((streams.shape[0], quarters, piece, width))]
        + [array(*s) for s in whole_shapes + small_shapes],
        compiler_params=params(),
        name="finish",
    )(
        me.reshape(1).astype(jnp.int32),
        grad_streams, grad_projections, sum_up, sum_down, sum_out, early, tiny, late, small,
    )
    return (
        next_streams.reshape(teacher.shape),
        mean_loss.reshape(()),
        grad_streams.reshape(streams.shape),
        grad_history.reshape(history.shape),
        grad_projections,
        sum_out,
        sum_up,
        sum_down,
        grad_first,
        grad_second,
        grad_bias.reshape(mixw),
        grad_gains,
    )


def layer_norm(values, gain_row):
    centered = values - jnp.mean(values, axis=-1, keepdims=True)
    return (
        centered
        * lax.rsqrt(jnp.mean(centered * centered, axis=-1, keepdims=True) + epsilon)
        * gain_row
    )


def rms_norm(values, gain_row):
    return (
        values * lax.rsqrt(jnp.mean(values * values, axis=-1, keepdims=True) + epsilon) * gain_row
    )


def gelu_exact(values):
    return jax.nn.gelu(values, approximate=False)


def rotary_tables(positions):
    frequency_steps = jnp.arange(ROT // 2).astype(positions.dtype)
    inverse = jnp.exp(frequency_steps * (-2.0 * math.log(10000.0) / ROT))
    angles = positions[:, None] * inverse[None, :]
    return (jnp.cos(angles)[:, None, :], jnp.sin(angles)[:, None, :])


def rotate(values, cosine_table, sine_table, direction):
    row_count = values.shape[0]
    shaped = values.reshape(row_count, HEADS, HEAD_DIM)
    half_rot = ROT // 2
    first_half = shaped[:, :, :half_rot]
    second_half = shaped[:, :, half_rot:ROT]
    remainder = shaped[:, :, ROT:]
    turned_first = first_half * cosine_table - direction * second_half * sine_table
    turned_second = second_half * cosine_table + direction * first_half * sine_table
    return jnp.concatenate([turned_first, turned_second, remainder], axis=-1).reshape(row_count, -1)


def masked_scores(query_heads, key_heads, query_index, key_index, prefix_len):
    scores = jnp.einsum(
        "qhd,khd->hqk", query_heads, key_heads, preferred_element_type=jnp.float32
    ) * HEAD_DIM ** (-0.5)
    allowed = (key_index[None, :] <= query_index[:, None]) | (key_index[None, :] < prefix_len)
    return jnp.where(allowed[None], scores, -1e30)


def local_plain(
    streams,
    history,
    teacher,
    prefix,
    valid_mask,
    loss_scale,
    projections,
    attention_out,
    up_weight,
    down_weight,
    mixer_first,
    mixer_second,
    mixer_bias,
    gains,
):
    micro_count = streams.shape[1]
    row_count = streams.shape[2]
    model_width = streams.shape[3]
    length = row_count * lax.axis_size("ctx")
    query_index = lax.axis_index("ctx") * row_count + jnp.arange(row_count, dtype=jnp.int32)
    key_index = jnp.arange(length, dtype=jnp.int32)
    cosine_table, sine_table = rotary_tables(query_index.astype(jnp.float32))
    score_scale = HEAD_DIM ** (-0.5)
    valid_float = valid_mask.astype(jnp.float32)
    token_total = lax.psum(jnp.sum(valid_float), ("dp", "ctx"))
    factor = loss_scale[0] * 2.0 / (4.0 * model_width * token_total)

    def one_batch(totals, number):
        (
            kept_projections,
            kept_attention,
            kept_gains,
            kept_up,
            kept_down,
            kept_first,
            kept_second,
            kept_bias,
            kept_loss,
        ) = totals
        stream_block = lax.dynamic_index_in_dim(streams, number, 1, keepdims=False)
        past_outputs = lax.dynamic_index_in_dim(history, number, 1, keepdims=False)
        target = lax.dynamic_index_in_dim(teacher, number, 1, keepdims=False).astype(jnp.float32)
        prefix_len = lax.dynamic_index_in_dim(prefix, number, 0, keepdims=False)
        valid_row = lax.dynamic_index_in_dim(valid_float, number, 0, keepdims=False)
        proj_full, out_full, gain_low, up_full, down_full, first_full = (
            lax.all_gather(projections, ("dp", "ctx"), axis=1, tiled=True),
            lax.all_gather(attention_out, ("dp", "ctx"), axis=0, tiled=True),
            lax.all_gather(gains, ("dp", "ctx"), axis=1, tiled=True),
            lax.all_gather(up_weight, ("dp", "ctx"), axis=0, tiled=True),
            lax.all_gather(down_weight, ("dp", "ctx"), axis=0, tiled=True),
            lax.all_gather(mixer_first, ("dp", "ctx"), axis=0, tiled=True),
        )
        gain_full = gain_low.astype(jnp.float32)
        inputs = stream_block.astype(jnp.float32)
        gain_three = gain_full[:3, None, :]
        normed_low = layer_norm(inputs[:3], gain_three).astype(jnp.bfloat16)
        projected = jnp.einsum(
            "std,sde->ste", normed_low, proj_full, preferred_element_type=jnp.float32
        )
        query_heads = (
            rotate(projected[0], cosine_table, sine_table, 1.0)
            .astype(jnp.bfloat16)
            .reshape(row_count, HEADS, HEAD_DIM)
        )
        key_low = rotate(projected[1], cosine_table, sine_table, 1.0).astype(jnp.bfloat16)
        value_low = projected[2].astype(jnp.bfloat16)
        all_keys, all_values = (
            lax.all_gather(key_low, "ctx", axis=0, tiled=True),
            lax.all_gather(value_low, "ctx", axis=0, tiled=True),
        )
        key_heads = all_keys.reshape(length, HEADS, HEAD_DIM)
        value_heads = all_values.reshape(length, HEADS, HEAD_DIM)
        scores = masked_scores(query_heads, key_heads, query_index, key_index, prefix_len)
        row_max = jnp.max(scores, axis=-1, keepdims=True)
        log_total = row_max + jnp.log(jnp.sum(jnp.exp(scores - row_max), axis=-1, keepdims=True))
        probs_low = jnp.exp(scores - log_total).astype(jnp.bfloat16)
        heads_low = (
            jnp.einsum("hqk,khd->qhd", probs_low, value_heads, preferred_element_type=jnp.float32)
            .reshape(row_count, model_width)
            .astype(jnp.bfloat16)
        )
        hidden = inputs[3] + jnp.dot(heads_low, out_full, preferred_element_type=jnp.float32)
        normed_mlp = layer_norm(hidden, gain_full[3]).astype(jnp.bfloat16)
        upper = jnp.dot(normed_mlp, up_full, preferred_element_type=jnp.float32)
        activated = gelu_exact(upper).astype(jnp.bfloat16)
        layer_out = hidden + jnp.dot(activated, down_full, preferred_element_type=jnp.float32)
        normed_mix = rms_norm(layer_out, gain_full[4]).astype(jnp.bfloat16)
        mix_hidden = jnp.dot(normed_mix, first_full, preferred_element_type=jnp.float32)
        mix_active = gelu_exact(mix_hidden)
        coeff = jnp.dot(mix_active, mixer_second, precision=highest) + mixer_bias
        coeff_grid = coeff.reshape(row_count, 4, -1)
        outputs_all = jnp.concatenate([past_outputs.astype(jnp.float32), layer_out[None]], axis=0)
        next_block = jnp.einsum("tsj,jtd->std", coeff_grid, outputs_all, precision=highest)
        difference = next_block - target
        loss_part = jnp.sum(jnp.sum(difference * difference, axis=(0, 2)) * valid_row) / (
            4.0 * model_width * token_total
        )
        grad_next = factor * valid_row[None, :, None] * difference
        grad_coeff = jnp.einsum("std,jtd->tsj", grad_next, outputs_all, precision=highest).reshape(
            row_count, -1
        )
        grad_outputs = jnp.einsum("tsj,std->jtd", coeff_grid, grad_next, precision=highest)
        grad_past = grad_outputs[:-1].astype(jnp.bfloat16)
        grad_second = jnp.dot(mix_active.T, grad_coeff, precision=highest)
        grad_bias = jnp.sum(grad_coeff, axis=0)
        grad_active = jnp.dot(grad_coeff, mixer_second.T, precision=highest)
        gelu_mix_back = jax.vjp(gelu_exact, mix_hidden)[1]
        grad_mix = gelu_mix_back(grad_active)[0].astype(jnp.bfloat16)
        grad_first = jnp.einsum(
            "td,tm->dm", normed_mix, grad_mix, preferred_element_type=jnp.float32
        )
        grad_normed_mix = jnp.einsum(
            "tm,dm->td", grad_mix, first_full, preferred_element_type=jnp.float32
        )
        rms_back = jax.vjp(rms_norm, layer_out, gain_full[4])[1]
        grad_layer_mix, grad_gain_mix = rms_back(grad_normed_mix)
        grad_layer = grad_outputs[-1] + grad_layer_mix
        grad_branch = grad_layer.astype(jnp.bfloat16)
        grad_down = jnp.einsum(
            "tf,td->fd", activated, grad_branch, preferred_element_type=jnp.float32
        )
        grad_active_up = jnp.einsum(
            "td,fd->tf", grad_branch, down_full, preferred_element_type=jnp.float32
        )
        gelu_up_back = jax.vjp(gelu_exact, upper)[1]
        grad_upper = gelu_up_back(grad_active_up)[0].astype(jnp.bfloat16)
        grad_up = jnp.einsum(
            "td,tf->df", normed_mlp, grad_upper, preferred_element_type=jnp.float32
        )
        grad_normed_mlp = jnp.einsum(
            "tf,df->td", grad_upper, up_full, preferred_element_type=jnp.float32
        )
        down_shard, first_shard, up_shard = (
            lax.psum_scatter(grad_down, ("dp", "ctx"), scatter_dimension=0, tiled=True),
            lax.psum_scatter(grad_first, ("dp", "ctx"), scatter_dimension=0, tiled=True),
            lax.psum_scatter(grad_up, ("dp", "ctx"), scatter_dimension=0, tiled=True),
        )
        down_next = kept_down + down_shard
        norm_mlp_back = jax.vjp(layer_norm, hidden, gain_full[3])[1]
        grad_hidden_mlp, grad_gain_mlp = norm_mlp_back(grad_normed_mlp)
        grad_hidden = grad_layer + grad_hidden_mlp
        grad_attn = grad_hidden.astype(jnp.bfloat16)
        grad_attention = jnp.einsum(
            "td,te->de", heads_low, grad_attn, preferred_element_type=jnp.float32
        )
        grad_heads = jnp.einsum(
            "te,de->td", grad_attn, out_full, preferred_element_type=jnp.float32
        ).astype(jnp.bfloat16)
        grad_head_grid = grad_heads.reshape(row_count, HEADS, HEAD_DIM)
        scores_again = masked_scores(query_heads, key_heads, query_index, key_index, prefix_len)
        probs_exact = jnp.exp(scores_again - log_total)
        probs_again = probs_exact.astype(jnp.bfloat16)
        grad_probs = jnp.einsum(
            "qhd,khd->hqk", grad_head_grid, value_heads, preferred_element_type=jnp.float32
        )
        row_inner = jnp.sum(probs_exact * grad_probs, axis=-1, keepdims=True)
        grad_scores = (probs_exact * (grad_probs - row_inner)).astype(jnp.bfloat16)
        grad_queries = (
            jnp.einsum(
                "hqk,khd->qhd", grad_scores, key_heads, preferred_element_type=jnp.float32
            ).reshape(row_count, model_width)
            * score_scale
        )
        grad_key_part = (
            jnp.einsum("hqk,qhd->khd", grad_scores, query_heads, preferred_element_type=jnp.float32)
            * score_scale
        )
        grad_value_part = jnp.einsum(
            "hqk,qhd->khd", probs_again, grad_head_grid, preferred_element_type=jnp.float32
        )
        key_grads = lax.psum_scatter(
            jnp.concatenate(
                [
                    grad_key_part.reshape(row_count * lax.axis_size("ctx"), -1),
                    grad_value_part.reshape(row_count * lax.axis_size("ctx"), -1),
                ],
                axis=-1,
            ).astype(jnp.bfloat16),
            "ctx",
            scatter_dimension=0,
            tiled=True,
        ).astype(jnp.float32)
        grad_query_low = rotate(grad_queries, cosine_table, sine_table, -1.0).astype(jnp.bfloat16)
        grad_key_low = rotate(key_grads[:, :model_width], cosine_table, sine_table, -1.0).astype(
            jnp.bfloat16
        )
        grad_value_low = key_grads[:, model_width:].astype(jnp.bfloat16)
        grad_projected = jnp.stack([grad_query_low, grad_key_low, grad_value_low])
        grad_proj = jnp.einsum(
            "std,ste->sde", normed_low, grad_projected, preferred_element_type=jnp.float32
        )
        grad_normed = jnp.einsum(
            "ste,sde->std", grad_projected, proj_full, preferred_element_type=jnp.float32
        )
        norm_three_back = jax.vjp(layer_norm, inputs[:3], gain_three)[1]
        grad_inputs_three, grad_gain_three = norm_three_back(grad_normed)
        grad_gain_all = jnp.concatenate(
            [grad_gain_three.reshape(3, -1), grad_gain_mlp[None], grad_gain_mix[None]], axis=0
        )
        proj_shard, attention_shard, gain_shard = (
            lax.psum_scatter(grad_proj, ("dp", "ctx"), scatter_dimension=1, tiled=True),
            lax.psum_scatter(grad_attention, ("dp", "ctx"), scatter_dimension=0, tiled=True),
            lax.psum_scatter(grad_gain_all, ("dp", "ctx"), scatter_dimension=1, tiled=True),
        )
        grad_block = jnp.concatenate([grad_inputs_three, grad_hidden[None]], axis=0).astype(
            jnp.bfloat16
        )
        new_totals = (
            kept_projections + proj_shard,
            kept_attention + attention_shard,
            kept_gains + gain_shard,
            kept_up + up_shard,
            down_next,
            kept_first + first_shard,
            kept_second + grad_second,
            kept_bias + grad_bias,
            kept_loss + loss_part,
        )
        return (new_totals, (next_block.astype(jnp.bfloat16), grad_block, grad_past))

    down_start = jnp.zeros(down_weight.shape, jnp.float32)
    start_totals = (
        jnp.zeros(projections.shape, jnp.float32),
        jnp.zeros(attention_out.shape, jnp.float32),
        jnp.zeros(gains.shape, jnp.float32),
        jnp.zeros(up_weight.shape, jnp.float32),
        down_start,
        jnp.zeros(mixer_first.shape, jnp.float32),
        jnp.zeros(mixer_second.shape, jnp.float32),
        jnp.zeros(mixer_bias.shape, jnp.float32),
        jnp.zeros((), jnp.float32),
    )
    final_totals, stacked = lax.scan(
        one_batch, start_totals, jnp.arange(micro_count, dtype=jnp.int32)
    )
    (
        sum_projections,
        sum_attention,
        sum_gains,
        sum_up,
        sum_down,
        sum_first,
        sum_second,
        sum_bias,
        sum_loss,
    ) = final_totals
    grad_second_all, grad_bias_all, loss_all = lax.psum(
        (sum_second, sum_bias, sum_loss), ("dp", "ctx")
    )
    next_streams = jnp.moveaxis(stacked[0], 0, 1)
    grad_streams = jnp.moveaxis(stacked[1], 0, 1)
    grad_history = jnp.moveaxis(stacked[2], 0, 1)
    return (
        next_streams,
        loss_all,
        grad_streams,
        grad_history,
        sum_projections,
        sum_attention,
        sum_up,
        sum_down,
        sum_first,
        grad_second_all,
        grad_bias_all,
        sum_gains,
    )


def fits(mesh):
    return mesh.shape["ctx"] == 4 and mesh.shape["dp"] == 8


def solution(mesh):
    specs = dict(
        in_specs=(
            P(None, "dp", "ctx", None),
            P(None, "dp", "ctx", None),
            P(None, "dp", "ctx", None),
            P("dp"),
            P("dp", "ctx"),
            P(),
            P(None, ("dp", "ctx"), None),
            P(("dp", "ctx"), None),
            P(("dp", "ctx"), None),
            P(("dp", "ctx"), None),
            P(("dp", "ctx"), None),
            P(),
            P(),
            P(None, ("dp", "ctx")),
        ),
        out_specs=(
            P(None, "dp", "ctx", None),
            P(),
            P(None, "dp", "ctx", None),
            P(None, "dp", "ctx", None),
            P(None, ("dp", "ctx"), None),
            P(("dp", "ctx"), None),
            P(("dp", "ctx"), None),
            P(("dp", "ctx"), None),
            P(("dp", "ctx"), None),
            P(),
            P(),
            P(None, ("dp", "ctx")),
        ),
        check_vma=False,
    )

    def chosen(*arrays):
        fast = fits(mesh) and arrays[0].shape[1] == 2 * mesh.shape["dp"]
        return jax.shard_map(local_fast if fast else local_plain, mesh=mesh, **specs)(*arrays)

    return chosen
```

```python
import functools
import math

import jax
import jax.numpy as jnp
from jax import lax
from jax.experimental import pallas as pl
from jax.experimental.pallas import tpu as pltpu
from jax.sharding import PartitionSpec as P

HEADS = 16
HEAD_DIM = 64
ROT = 16
AXES = ("dp", "ctx")

highest = lax.Precision.HIGHEST
epsilon = 1e-05
f32 = jnp.float32
bf16 = jnp.bfloat16
VMEM_BYTES = 60 * 1024 * 1024


def dot_nn(a, b, precision=None):
    return lax.dot_general(
        a, b, (((1,), (0,)), ((), ())), precision=precision, preferred_element_type=f32
    )


def dot_nt(a, b, precision=None):
    return lax.dot_general(
        a, b, (((1,), (1,)), ((), ())), precision=precision, preferred_element_type=f32
    )


def dot_tn(a, b, precision=None):
    return lax.dot_general(
        a, b, (((0,), (0,)), ((), ())), precision=precision, preferred_element_type=f32
    )


def normal_cdf(v):
    z = jnp.abs(v) * math.sqrt(0.5)
    t = 1.0 / (1.0 + 0.39 * z)
    bell = jnp.exp(-0.5 * v * v)
    poly = -0.22760540438261295
    for c in (
        0.8869388009365644,
        -0.6358388689155755,
        0.649907738051149,
        0.09125094908545259,
        0.23534677935551734,
    ):
        poly = poly * t + c
    half_tail = (0.5 * poly) * t * bell
    return jnp.where(v < 0.0, half_tail, 1.0 - half_tail), bell


def gelu_pair(v):
    cdf, bell = normal_cdf(v)
    return v * cdf, cdf + v * bell * (1.0 / math.sqrt(2.0 * math.pi))


def vmem(block=None, index_map=None):
    if block is None:
        return pl.BlockSpec(memory_space=pltpu.VMEM)
    return pl.BlockSpec(block, index_map)


def params(**kw):
    return pltpu.CompilerParams(vmem_limit_bytes=VMEM_BYTES, **kw)


Z_ORDER = (0, 2, 1, 3)


UP_BITS = (8, 16)
DOWN_BITS = (16, 8)


def gathered_from(me, place, outer):
    distance = 4 * (place // 16) + outer[0] * (place // 8 % 2) + outer[1] * (place // 4 % 2)
    return jnp.bitwise_xor(me, distance + Z_ORDER[place % 4])


def place_rows(me, ref, outer, out_ref):
    rows = ref.shape[-2]
    for place in range(ref.shape[0]):
        device = gathered_from(me, place, outer)
        out_ref[pl.ds(pl.multiple_of(device * rows, rows), rows), :] = ref[place]


def take_rows(me, from_ref, outer, refs):
    rows = refs[0].shape[-2]
    each_has = refs[0].shape[0]
    for place in range(each_has * len(refs)):
        device = gathered_from(me, place, outer)
        refs[place // each_has][place % each_has] = from_ref[
            pl.ds(pl.multiple_of(device * rows, rows), rows), :
        ]


def place_tile(me, all_up_ref, some_down_ref, up_ref, down_ref):
    place_rows(me, all_up_ref, UP_BITS, up_ref)
    rows = some_down_ref.shape[1]
    for q, z in enumerate(Z_ORDER):
        at = pl.multiple_of(jnp.bitwise_xor(lax.rem(me, 4), z) * rows, rows)
        down_ref[pl.ds(at, rows), :] = some_down_ref[q]


def turn(x, cosine, sine_up, sine_down):
    return (
        x * cosine + pltpu.roll(x, ROT // 2, 1) * sine_up + pltpu.roll(x, 128 - ROT // 2, 1) * sine_down
    )


def allowed_limit(base, rows, prefix, axis):
    shape = (rows, 1) if axis == 0 else (1, rows)
    position = base + lax.broadcasted_iota(jnp.int32, shape, axis)
    return jnp.maximum(position, prefix - 1)


def flip(bit, by):
    return bit + by - 2 * bit * by


class Place:
    def __init__(self):
        self.group = lax.axis_index("dp")
        self.z = lax.axis_index("ctx")
        self.core = lax.rem(self.group, 2)
        self.x = lax.rem(lax.div(self.group, 2), 2)
        self.y = lax.div(self.group, 4)
        self.z_low = lax.rem(self.z, 2)
        self.z_high = lax.div(self.z, 2)

    def across(self, axis):
        if axis == "core":
            return (self.group + 1 - 2 * self.core, self.z)
        if axis == "x":
            return (self.group + 2 - 4 * self.x, self.z)
        if axis == "y":
            return (self.group + 4 - 8 * self.y, self.z)
        if axis == "zl":
            return (self.group, self.z + 1 - 2 * self.z_low)
        return (self.group, self.z + 2 - 4 * self.z_high)

    def device(self, y, x, core, z):
        pair = flip(self.y, y) * 4 + flip(self.x, x) * 2 + flip(self.core, core)
        return pair * 4 + flip(self.z_high, z // 2) * 2 + flip(self.z_low, z % 2)

    def code(self, k):
        return flip(self.z_high, lax.div(k, 2)), flip(self.z_low, lax.rem(k, 2))

    def block(self, k):
        return flip(self.z_low, lax.div(k, 2)) * 2 + flip(self.core, lax.rem(k, 2))

    def out_to(self, k):
        seq, half = self.code(k)
        return (self.group - self.core + half, 2 * self.core + seq)

    def back_to(self, k):
        return (self.group - self.core + self.z_high, self.block(k))

    def is_self(self, device):
        return jnp.logical_and(device[0] == self.group, device[1] == self.z)

    def meet(self, names):
        barrier = pltpu.get_barrier_semaphore()
        others = [self.across(name) for name in names]
        for step in range(1, 8):
            place = self.core * 4 + self.z + step
            others.append(
                (self.group - self.core + lax.rem(lax.div(place, 4), 2), lax.rem(place, 4))
            )
        for other in others:
            pl.semaphore_signal(barrier, inc=1, device_id=other, device_id_type=pl.DeviceIdType.MESH)
        pl.semaphore_wait(barrier, len(others))


class Sends:
    def __init__(self, here, send_sems, recv_sems):
        self.here, self.send_sems, self.recv_sems = here, send_sems, recv_sems
        self.used, self.open = 0, []

    def make(self, n, source, target, device):
        return pltpu.make_async_remote_copy(
            src_ref=source,
            dst_ref=target,
            send_sem=self.send_sems.at[n],
            recv_sem=self.recv_sems.at[n],
            device_id=device,
            device_id_type=pl.DeviceIdType.MESH,
        )

    def start(self, source, target, device):
        copy = self.make(self.used, source, target, device)
        self.used += 1
        copy.start()
        self.open.append(copy)
        return copy

    def four(self, source, target, device):
        base = self.used
        self.used += 4

        def copy(k):
            return self.make(base + k, source(k), target(k), device(k))

        def start(k):
            stays = self.here.is_self(device(k))

            @pl.when(stays)
            def _():
                pltpu.make_async_copy(source(k), target(k), self.recv_sems.at[base + k]).start()

            @pl.when(jnp.logical_not(stays))
            def _():
                copy(k).start()

        def sent(k):
            @pl.when(jnp.logical_not(self.here.is_self(device(k))))
            def _():
                copy(k).wait_send()

        def came(k):
            copy(k).wait_recv()

        return start, sent, came

    def finish(self):
        for copy in self.open:
            copy.wait_send()


def each(n, body):
    def step(i, _):
        body(i)
        return 0

    lax.fori_loop(0, n, step, 0)


class Gathers:
    def __init__(self, here, sends, refs):
        self.here, self.sends, self.refs = here, sends, refs
        self.coming = {name: [] for name in refs}

    def settle(self, name, first=0, count=1 << 20):
        left = []
        for at, n, copy in self.coming[name]:
            if at < first + count and first < at + n:
                copy.wait_recv()
            else:
                left.append((at, n, copy))
        self.coming[name] = left

    def move(self, name, axis, first, count, to):
        self.settle(name, first, count)
        ref = self.refs[name]
        copy = self.sends.start(
            ref.at[pl.ds(first, count)], ref.at[pl.ds(to, count)], self.here.across(axis)
        )
        self.coming[name].append((to, count, copy))


def key_positions(length, blocks, axis):
    shape = (length, 1) if axis == 0 else (1, length)
    i = lax.broadcasted_iota(jnp.int32, shape, axis)
    piece = length // (2 * blocks)
    return (
        lax.rem(lax.div(i, piece), blocks) * (2 * piece)
        + lax.div(i, length // 2) * piece
        + lax.rem(i, piece)
    )


FRONT_PLAN = (
    ("start", "zl"),
    ("move", "proj", "zh", 0, 1, 1),
    ("move", "proj", "zl", 0, 1, 2),
    ("add",),
    ("start", "zh"),
    ("move", "up", "zh", 0, 1, 1),
    ("move", "up", "zl", 0, 1, 2),
    ("move", "down", "zh", 0, 1, 1),
    ("move", "down", "zl", 0, 1, 2),
    ("add",),
    ("start", "x"),
    ("move", "proj", "y", 0, 1, 4),
    ("move", "proj", "x", 0, 1, 8),
    ("move", "up", "y", 0, 1, 4),
    ("move", "down", "x", 0, 1, 4),
    ("move", "up", "x", 0, 1, 8),
    ("move", "down", "y", 0, 1, 8),
    ("rows", 1),
    ("add",),
    ("start", "y"),
    ("move", "proj", "zl", 1, 1, 3),
    ("move", "proj", "y", 1, 1, 5),
    ("move", "proj", "x", 1, 1, 9),
    ("add",),
    ("start", "core"),
    ("move", "proj", "x", 4, 1, 12),
    ("move", "up", "zl", 1, 1, 3),
    ("move", "down", "zl", 1, 1, 3),
    ("add",),
    ("rows", 2),
    ("move", "up", "y", 1, 1, 5),
    ("move", "down", "x", 1, 1, 5),
    ("move", "up", "x", 1, 1, 9),
    ("move", "down", "y", 1, 1, 9),
    ("rows", 0),
    ("move", "proj", "y", 2, 2, 6),
    ("move", "proj", "x", 2, 2, 10),
    ("move", "proj", "x", 5, 1, 13),
    ("move", "up", "x", 4, 1, 12),
    ("move", "down", "y", 4, 1, 12),
    ("move", "up", "y", 2, 2, 6),
    ("move", "down", "x", 2, 2, 6),
    ("norm", 1),
    ("move", "proj", "x", 6, 2, 14),
    ("move", "up", "x", 2, 2, 10),
    ("move", "down", "y", 2, 2, 10),
    ("move", "up", "x", 5, 1, 13),
    ("move", "down", "y", 5, 1, 13),
    ("norm", 2),
    ("move", "up", "x", 6, 2, 14),
    ("move", "down", "y", 6, 2, 14),
    ("move", "up", "core", 0, 8, 16),
    ("move", "down", "core", 0, 8, 16),
    ("assemble",),
    ("project", 1),
    ("project", 2),
    ("norm", 0),
    ("project", 0),
    ("move", "up", "core", 8, 4, 24),
    ("move", "down", "core", 8, 4, 24),
    ("attend",),
    ("move", "up", "core", 12, 4, 28),
    ("move", "down", "core", 12, 4, 28),
)


def front_body(
    prefix_in, streams_ref, proj_in, up_in, down_in, out_in, gains_in, first_in, valid_in, cos_ref, rise_ref, fall_ref,
    received_out, normed_out, weight_out, far_out, up_ref, down_ref, small_ref, first_ref, prefix_ref,
    q_out, k_out, v_out, heads_out, lse_ref, got_ref,
    received_ref, normed_ref, proj_ref, weight_ref, q_ref, k_ref, v_ref, heads_ref,
    small_got, first_got, prefix_own, prefix_got, local_sems, send_sems, recv_sems,
):
    here = Place()
    sends = Sends(here, send_sems, recv_sems)
    gathers = Gathers(here, sends, {"proj": proj_ref, "up": up_ref, "down": down_ref})
    features = proj_ref.shape[-1]
    units = down_in.shape[0]
    kept = []

    def keep(source, target):
        copy = pltpu.make_async_copy(source, target, local_sems.at[len(kept)])
        kept.append(copy)
        copy.start()
        return copy

    def columns(which):
        return proj_in.at[:, :, pl.ds(pl.multiple_of(which * features, features), features)]

    shard = gains_in.shape[1]
    lanes = small_ref.shape[1]
    column = lax.broadcasted_iota(jnp.int32, (shard, lanes), 1)
    row = lax.broadcasted_iota(jnp.int32, (shard, lanes), 0)
    chosen = (column == row + here.device(0, 0, 0, 0) * shard).astype(bf16)
    count = jnp.sum(valid_in[...].astype(f32))
    small_ref[...] = jnp.zeros_like(small_ref)
    small_ref[0:5, :] = dot_nn(gains_in[...], chosen)
    small_ref[7:8, :] = jnp.full((1, lanes), 1.0, f32) * count
    first_ref[...] = jnp.zeros_like(first_ref)
    first_ref[0 : first_in.shape[1], :] = dot_tn(first_in[...], chosen).astype(bf16)
    second_row = lax.broadcasted_iota(jnp.int32, prefix_own.shape, 0) == 1
    prefix_own[...] = jnp.where(second_row, prefix_in[1], prefix_in[0])
    here.meet(("x", "y"))
    small_steps = []

    def small_start(axis):
        n = len(small_steps)
        device = here.across(axis)
        small_steps.append(
            (
                sends.start(small_ref, small_got.at[n], device),
                sends.start(first_ref, first_got.at[n], device),
            )
        )

    def small_end():
        n = len(small_steps) - 1
        for copy in small_steps[n]:
            copy.wait()
        sends.open = [c for c in sends.open if not any(c is s for s in small_steps[n])]
        small_ref[...] += small_got[n]
        first_ref[...] += first_got[n]

    def stream(s):
        def source(k):
            seq, half = here.code(k)
            return streams_ref.at[s, 2 * seq + half]

        steps = sends.four(source, lambda k: received_ref.at[s, k], here.out_to)
        each(4, steps[0])
        return steps

    chunk = 32

    def norm(s, steps):
        gain = small_ref[s : s + 1, :].astype(f32)

        def step(k):
            steps[2](k)
            block = here.block(k)

            def body(i, _):
                at = pl.ds(pl.multiple_of(i * chunk, chunk), chunk)
                x = received_ref[s, k, at, :].astype(f32)
                x = x - jnp.mean(x, axis=-1, keepdims=True)
                scale = lax.rsqrt(jnp.mean(x * x, axis=-1, keepdims=True) + epsilon)
                normed_ref[s, here.core, block, at, :] = (x * scale * gain).astype(bf16)
                return 0

            lax.fori_loop(0, received_ref.shape[2] // chunk, body, 0, unroll=2)

        each(4, step)
        keep(received_ref.at[s], received_out.at[s])
        keep(normed_ref.at[s, here.core], normed_out.at[s, here.core])
        return sends.start(
            normed_ref.at[s, here.core], normed_ref.at[s, here.core], here.across("core")
        )

    prefix_send = sends.start(prefix_own, prefix_got, here.across("core"))
    gathers.coming["proj"].append(
        (0, 1, sends.start(columns(1 - here.core), proj_ref.at[0, 1], here.across("core")))
    )
    own = [
        keep(columns(here.core), proj_ref.at[0, 0]),
        keep(up_in, up_ref.at[0]),
        keep(down_in, down_ref.at[0, pl.ds(0, units)]),
        keep(out_in, down_ref.at[0, pl.ds(units, out_in.shape[0])]),
    ]
    for copy in own:
        copy.wait()
    prefix_send.wait_recv()
    prefixes = jnp.where(here.z_high == here.core, prefix_own[...], prefix_got[...])
    prefix_ref[...] = jnp.broadcast_to(
        jnp.where(here.z_low == 0, prefixes[0:1], prefixes[1:2]), prefix_ref.shape
    )
    def assemble(s):
        rows = proj_ref.shape[-2]
        for x in range(2):
            for y in range(2):
                for q, z in enumerate(Z_ORDER):
                    for core in range(2):
                        device = here.device(y, x, core, z)
                        at = pl.ds(pl.multiple_of(device * rows, rows), rows)
                        weight_ref[s, at, :] = proj_ref[(x * 2 + y) * 4 + q, core, s]


    _, blocks, piece, width = q_ref.shape
    half_rows = blocks * piece
    length = 2 * half_rows

    def project(s, out_ref):
        def step(half):
            y = dot_nn(normed_ref[s, half].reshape(half_rows, -1), weight_ref[s])
            if s < 2:
                tables = [r[half].reshape(half_rows, 128) for r in (cos_ref, rise_ref, fall_ref)]
                y = jnp.concatenate(
                    [turn(y[:, i : i + 128], *tables) for i in range(0, width, 128)], axis=1
                )
            y = y.astype(bf16)
            if s == 0:
                y = y * jnp.asarray(HEAD_DIM**-0.5, bf16)
            out_ref[half] = y.reshape(blocks, piece, width)

        each(2, step)

    rows = 2 * piece
    lane = lax.broadcasted_iota(jnp.int32, (rows, 128), 1)
    key_index = key_positions(length, blocks, 1)
    heads_steps = sends.four(
        lambda k: heads_ref.at[here.block(k)], lambda k: got_ref.at[k], here.back_to
    )

    def block_body(k):
        block = here.block(k)
        allowed = key_index <= allowed_limit(block * rows, rows, prefix_ref[0:1, 0:1], 0)
        lse_all = jnp.zeros((rows, 128), f32)
        for pair in range(width // 128):
            at = slice(pair * 128, pair * 128 + 128)
            queries = q_ref[:, block, :, at].reshape(rows, 128)
            keys = k_ref[:, :, :, at].reshape(length, 128)
            values = v_ref[:, :, :, at].reshape(length, 128)
            results = []
            for h in range(2):
                chosen = (lane < 64) if h == 0 else (lane >= 64)
                scores = dot_nt(jnp.where(chosen, queries, jnp.zeros_like(queries)), keys)
                scores = jnp.where(allowed, scores, -1e30)
                top = jnp.max(scores, axis=-1, keepdims=True)
                weights = jnp.exp(scores - top)
                total = jnp.sum(weights, axis=-1, keepdims=True)
                results.append(dot_nn(weights.astype(bf16), values) / total)
                lse_all = jnp.where(lane == pair * 2 + h, top + jnp.log(total), lse_all)
            heads_ref[block, :, at] = jnp.where(lane < 64, results[0], results[1]).astype(bf16)
        lse_ref[block] = lse_all.T[0:8]
        heads_steps[0](k)


    rows_steps, others, far = {}, {}, []
    for step in FRONT_PLAN:
        kind = step[0]
        if kind == "start":
            small_start(step[1])
        elif kind == "add":
            small_end()
        elif kind == "rows":
            rows_steps[step[1]] = stream(step[1])
        elif kind == "move":
            gathers.move(*step[1:])
        elif kind == "norm":
            others[step[1]] = norm(step[1], rows_steps[step[1]])
        elif kind == "assemble":
            gathers.settle("proj")
            each(3, assemble)
            far.append(sends.start(weight_ref, far_out, here.across("core")))
            keep(weight_ref, weight_out)
        elif kind == "project":
            s = step[1]
            others[s].wait_recv()
            keep(normed_ref.at[s, 1 - here.core], normed_out.at[s, 1 - here.core])
            ref, out = ((q_ref, q_out), (k_ref, k_out), (v_ref, v_out))[s]
            project(s, ref)
            keep(ref, out)
        else:
            each(4, block_body)
            keep(heads_ref, heads_out)
    each(4, heads_steps[2])
    for name in ("up", "down"):
        gathers.settle(name)
    far[0].wait_recv()
    for steps in list(rows_steps.values()) + [heads_steps]:
        each(4, steps[1])
    sends.finish()
    for copy in kept[len(own) :]:
        copy.wait()


def mlp_forward_body(
    ids, heads_ref, res_ref, gain_ref, all_up_ref, some_down_ref, gathered_out_ref,
    hidden_ref, normed_ref, active_ref, slope_ref, layer_ref,
    out_w_ref, up_ref, down_ref,
):
    step = pl.program_id(0)
    seqs, rows, width = res_ref.shape[1:]
    me = ids[4]

    @pl.when(step == 0)
    def _():
        place_rows(me, gathered_out_ref, DOWN_BITS, out_w_ref)
        hidden_ref[...] = res_ref[0].astype(f32)
        for k in range(heads_ref.shape[0]):
            code = jnp.bitwise_xor(ids[0], k)
            features = heads_ref.shape[-1]
            at = pl.ds(pl.multiple_of(lax.rem(code, 2) * features, features), features)
            hidden_ref[lax.div(code, 2)] += dot_nn(heads_ref[k], out_w_ref[at, :])
        gain = gain_ref[3:4, :].astype(f32)
        for j in range(seqs):
            x = hidden_ref[j]
            layer_ref[j] = x
            x = x - jnp.mean(x, axis=-1, keepdims=True)
            scale = lax.rsqrt(jnp.mean(x * x, axis=-1, keepdims=True) + epsilon)
            normed_ref[j] = (x * scale * gain).astype(bf16)

    place_tile(me, all_up_ref, some_down_ref, up_ref, down_ref)
    upper = dot_nn(normed_ref[...].reshape(seqs * rows, width), up_ref[...])
    active, slope = gelu_pair(upper)
    active = active.astype(bf16)
    active_ref[...] = active
    slope_ref[...] = slope.astype(bf16)
    layer_ref[...] += dot_nn(active, down_ref[...]).reshape(seqs, rows, width)


def mixer_body(
    scal_ref, layer_ref, hist_ref, teacher_ref, valid_in, gain_ref, first_ref, second_in, bias_in,
    next_ref, ghist_ref, glayer_ref, gfirst_ref, gsecond_ref, stats_ref, ggain_ref,
    coef_ref, part_ref, gnext_ref, valid_ref, second_ref, bias_ref,
):
    step = pl.program_id(0)
    past, rows, width = hist_ref.shape
    streams = teacher_ref.shape[0]
    outs = past + 1
    span = first_ref.shape[0]

    @pl.when(step == 0)
    def _():
        gfirst_ref[...] = jnp.zeros_like(gfirst_ref)
        gsecond_ref[...] = jnp.zeros_like(gsecond_ref)
        stats_ref[...] = jnp.zeros_like(stats_ref)
        ggain_ref[...] = jnp.zeros_like(ggain_ref)
        second_ref[...] = jnp.zeros_like(second_ref)
        second_ref[0 : second_in.shape[0], 0 : second_in.shape[1]] = second_in[...]
        bias_ref[...] = jnp.zeros_like(bias_ref)
        bias_ref[:, 0 : bias_in.shape[1]] = bias_in[...]

    factor = scal_ref[0] * 2.0 / (4.0 * width * gain_ref[7:8, 0:128])
    diagonal = lax.broadcasted_iota(jnp.int32, (rows, rows), 0) == lax.broadcasted_iota(
        jnp.int32, (rows, rows), 1
    )
    valid_row = jnp.broadcast_to(valid_in[0].astype(f32), (rows, rows))
    valid_ref[...] = jnp.sum(jnp.where(diagonal, valid_row, 0.0), axis=1, keepdims=True)
    x = layer_ref[...]
    scale = lax.rsqrt(jnp.mean(x * x, axis=-1, keepdims=True) + epsilon)
    gain = gain_ref[4:5, :].astype(f32)
    normed = (x * scale * gain).astype(bf16)
    mix_hidden = dot_nt(normed, first_ref[...])
    mix_active, mix_slope = gelu_pair(mix_hidden)
    coeff = dot_nn(mix_active, second_ref[...], highest) + bias_ref[...]
    for c in range(streams * outs):
        coef_ref[c] = jnp.broadcast_to(coeff[:, c : c + 1], (rows, 128))
    part_ref[...] = jnp.zeros_like(part_ref)

    chunk = 16
    lanes = 512

    def rows_body(i, loss_rows):
        at = pl.ds(pl.multiple_of(i * chunk, chunk), chunk)
        valid = jnp.broadcast_to(valid_ref[at, :], (chunk, 128))

        def read(j, lane_at):
            return layer_ref[at, lane_at] if j == past else hist_ref[j, at, lane_at].astype(f32)

        for l0 in range(0, width, 256):
            lane_at = slice(l0, l0 + 256)
            sums = [jnp.zeros((chunk, 256), f32) for _ in range(streams)]
            for j in range(outs):
                value = read(j, lane_at)
                for s in range(streams):
                    c = coef_ref[s * outs + j, at, :]
                    sums[s] = sums[s] + jnp.concatenate([c, c], axis=1) * value
            both = jnp.concatenate([valid, valid], axis=1)
            for s in range(streams):
                next_ref[s, at, lane_at] = sums[s].astype(bf16)
                difference = sums[s] - teacher_ref[s, at, lane_at].astype(f32)
                weighted = both * difference
                gnext_ref[s, at, lane_at] = jnp.concatenate([factor, factor], axis=1) * weighted
                square = weighted * difference
                loss_rows = loss_rows + square[:, :128] + square[:, 128:]
        for l0 in range(0, width, lanes):
            lane_at = slice(l0, l0 + lanes)
            for j in range(outs):
                value = read(j, lane_at)
                total = jnp.zeros((chunk, lanes), f32)
                for s in range(streams):
                    grad = gnext_ref[s, at, lane_at]
                    c = coef_ref[s * outs + j, at, :]
                    total = total + jnp.concatenate([c] * (lanes // 128), axis=1) * grad
                    product = grad * value
                    folded = product[:, :128]
                    for q in range(128, lanes, 128):
                        folded = folded + product[:, q : q + 128]
                    part_ref[s * outs + j, at, :] += folded
                if j == past:
                    glayer_ref[at, lane_at] = total
                else:
                    ghist_ref[j, at, lane_at] = total.astype(bf16)
        return loss_rows

    loss_rows = lax.fori_loop(0, rows // chunk, rows_body, jnp.zeros((chunk, 128), f32))
    lane = lax.broadcasted_iota(jnp.int32, (rows, span), 1)
    grad_coeff = jnp.zeros((rows, span), f32)
    for c in range(streams * outs):
        grad_coeff = jnp.where(lane == c, jnp.sum(part_ref[c], axis=-1, keepdims=True), grad_coeff)
    gsecond_ref[...] += dot_tn(mix_active, grad_coeff, highest)
    stats_ref[0:1, :] += jnp.sum(grad_coeff, axis=0, keepdims=True)
    stats_ref[1:2, :] += jnp.broadcast_to(jnp.sum(loss_rows), (1, span))
    grad_active = dot_nt(grad_coeff, second_ref[...], highest)
    grad_mix = (grad_active * mix_slope).astype(bf16)
    gfirst_ref[...] += dot_tn(grad_mix, normed)
    grad_normed = dot_nn(grad_mix, first_ref[...])
    x = layer_ref[...]
    ggain_ref[...] += jnp.sum(grad_normed * (x * scale), axis=0, keepdims=True)
    inner = grad_normed * gain
    mean = jnp.mean(inner * x, axis=-1, keepdims=True)
    glayer_ref[...] += scale * inner - x * (scale * scale * scale * mean)


def norm_back(x, grad, gain):
    centered = x - jnp.mean(x, axis=-1, keepdims=True)
    scale = lax.rsqrt(jnp.mean(centered * centered, axis=-1, keepdims=True) + epsilon)
    unit = centered * scale
    grad_gain = jnp.sum(grad * unit, axis=0, keepdims=True)
    inner = grad * gain
    inner = (
        inner
        - jnp.mean(inner, axis=-1, keepdims=True)
        - unit * jnp.mean(inner * unit, axis=-1, keepdims=True)
    )
    return scale * inner, grad_gain


def mlp_backward_body(
    ids, glayer_ref, active_ref, slope_ref, normed_ref, all_up_ref, some_down_ref,
    gu0, gu1, gu2, gu3, gd0, gd1, gd2, gd3, sum_ref,
    low_ref, normed_t_ref, up_ref, down_ref, tile_ref,
):
    step = pl.program_id(0)
    seqs, rows, width = glayer_ref.shape
    tokens = seqs * rows
    me = ids[4]
    place = lax.rem(me, 4)

    @pl.when(step == 0)
    def _():
        low_ref[...] = glayer_ref[...].astype(bf16)
        sum_ref[...] = jnp.zeros_like(sum_ref)
        normed_t_ref[...] = normed_ref[...].reshape(tokens, width).T

    place_tile(me, all_up_ref, some_down_ref, up_ref, down_ref)
    grad = low_ref[...].reshape(tokens, width)
    grad_active = dot_nt(grad, down_ref[...])
    grad_upper = (grad_active * slope_ref[...].astype(f32)).astype(bf16)
    sum_ref[...] += dot_nt(grad_upper, up_ref[...]).reshape(seqs, rows, width)
    down_ref[...] = dot_tn(active_ref[...], grad).astype(bf16)
    for p, ref in enumerate((gd0, gd1, gd2, gd3)):

        @pl.when(lax.div(step, 2) == p)
        def _(ref=ref):
            block_rows = ref.shape[1]
            for q, z in enumerate(Z_ORDER):
                at = pl.multiple_of(jnp.bitwise_xor(place, z) * block_rows, block_rows)
                ref[q] = down_ref[pl.ds(at, block_rows), :]

    tile_ref[...] = dot_nn(normed_t_ref[...], grad_upper).astype(bf16)
    take_rows(me, tile_ref, UP_BITS, (gu0, gu1, gu2, gu3))


def hidden_backward_body(
    ids, glayer_ref, sum_ref, hidden_ref, heads_ref, gain_ref, gathered_out_ref,
    gres_ref, g0, g1, g2, g3, go0, go1, go2, go3, ggain_ref,
    out_w_ref, gout_ref,
):
    seqs, rows, width = hidden_ref.shape
    me = ids[4]
    place_rows(me, gathered_out_ref, DOWN_BITS, out_w_ref)
    gain = gain_ref[3:4, :].astype(f32)
    ggain = jnp.zeros((1, width), f32)
    for j in range(seqs):
        back, part = norm_back(hidden_ref[j], sum_ref[j], gain)
        ggain = ggain + part
        gres_ref[j] = (glayer_ref[j] + back).astype(bf16)
    ggain_ref[...] = ggain
    gout_ref[...] = jnp.zeros_like(gout_ref)
    for k, out in enumerate((g0, g1, g2, g3)):
        code = jnp.bitwise_xor(ids[0], k)
        features = out.shape[-1]
        at = pl.ds(pl.multiple_of(lax.rem(code, 2) * features, features), features)
        low = gres_ref[lax.div(code, 2)]
        out[...] = dot_nt(low, out_w_ref[at, :]).astype(bf16)
        gout_ref[at, :] += dot_tn(heads_ref[k], low)
    out_w_ref[...] = gout_ref[...].astype(bf16)
    take_rows(me, out_w_ref, DOWN_BITS, (go0, go1, go2, go3))


def back_body(
    prefix_ref, q_in, k_in, v_in, heads_in, lse_ref, cos_ref, rise_ref, fall_ref,
    normed_in, received_in, weight_in, far_in, gain_ref, gfirst_in, gmlp_in, gmix_in, gsecond_in, stats_in, res_in,
    gh0, gh1, gh2, gh3, gu0, gu1, gu2, gu3, gd0, gd1, gd2, gd3, go0, go1, go2, go3,
    gstreams_ref, gproj_ref, gup_ref, gdown_ref, gout_ref, near_ref, tiny_ref, late_ref,
    q_ref, k_ref, v_ref, heads_ref, g_ref, d_ref, d_got, dk_ref, dv_ref, kt_ref,
    normed_ref, received_ref, weight_ref, gn_ref, b_ref, grad_ref,
    up_keep, down_keep, up_sum, up_a, up_b, up_c, up_d, down_sum, down_a, down_b, down_c, down_d,
    down_p, down_q, down_r, down_s,
    proj_sum, proj_a, proj_b, proj_c, proj_d, proj_e, early_ref, early_y, early_x, early_core, near_got, tiny_got, late_got,
    local_sems, send_sems, recv_sems,
):
    here = Place()
    sends = Sends(here, send_sems, recv_sems)
    used = []

    def load(source, target):
        copy = pltpu.make_async_copy(source, target, local_sems.at[len(used)])
        used.append(copy)
        copy.start()
        return copy

    def ready(source, target, axis):
        copy = sends.make(sends.used, source, target, here.across(axis))
        sends.used += 1
        sends.open.append(copy)
        return copy

    def send(source, target, axis):
        copy = ready(source, target, axis)
        copy.start()
        return copy

    def add(into, first, source, count, start=0):
        def body(i):
            into[first + i] = into[first + i] + source[start + i]

        each(count, body)

    span = gfirst_in.shape[0]
    early_ref[0:span, :] = gfirst_in[...]
    early_ref[span:, :] = jnp.zeros((8, early_ref.shape[1]), f32)
    early_ref[span : span + 1, :] = gmlp_in[...]
    early_ref[span + 1 : span + 2, :] = gmix_in[...]
    tiny_ref[0:span, :] = gsecond_in[...]
    tiny_ref[span:, :] = stats_in[...]
    here.meet(("x", "y"))

    def ring(*refs):
        stages = []

        def start(axis):
            n = len(stages)
            stages.append([send(value, got.at[n], axis) for value, got in refs])

        def end():
            n = len(stages) - 1
            for copy in stages[n]:
                copy.wait()
            sends.open = [c for c in sends.open if not any(c is s for s in stages[n])]
            for value, got in refs:
                value[...] += got[n]

        return start, end

    late_start, late_end = ring((late_ref, late_got))
    near_start, near_end = ring((near_ref, near_got))
    tiny_start, tiny_end = ring((tiny_ref, tiny_got))

    column = [0]
    halvings = []

    def early_start(axis):
        tiny_start(axis)
        got = {"y": early_y, "x": early_x, "core": early_core}.get(axis)
        if got is None:
            near_start(axis)
            return
        bit = {"y": here.y, "x": here.x, "core": here.core}[axis]
        size = got.shape[1]
        give = pl.multiple_of(column[0] + (1 - bit) * size, 128)
        column[0] = column[0] + bit * size
        halvings.append((send(early_ref.at[:, pl.ds(give, size)], got, axis), got))

    def early_end():
        tiny_end()
        if not halvings:
            near_end()
            return
        copy, got = halvings.pop()
        copy.wait()
        sends.open = [c for c in sends.open if c is not copy]
        at = pl.ds(pl.multiple_of(column[0], 128), got.shape[1])
        if got is early_core:
            near_ref[...] = early_ref[:, at] + got[...]
        else:
            early_ref[:, at] += got[...]

    early_start("y")
    gs = (gh0, gh1, gh2, gh3)
    base = sends.used
    sends.used += 4
    exchange = []
    for n, g in enumerate(gs):
        device = here.out_to(n)
        stays = here.is_self(device)
        copy = sends.make(base + n, g, g_ref.at[n], device)
        own = pltpu.make_async_copy(g, g_ref.at[n], recv_sems.at[base + n])

        @pl.when(stays)
        def _(own=own):
            own.start()

        @pl.when(jnp.logical_not(stays))
        def _(copy=copy):
            copy.start()

        exchange.append((copy, stays))
    units = gd0.shape[3]
    shard = go0.shape[3]
    cut = down_a.shape[-1]
    left, right = pl.ds(0, cut), pl.ds(cut, cut)

    def down_parts(ref):
        lead = (slice(None),) * (len(ref.shape) - 2)
        return ref.at[lead + (pl.ds(0, units),)], ref.at[lead + (pl.ds(units, shard),)]

    up_come, down_come = {}, {}
    for n, u, d, o in ((1, gu3, gd3, go3), (0, gu2, gd2, go2)):
        up_come[n] = [send(u, up_sum.at[pl.ds(8 * n, 8)], "core")]
        to_d, to_o = down_parts(down_sum.at[pl.ds(2 * n, 2)])
        down_come[n] = [send(d, to_d, "core"), send(o, to_o, "core")]
    attention_loads = [
        load(a, b)
        for a, b in ((q_in, q_ref), (k_in, k_ref), (v_in, v_ref), (heads_in, heads_ref))
    ]

    def load_stream(s, slot):
        return [
            load(normed_in.at[s], normed_ref.at[slot]),
            load(received_in.at[s], received_ref.at[slot]),
            load(weight_in.at[s], weight_ref.at[slot, 0]),
            load(far_in.at[s], weight_ref.at[slot, 1]),
        ]

    own_up = {1: gu1, 0: gu0}
    own_down = {1: (gd1, go1), 0: (gd0, go0)}

    def load_up(n, half):
        return [load(own_up[n].at[pl.ds(4 * half, 4)], up_keep)]

    def load_down(n, half):
        d, o = own_down[n]
        to_d, to_o = down_parts(down_keep)
        return [load(d.at[half], to_d), load(o.at[half], to_o)]

    def add_down(place, source, lanes, lows=(0, 1)):
        for low in lows:

            def body(high):
                down_sum[place, low, high, :, lanes] += source[low, high]

            each(2, body)

    order = ((1, 1), (1, 0), (0, 1), (0, 0))
    up_load, down_load = load_up(*order[0]), load_down(*order[0])
    up_hops, down_hops = {}, {}
    everything = pl.ds(0, 2 * cut)
    for i, (n, half) in enumerate(order):
        first = 8 * n + 4 * half
        for copy in up_come.pop(n, []):
            copy.wait_recv()
        for copy in up_load:
            copy.wait()
        add(up_sum, first, up_keep, 4)
        if n == 1:
            up_hops[half] = send(up_sum.at[pl.ds(first, 4)], up_a.at[pl.ds(4 * half, 4)], "x")
        if i < 3:
            up_load = load_up(*order[i + 1])
        for copy in down_come.pop(n, []):
            copy.wait_recv()
        for copy in down_load:
            copy.wait()
        add_down(2 * n + half, down_keep, everything)
        if n == 1:
            down_hops[half] = send(
                down_sum.at[2 + half, :, :, :, right], down_a.at[half], "y"
            )
        if i < 3:
            down_load = load_down(*order[i + 1])
        if i < 2:
            early_end()
            early_start(("x", "core")[i])
    early_end()
    early_start("zl")
    down_zl = {
        high: send(down_sum.at[:, 1, high, :, left], down_p.at[high], "zl") for high in (1, 0)
    }
    streams_loads = {2: load_stream(2, 0), 1: load_stream(1, 1)}
    res_copy = load(res_in, gstreams_ref.at[3])

    _, blocks, piece, width = q_ref.shape
    rows = 2 * piece
    half_rows = blocks * piece
    length = 2 * half_rows
    lane = lax.broadcasted_iota(jnp.int32, (rows, 128), 1)
    key_index = key_positions(length, blocks, 0)
    choose = (
        lax.div(lax.broadcasted_iota(jnp.int32, (8, 128), 1), 64)
        == lax.broadcasted_iota(jnp.int32, (8, 128), 0)
    ).astype(f32)

    def unturn(x, tables):
        return (
            x * tables[0]
            - pltpu.roll(x, ROT // 2, 1) * tables[1]
            - pltpu.roll(x, 128 - ROT // 2, 1) * tables[2]
        )

    rotary = (cos_ref, rise_ref, fall_ref)
    for copy in attention_loads:
        copy.wait()
    for copy, _ in exchange:
        copy.wait_recv()

    up_y = ready(up_sum.at[pl.ds(4, 4)], up_b, "y")
    down_x = ready(down_sum.at[1, :, :, :, right], down_b, "x")
    down_zh = ready(down_sum.at[:, 0, 1, :, left], down_q, "zh")

    def add_left(high, source):
        def body(place):
            down_sum[place, 0, high, :, left] += source[place]

        each(4, body)

    def hook_0():
        down_hops[1].wait_recv()
        add_down(1, down_a.at[1], right)
        down_x.start()
        up_hops[1].wait_recv()
        add(up_sum, 4, up_a, 4, 4)
        up_y.start()

    def hook_1():
        down_zl[1].wait_recv()
        add_left(1, down_p.at[1])
        down_zh.start()

    def hook_2():
        down_hops[0].wait_recv()
        add_down(0, down_a.at[0], right)

    hooks = (hook_0, hook_1, hook_2)

    def one_pair(pair):
        at = pl.ds(pl.multiple_of(pair * 128, 128), 128)
        dk_ref[...] = jnp.zeros_like(dk_ref)
        dv_ref[...] = jnp.zeros_like(dv_ref)
        keys = k_ref[:, :, :, at].reshape(length, 128)
        values = v_ref[:, :, :, at].reshape(length, 128)
        kt_ref[...] = keys.T

        def one_block(k):
            block = here.block(k)
            queries = q_ref[:, block, :, at].reshape(rows, 128)
            grads = g_ref[k, :, at]
            inner_rows = dot_nt(
                choose, grads.astype(f32) * heads_ref[block, :, at].astype(f32), highest
            )
            allowed = key_index <= allowed_limit(block * rows, rows, prefix_ref[0:1, 0:1], 1)
            dqt = []
            for h in range(2):
                chosen = (lane < 64) if h == 0 else (lane >= 64)
                q_h = jnp.where(chosen, queries, jnp.zeros_like(queries))
                g_h = jnp.where(chosen, grads, jnp.zeros_like(grads))
                scores = dot_nt(keys, q_h)
                probs = jnp.where(allowed, jnp.exp(scores - lse_ref[block, pl.ds(pair * 2 + h, 1), :]), 0.0)
                grad_probs = dot_nt(values, g_h)
                grad_scores = (probs * (grad_probs - inner_rows[h : h + 1, :])).astype(bf16)
                dv_ref[...] += dot_nn(probs.astype(bf16), g_h)
                dk_ref[...] += dot_nn(grad_scores, q_h)
                dqt.append(dot_nn(kt_ref[...], grad_scores)[h * 64 : h * 64 + 64, :])
            dq = jnp.concatenate(dqt, axis=0).T * (HEAD_DIM**-0.5)
            dq = unturn(dq, [r[:, block].reshape(rows, 128) for r in rotary])
            d_ref[0, :, block, :, at] = dq.astype(bf16).reshape(2, piece, 128)

        each(4, one_block)
        dk = unturn(dk_ref[...], [r[...].reshape(length, 128) for r in rotary])
        d_ref[1, :, :, :, at] = dk.astype(bf16).reshape(2, blocks, piece, 128)
        d_ref[2, :, :, :, at] = dv_ref[...].astype(bf16).reshape(2, blocks, piece, 128)
        for i, hook in enumerate(hooks):
            pl.when(pair == i)(hook)

    each(4, one_pair)

    far_half = 1 - here.core
    d_hops = {s: send(d_ref.at[s, far_half], d_got.at[s], "core") for s in (2, 1, 0)}
    early_end()
    early_start("zh")
    late_ref[...] = jnp.zeros_like(late_ref)
    back = {}

    def mine():
        return here.z_low * 2 + here.core

    def one_stream(s, slot):
        for copy in streams_loads[s]:
            copy.wait()
        d_hops[s].wait_recv()
        near = d_ref[s, here.core].reshape(half_rows, width)
        gn = dot_nt(near, weight_ref[slot, 0])
        gn = gn + dot_nt(d_got[s].reshape(half_rows, width), weight_ref[slot, 1])
        gn_ref[...] = gn.reshape(gn_ref.shape)
        gain = gain_ref[s : s + 1, :]

        def step(k):
            block = here.block(k)
            grad, part = norm_back(received_ref[slot, k].astype(f32), gn_ref[block], gain)
            b_ref[s, k] = grad.astype(bf16)
            late_ref[s : s + 1, :] += part

        each(4, step)

    def send_stream(s):
        steps = sends.four(
            lambda k: b_ref.at[s, k], lambda k: gstreams_ref.at[s, mine()], here.back_to
        )
        each(4, steps[0])
        back[s] = steps

    def project_back(s, slot):
        grad = dot_tn(
            normed_ref[slot, 0].reshape(half_rows, -1), d_ref[s, 0].reshape(half_rows, width)
        )
        grad = grad + dot_tn(
            normed_ref[slot, 1].reshape(half_rows, -1), d_ref[s, 1].reshape(half_rows, width)
        )
        grad_ref[...] = grad.astype(bf16)
        for x in range(2):
            for y in range(2):
                for q, z in enumerate(Z_ORDER):
                    for core in range(2):
                        at = pl.multiple_of(here.device(y, x, core, z) * shard, shard)
                        proj_sum[(x * 2 + y) * 4 + q, core, s] = grad_ref[pl.ds(at, shard), :]

    def settle_left():
        down_zl[0].wait_recv()
        add_left(0, down_p.at[0])

    def give_down(lanes, other):
        value = down_sum[0, 0, 0, :, lanes].astype(f32) + other[...].astype(f32)
        gdown_ref[:, lanes] = value[:units]
        gout_ref[:, lanes] = value[units:]

    one_stream(2, 0)
    send_stream(2)
    project_back(2, 0)
    streams_loads[0] = load_stream(0, 0)
    up_hops[0].wait_recv()
    add(up_sum, 0, up_a, 4)
    settle_left()
    one_stream(1, 1)
    early_end()
    up_y.wait_recv()
    add(up_sum, 0, up_b, 4)
    up_zl = send(up_sum.at[pl.ds(2, 2)], up_c, "zl")
    send_stream(1)
    project_back(1, 1)
    one_stream(0, 0)
    project_back(0, 0)
    proj_hops = {}
    for half in (1, 0):
        proj_hops[half] = send(
            proj_sum.at[pl.ds(8 + 4 * half, 4)], proj_a.at[pl.ds(4 * half, 4)], "x"
        )
    late_start("core")
    down_x.wait_recv()
    add_down(0, down_b, right)
    down_low = send(down_sum.at[0, 1, :, :, right], down_c, "zl")
    late_end()
    late_start("y")
    down_zh.wait_recv()
    add_left(0, down_q)
    left_y = send(down_sum.at[pl.ds(2, 2), 0, 0, :, left], down_r, "y")
    late_end()
    late_start("x")
    up_zl.wait_recv()
    add(up_sum, 0, up_c, 2)
    up_zh = send(up_sum.at[pl.ds(1, 1)], up_d, "zh")
    send_stream(0)
    left_y.wait_recv()
    for place in range(2):
        down_sum[place, 0, 0, :, left] += down_r[place]
    left_x = send(down_sum.at[1, 0, 0, :, left], down_s, "x")
    proj_hops[1].wait_recv()
    add(proj_sum, 4, proj_a, 4, 4)
    proj_y = send(proj_sum.at[pl.ds(4, 4)], proj_b, "y")
    late_end()
    late_start("zl")
    proj_hops[0].wait_recv()
    add(proj_sum, 0, proj_a, 4)
    proj_y.wait_recv()
    add(proj_sum, 0, proj_b, 4)
    proj_zl = send(proj_sum.at[pl.ds(2, 2)], proj_c, "zl")
    left_x.wait_recv()
    give_down(left, down_s)
    down_low.wait_recv()
    for high in range(2):
        down_sum[0, 0, high, :, right] += down_c[high]
    down_high = send(down_sum.at[0, 0, 1, :, right], down_d, "zh")
    up_zh.wait_recv()
    gup_ref[...] = up_sum[0].astype(f32) + up_d[0].astype(f32)
    late_end()
    late_start("zh")
    proj_zl.wait_recv()
    add(proj_sum, 0, proj_c, 2)
    proj_zh = send(proj_sum.at[pl.ds(1, 1)], proj_d, "zh")
    down_high.wait_recv()
    give_down(right, down_d)
    late_end()
    proj_zh.wait_recv()
    add(proj_sum, 0, proj_d, 1)
    proj_core = send(proj_sum.at[0, 1], proj_e, "core")
    for which, source in ((here.core, proj_sum.at[0, 0]), (1 - here.core, proj_e)):
        if source is proj_e:
            proj_core.wait_recv()
        at = pl.ds(pl.multiple_of(which * width, width), width)
        gproj_ref[:, :, at] = source[...].astype(f32)
    for s in range(3):
        each(4, back[s][2])
        each(4, back[s][1])
    for copy, stays in exchange:

        @pl.when(jnp.logical_not(stays))
        def _(copy=copy):
            copy.wait_send()

    res_copy.wait()
    sends.finish()


def finish_body(
    me_ref, streams_ref, proj_ref, up_ref, down_ref, out_ref, early_ref, tiny_ref, late_ref, small_ref,
    streams_out, proj_out, up_out, down_out, out_out, first_out, second_out, bias_out, gains_out, loss_out,
):
    streams_out[...] = streams_ref[...]

    @pl.when(pl.program_id(0) == 0)
    def _():
        for source, target in (
            (proj_ref, proj_out),
            (up_ref, up_out),
            (down_ref, down_out),
            (out_ref, out_out),
        ):
            target[...] = source[...]
        shard, mixw = first_out.shape
        width = late_ref.shape[1]
        near = early_ref.shape[1]
        span = tiny_ref.shape[1]

        def chosen(size, first):
            column = lax.broadcasted_iota(jnp.int32, (shard, size), 1)
            row = lax.broadcasted_iota(jnp.int32, (shard, size), 0)
            return (column == row + first).astype(f32)

        mine = chosen(near, lax.rem(me_ref[0] * shard, near))
        first_out[...] = dot_nt(mine, early_ref[...], highest)[:, 0:mixw]
        gains_out[3:5, :] = dot_nt(early_ref[span : span + 8, :], mine, highest)[0:2]
        gains_out[0:3, :] = dot_nt(late_ref[...], chosen(width, me_ref[0] * shard), highest)[0:3]
        second_out[...] = tiny_ref[0:mixw, 0:mixw]
        bias_out[...] = tiny_ref[span : span + 1, 0:mixw]
        loss_out[...] = tiny_ref[span + 1 : span + 2, 0:1] / (4.0 * width * small_ref[7:8, 0:1])


def rotary_lanes(length, piece):
    lane = jnp.arange(128, dtype=jnp.int32) % HEAD_DIM
    step = (lane % (ROT // 2)).astype(f32)
    inverse = jnp.exp(step * (-2.0 * math.log(10000.0) / ROT))
    angles = jnp.arange(length, dtype=jnp.int32).astype(f32)[:, None] * inverse[None, :]
    cosine = jnp.where(lane < ROT, jnp.cos(angles), 1.0)
    sine = jnp.sin(angles)
    up = jnp.where((lane >= ROT // 2) & (lane < ROT), sine, 0.0)
    down = jnp.where(lane < ROT // 2, -sine, 0.0)
    return [
        t.reshape(-1, 2, piece, 128).transpose(1, 0, 2, 3) for t in (cosine, up, down)
    ]


def local_fast(
    streams, history, teacher, prefix, valid_mask, loss_scale, projections, attention_out,
    up_weight, down_weight, mixer_first, mixer_second, mixer_bias, gains,
):
    lines = lax.axis_size("ctx")
    count = lax.axis_size("dp") * lines
    place = lax.axis_index("ctx")
    group = lax.axis_index("dp")
    me = group * lines + place
    half = group % 2
    mine = 2 * (place % 2) + half
    seqs, rows, width = streams.shape[1:]
    tokens = seqs * rows
    piece = rows // 2
    length = rows * lines
    features = width // 2
    hidden_units = down_weight.shape[0] * count
    past = history.shape[0]
    count_of_streams = teacher.shape[0]
    mixw = mixer_bias.shape[0]
    span = 64

    ids = jnp.stack([place, half, mine, mine, me]).astype(jnp.int32)
    shard = width // count
    unit_shard = hidden_units // count

    smem = pl.BlockSpec(memory_space=pltpu.SMEM)
    anywhere = pl.BlockSpec(memory_space=pl.ANY)
    proj_shape = (count // 2, 2, 3, shard, features)
    tables = rotary_lanes(length, piece)
    row_shape = (3, 4, piece, width)
    normed_shape = (3, 2, lines, piece, width)
    wide_shape = (2, lines, piece, features)
    heads_shape = (lines, rows, features)

    def array(shape, dtype=bf16):
        return jax.ShapeDtypeStruct(shape, dtype)

    (
        received, normed, proj, proj_other, up_all, down_all, small, first_t, prefix_rows,
        queries, keys, values, heads_seq, lse, heads,
    ) = pl.pallas_call(
        front_body,
        in_specs=[smem, anywhere] + [vmem()] * 10,
        out_specs=[anywhere] * 6 + [vmem()] * 3 + [anywhere] * 4 + [vmem(), anywhere],
        out_shape=[
            array(row_shape),
            array(normed_shape),
            array((3, width, features)),
            array((3, width, features)),
            array((count, shard, hidden_units)),
            array((count, unit_shard + shard, width)),
            array((8, width), f32),
            array((span, width)),
            array((8, 128), jnp.int32),
            array(wide_shape),
            array(wide_shape),
            array(wide_shape),
            array(heads_shape),
            array((lines, 8, rows), f32),
            array((4, rows, features)),
        ],
        scratch_shapes=[
            pltpu.VMEM(row_shape, bf16),
            pltpu.VMEM(normed_shape, bf16),
            pltpu.VMEM(proj_shape, bf16),
            pltpu.VMEM((3, width, features), bf16),
            pltpu.VMEM(wide_shape, bf16),
            pltpu.VMEM(wide_shape, bf16),
            pltpu.VMEM(wide_shape, bf16),
            pltpu.VMEM(heads_shape, bf16),
            pltpu.VMEM((5, 8, width), f32),
            pltpu.VMEM((5, span, width), bf16),
            pltpu.VMEM((8, 128), jnp.int32),
            pltpu.VMEM((8, 128), jnp.int32),
            pltpu.SemaphoreType.DMA((24,)),
            pltpu.SemaphoreType.DMA((112,)),
            pltpu.SemaphoreType.DMA((112,)),
        ],
        compiler_params=params(collective_id=0, has_side_effects=True),
        name="front",
    )(
        prefix,
        streams.reshape(streams.shape[0], 2 * seqs, piece, width),
        projections, up_weight, down_weight, attention_out, gains, mixer_first, valid_mask, *tables,
    )
    gain_full = small
    tile = 512
    tiles = hidden_units // tile
    token_shape = (seqs, rows, width)

    def fixed(shape, index=None):
        index = index or (0,) * len(shape)
        return pl.BlockSpec(shape, lambda i, *_: index)

    def up_column(i, ids):
        distance = lax.rem(lax.div(i, 2), 2) * 4 + lax.rem(i, 2) * 2 + lax.div(i, 4)
        return (0, 0, jnp.bitwise_xor(lax.div(ids[4], 4), distance))

    def down_block(p):
        return lambda i, *_: (jnp.clip(i - 2 * p, 0, 1), 0, 0)

    weight_specs = [
        pl.BlockSpec((count, shard, tile), up_column),
        pl.BlockSpec((4, unit_shard, width), lambda i, *_: (i, 0, 0)),
    ]
    out_weight_spec = pl.BlockSpec(
        (count, shard, width), lambda i, *_: (0, unit_shard // shard, 0)
    )
    tile_specs = [pl.BlockSpec((8, shard, tile), up_column)] * 4
    tile_specs += [pl.BlockSpec((4, unit_shard, width), down_block(p)) for p in range(4)]

    hidden, normed_mlp, active, slope, layer_out = pl.pallas_call(
        mlp_forward_body,
        grid_spec=pltpu.PrefetchScalarGridSpec(
            num_scalar_prefetch=1,
            grid=(tiles,),
            in_specs=[
                fixed((4, rows, features)),
                fixed((1,) + token_shape, (3, 0, 0, 0)),
                fixed((8, width)),
            ]
            + weight_specs
            + [out_weight_spec],
            out_specs=[
                fixed(token_shape),
                fixed(token_shape),
                pl.BlockSpec((tokens, tile), lambda i, *_: (0, i)),
                pl.BlockSpec((tokens, tile), lambda i, *_: (0, i)),
                fixed(token_shape),
            ],
            scratch_shapes=[
                pltpu.VMEM((width, width), bf16),
                pltpu.VMEM((width, tile), bf16),
                pltpu.VMEM((tile, width), bf16),
            ],
        ),
        out_shape=[
            jax.ShapeDtypeStruct(token_shape, f32),
            jax.ShapeDtypeStruct(token_shape, bf16),
            jax.ShapeDtypeStruct((tokens, hidden_units), bf16),
            jax.ShapeDtypeStruct((tokens, hidden_units), bf16),
            jax.ShapeDtypeStruct(token_shape, f32),
        ],
        compiler_params=params(),
        name="mlp_forward",
    )(ids, heads, streams, gain_full, up_all, down_all, down_all)

    block = 128
    next_streams, grad_history, grad_layer, g_first, g_second, stats, g_gain_mix = pl.pallas_call(
        mixer_body,
        grid=(tokens // block,),
        in_specs=[
            smem,
            pl.BlockSpec((block, width), lambda i: (i, 0)),
            pl.BlockSpec((past, block, width), lambda i: (0, i, 0)),
            pl.BlockSpec((count_of_streams, block, width), lambda i: (0, i, 0)),
            pl.BlockSpec((1, 1, block), lambda i: (i, 0, 0)),
            fixed((8, width)),
            fixed((span, width)),
            fixed((mixw, mixw)),
            fixed((1, mixw)),
        ],
        out_specs=[
            pl.BlockSpec((count_of_streams, block, width), lambda i: (0, i, 0)),
            pl.BlockSpec((past, block, width), lambda i: (0, i, 0)),
            pl.BlockSpec((block, width), lambda i: (i, 0)),
            fixed((span, width)),
            fixed((span, span)),
            fixed((8, span)),
            fixed((1, width)),
        ],
        out_shape=[
            jax.ShapeDtypeStruct((count_of_streams, tokens, width), bf16),
            jax.ShapeDtypeStruct((past, tokens, width), bf16),
            jax.ShapeDtypeStruct((tokens, width), f32),
            jax.ShapeDtypeStruct((span, width), f32),
            jax.ShapeDtypeStruct((span, span), f32),
            jax.ShapeDtypeStruct((8, span), f32),
            jax.ShapeDtypeStruct((1, width), f32),
        ],
        scratch_shapes=[
            pltpu.VMEM((mixw, block, 128), f32),
            pltpu.VMEM((mixw, block, 128), f32),
            pltpu.VMEM((count_of_streams, block, width), f32),
            pltpu.VMEM((block, 1), f32),
            pltpu.VMEM((span, span), f32),
            pltpu.VMEM((1, span), f32),
        ],
        compiler_params=params(),
        name="mixer",
    )(
        loss_scale,
        layer_out.reshape(tokens, width),
        history.reshape(past, tokens, width),
        teacher.reshape(count_of_streams, tokens, width),
        valid_mask.reshape(-1, 1, block),
        gain_full,
        first_t,
        mixer_second,
        mixer_bias.reshape(1, mixw),
    )

    *g_ups, gd0, gd1, gd2, gd3, g_normed = pl.pallas_call(
        mlp_backward_body,
        grid_spec=pltpu.PrefetchScalarGridSpec(
            num_scalar_prefetch=1,
            grid=(tiles,),
            in_specs=[
                fixed(token_shape),
                pl.BlockSpec((tokens, tile), lambda i, *_: (0, i)),
                pl.BlockSpec((tokens, tile), lambda i, *_: (0, i)),
                fixed(token_shape),
            ]
            + weight_specs,
            out_specs=tile_specs + [fixed(token_shape)],
            scratch_shapes=[
                pltpu.VMEM(token_shape, bf16),
                pltpu.VMEM((width, tokens), bf16),
                pltpu.VMEM((width, tile), bf16),
                pltpu.VMEM((tile, width), bf16),
                pltpu.VMEM((width, tile), bf16),
            ],
        ),
        out_shape=[jax.ShapeDtypeStruct((8, shard, hidden_units), bf16)] * 4
        + [jax.ShapeDtypeStruct((8, unit_shard, width), bf16)] * 4
        + [jax.ShapeDtypeStruct(token_shape, f32)],
        compiler_params=params(),
        name="mlp_backward",
    )(ids, grad_layer.reshape(token_shape), active, slope, normed_mlp, up_all, down_all)
    g_downs = [gd0, gd1, gd2, gd3]

    hidden_results = pl.pallas_call(
        hidden_backward_body,
        grid_spec=pltpu.PrefetchScalarGridSpec(
            num_scalar_prefetch=1,
            grid=(1,),
            in_specs=[fixed(token_shape)] * 3
            + [fixed((4, rows, features)), fixed((8, width)), out_weight_spec],
            out_specs=[fixed(token_shape)]
            + [fixed((rows, features))] * 4
            + [fixed((8, shard, width))] * 4
            + [fixed((1, width))],
            scratch_shapes=[pltpu.VMEM((width, width), bf16), pltpu.VMEM((width, width), f32)],
        ),
        out_shape=[jax.ShapeDtypeStruct(token_shape, bf16)]
        + [jax.ShapeDtypeStruct((rows, features), bf16)] * 4
        + [jax.ShapeDtypeStruct((8, shard, width), bf16)] * 4
        + [jax.ShapeDtypeStruct((1, width), f32)],
        compiler_params=params(),
        name="hidden_backward",
    )(ids, grad_layer.reshape(token_shape), g_normed, hidden, heads, gain_full, down_all)
    g_res, gh0, gh1, gh2, gh3, go0, go1, go2, go3, g_gain_mlp = hidden_results

    down_block_shape = (unit_shard + shard, width)
    down_half = (unit_shard + shard, width // 2)
    slot_shape = (2, lines, piece, width)

    def buffer(shape, dtype=bf16):
        return pltpu.VMEM(shape, dtype)

    grad_streams, grad_projections, sum_up, sum_down, sum_out, early, tiny, late = pl.pallas_call(
        back_body,
        in_specs=[vmem()]
        + [anywhere] * 4
        + [vmem()] * 4
        + [anywhere] * 4
        + [vmem()] * 6
        + [anywhere] * 17,
        out_specs=[anywhere] + [vmem()] * 7,
        out_shape=[
            array((streams.shape[0], 2 * seqs, piece, width)),
            array((3, shard, width), f32),
            array((shard, hidden_units), f32),
            array((unit_shard, width), f32),
            array((shard, width), f32),
            array((span + 8, width // 8), f32),
            array((span + 8, span), f32),
            array((8, width), f32),
        ],
        scratch_shapes=[
            buffer(wide_shape),
            buffer(wide_shape),
            buffer(wide_shape),
            buffer(heads_shape),
            buffer((4, rows, features)),
            buffer((3,) + wide_shape),
            buffer((3,) + wide_shape[1:]),
            buffer((length, 128), f32),
            buffer((length, 128), f32),
            buffer((128, length)),
            buffer((2,) + slot_shape),
            buffer((2,) + row_shape[1:]),
            buffer((2, 2, width, features)),
            buffer((lines, piece, width), f32),
            buffer(row_shape),
            buffer((width, features)),
            buffer((4, shard, hidden_units)),
            buffer((2, 2) + down_block_shape),
            buffer((16, shard, hidden_units)),
            buffer((8, shard, hidden_units)),
            buffer((4, shard, hidden_units)),
            buffer((2, shard, hidden_units)),
            buffer((1, shard, hidden_units)),
            buffer((4, 2, 2) + down_block_shape),
            buffer((2, 2, 2) + down_half),
            buffer((2, 2) + down_half),
            buffer((2,) + down_half),
            buffer(down_half),
            buffer((2, 4) + down_half),
            buffer((4,) + down_half),
            buffer((2,) + down_half),
            buffer(down_half),
            buffer(proj_shape),
            buffer((8,) + proj_shape[1:]),
            buffer((4,) + proj_shape[1:]),
            buffer((2,) + proj_shape[1:]),
            buffer((1,) + proj_shape[1:]),
            buffer(proj_shape[2:]),
            buffer((span + 8, width), f32),
            buffer((span + 8, width // 2), f32),
            buffer((span + 8, width // 4), f32),
            buffer((span + 8, width // 8), f32),
            buffer((2, span + 8, width // 8), f32),
            buffer((5, span + 8, span), f32),
            buffer((5, 8, width), f32),
            pltpu.SemaphoreType.DMA((40,)),
            pltpu.SemaphoreType.DMA((64,)),
            pltpu.SemaphoreType.DMA((64,)),
        ],
        compiler_params=pltpu.CompilerParams(
            vmem_limit_bytes=63 * 1024 * 1024, collective_id=1, has_side_effects=True
        ),
        name="back",
    )(
        prefix_rows,
        queries, keys, values, heads_seq,
        lse,
        *tables,
        normed, received, proj, proj_other, gain_full, g_first, g_gain_mlp, g_gain_mix, g_second, stats,
        g_res.reshape(2 * seqs, piece, width),
        gh0, gh1, gh2, gh3, *g_ups,
        *[g.reshape(2, 2, 2, -1, width) for g in (*g_downs, go0, go1, go2, go3)],
    )
    quarters = 2 * seqs
    stream_block = pl.BlockSpec((1, quarters // 2, piece, width), lambda i: (i // 2, i % 2, 0, 0))
    whole_shapes = [
        ((3, shard, width), f32),
        ((shard, hidden_units), f32),
        ((unit_shard, width), f32),
        ((shard, width), f32),
    ]
    small_shapes = [((shard, mixw), f32), ((mixw, mixw), f32), ((1, mixw), f32), ((5, shard), f32), ((1, 1), f32)]
    (
        grad_streams, grad_projections, sum_up, sum_down, sum_out,
        grad_first, grad_second, grad_bias, grad_gains, mean_loss,
    ) = pl.pallas_call(
        finish_body,
        grid=(2 * streams.shape[0],),
        in_specs=[smem, stream_block]
        + [fixed(s) for s, _ in whole_shapes]
        + [
            fixed((span + 8, width // 8)),
            fixed((span + 8, span)),
            fixed((8, width)),
            fixed((8, width)),
        ],
        out_specs=[stream_block] + [fixed(s) for s, _ in whole_shapes + small_shapes],
        out_shape=[array((streams.shape[0], quarters, piece, width))]
        + [array(*s) for s in whole_shapes + small_shapes],
        compiler_params=params(),
        name="finish",
    )(
        me.reshape(1).astype(jnp.int32),
        grad_streams, grad_projections, sum_up, sum_down, sum_out, early, tiny, late, small,
    )
    return (
        next_streams.reshape(teacher.shape),
        mean_loss.reshape(()),
        grad_streams.reshape(streams.shape),
        grad_history.reshape(history.shape),
        grad_projections,
        sum_out,
        sum_up,
        sum_down,
        grad_first,
        grad_second,
        grad_bias.reshape(mixw),
        grad_gains,
    )


def layer_norm(values, gain_row):
    centered = values - jnp.mean(values, axis=-1, keepdims=True)
    return (
        centered
        * lax.rsqrt(jnp.mean(centered * centered, axis=-1, keepdims=True) + epsilon)
        * gain_row
    )


def rms_norm(values, gain_row):
    return (
        values * lax.rsqrt(jnp.mean(values * values, axis=-1, keepdims=True) + epsilon) * gain_row
    )


def gelu_exact(values):
    return jax.nn.gelu(values, approximate=False)


def rotary_tables(positions):
    frequency_steps = jnp.arange(ROT // 2).astype(positions.dtype)
    inverse = jnp.exp(frequency_steps * (-2.0 * math.log(10000.0) / ROT))
    angles = positions[:, None] * inverse[None, :]
    return (jnp.cos(angles)[:, None, :], jnp.sin(angles)[:, None, :])


def rotate(values, cosine_table, sine_table, direction):
    row_count = values.shape[0]
    shaped = values.reshape(row_count, HEADS, HEAD_DIM)
    half_rot = ROT // 2
    first_half = shaped[:, :, :half_rot]
    second_half = shaped[:, :, half_rot:ROT]
    remainder = shaped[:, :, ROT:]
    turned_first = first_half * cosine_table - direction * second_half * sine_table
    turned_second = second_half * cosine_table + direction * first_half * sine_table
    return jnp.concatenate([turned_first, turned_second, remainder], axis=-1).reshape(row_count, -1)


def masked_scores(query_heads, key_heads, query_index, key_index, prefix_len):
    scores = jnp.einsum(
        "qhd,khd->hqk", query_heads, key_heads, preferred_element_type=jnp.float32
    ) * HEAD_DIM ** (-0.5)
    allowed = (key_index[None, :] <= query_index[:, None]) | (key_index[None, :] < prefix_len)
    return jnp.where(allowed[None], scores, -1e30)


def local_plain(
    streams,
    history,
    teacher,
    prefix,
    valid_mask,
    loss_scale,
    projections,
    attention_out,
    up_weight,
    down_weight,
    mixer_first,
    mixer_second,
    mixer_bias,
    gains,
):
    micro_count = streams.shape[1]
    row_count = streams.shape[2]
    model_width = streams.shape[3]
    length = row_count * lax.axis_size("ctx")
    query_index = lax.axis_index("ctx") * row_count + jnp.arange(row_count, dtype=jnp.int32)
    key_index = jnp.arange(length, dtype=jnp.int32)
    cosine_table, sine_table = rotary_tables(query_index.astype(jnp.float32))
    score_scale = HEAD_DIM ** (-0.5)
    valid_float = valid_mask.astype(jnp.float32)
    token_total = lax.psum(jnp.sum(valid_float), ("dp", "ctx"))
    factor = loss_scale[0] * 2.0 / (4.0 * model_width * token_total)

    def one_batch(totals, number):
        (
            kept_projections,
            kept_attention,
            kept_gains,
            kept_up,
            kept_down,
            kept_first,
            kept_second,
            kept_bias,
            kept_loss,
        ) = totals
        stream_block = lax.dynamic_index_in_dim(streams, number, 1, keepdims=False)
        past_outputs = lax.dynamic_index_in_dim(history, number, 1, keepdims=False)
        target = lax.dynamic_index_in_dim(teacher, number, 1, keepdims=False).astype(jnp.float32)
        prefix_len = lax.dynamic_index_in_dim(prefix, number, 0, keepdims=False)
        valid_row = lax.dynamic_index_in_dim(valid_float, number, 0, keepdims=False)
        proj_full, out_full, gain_low, up_full, down_full, first_full = (
            lax.all_gather(projections, ("dp", "ctx"), axis=1, tiled=True),
            lax.all_gather(attention_out, ("dp", "ctx"), axis=0, tiled=True),
            lax.all_gather(gains, ("dp", "ctx"), axis=1, tiled=True),
            lax.all_gather(up_weight, ("dp", "ctx"), axis=0, tiled=True),
            lax.all_gather(down_weight, ("dp", "ctx"), axis=0, tiled=True),
            lax.all_gather(mixer_first, ("dp", "ctx"), axis=0, tiled=True),
        )
        gain_full = gain_low.astype(jnp.float32)
        inputs = stream_block.astype(jnp.float32)
        gain_three = gain_full[:3, None, :]
        normed_low = layer_norm(inputs[:3], gain_three).astype(jnp.bfloat16)
        projected = jnp.einsum(
            "std,sde->ste", normed_low, proj_full, preferred_element_type=jnp.float32
        )
        query_heads = (
            rotate(projected[0], cosine_table, sine_table, 1.0)
            .astype(jnp.bfloat16)
            .reshape(row_count, HEADS, HEAD_DIM)
        )
        key_low = rotate(projected[1], cosine_table, sine_table, 1.0).astype(jnp.bfloat16)
        value_low = projected[2].astype(jnp.bfloat16)
        all_keys, all_values = (
            lax.all_gather(key_low, "ctx", axis=0, tiled=True),
            lax.all_gather(value_low, "ctx", axis=0, tiled=True),
        )
        key_heads = all_keys.reshape(length, HEADS, HEAD_DIM)
        value_heads = all_values.reshape(length, HEADS, HEAD_DIM)
        scores = masked_scores(query_heads, key_heads, query_index, key_index, prefix_len)
        row_max = jnp.max(scores, axis=-1, keepdims=True)
        log_total = row_max + jnp.log(jnp.sum(jnp.exp(scores - row_max), axis=-1, keepdims=True))
        probs_low = jnp.exp(scores - log_total).astype(jnp.bfloat16)
        heads_low = (
            jnp.einsum("hqk,khd->qhd", probs_low, value_heads, preferred_element_type=jnp.float32)
            .reshape(row_count, model_width)
            .astype(jnp.bfloat16)
        )
        hidden = inputs[3] + jnp.dot(heads_low, out_full, preferred_element_type=jnp.float32)
        normed_mlp = layer_norm(hidden, gain_full[3]).astype(jnp.bfloat16)
        upper = jnp.dot(normed_mlp, up_full, preferred_element_type=jnp.float32)
        activated = gelu_exact(upper).astype(jnp.bfloat16)
        layer_out = hidden + jnp.dot(activated, down_full, preferred_element_type=jnp.float32)
        normed_mix = rms_norm(layer_out, gain_full[4]).astype(jnp.bfloat16)
        mix_hidden = jnp.dot(normed_mix, first_full, preferred_element_type=jnp.float32)
        mix_active = gelu_exact(mix_hidden)
        coeff = jnp.dot(mix_active, mixer_second, precision=highest) + mixer_bias
        coeff_grid = coeff.reshape(row_count, 4, -1)
        outputs_all = jnp.concatenate([past_outputs.astype(jnp.float32), layer_out[None]], axis=0)
        next_block = jnp.einsum("tsj,jtd->std", coeff_grid, outputs_all, precision=highest)
        difference = next_block - target
        loss_part = jnp.sum(jnp.sum(difference * difference, axis=(0, 2)) * valid_row) / (
            4.0 * model_width * token_total
        )
        grad_next = factor * valid_row[None, :, None] * difference
        grad_coeff = jnp.einsum("std,jtd->tsj", grad_next, outputs_all, precision=highest).reshape(
            row_count, -1
        )
        grad_outputs = jnp.einsum("tsj,std->jtd", coeff_grid, grad_next, precision=highest)
        grad_past = grad_outputs[:-1].astype(jnp.bfloat16)
        grad_second = jnp.dot(mix_active.T, grad_coeff, precision=highest)
        grad_bias = jnp.sum(grad_coeff, axis=0)
        grad_active = jnp.dot(grad_coeff, mixer_second.T, precision=highest)
        gelu_mix_back = jax.vjp(gelu_exact, mix_hidden)[1]
        grad_mix = gelu_mix_back(grad_active)[0].astype(jnp.bfloat16)
        grad_first = jnp.einsum(
            "td,tm->dm", normed_mix, grad_mix, preferred_element_type=jnp.float32
        )
        grad_normed_mix = jnp.einsum(
            "tm,dm->td", grad_mix, first_full, preferred_element_type=jnp.float32
        )
        rms_back = jax.vjp(rms_norm, layer_out, gain_full[4])[1]
        grad_layer_mix, grad_gain_mix = rms_back(grad_normed_mix)
        grad_layer = grad_outputs[-1] + grad_layer_mix
        grad_branch = grad_layer.astype(jnp.bfloat16)
        grad_down = jnp.einsum(
            "tf,td->fd", activated, grad_branch, preferred_element_type=jnp.float32
        )
        grad_active_up = jnp.einsum(
            "td,fd->tf", grad_branch, down_full, preferred_element_type=jnp.float32
        )
        gelu_up_back = jax.vjp(gelu_exact, upper)[1]
        grad_upper = gelu_up_back(grad_active_up)[0].astype(jnp.bfloat16)
        grad_up = jnp.einsum(
            "td,tf->df", normed_mlp, grad_upper, preferred_element_type=jnp.float32
        )
        grad_normed_mlp = jnp.einsum(
            "tf,df->td", grad_upper, up_full, preferred_element_type=jnp.float32
        )
        down_shard, first_shard, up_shard = (
            lax.psum_scatter(grad_down, ("dp", "ctx"), scatter_dimension=0, tiled=True),
            lax.psum_scatter(grad_first, ("dp", "ctx"), scatter_dimension=0, tiled=True),
            lax.psum_scatter(grad_up, ("dp", "ctx"), scatter_dimension=0, tiled=True),
        )
        down_next = kept_down + down_shard
        norm_mlp_back = jax.vjp(layer_norm, hidden, gain_full[3])[1]
        grad_hidden_mlp, grad_gain_mlp = norm_mlp_back(grad_normed_mlp)
        grad_hidden = grad_layer + grad_hidden_mlp
        grad_attn = grad_hidden.astype(jnp.bfloat16)
        grad_attention = jnp.einsum(
            "td,te->de", heads_low, grad_attn, preferred_element_type=jnp.float32
        )
        grad_heads = jnp.einsum(
            "te,de->td", grad_attn, out_full, preferred_element_type=jnp.float32
        ).astype(jnp.bfloat16)
        grad_head_grid = grad_heads.reshape(row_count, HEADS, HEAD_DIM)
        scores_again = masked_scores(query_heads, key_heads, query_index, key_index, prefix_len)
        probs_exact = jnp.exp(scores_again - log_total)
        probs_again = probs_exact.astype(jnp.bfloat16)
        grad_probs = jnp.einsum(
            "qhd,khd->hqk", grad_head_grid, value_heads, preferred_element_type=jnp.float32
        )
        row_inner = jnp.sum(probs_exact * grad_probs, axis=-1, keepdims=True)
        grad_scores = (probs_exact * (grad_probs - row_inner)).astype(jnp.bfloat16)
        grad_queries = (
            jnp.einsum(
                "hqk,khd->qhd", grad_scores, key_heads, preferred_element_type=jnp.float32
            ).reshape(row_count, model_width)
            * score_scale
        )
        grad_key_part = (
            jnp.einsum("hqk,qhd->khd", grad_scores, query_heads, preferred_element_type=jnp.float32)
            * score_scale
        )
        grad_value_part = jnp.einsum(
            "hqk,qhd->khd", probs_again, grad_head_grid, preferred_element_type=jnp.float32
        )
        key_grads = lax.psum_scatter(
            jnp.concatenate(
                [
                    grad_key_part.reshape(row_count * lax.axis_size("ctx"), -1),
                    grad_value_part.reshape(row_count * lax.axis_size("ctx"), -1),
                ],
                axis=-1,
            ).astype(jnp.bfloat16),
            "ctx",
            scatter_dimension=0,
            tiled=True,
        ).astype(jnp.float32)
        grad_query_low = rotate(grad_queries, cosine_table, sine_table, -1.0).astype(jnp.bfloat16)
        grad_key_low = rotate(key_grads[:, :model_width], cosine_table, sine_table, -1.0).astype(
            jnp.bfloat16
        )
        grad_value_low = key_grads[:, model_width:].astype(jnp.bfloat16)
        grad_projected = jnp.stack([grad_query_low, grad_key_low, grad_value_low])
        grad_proj = jnp.einsum(
            "std,ste->sde", normed_low, grad_projected, preferred_element_type=jnp.float32
        )
        grad_normed = jnp.einsum(
            "ste,sde->std", grad_projected, proj_full, preferred_element_type=jnp.float32
        )
        norm_three_back = jax.vjp(layer_norm, inputs[:3], gain_three)[1]
        grad_inputs_three, grad_gain_three = norm_three_back(grad_normed)
        grad_gain_all = jnp.concatenate(
            [grad_gain_three.reshape(3, -1), grad_gain_mlp[None], grad_gain_mix[None]], axis=0
        )
        proj_shard, attention_shard, gain_shard = (
            lax.psum_scatter(grad_proj, ("dp", "ctx"), scatter_dimension=1, tiled=True),
            lax.psum_scatter(grad_attention, ("dp", "ctx"), scatter_dimension=0, tiled=True),
            lax.psum_scatter(grad_gain_all, ("dp", "ctx"), scatter_dimension=1, tiled=True),
        )
        grad_block = jnp.concatenate([grad_inputs_three, grad_hidden[None]], axis=0).astype(
            jnp.bfloat16
        )
        new_totals = (
            kept_projections + proj_shard,
            kept_attention + attention_shard,
            kept_gains + gain_shard,
            kept_up + up_shard,
            down_next,
            kept_first + first_shard,
            kept_second + grad_second,
            kept_bias + grad_bias,
            kept_loss + loss_part,
        )
        return (new_totals, (next_block.astype(jnp.bfloat16), grad_block, grad_past))

    down_start = jnp.zeros(down_weight.shape, jnp.float32)
    start_totals = (
        jnp.zeros(projections.shape, jnp.float32),
        jnp.zeros(attention_out.shape, jnp.float32),
        jnp.zeros(gains.shape, jnp.float32),
        jnp.zeros(up_weight.shape, jnp.float32),
        down_start,
        jnp.zeros(mixer_first.shape, jnp.float32),
        jnp.zeros(mixer_second.shape, jnp.float32),
        jnp.zeros(mixer_bias.shape, jnp.float32),
        jnp.zeros((), jnp.float32),
    )
    final_totals, stacked = lax.scan(
        one_batch, start_totals, jnp.arange(micro_count, dtype=jnp.int32)
    )
    (
        sum_projections,
        sum_attention,
        sum_gains,
        sum_up,
        sum_down,
        sum_first,
        sum_second,
        sum_bias,
        sum_loss,
    ) = final_totals
    grad_second_all, grad_bias_all, loss_all = lax.psum(
        (sum_second, sum_bias, sum_loss), ("dp", "ctx")
    )
    next_streams = jnp.moveaxis(stacked[0], 0, 1)
    grad_streams = jnp.moveaxis(stacked[1], 0, 1)
    grad_history = jnp.moveaxis(stacked[2], 0, 1)
    return (
        next_streams,
        loss_all,
        grad_streams,
        grad_history,
        sum_projections,
        sum_attention,
        sum_up,
        sum_down,
        sum_first,
        grad_second_all,
        grad_bias_all,
        sum_gains,
    )


def fits(mesh):
    return mesh.shape["ctx"] == 4 and mesh.shape["dp"] == 8


def solution(mesh):
    specs = dict(
        in_specs=(
            P(None, "dp", "ctx", None),
            P(None, "dp", "ctx", None),
            P(None, "dp", "ctx", None),
            P("dp"),
            P("dp", "ctx"),
            P(),
            P(None, ("dp", "ctx"), None),
            P(("dp", "ctx"), None),
            P(("dp", "ctx"), None),
            P(("dp", "ctx"), None),
            P(("dp", "ctx"), None),
            P(),
            P(),
            P(None, ("dp", "ctx")),
        ),
        out_specs=(
            P(None, "dp", "ctx", None),
            P(),
            P(None, "dp", "ctx", None),
            P(None, "dp", "ctx", None),
            P(None, ("dp", "ctx"), None),
            P(("dp", "ctx"), None),
            P(("dp", "ctx"), None),
            P(("dp", "ctx"), None),
            P(("dp", "ctx"), None),
            P(),
            P(),
            P(None, ("dp", "ctx")),
        ),
        check_vma=False,
    )

    def chosen(*arrays):
        fast = fits(mesh) and arrays[0].shape[1] == 2 * mesh.shape["dp"]
        return jax.shard_map(local_fast if fast else local_plain, mesh=mesh, **specs)(*arrays)

    return chosen
```

```python
import functools
import math

import jax
import jax.numpy as jnp
from jax import lax
from jax.experimental import pallas as pl
from jax.experimental.pallas import tpu as pltpu
from jax.sharding import PartitionSpec as P

HEADS = 16
HEAD_DIM = 64
ROT = 16
AXES = ("dp", "ctx")

highest = lax.Precision.HIGHEST
epsilon = 1e-05
f32 = jnp.float32
bf16 = jnp.bfloat16
VMEM_BYTES = 60 * 1024 * 1024


def dot_nn(a, b, precision=None):
    return lax.dot_general(
        a, b, (((1,), (0,)), ((), ())), precision=precision, preferred_element_type=f32
    )


def dot_nt(a, b, precision=None):
    return lax.dot_general(
        a, b, (((1,), (1,)), ((), ())), precision=precision, preferred_element_type=f32
    )


def dot_tn(a, b, precision=None):
    return lax.dot_general(
        a, b, (((0,), (0,)), ((), ())), precision=precision, preferred_element_type=f32
    )


def normal_cdf(v):
    z = jnp.abs(v) * math.sqrt(0.5)
    t = 1.0 / (1.0 + 0.39 * z)
    bell = jnp.exp(-0.5 * v * v)
    poly = -0.22760540438261295
    for c in (
        0.8869388009365644,
        -0.6358388689155755,
        0.649907738051149,
        0.09125094908545259,
        0.23534677935551734,
    ):
        poly = poly * t + c
    half_tail = (0.5 * poly) * t * bell
    return jnp.where(v < 0.0, half_tail, 1.0 - half_tail), bell


def gelu_pair(v):
    cdf, bell = normal_cdf(v)
    return v * cdf, cdf + v * bell * (1.0 / math.sqrt(2.0 * math.pi))


def vmem(block=None, index_map=None):
    if block is None:
        return pl.BlockSpec(memory_space=pltpu.VMEM)
    return pl.BlockSpec(block, index_map)


def params(**kw):
    return pltpu.CompilerParams(vmem_limit_bytes=VMEM_BYTES, **kw)


Z_ORDER = (0, 2, 1, 3)


UP_BITS = (8, 16)
DOWN_BITS = (16, 8)


def gathered_from(me, place, outer):
    distance = 4 * (place // 16) + outer[0] * (place // 8 % 2) + outer[1] * (place // 4 % 2)
    return jnp.bitwise_xor(me, distance + Z_ORDER[place % 4])


def place_rows(me, ref, outer, out_ref):
    rows = ref.shape[-2]
    for place in range(ref.shape[0]):
        device = gathered_from(me, place, outer)
        out_ref[pl.ds(pl.multiple_of(device * rows, rows), rows), :] = ref[place]


def take_rows(me, from_ref, outer, refs):
    rows = refs[0].shape[-2]
    each_has = refs[0].shape[0]
    for place in range(each_has * len(refs)):
        device = gathered_from(me, place, outer)
        refs[place // each_has][place % each_has] = from_ref[
            pl.ds(pl.multiple_of(device * rows, rows), rows), :
        ]


def place_tile(me, all_up_ref, some_down_ref, up_ref, down_ref):
    place_rows(me, all_up_ref, UP_BITS, up_ref)
    rows = some_down_ref.shape[1]
    for q, z in enumerate(Z_ORDER):
        at = pl.multiple_of(jnp.bitwise_xor(lax.rem(me, 4), z) * rows, rows)
        down_ref[pl.ds(at, rows), :] = some_down_ref[q]


def turn(x, cosine, sine_up, sine_down):
    return (
        x * cosine + pltpu.roll(x, ROT // 2, 1) * sine_up + pltpu.roll(x, 128 - ROT // 2, 1) * sine_down
    )


def allowed_limit(base, rows, prefix, axis):
    shape = (rows, 1) if axis == 0 else (1, rows)
    position = base + lax.broadcasted_iota(jnp.int32, shape, axis)
    return jnp.maximum(position, prefix - 1)


def flip(bit, by):
    return bit + by - 2 * bit * by


class Place:
    def __init__(self):
        self.group = lax.axis_index("dp")
        self.z = lax.axis_index("ctx")
        self.core = lax.rem(self.group, 2)
        self.x = lax.rem(lax.div(self.group, 2), 2)
        self.y = lax.div(self.group, 4)
        self.z_low = lax.rem(self.z, 2)
        self.z_high = lax.div(self.z, 2)

    def across(self, axis):
        if axis == "core":
            return (self.group + 1 - 2 * self.core, self.z)
        if axis == "x":
            return (self.group + 2 - 4 * self.x, self.z)
        if axis == "y":
            return (self.group + 4 - 8 * self.y, self.z)
        if axis == "zl":
            return (self.group, self.z + 1 - 2 * self.z_low)
        return (self.group, self.z + 2 - 4 * self.z_high)

    def device(self, y, x, core, z):
        pair = flip(self.y, y) * 4 + flip(self.x, x) * 2 + flip(self.core, core)
        return pair * 4 + flip(self.z_high, z // 2) * 2 + flip(self.z_low, z % 2)

    def code(self, k):
        return flip(self.z_high, lax.div(k, 2)), flip(self.z_low, lax.rem(k, 2))

    def block(self, k):
        return flip(self.z_low, lax.div(k, 2)) * 2 + flip(self.core, lax.rem(k, 2))

    def out_to(self, k):
        seq, half = self.code(k)
        return (self.group - self.core + half, 2 * self.core + seq)

    def back_to(self, k):
        return (self.group - self.core + self.z_high, self.block(k))

    def is_self(self, device):
        return jnp.logical_and(device[0] == self.group, device[1] == self.z)

    def meet(self, names):
        barrier = pltpu.get_barrier_semaphore()
        others = [self.across(name) for name in names]
        for step in range(1, 8):
            place = self.core * 4 + self.z + step
            others.append(
                (self.group - self.core + lax.rem(lax.div(place, 4), 2), lax.rem(place, 4))
            )
        for other in others:
            pl.semaphore_signal(barrier, inc=1, device_id=other, device_id_type=pl.DeviceIdType.MESH)
        pl.semaphore_wait(barrier, len(others))


class Sends:
    def __init__(self, here, send_sems, recv_sems):
        self.here, self.send_sems, self.recv_sems = here, send_sems, recv_sems
        self.used, self.open = 0, []

    def make(self, n, source, target, device):
        return pltpu.make_async_remote_copy(
            src_ref=source,
            dst_ref=target,
            send_sem=self.send_sems.at[n],
            recv_sem=self.recv_sems.at[n],
            device_id=device,
            device_id_type=pl.DeviceIdType.MESH,
        )

    def start(self, source, target, device):
        copy = self.make(self.used, source, target, device)
        self.used += 1
        copy.start()
        self.open.append(copy)
        return copy

    def four(self, source, target, device):
        base = self.used
        self.used += 4

        def copy(k):
            return self.make(base + k, source(k), target(k), device(k))

        def start(k):
            stays = self.here.is_self(device(k))

            @pl.when(stays)
            def _():
                pltpu.make_async_copy(source(k), target(k), self.recv_sems.at[base + k]).start()

            @pl.when(jnp.logical_not(stays))
            def _():
                copy(k).start()

        def sent(k):
            @pl.when(jnp.logical_not(self.here.is_self(device(k))))
            def _():
                copy(k).wait_send()

        def came(k):
            copy(k).wait_recv()

        return start, sent, came

    def finish(self):
        for copy in self.open:
            copy.wait_send()


def each(n, body):
    def step(i, _):
        body(i)
        return 0

    lax.fori_loop(0, n, step, 0)


class Gathers:
    def __init__(self, here, sends, refs):
        self.here, self.sends, self.refs = here, sends, refs
        self.coming = {name: [] for name in refs}

    def settle(self, name, first=0, count=1 << 20):
        left = []
        for at, n, copy in self.coming[name]:
            if at < first + count and first < at + n:
                copy.wait_recv()
            else:
                left.append((at, n, copy))
        self.coming[name] = left

    def move(self, name, axis, first, count, to):
        self.settle(name, first, count)
        ref = self.refs[name]
        copy = self.sends.start(
            ref.at[pl.ds(first, count)], ref.at[pl.ds(to, count)], self.here.across(axis)
        )
        self.coming[name].append((to, count, copy))


def key_positions(length, blocks, axis):
    shape = (length, 1) if axis == 0 else (1, length)
    i = lax.broadcasted_iota(jnp.int32, shape, axis)
    piece = length // (2 * blocks)
    return (
        lax.rem(lax.div(i, piece), blocks) * (2 * piece)
        + lax.div(i, length // 2) * piece
        + lax.rem(i, piece)
    )


FRONT_PLAN = (
    ("start", "zl"),
    ("move", "proj", "zh", 0, 1, 1),
    ("move", "proj", "zl", 0, 1, 2),
    ("add",),
    ("start", "zh"),
    ("move", "up", "zh", 0, 1, 1),
    ("move", "up", "zl", 0, 1, 2),
    ("move", "down", "zh", 0, 1, 1),
    ("move", "down", "zl", 0, 1, 2),
    ("add",),
    ("start", "x"),
    ("move", "proj", "y", 0, 1, 4),
    ("move", "proj", "x", 0, 1, 8),
    ("move", "up", "y", 0, 1, 4),
    ("move", "down", "x", 0, 1, 4),
    ("move", "up", "x", 0, 1, 8),
    ("move", "down", "y", 0, 1, 8),
    ("move", "proj", "zl", 1, 1, 3),
    ("move", "up", "zl", 1, 1, 3),
    ("move", "down", "zl", 1, 1, 3),
    ("rows", 1),
    ("add",),
    ("start", "y"),
    ("move", "proj", "y", 1, 1, 5),
    ("move", "proj", "x", 1, 1, 9),
    ("add",),
    ("start", "core"),
    ("move", "proj", "x", 4, 1, 12),
    ("add",),
    ("rows", 2),
    ("move", "up", "y", 1, 1, 5),
    ("move", "down", "x", 1, 1, 5),
    ("move", "up", "x", 1, 1, 9),
    ("move", "down", "y", 1, 1, 9),
    ("rows", 0),
    ("move", "proj", "y", 2, 2, 6),
    ("move", "proj", "x", 2, 2, 10),
    ("move", "proj", "x", 5, 1, 13),
    ("move", "up", "x", 4, 1, 12),
    ("move", "down", "y", 4, 1, 12),
    ("move", "up", "y", 2, 2, 6),
    ("move", "down", "x", 2, 2, 6),
    ("norm", 1),
    ("move", "proj", "x", 6, 2, 14),
    ("move", "up", "x", 2, 2, 10),
    ("move", "down", "y", 2, 2, 10),
    ("move", "up", "x", 5, 1, 13),
    ("move", "down", "y", 5, 1, 13),
    ("norm", 2),
    ("move", "up", "x", 6, 2, 14),
    ("move", "down", "y", 6, 2, 14),
    ("move", "up", "core", 0, 8, 16),
    ("move", "down", "core", 0, 8, 16),
    ("assemble",),
    ("project", 1),
    ("project", 2),
    ("norm", 0),
    ("project", 0),
    ("move", "up", "core", 8, 4, 24),
    ("move", "down", "core", 8, 4, 24),
    ("attend",),
    ("move", "up", "core", 12, 4, 28),
    ("move", "down", "core", 12, 4, 28),
)


def front_body(
    prefix_in, streams_ref, proj_in, up_in, down_in, out_in, gains_in, first_in, valid_in, cos_ref, rise_ref, fall_ref,
    received_out, normed_out, weight_out, far_out, up_ref, down_ref, small_ref, first_ref, prefix_ref,
    q_out, k_out, v_out, heads_out, lse_ref, got_ref,
    received_ref, normed_ref, proj_ref, weight_ref, q_ref, k_ref, v_ref, heads_ref,
    small_got, first_got, prefix_own, prefix_got, local_sems, send_sems, recv_sems,
):
    here = Place()
    sends = Sends(here, send_sems, recv_sems)
    gathers = Gathers(here, sends, {"proj": proj_ref, "up": up_ref, "down": down_ref})
    features = proj_ref.shape[-1]
    units = down_in.shape[0]
    kept = []

    def keep(source, target):
        copy = pltpu.make_async_copy(source, target, local_sems.at[len(kept)])
        kept.append(copy)
        copy.start()
        return copy

    def columns(which):
        return proj_in.at[:, :, pl.ds(pl.multiple_of(which * features, features), features)]

    shard = gains_in.shape[1]
    lanes = small_ref.shape[1]
    column = lax.broadcasted_iota(jnp.int32, (shard, lanes), 1)
    row = lax.broadcasted_iota(jnp.int32, (shard, lanes), 0)
    chosen = (column == row + here.device(0, 0, 0, 0) * shard).astype(bf16)
    count = jnp.sum(valid_in[...].astype(f32))
    small_ref[...] = jnp.zeros_like(small_ref)
    small_ref[0:5, :] = dot_nn(gains_in[...], chosen)
    small_ref[7:8, :] = jnp.full((1, lanes), 1.0, f32) * count
    first_ref[...] = jnp.zeros_like(first_ref)
    first_ref[0 : first_in.shape[1], :] = dot_tn(first_in[...], chosen).astype(bf16)
    second_row = lax.broadcasted_iota(jnp.int32, prefix_own.shape, 0) == 1
    prefix_own[...] = jnp.where(second_row, prefix_in[1], prefix_in[0])
    here.meet(("x", "y"))
    small_steps = []

    def small_start(axis):
        n = len(small_steps)
        device = here.across(axis)
        small_steps.append(
            (
                sends.start(small_ref, small_got.at[n], device),
                sends.start(first_ref, first_got.at[n], device),
            )
        )

    def small_end():
        n = len(small_steps) - 1
        for copy in small_steps[n]:
            copy.wait()
        sends.open = [c for c in sends.open if not any(c is s for s in small_steps[n])]
        small_ref[...] += small_got[n]
        first_ref[...] += first_got[n]

    def stream(s):
        def source(k):
            seq, half = here.code(k)
            return streams_ref.at[s, 2 * seq + half]

        steps = sends.four(source, lambda k: received_ref.at[s, k], here.out_to)
        each(4, steps[0])
        return steps

    chunk = 32

    def norm(s, steps):
        gain = small_ref[s : s + 1, :].astype(f32)

        def step(k):
            steps[2](k)
            block = here.block(k)

            def body(i, _):
                at = pl.ds(pl.multiple_of(i * chunk, chunk), chunk)
                x = received_ref[s, k, at, :].astype(f32)
                x = x - jnp.mean(x, axis=-1, keepdims=True)
                scale = lax.rsqrt(jnp.mean(x * x, axis=-1, keepdims=True) + epsilon)
                normed_ref[s, here.core, block, at, :] = (x * scale * gain).astype(bf16)
                return 0

            lax.fori_loop(0, received_ref.shape[2] // chunk, body, 0, unroll=2)

        each(4, step)
        keep(received_ref.at[s], received_out.at[s])
        keep(normed_ref.at[s, here.core], normed_out.at[s, here.core])
        return sends.start(
            normed_ref.at[s, here.core], normed_ref.at[s, here.core], here.across("core")
        )

    prefix_send = sends.start(prefix_own, prefix_got, here.across("core"))
    gathers.coming["proj"].append(
        (0, 1, sends.start(columns(1 - here.core), proj_ref.at[0, 1], here.across("core")))
    )
    own = [
        keep(columns(here.core), proj_ref.at[0, 0]),
        keep(up_in, up_ref.at[0]),
        keep(down_in, down_ref.at[0, pl.ds(0, units)]),
        keep(out_in, down_ref.at[0, pl.ds(units, out_in.shape[0])]),
    ]
    for copy in own:
        copy.wait()
    prefix_send.wait_recv()
    prefixes = jnp.where(here.z_high == here.core, prefix_own[...], prefix_got[...])
    prefix_ref[...] = jnp.broadcast_to(
        jnp.where(here.z_low == 0, prefixes[0:1], prefixes[1:2]), prefix_ref.shape
    )
    def assemble(s):
        rows = proj_ref.shape[-2]
        for x in range(2):
            for y in range(2):
                for q, z in enumerate(Z_ORDER):
                    for core in range(2):
                        device = here.device(y, x, core, z)
                        at = pl.ds(pl.multiple_of(device * rows, rows), rows)
                        weight_ref[s, at, :] = proj_ref[(x * 2 + y) * 4 + q, core, s]


    _, blocks, piece, width = q_ref.shape
    half_rows = blocks * piece
    length = 2 * half_rows

    def project(s, out_ref):
        def step(half):
            y = dot_nn(normed_ref[s, half].reshape(half_rows, -1), weight_ref[s])
            if s < 2:
                tables = [r[half].reshape(half_rows, 128) for r in (cos_ref, rise_ref, fall_ref)]
                y = jnp.concatenate(
                    [turn(y[:, i : i + 128], *tables) for i in range(0, width, 128)], axis=1
                )
            y = y.astype(bf16)
            if s == 0:
                y = y * jnp.asarray(HEAD_DIM**-0.5, bf16)
            out_ref[half] = y.reshape(blocks, piece, width)

        each(2, step)

    rows = 2 * piece
    lane = lax.broadcasted_iota(jnp.int32, (rows, 128), 1)
    key_index = key_positions(length, blocks, 1)
    heads_steps = sends.four(
        lambda k: heads_ref.at[here.block(k)], lambda k: got_ref.at[k], here.back_to
    )

    def block_body(k):
        block = here.block(k)
        allowed = key_index <= allowed_limit(block * rows, rows, prefix_ref[0:1, 0:1], 0)
        lse_all = jnp.zeros((rows, 128), f32)
        for pair in range(width // 128):
            at = slice(pair * 128, pair * 128 + 128)
            queries = q_ref[:, block, :, at].reshape(rows, 128)
            keys = k_ref[:, :, :, at].reshape(length, 128)
            values = v_ref[:, :, :, at].reshape(length, 128)
            results = []
            for h in range(2):
                chosen = (lane < 64) if h == 0 else (lane >= 64)
                scores = dot_nt(jnp.where(chosen, queries, jnp.zeros_like(queries)), keys)
                scores = jnp.where(allowed, scores, -1e30)
                top = jnp.max(scores, axis=-1, keepdims=True)
                weights = jnp.exp(scores - top)
                total = jnp.sum(weights, axis=-1, keepdims=True)
                results.append(dot_nn(weights.astype(bf16), values) / total)
                lse_all = jnp.where(lane == pair * 2 + h, top + jnp.log(total), lse_all)
            heads_ref[block, :, at] = jnp.where(lane < 64, results[0], results[1]).astype(bf16)
        lse_ref[block] = lse_all.T[0:8]
        heads_steps[0](k)


    rows_steps, others, far = {}, {}, []
    for step in FRONT_PLAN:
        kind = step[0]
        if kind == "start":
            small_start(step[1])
        elif kind == "add":
            small_end()
        elif kind == "rows":
            rows_steps[step[1]] = stream(step[1])
        elif kind == "move":
            gathers.move(*step[1:])
        elif kind == "norm":
            others[step[1]] = norm(step[1], rows_steps[step[1]])
        elif kind == "assemble":
            gathers.settle("proj")
            each(3, assemble)
            far.append(sends.start(weight_ref, far_out, here.across("core")))
            keep(weight_ref, weight_out)
        elif kind == "project":
            s = step[1]
            others[s].wait_recv()
            keep(normed_ref.at[s, 1 - here.core], normed_out.at[s, 1 - here.core])
            ref, out = ((q_ref, q_out), (k_ref, k_out), (v_ref, v_out))[s]
            project(s, ref)
            keep(ref, out)
        else:
            each(4, block_body)
            keep(heads_ref, heads_out)
    each(4, heads_steps[2])
    for name in ("up", "down"):
        gathers.settle(name)
    far[0].wait_recv()
    for steps in list(rows_steps.values()) + [heads_steps]:
        each(4, steps[1])
    sends.finish()
    for copy in kept[len(own) :]:
        copy.wait()


def mlp_forward_body(
    ids, heads_ref, res_ref, gain_ref, all_up_ref, some_down_ref, gathered_out_ref,
    hidden_ref, normed_ref, active_ref, slope_ref, layer_ref,
    out_w_ref, up_ref, down_ref,
):
    step = pl.program_id(0)
    seqs, rows, width = res_ref.shape[1:]
    me = ids[4]

    @pl.when(step == 0)
    def _():
        place_rows(me, gathered_out_ref, DOWN_BITS, out_w_ref)
        hidden_ref[...] = res_ref[0].astype(f32)
        for k in range(heads_ref.shape[0]):
            code = jnp.bitwise_xor(ids[0], k)
            features = heads_ref.shape[-1]
            at = pl.ds(pl.multiple_of(lax.rem(code, 2) * features, features), features)
            hidden_ref[lax.div(code, 2)] += dot_nn(heads_ref[k], out_w_ref[at, :])
        gain = gain_ref[3:4, :].astype(f32)
        for j in range(seqs):
            x = hidden_ref[j]
            layer_ref[j] = x
            x = x - jnp.mean(x, axis=-1, keepdims=True)
            scale = lax.rsqrt(jnp.mean(x * x, axis=-1, keepdims=True) + epsilon)
            normed_ref[j] = (x * scale * gain).astype(bf16)

    place_tile(me, all_up_ref, some_down_ref, up_ref, down_ref)
    upper = dot_nn(normed_ref[...].reshape(seqs * rows, width), up_ref[...])
    active, slope = gelu_pair(upper)
    active = active.astype(bf16)
    active_ref[...] = active
    slope_ref[...] = slope.astype(bf16)
    layer_ref[...] += dot_nn(active, down_ref[...]).reshape(seqs, rows, width)


def mixer_body(
    scal_ref, layer_ref, hist_ref, teacher_ref, valid_in, gain_ref, first_ref, second_in, bias_in,
    next_ref, ghist_ref, glayer_ref, gfirst_ref, gsecond_ref, stats_ref, ggain_ref,
    coef_ref, part_ref, gnext_ref, valid_ref, second_ref, bias_ref,
):
    step = pl.program_id(0)
    past, rows, width = hist_ref.shape
    streams = teacher_ref.shape[0]
    outs = past + 1
    span = first_ref.shape[0]

    @pl.when(step == 0)
    def _():
        gfirst_ref[...] = jnp.zeros_like(gfirst_ref)
        gsecond_ref[...] = jnp.zeros_like(gsecond_ref)
        stats_ref[...] = jnp.zeros_like(stats_ref)
        ggain_ref[...] = jnp.zeros_like(ggain_ref)
        second_ref[...] = jnp.zeros_like(second_ref)
        second_ref[0 : second_in.shape[0], 0 : second_in.shape[1]] = second_in[...]
        bias_ref[...] = jnp.zeros_like(bias_ref)
        bias_ref[:, 0 : bias_in.shape[1]] = bias_in[...]

    factor = scal_ref[0] * 2.0 / (4.0 * width * gain_ref[7:8, 0:128])
    diagonal = lax.broadcasted_iota(jnp.int32, (rows, rows), 0) == lax.broadcasted_iota(
        jnp.int32, (rows, rows), 1
    )
    valid_row = jnp.broadcast_to(valid_in[0].astype(f32), (rows, rows))
    valid_ref[...] = jnp.sum(jnp.where(diagonal, valid_row, 0.0), axis=1, keepdims=True)
    x = layer_ref[...]
    scale = lax.rsqrt(jnp.mean(x * x, axis=-1, keepdims=True) + epsilon)
    gain = gain_ref[4:5, :].astype(f32)
    normed = (x * scale * gain).astype(bf16)
    mix_hidden = dot_nt(normed, first_ref[...])
    mix_active, mix_slope = gelu_pair(mix_hidden)
    coeff = dot_nn(mix_active, second_ref[...], highest) + bias_ref[...]
    for c in range(streams * outs):
        coef_ref[c] = jnp.broadcast_to(coeff[:, c : c + 1], (rows, 128))
    part_ref[...] = jnp.zeros_like(part_ref)

    chunk = 16
    lanes = 512

    def rows_body(i, loss_rows):
        at = pl.ds(pl.multiple_of(i * chunk, chunk), chunk)
        valid = jnp.broadcast_to(valid_ref[at, :], (chunk, 128))

        def read(j, lane_at):
            return layer_ref[at, lane_at] if j == past else hist_ref[j, at, lane_at].astype(f32)

        for l0 in range(0, width, 256):
            lane_at = slice(l0, l0 + 256)
            sums = [jnp.zeros((chunk, 256), f32) for _ in range(streams)]
            for j in range(outs):
                value = read(j, lane_at)
                for s in range(streams):
                    c = coef_ref[s * outs + j, at, :]
                    sums[s] = sums[s] + jnp.concatenate([c, c], axis=1) * value
            both = jnp.concatenate([valid, valid], axis=1)
            for s in range(streams):
                next_ref[s, at, lane_at] = sums[s].astype(bf16)
                difference = sums[s] - teacher_ref[s, at, lane_at].astype(f32)
                weighted = both * difference
                gnext_ref[s, at, lane_at] = jnp.concatenate([factor, factor], axis=1) * weighted
                square = weighted * difference
                loss_rows = loss_rows + square[:, :128] + square[:, 128:]
        for l0 in range(0, width, lanes):
            lane_at = slice(l0, l0 + lanes)
            for j in range(outs):
                value = read(j, lane_at)
                total = jnp.zeros((chunk, lanes), f32)
                for s in range(streams):
                    grad = gnext_ref[s, at, lane_at]
                    c = coef_ref[s * outs + j, at, :]
                    total = total + jnp.concatenate([c] * (lanes // 128), axis=1) * grad
                    product = grad * value
                    folded = product[:, :128]
                    for q in range(128, lanes, 128):
                        folded = folded + product[:, q : q + 128]
                    part_ref[s * outs + j, at, :] += folded
                if j == past:
                    glayer_ref[at, lane_at] = total
                else:
                    ghist_ref[j, at, lane_at] = total.astype(bf16)
        return loss_rows

    loss_rows = lax.fori_loop(0, rows // chunk, rows_body, jnp.zeros((chunk, 128), f32))
    lane = lax.broadcasted_iota(jnp.int32, (rows, span), 1)
    grad_coeff = jnp.zeros((rows, span), f32)
    for c in range(streams * outs):
        grad_coeff = jnp.where(lane == c, jnp.sum(part_ref[c], axis=-1, keepdims=True), grad_coeff)
    gsecond_ref[...] += dot_tn(mix_active, grad_coeff, highest)
    stats_ref[0:1, :] += jnp.sum(grad_coeff, axis=0, keepdims=True)
    stats_ref[1:2, :] += jnp.broadcast_to(jnp.sum(loss_rows), (1, span))
    grad_active = dot_nt(grad_coeff, second_ref[...], highest)
    grad_mix = (grad_active * mix_slope).astype(bf16)
    gfirst_ref[...] += dot_tn(grad_mix, normed)
    grad_normed = dot_nn(grad_mix, first_ref[...])
    x = layer_ref[...]
    ggain_ref[...] += jnp.sum(grad_normed * (x * scale), axis=0, keepdims=True)
    inner = grad_normed * gain
    mean = jnp.mean(inner * x, axis=-1, keepdims=True)
    glayer_ref[...] += scale * inner - x * (scale * scale * scale * mean)


def norm_back(x, grad, gain):
    centered = x - jnp.mean(x, axis=-1, keepdims=True)
    scale = lax.rsqrt(jnp.mean(centered * centered, axis=-1, keepdims=True) + epsilon)
    unit = centered * scale
    grad_gain = jnp.sum(grad * unit, axis=0, keepdims=True)
    inner = grad * gain
    inner = (
        inner
        - jnp.mean(inner, axis=-1, keepdims=True)
        - unit * jnp.mean(inner * unit, axis=-1, keepdims=True)
    )
    return scale * inner, grad_gain


def mlp_backward_body(
    ids, glayer_ref, active_ref, slope_ref, normed_ref, all_up_ref, some_down_ref,
    gu0, gu1, gu2, gu3, gd0, gd1, gd2, gd3, sum_ref,
    low_ref, normed_t_ref, up_ref, down_ref, tile_ref,
):
    step = pl.program_id(0)
    seqs, rows, width = glayer_ref.shape
    tokens = seqs * rows
    me = ids[4]
    place = lax.rem(me, 4)

    @pl.when(step == 0)
    def _():
        low_ref[...] = glayer_ref[...].astype(bf16)
        sum_ref[...] = jnp.zeros_like(sum_ref)
        normed_t_ref[...] = normed_ref[...].reshape(tokens, width).T

    place_tile(me, all_up_ref, some_down_ref, up_ref, down_ref)
    grad = low_ref[...].reshape(tokens, width)
    grad_active = dot_nt(grad, down_ref[...])
    grad_upper = (grad_active * slope_ref[...].astype(f32)).astype(bf16)
    sum_ref[...] += dot_nt(grad_upper, up_ref[...]).reshape(seqs, rows, width)
    down_ref[...] = dot_tn(active_ref[...], grad).astype(bf16)
    for p, ref in enumerate((gd0, gd1, gd2, gd3)):

        @pl.when(lax.div(step, 2) == p)
        def _(ref=ref):
            block_rows = ref.shape[1]
            for q, z in enumerate(Z_ORDER):
                at = pl.multiple_of(jnp.bitwise_xor(place, z) * block_rows, block_rows)
                ref[q] = down_ref[pl.ds(at, block_rows), :]

    tile_ref[...] = dot_nn(normed_t_ref[...], grad_upper).astype(bf16)
    take_rows(me, tile_ref, UP_BITS, (gu0, gu1, gu2, gu3))


def hidden_backward_body(
    ids, glayer_ref, sum_ref, hidden_ref, heads_ref, gain_ref, gathered_out_ref,
    gres_ref, g0, g1, g2, g3, go0, go1, go2, go3, ggain_ref,
    out_w_ref, gout_ref,
):
    seqs, rows, width = hidden_ref.shape
    me = ids[4]
    place_rows(me, gathered_out_ref, DOWN_BITS, out_w_ref)
    gain = gain_ref[3:4, :].astype(f32)
    ggain = jnp.zeros((1, width), f32)
    for j in range(seqs):
        back, part = norm_back(hidden_ref[j], sum_ref[j], gain)
        ggain = ggain + part
        gres_ref[j] = (glayer_ref[j] + back).astype(bf16)
    ggain_ref[...] = ggain
    gout_ref[...] = jnp.zeros_like(gout_ref)
    for k, out in enumerate((g0, g1, g2, g3)):
        code = jnp.bitwise_xor(ids[0], k)
        features = out.shape[-1]
        at = pl.ds(pl.multiple_of(lax.rem(code, 2) * features, features), features)
        low = gres_ref[lax.div(code, 2)]
        out[...] = dot_nt(low, out_w_ref[at, :]).astype(bf16)
        gout_ref[at, :] += dot_tn(heads_ref[k], low)
    out_w_ref[...] = gout_ref[...].astype(bf16)
    take_rows(me, out_w_ref, DOWN_BITS, (go0, go1, go2, go3))


def back_body(
    prefix_ref, q_in, k_in, v_in, heads_in, lse_ref, cos_ref, rise_ref, fall_ref,
    normed_in, received_in, weight_in, far_in, gain_ref, gfirst_in, gmlp_in, gmix_in, gsecond_in, stats_in, res_in,
    gh0, gh1, gh2, gh3, gu0, gu1, gu2, gu3, gd0, gd1, gd2, gd3, go0, go1, go2, go3,
    gstreams_ref, gproj_ref, gup_ref, gdown_ref, gout_ref, near_ref, tiny_ref, late_ref,
    q_ref, k_ref, v_ref, heads_ref, g_ref, d_ref, d_got, dk_ref, dv_ref, kt_ref,
    normed_ref, received_ref, weight_ref, gn_ref, b_ref, grad_ref,
    up_keep, down_keep, up_sum, up_a, up_b, up_c, up_d, down_sum, down_a, down_b, down_c, down_d,
    down_p, down_q, down_r, down_s,
    proj_sum, proj_a, proj_b, proj_c, proj_d, proj_e, early_ref, early_y, early_x, early_core, near_got, tiny_got, late_got,
    local_sems, send_sems, recv_sems,
):
    here = Place()
    sends = Sends(here, send_sems, recv_sems)
    used = []

    def load(source, target):
        copy = pltpu.make_async_copy(source, target, local_sems.at[len(used)])
        used.append(copy)
        copy.start()
        return copy

    def ready(source, target, axis):
        copy = sends.make(sends.used, source, target, here.across(axis))
        sends.used += 1
        sends.open.append(copy)
        return copy

    def send(source, target, axis):
        copy = ready(source, target, axis)
        copy.start()
        return copy

    def add(into, first, source, count, start=0):
        def body(i):
            into[first + i] = into[first + i] + source[start + i]

        each(count, body)

    span = gfirst_in.shape[0]
    early_ref[0:span, :] = gfirst_in[...]
    early_ref[span:, :] = jnp.zeros((8, early_ref.shape[1]), f32)
    early_ref[span : span + 1, :] = gmlp_in[...]
    early_ref[span + 1 : span + 2, :] = gmix_in[...]
    tiny_ref[0:span, :] = gsecond_in[...]
    tiny_ref[span:, :] = stats_in[...]
    here.meet(("x", "y"))

    def ring(*refs):
        stages = []

        def start(axis):
            n = len(stages)
            stages.append([send(value, got.at[n], axis) for value, got in refs])

        def end():
            n = len(stages) - 1
            for copy in stages[n]:
                copy.wait()
            sends.open = [c for c in sends.open if not any(c is s for s in stages[n])]
            for value, got in refs:
                value[...] += got[n]

        return start, end

    late_start, late_end = ring((late_ref, late_got))
    near_start, near_end = ring((near_ref, near_got))
    tiny_start, tiny_end = ring((tiny_ref, tiny_got))

    column = [0]
    halvings = []

    def early_start(axis):
        tiny_start(axis)
        got = {"y": early_y, "x": early_x, "core": early_core}.get(axis)
        if got is None:
            near_start(axis)
            return
        bit = {"y": here.y, "x": here.x, "core": here.core}[axis]
        size = got.shape[1]
        give = pl.multiple_of(column[0] + (1 - bit) * size, 128)
        column[0] = column[0] + bit * size
        halvings.append((send(early_ref.at[:, pl.ds(give, size)], got, axis), got))

    def early_end():
        tiny_end()
        if not halvings:
            near_end()
            return
        copy, got = halvings.pop()
        copy.wait()
        sends.open = [c for c in sends.open if c is not copy]
        at = pl.ds(pl.multiple_of(column[0], 128), got.shape[1])
        if got is early_core:
            near_ref[...] = early_ref[:, at] + got[...]
        else:
            early_ref[:, at] += got[...]

    early_start("y")
    gs = (gh0, gh1, gh2, gh3)
    base = sends.used
    sends.used += 4
    exchange = []
    for n, g in enumerate(gs):
        device = here.out_to(n)
        stays = here.is_self(device)
        copy = sends.make(base + n, g, g_ref.at[n], device)
        own = pltpu.make_async_copy(g, g_ref.at[n], recv_sems.at[base + n])

        @pl.when(stays)
        def _(own=own):
            own.start()

        @pl.when(jnp.logical_not(stays))
        def _(copy=copy):
            copy.start()

        exchange.append((copy, stays))
    units = gd0.shape[3]
    shard = go0.shape[3]
    cut = down_a.shape[-1]
    left, right = pl.ds(0, cut), pl.ds(cut, cut)

    def down_parts(ref):
        lead = (slice(None),) * (len(ref.shape) - 2)
        return ref.at[lead + (pl.ds(0, units),)], ref.at[lead + (pl.ds(units, shard),)]

    up_come, down_come = {}, {}
    for n, u, d, o in ((1, gu3, gd3, go3), (0, gu2, gd2, go2)):
        up_come[n] = [send(u, up_sum.at[pl.ds(8 * n, 8)], "core")]
        to_d, to_o = down_parts(down_sum.at[pl.ds(2 * n, 2)])
        down_come[n] = [send(d, to_d, "core"), send(o, to_o, "core")]
    attention_loads = [
        load(a, b)
        for a, b in ((q_in, q_ref), (k_in, k_ref), (v_in, v_ref), (heads_in, heads_ref))
    ]

    def load_stream(s, slot):
        return [
            load(normed_in.at[s], normed_ref.at[slot]),
            load(received_in.at[s], received_ref.at[slot]),
            load(weight_in.at[s], weight_ref.at[slot, 0]),
            load(far_in.at[s], weight_ref.at[slot, 1]),
        ]

    own_up = {1: gu1, 0: gu0}
    own_down = {1: (gd1, go1), 0: (gd0, go0)}

    def load_up(n, half):
        return [load(own_up[n].at[pl.ds(4 * half, 4)], up_keep)]

    def load_down(n, half):
        d, o = own_down[n]
        to_d, to_o = down_parts(down_keep)
        return [load(d.at[half], to_d), load(o.at[half], to_o)]

    def add_down(place, source, lanes, lows=(0, 1)):
        for low in lows:

            def body(high):
                down_sum[place, low, high, :, lanes] += source[low, high]

            each(2, body)

    order = ((1, 1), (1, 0), (0, 1), (0, 0))
    up_load, down_load = load_up(*order[0]), load_down(*order[0])
    up_hops, down_hops = {}, {}
    everything = pl.ds(0, 2 * cut)
    for i, (n, half) in enumerate(order):
        first = 8 * n + 4 * half
        for copy in up_come.pop(n, []):
            copy.wait_recv()
        for copy in up_load:
            copy.wait()
        add(up_sum, first, up_keep, 4)
        if n == 1:
            up_hops[half] = send(up_sum.at[pl.ds(first, 4)], up_a.at[pl.ds(4 * half, 4)], "x")
        if i < 3:
            up_load = load_up(*order[i + 1])
        for copy in down_come.pop(n, []):
            copy.wait_recv()
        for copy in down_load:
            copy.wait()
        add_down(2 * n + half, down_keep, everything)
        if n == 1:
            down_hops[half] = send(
                down_sum.at[2 + half, :, :, :, right], down_a.at[half], "y"
            )
        if i < 3:
            down_load = load_down(*order[i + 1])
        if i < 2:
            early_end()
            early_start(("x", "core")[i])
    early_end()
    early_start("zl")
    down_zl = {
        high: send(down_sum.at[:, 1, high, :, left], down_p.at[high], "zl") for high in (1, 0)
    }
    streams_loads = {2: load_stream(2, 0), 1: load_stream(1, 1)}
    res_copy = load(res_in, gstreams_ref.at[3])

    _, blocks, piece, width = q_ref.shape
    rows = 2 * piece
    half_rows = blocks * piece
    length = 2 * half_rows
    lane = lax.broadcasted_iota(jnp.int32, (rows, 128), 1)
    key_index = key_positions(length, blocks, 0)
    choose = (
        lax.div(lax.broadcasted_iota(jnp.int32, (8, 128), 1), 64)
        == lax.broadcasted_iota(jnp.int32, (8, 128), 0)
    ).astype(f32)

    def unturn(x, tables):
        return (
            x * tables[0]
            - pltpu.roll(x, ROT // 2, 1) * tables[1]
            - pltpu.roll(x, 128 - ROT // 2, 1) * tables[2]
        )

    rotary = (cos_ref, rise_ref, fall_ref)
    for copy in attention_loads:
        copy.wait()
    for copy, _ in exchange:
        copy.wait_recv()

    up_y = ready(up_sum.at[pl.ds(4, 4)], up_b, "y")
    down_x = ready(down_sum.at[1, :, :, :, right], down_b, "x")
    down_zh = ready(down_sum.at[:, 0, 1, :, left], down_q, "zh")

    def add_left(high, source):
        def body(place):
            down_sum[place, 0, high, :, left] += source[place]

        each(4, body)

    def hook_0():
        down_hops[1].wait_recv()
        add_down(1, down_a.at[1], right)
        down_x.start()
        up_hops[1].wait_recv()
        add(up_sum, 4, up_a, 4, 4)
        up_y.start()

    def hook_1():
        down_zl[1].wait_recv()
        add_left(1, down_p.at[1])
        down_zh.start()

    def hook_2():
        down_hops[0].wait_recv()
        add_down(0, down_a.at[0], right)

    hooks = (hook_0, hook_1, hook_2)

    def one_pair(pair):
        at = pl.ds(pl.multiple_of(pair * 128, 128), 128)
        dk_ref[...] = jnp.zeros_like(dk_ref)
        dv_ref[...] = jnp.zeros_like(dv_ref)
        keys = k_ref[:, :, :, at].reshape(length, 128)
        values = v_ref[:, :, :, at].reshape(length, 128)
        kt_ref[...] = keys.T

        def one_block(k):
            block = here.block(k)
            queries = q_ref[:, block, :, at].reshape(rows, 128)
            grads = g_ref[k, :, at]
            inner_rows = dot_nt(
                choose, grads.astype(f32) * heads_ref[block, :, at].astype(f32), highest
            )
            allowed = key_index <= allowed_limit(block * rows, rows, prefix_ref[0:1, 0:1], 1)
            dqt = []
            for h in range(2):
                chosen = (lane < 64) if h == 0 else (lane >= 64)
                q_h = jnp.where(chosen, queries, jnp.zeros_like(queries))
                g_h = jnp.where(chosen, grads, jnp.zeros_like(grads))
                scores = dot_nt(keys, q_h)
                probs = jnp.where(allowed, jnp.exp(scores - lse_ref[block, pl.ds(pair * 2 + h, 1), :]), 0.0)
                grad_probs = dot_nt(values, g_h)
                grad_scores = (probs * (grad_probs - inner_rows[h : h + 1, :])).astype(bf16)
                dv_ref[...] += dot_nn(probs.astype(bf16), g_h)
                dk_ref[...] += dot_nn(grad_scores, q_h)
                dqt.append(dot_nn(kt_ref[...], grad_scores)[h * 64 : h * 64 + 64, :])
            dq = jnp.concatenate(dqt, axis=0).T * (HEAD_DIM**-0.5)
            dq = unturn(dq, [r[:, block].reshape(rows, 128) for r in rotary])
            d_ref[0, :, block, :, at] = dq.astype(bf16).reshape(2, piece, 128)

        each(4, one_block)
        dk = unturn(dk_ref[...], [r[...].reshape(length, 128) for r in rotary])
        d_ref[1, :, :, :, at] = dk.astype(bf16).reshape(2, blocks, piece, 128)
        d_ref[2, :, :, :, at] = dv_ref[...].astype(bf16).reshape(2, blocks, piece, 128)
        for i, hook in enumerate(hooks):
            pl.when(pair == i)(hook)

    each(4, one_pair)

    far_half = 1 - here.core
    d_hops = {s: send(d_ref.at[s, far_half], d_got.at[s], "core") for s in (2, 1, 0)}
    early_end()
    early_start("zh")
    late_ref[...] = jnp.zeros_like(late_ref)
    back = {}

    def mine():
        return here.z_low * 2 + here.core

    def one_stream(s, slot):
        for copy in streams_loads[s]:
            copy.wait()
        d_hops[s].wait_recv()
        near = d_ref[s, here.core].reshape(half_rows, width)
        gn = dot_nt(near, weight_ref[slot, 0])
        gn = gn + dot_nt(d_got[s].reshape(half_rows, width), weight_ref[slot, 1])
        gn_ref[...] = gn.reshape(gn_ref.shape)
        gain = gain_ref[s : s + 1, :]

        def step(k):
            block = here.block(k)
            grad, part = norm_back(received_ref[slot, k].astype(f32), gn_ref[block], gain)
            b_ref[s, k] = grad.astype(bf16)
            late_ref[s : s + 1, :] += part

        each(4, step)

    def send_stream(s):
        steps = sends.four(
            lambda k: b_ref.at[s, k], lambda k: gstreams_ref.at[s, mine()], here.back_to
        )
        each(4, steps[0])
        back[s] = steps

    def project_back(s, slot):
        grad = dot_tn(
            normed_ref[slot, 0].reshape(half_rows, -1), d_ref[s, 0].reshape(half_rows, width)
        )
        grad = grad + dot_tn(
            normed_ref[slot, 1].reshape(half_rows, -1), d_ref[s, 1].reshape(half_rows, width)
        )
        grad_ref[...] = grad.astype(bf16)
        for x in range(2):
            for y in range(2):
                for q, z in enumerate(Z_ORDER):
                    for core in range(2):
                        at = pl.multiple_of(here.device(y, x, core, z) * shard, shard)
                        proj_sum[(x * 2 + y) * 4 + q, core, s] = grad_ref[pl.ds(at, shard), :]

    def settle_left():
        down_zl[0].wait_recv()
        add_left(0, down_p.at[0])

    def give_down(lanes, other):
        value = down_sum[0, 0, 0, :, lanes].astype(f32) + other[...].astype(f32)
        gdown_ref[:, lanes] = value[:units]
        gout_ref[:, lanes] = value[units:]

    one_stream(2, 0)
    send_stream(2)
    project_back(2, 0)
    streams_loads[0] = load_stream(0, 0)
    up_hops[0].wait_recv()
    add(up_sum, 0, up_a, 4)
    settle_left()
    one_stream(1, 1)
    early_end()
    up_y.wait_recv()
    add(up_sum, 0, up_b, 4)
    up_zl = send(up_sum.at[pl.ds(2, 2)], up_c, "zl")
    send_stream(1)
    project_back(1, 1)
    one_stream(0, 0)
    project_back(0, 0)
    lanes_of = {"x": pl.ds(0, width // 2), "y": pl.ds(width // 2, width // 2)}
    far_of = {"x": (8, 4), "y": (4, 8)}
    proj_hops = {}

    def proj_send(first, target, start, axis, side):
        lanes = lanes_of[side]
        return send(
            proj_sum.at[pl.ds(first, 4), :, :, :, lanes],
            target.at[pl.ds(start, 4), :, :, :, lanes],
            axis,
        )

    def proj_add(first, source, start, side):
        lanes = lanes_of[side]

        def body(i):
            proj_sum[first + i, :, :, :, lanes] += source[start + i, :, :, :, lanes]

        each(4, body)

    for half in (1, 0):
        for side in ("x", "y"):
            far, other = far_of[side]
            proj_hops[side, half] = proj_send(far + other * half, proj_a, 4 * half, side, side)
    late_start("core")
    down_x.wait_recv()
    add_down(0, down_b, right)
    down_low = send(down_sum.at[0, 1, :, :, right], down_c, "zl")
    late_end()
    late_start("y")
    down_zh.wait_recv()
    add_left(0, down_q)
    left_y = send(down_sum.at[pl.ds(2, 2), 0, 0, :, left], down_r, "y")
    late_end()
    late_start("x")
    up_zl.wait_recv()
    add(up_sum, 0, up_c, 2)
    up_zh = send(up_sum.at[pl.ds(1, 1)], up_d, "zh")
    send_stream(0)
    left_y.wait_recv()
    for place in range(2):
        down_sum[place, 0, 0, :, left] += down_r[place]
    left_x = send(down_sum.at[1, 0, 0, :, left], down_s, "x")
    proj_next = {}
    for side, axis in (("x", "y"), ("y", "x")):
        other = far_of[side][1]
        proj_hops[side, 1].wait_recv()
        proj_add(other, proj_a, 4, side)
        proj_next[side] = proj_send(other, proj_b, 0, axis, side)
    late_end()
    late_start("zl")
    for side in ("x", "y"):
        proj_hops[side, 0].wait_recv()
        proj_add(0, proj_a, 0, side)
    for side in ("x", "y"):
        proj_next[side].wait_recv()
        proj_add(0, proj_b, 0, side)
    proj_zl = send(proj_sum.at[pl.ds(2, 2)], proj_c, "zl")
    left_x.wait_recv()
    give_down(left, down_s)
    down_low.wait_recv()
    for high in range(2):
        down_sum[0, 0, high, :, right] += down_c[high]
    down_high = send(down_sum.at[0, 0, 1, :, right], down_d, "zh")
    up_zh.wait_recv()
    gup_ref[...] = up_sum[0].astype(f32) + up_d[0].astype(f32)
    late_end()
    late_start("zh")
    proj_zl.wait_recv()
    add(proj_sum, 0, proj_c, 2)
    proj_zh = send(proj_sum.at[pl.ds(1, 1)], proj_d, "zh")
    down_high.wait_recv()
    give_down(right, down_d)
    late_end()
    proj_zh.wait_recv()
    add(proj_sum, 0, proj_d, 1)
    proj_core = send(proj_sum.at[0, 1], proj_e, "core")
    for which, source in ((here.core, proj_sum.at[0, 0]), (1 - here.core, proj_e)):
        if source is proj_e:
            proj_core.wait_recv()
        at = pl.ds(pl.multiple_of(which * width, width), width)
        gproj_ref[:, :, at] = source[...].astype(f32)
    for s in range(3):
        each(4, back[s][2])
        each(4, back[s][1])
    for copy, stays in exchange:

        @pl.when(jnp.logical_not(stays))
        def _(copy=copy):
            copy.wait_send()

    res_copy.wait()
    sends.finish()


def finish_body(
    me_ref, streams_ref, proj_ref, up_ref, down_ref, out_ref, early_ref, tiny_ref, late_ref, small_ref,
    streams_out, proj_out, up_out, down_out, out_out, first_out, second_out, bias_out, gains_out, loss_out,
):
    streams_out[...] = streams_ref[...]

    @pl.when(pl.program_id(0) == 0)
    def _():
        for source, target in (
            (proj_ref, proj_out),
            (up_ref, up_out),
            (down_ref, down_out),
            (out_ref, out_out),
        ):
            target[...] = source[...]
        shard, mixw = first_out.shape
        width = late_ref.shape[1]
        near = early_ref.shape[1]
        span = tiny_ref.shape[1]

        def chosen(size, first):
            column = lax.broadcasted_iota(jnp.int32, (shard, size), 1)
            row = lax.broadcasted_iota(jnp.int32, (shard, size), 0)
            return (column == row + first).astype(f32)

        mine = chosen(near, lax.rem(me_ref[0] * shard, near))
        first_out[...] = dot_nt(mine, early_ref[...], highest)[:, 0:mixw]
        gains_out[3:5, :] = dot_nt(early_ref[span : span + 8, :], mine, highest)[0:2]
        gains_out[0:3, :] = dot_nt(late_ref[...], chosen(width, me_ref[0] * shard), highest)[0:3]
        second_out[...] = tiny_ref[0:mixw, 0:mixw]
        bias_out[...] = tiny_ref[span : span + 1, 0:mixw]
        loss_out[...] = tiny_ref[span + 1 : span + 2, 0:1] / (4.0 * width * small_ref[7:8, 0:1])


def rotary_lanes(length, piece):
    lane = jnp.arange(128, dtype=jnp.int32) % HEAD_DIM
    step = (lane % (ROT // 2)).astype(f32)
    inverse = jnp.exp(step * (-2.0 * math.log(10000.0) / ROT))
    angles = jnp.arange(length, dtype=jnp.int32).astype(f32)[:, None] * inverse[None, :]
    cosine = jnp.where(lane < ROT, jnp.cos(angles), 1.0)
    sine = jnp.sin(angles)
    up = jnp.where((lane >= ROT // 2) & (lane < ROT), sine, 0.0)
    down = jnp.where(lane < ROT // 2, -sine, 0.0)
    return [
        t.reshape(-1, 2, piece, 128).transpose(1, 0, 2, 3) for t in (cosine, up, down)
    ]


def local_fast(
    streams, history, teacher, prefix, valid_mask, loss_scale, projections, attention_out,
    up_weight, down_weight, mixer_first, mixer_second, mixer_bias, gains,
):
    lines = lax.axis_size("ctx")
    count = lax.axis_size("dp") * lines
    place = lax.axis_index("ctx")
    group = lax.axis_index("dp")
    me = group * lines + place
    half = group % 2
    mine = 2 * (place % 2) + half
    seqs, rows, width = streams.shape[1:]
    tokens = seqs * rows
    piece = rows // 2
    length = rows * lines
    features = width // 2
    hidden_units = down_weight.shape[0] * count
    past = history.shape[0]
    count_of_streams = teacher.shape[0]
    mixw = mixer_bias.shape[0]
    span = 64

    ids = jnp.stack([place, half, mine, mine, me]).astype(jnp.int32)
    shard = width // count
    unit_shard = hidden_units // count

    smem = pl.BlockSpec(memory_space=pltpu.SMEM)
    anywhere = pl.BlockSpec(memory_space=pl.ANY)
    proj_shape = (count // 2, 2, 3, shard, features)
    tables = rotary_lanes(length, piece)
    row_shape = (3, 4, piece, width)
    normed_shape = (3, 2, lines, piece, width)
    wide_shape = (2, lines, piece, features)
    heads_shape = (lines, rows, features)

    def array(shape, dtype=bf16):
        return jax.ShapeDtypeStruct(shape, dtype)

    (
        received, normed, proj, proj_other, up_all, down_all, small, first_t, prefix_rows,
        queries, keys, values, heads_seq, lse, heads,
    ) = pl.pallas_call(
        front_body,
        in_specs=[smem, anywhere] + [vmem()] * 10,
        out_specs=[anywhere] * 6 + [vmem()] * 3 + [anywhere] * 4 + [vmem(), anywhere],
        out_shape=[
            array(row_shape),
            array(normed_shape),
            array((3, width, features)),
            array((3, width, features)),
            array((count, shard, hidden_units)),
            array((count, unit_shard + shard, width)),
            array((8, width), f32),
            array((span, width)),
            array((8, 128), jnp.int32),
            array(wide_shape),
            array(wide_shape),
            array(wide_shape),
            array(heads_shape),
            array((lines, 8, rows), f32),
            array((4, rows, features)),
        ],
        scratch_shapes=[
            pltpu.VMEM(row_shape, bf16),
            pltpu.VMEM(normed_shape, bf16),
            pltpu.VMEM(proj_shape, bf16),
            pltpu.VMEM((3, width, features), bf16),
            pltpu.VMEM(wide_shape, bf16),
            pltpu.VMEM(wide_shape, bf16),
            pltpu.VMEM(wide_shape, bf16),
            pltpu.VMEM(heads_shape, bf16),
            pltpu.VMEM((5, 8, width), f32),
            pltpu.VMEM((5, span, width), bf16),
            pltpu.VMEM((8, 128), jnp.int32),
            pltpu.VMEM((8, 128), jnp.int32),
            pltpu.SemaphoreType.DMA((24,)),
            pltpu.SemaphoreType.DMA((112,)),
            pltpu.SemaphoreType.DMA((112,)),
        ],
        compiler_params=params(collective_id=0, has_side_effects=True),
        name="front",
    )(
        prefix,
        streams.reshape(streams.shape[0], 2 * seqs, piece, width),
        projections, up_weight, down_weight, attention_out, gains, mixer_first, valid_mask, *tables,
    )
    gain_full = small
    tile = 512
    tiles = hidden_units // tile
    token_shape = (seqs, rows, width)

    def fixed(shape, index=None):
        index = index or (0,) * len(shape)
        return pl.BlockSpec(shape, lambda i, *_: index)

    def up_column(i, ids):
        distance = lax.rem(lax.div(i, 2), 2) * 4 + lax.rem(i, 2) * 2 + lax.div(i, 4)
        return (0, 0, jnp.bitwise_xor(lax.div(ids[4], 4), distance))

    def down_block(p):
        return lambda i, *_: (jnp.clip(i - 2 * p, 0, 1), 0, 0)

    weight_specs = [
        pl.BlockSpec((count, shard, tile), up_column),
        pl.BlockSpec((4, unit_shard, width), lambda i, *_: (i, 0, 0)),
    ]
    out_weight_spec = pl.BlockSpec(
        (count, shard, width), lambda i, *_: (0, unit_shard // shard, 0)
    )
    tile_specs = [pl.BlockSpec((8, shard, tile), up_column)] * 4
    tile_specs += [pl.BlockSpec((4, unit_shard, width), down_block(p)) for p in range(4)]

    hidden, normed_mlp, active, slope, layer_out = pl.pallas_call(
        mlp_forward_body,
        grid_spec=pltpu.PrefetchScalarGridSpec(
            num_scalar_prefetch=1,
            grid=(tiles,),
            in_specs=[
                fixed((4, rows, features)),
                fixed((1,) + token_shape, (3, 0, 0, 0)),
                fixed((8, width)),
            ]
            + weight_specs
            + [out_weight_spec],
            out_specs=[
                fixed(token_shape),
                fixed(token_shape),
                pl.BlockSpec((tokens, tile), lambda i, *_: (0, i)),
                pl.BlockSpec((tokens, tile), lambda i, *_: (0, i)),
                fixed(token_shape),
            ],
            scratch_shapes=[
                pltpu.VMEM((width, width), bf16),
                pltpu.VMEM((width, tile), bf16),
                pltpu.VMEM((tile, width), bf16),
            ],
        ),
        out_shape=[
            jax.ShapeDtypeStruct(token_shape, f32),
            jax.ShapeDtypeStruct(token_shape, bf16),
            jax.ShapeDtypeStruct((tokens, hidden_units), bf16),
            jax.ShapeDtypeStruct((tokens, hidden_units), bf16),
            jax.ShapeDtypeStruct(token_shape, f32),
        ],
        compiler_params=params(),
        name="mlp_forward",
    )(ids, heads, streams, gain_full, up_all, down_all, down_all)

    block = 128
    next_streams, grad_history, grad_layer, g_first, g_second, stats, g_gain_mix = pl.pallas_call(
        mixer_body,
        grid=(tokens // block,),
        in_specs=[
            smem,
            pl.BlockSpec((block, width), lambda i: (i, 0)),
            pl.BlockSpec((past, block, width), lambda i: (0, i, 0)),
            pl.BlockSpec((count_of_streams, block, width), lambda i: (0, i, 0)),
            pl.BlockSpec((1, 1, block), lambda i: (i, 0, 0)),
            fixed((8, width)),
            fixed((span, width)),
            fixed((mixw, mixw)),
            fixed((1, mixw)),
        ],
        out_specs=[
            pl.BlockSpec((count_of_streams, block, width), lambda i: (0, i, 0)),
            pl.BlockSpec((past, block, width), lambda i: (0, i, 0)),
            pl.BlockSpec((block, width), lambda i: (i, 0)),
            fixed((span, width)),
            fixed((span, span)),
            fixed((8, span)),
            fixed((1, width)),
        ],
        out_shape=[
            jax.ShapeDtypeStruct((count_of_streams, tokens, width), bf16),
            jax.ShapeDtypeStruct((past, tokens, width), bf16),
            jax.ShapeDtypeStruct((tokens, width), f32),
            jax.ShapeDtypeStruct((span, width), f32),
            jax.ShapeDtypeStruct((span, span), f32),
            jax.ShapeDtypeStruct((8, span), f32),
            jax.ShapeDtypeStruct((1, width), f32),
        ],
        scratch_shapes=[
            pltpu.VMEM((mixw, block, 128), f32),
            pltpu.VMEM((mixw, block, 128), f32),
            pltpu.VMEM((count_of_streams, block, width), f32),
            pltpu.VMEM((block, 1), f32),
            pltpu.VMEM((span, span), f32),
            pltpu.VMEM((1, span), f32),
        ],
        compiler_params=params(),
        name="mixer",
    )(
        loss_scale,
        layer_out.reshape(tokens, width),
        history.reshape(past, tokens, width),
        teacher.reshape(count_of_streams, tokens, width),
        valid_mask.reshape(-1, 1, block),
        gain_full,
        first_t,
        mixer_second,
        mixer_bias.reshape(1, mixw),
    )

    *g_ups, gd0, gd1, gd2, gd3, g_normed = pl.pallas_call(
        mlp_backward_body,
        grid_spec=pltpu.PrefetchScalarGridSpec(
            num_scalar_prefetch=1,
            grid=(tiles,),
            in_specs=[
                fixed(token_shape),
                pl.BlockSpec((tokens, tile), lambda i, *_: (0, i)),
                pl.BlockSpec((tokens, tile), lambda i, *_: (0, i)),
                fixed(token_shape),
            ]
            + weight_specs,
            out_specs=tile_specs + [fixed(token_shape)],
            scratch_shapes=[
                pltpu.VMEM(token_shape, bf16),
                pltpu.VMEM((width, tokens), bf16),
                pltpu.VMEM((width, tile), bf16),
                pltpu.VMEM((tile, width), bf16),
                pltpu.VMEM((width, tile), bf16),
            ],
        ),
        out_shape=[jax.ShapeDtypeStruct((8, shard, hidden_units), bf16)] * 4
        + [jax.ShapeDtypeStruct((8, unit_shard, width), bf16)] * 4
        + [jax.ShapeDtypeStruct(token_shape, f32)],
        compiler_params=params(),
        name="mlp_backward",
    )(ids, grad_layer.reshape(token_shape), active, slope, normed_mlp, up_all, down_all)
    g_downs = [gd0, gd1, gd2, gd3]

    hidden_results = pl.pallas_call(
        hidden_backward_body,
        grid_spec=pltpu.PrefetchScalarGridSpec(
            num_scalar_prefetch=1,
            grid=(1,),
            in_specs=[fixed(token_shape)] * 3
            + [fixed((4, rows, features)), fixed((8, width)), out_weight_spec],
            out_specs=[fixed(token_shape)]
            + [fixed((rows, features))] * 4
            + [fixed((8, shard, width))] * 4
            + [fixed((1, width))],
            scratch_shapes=[pltpu.VMEM((width, width), bf16), pltpu.VMEM((width, width), f32)],
        ),
        out_shape=[jax.ShapeDtypeStruct(token_shape, bf16)]
        + [jax.ShapeDtypeStruct((rows, features), bf16)] * 4
        + [jax.ShapeDtypeStruct((8, shard, width), bf16)] * 4
        + [jax.ShapeDtypeStruct((1, width), f32)],
        compiler_params=params(),
        name="hidden_backward",
    )(ids, grad_layer.reshape(token_shape), g_normed, hidden, heads, gain_full, down_all)
    g_res, gh0, gh1, gh2, gh3, go0, go1, go2, go3, g_gain_mlp = hidden_results

    down_block_shape = (unit_shard + shard, width)
    down_half = (unit_shard + shard, width // 2)
    slot_shape = (2, lines, piece, width)

    def buffer(shape, dtype=bf16):
        return pltpu.VMEM(shape, dtype)

    grad_streams, grad_projections, sum_up, sum_down, sum_out, early, tiny, late = pl.pallas_call(
        back_body,
        in_specs=[vmem()]
        + [anywhere] * 4
        + [vmem()] * 4
        + [anywhere] * 4
        + [vmem()] * 6
        + [anywhere] * 17,
        out_specs=[anywhere] + [vmem()] * 7,
        out_shape=[
            array((streams.shape[0], 2 * seqs, piece, width)),
            array((3, shard, width), f32),
            array((shard, hidden_units), f32),
            array((unit_shard, width), f32),
            array((shard, width), f32),
            array((span + 8, width // 8), f32),
            array((span + 8, span), f32),
            array((8, width), f32),
        ],
        scratch_shapes=[
            buffer(wide_shape),
            buffer(wide_shape),
            buffer(wide_shape),
            buffer(heads_shape),
            buffer((4, rows, features)),
            buffer((3,) + wide_shape),
            buffer((3,) + wide_shape[1:]),
            buffer((length, 128), f32),
            buffer((length, 128), f32),
            buffer((128, length)),
            buffer((2,) + slot_shape),
            buffer((2,) + row_shape[1:]),
            buffer((2, 2, width, features)),
            buffer((lines, piece, width), f32),
            buffer(row_shape),
            buffer((width, features)),
            buffer((4, shard, hidden_units)),
            buffer((2, 2) + down_block_shape),
            buffer((16, shard, hidden_units)),
            buffer((8, shard, hidden_units)),
            buffer((4, shard, hidden_units)),
            buffer((2, shard, hidden_units)),
            buffer((1, shard, hidden_units)),
            buffer((4, 2, 2) + down_block_shape),
            buffer((2, 2, 2) + down_half),
            buffer((2, 2) + down_half),
            buffer((2,) + down_half),
            buffer(down_half),
            buffer((2, 4) + down_half),
            buffer((4,) + down_half),
            buffer((2,) + down_half),
            buffer(down_half),
            buffer(proj_shape),
            buffer((8,) + proj_shape[1:]),
            buffer((4,) + proj_shape[1:]),
            buffer((2,) + proj_shape[1:]),
            buffer((1,) + proj_shape[1:]),
            buffer(proj_shape[2:]),
            buffer((span + 8, width), f32),
            buffer((span + 8, width // 2), f32),
            buffer((span + 8, width // 4), f32),
            buffer((span + 8, width // 8), f32),
            buffer((2, span + 8, width // 8), f32),
            buffer((5, span + 8, span), f32),
            buffer((5, 8, width), f32),
            pltpu.SemaphoreType.DMA((40,)),
            pltpu.SemaphoreType.DMA((64,)),
            pltpu.SemaphoreType.DMA((64,)),
        ],
        compiler_params=pltpu.CompilerParams(
            vmem_limit_bytes=63 * 1024 * 1024, collective_id=1, has_side_effects=True
        ),
        name="back",
    )(
        prefix_rows,
        queries, keys, values, heads_seq,
        lse,
        *tables,
        normed, received, proj, proj_other, gain_full, g_first, g_gain_mlp, g_gain_mix, g_second, stats,
        g_res.reshape(2 * seqs, piece, width),
        gh0, gh1, gh2, gh3, *g_ups,
        *[g.reshape(2, 2, 2, -1, width) for g in (*g_downs, go0, go1, go2, go3)],
    )
    quarters = 2 * seqs
    stream_block = pl.BlockSpec((1, quarters, piece, width), lambda i: (i, 0, 0, 0))
    whole_shapes = [
        ((3, shard, width), f32),
        ((shard, hidden_units), f32),
        ((unit_shard, width), f32),
        ((shard, width), f32),
    ]
    small_shapes = [((shard, mixw), f32), ((mixw, mixw), f32), ((1, mixw), f32), ((5, shard), f32), ((1, 1), f32)]
    (
        grad_streams, grad_projections, sum_up, sum_down, sum_out,
        grad_first, grad_second, grad_bias, grad_gains, mean_loss,
    ) = pl.pallas_call(
        finish_body,
        grid=(streams.shape[0],),
        in_specs=[smem, stream_block]
        + [fixed(s) for s, _ in whole_shapes]
        + [
            fixed((span + 8, width // 8)),
            fixed((span + 8, span)),
            fixed((8, width)),
            fixed((8, width)),
        ],
        out_specs=[stream_block] + [fixed(s) for s, _ in whole_shapes + small_shapes],
        out_shape=[array((streams.shape[0], quarters, piece, width))]
        + [array(*s) for s in whole_shapes + small_shapes],
        compiler_params=params(),
        name="finish",
    )(
        me.reshape(1).astype(jnp.int32),
        grad_streams, grad_projections, sum_up, sum_down, sum_out, early, tiny, late, small,
    )
    return (
        next_streams.reshape(teacher.shape),
        mean_loss.reshape(()),
        grad_streams.reshape(streams.shape),
        grad_history.reshape(history.shape),
        grad_projections,
        sum_out,
        sum_up,
        sum_down,
        grad_first,
        grad_second,
        grad_bias.reshape(mixw),
        grad_gains,
    )


def layer_norm(values, gain_row):
    centered = values - jnp.mean(values, axis=-1, keepdims=True)
    return (
        centered
        * lax.rsqrt(jnp.mean(centered * centered, axis=-1, keepdims=True) + epsilon)
        * gain_row
    )


def rms_norm(values, gain_row):
    return (
        values * lax.rsqrt(jnp.mean(values * values, axis=-1, keepdims=True) + epsilon) * gain_row
    )


def gelu_exact(values):
    return jax.nn.gelu(values, approximate=False)


def rotary_tables(positions):
    frequency_steps = jnp.arange(ROT // 2).astype(positions.dtype)
    inverse = jnp.exp(frequency_steps * (-2.0 * math.log(10000.0) / ROT))
    angles = positions[:, None] * inverse[None, :]
    return (jnp.cos(angles)[:, None, :], jnp.sin(angles)[:, None, :])


def rotate(values, cosine_table, sine_table, direction):
    row_count = values.shape[0]
    shaped = values.reshape(row_count, HEADS, HEAD_DIM)
    half_rot = ROT // 2
    first_half = shaped[:, :, :half_rot]
    second_half = shaped[:, :, half_rot:ROT]
    remainder = shaped[:, :, ROT:]
    turned_first = first_half * cosine_table - direction * second_half * sine_table
    turned_second = second_half * cosine_table + direction * first_half * sine_table
    return jnp.concatenate([turned_first, turned_second, remainder], axis=-1).reshape(row_count, -1)


def masked_scores(query_heads, key_heads, query_index, key_index, prefix_len):
    scores = jnp.einsum(
        "qhd,khd->hqk", query_heads, key_heads, preferred_element_type=jnp.float32
    ) * HEAD_DIM ** (-0.5)
    allowed = (key_index[None, :] <= query_index[:, None]) | (key_index[None, :] < prefix_len)
    return jnp.where(allowed[None], scores, -1e30)


def local_plain(
    streams,
    history,
    teacher,
    prefix,
    valid_mask,
    loss_scale,
    projections,
    attention_out,
    up_weight,
    down_weight,
    mixer_first,
    mixer_second,
    mixer_bias,
    gains,
):
    micro_count = streams.shape[1]
    row_count = streams.shape[2]
    model_width = streams.shape[3]
    length = row_count * lax.axis_size("ctx")
    query_index = lax.axis_index("ctx") * row_count + jnp.arange(row_count, dtype=jnp.int32)
    key_index = jnp.arange(length, dtype=jnp.int32)
    cosine_table, sine_table = rotary_tables(query_index.astype(jnp.float32))
    score_scale = HEAD_DIM ** (-0.5)
    valid_float = valid_mask.astype(jnp.float32)
    token_total = lax.psum(jnp.sum(valid_float), ("dp", "ctx"))
    factor = loss_scale[0] * 2.0 / (4.0 * model_width * token_total)

    def one_batch(totals, number):
        (
            kept_projections,
            kept_attention,
            kept_gains,
            kept_up,
            kept_down,
            kept_first,
            kept_second,
            kept_bias,
            kept_loss,
        ) = totals
        stream_block = lax.dynamic_index_in_dim(streams, number, 1, keepdims=False)
        past_outputs = lax.dynamic_index_in_dim(history, number, 1, keepdims=False)
        target = lax.dynamic_index_in_dim(teacher, number, 1, keepdims=False).astype(jnp.float32)
        prefix_len = lax.dynamic_index_in_dim(prefix, number, 0, keepdims=False)
        valid_row = lax.dynamic_index_in_dim(valid_float, number, 0, keepdims=False)
        proj_full, out_full, gain_low, up_full, down_full, first_full = (
            lax.all_gather(projections, ("dp", "ctx"), axis=1, tiled=True),
            lax.all_gather(attention_out, ("dp", "ctx"), axis=0, tiled=True),
            lax.all_gather(gains, ("dp", "ctx"), axis=1, tiled=True),
            lax.all_gather(up_weight, ("dp", "ctx"), axis=0, tiled=True),
            lax.all_gather(down_weight, ("dp", "ctx"), axis=0, tiled=True),
            lax.all_gather(mixer_first, ("dp", "ctx"), axis=0, tiled=True),
        )
        gain_full = gain_low.astype(jnp.float32)
        inputs = stream_block.astype(jnp.float32)
        gain_three = gain_full[:3, None, :]
        normed_low = layer_norm(inputs[:3], gain_three).astype(jnp.bfloat16)
        projected = jnp.einsum(
            "std,sde->ste", normed_low, proj_full, preferred_element_type=jnp.float32
        )
        query_heads = (
            rotate(projected[0], cosine_table, sine_table, 1.0)
            .astype(jnp.bfloat16)
            .reshape(row_count, HEADS, HEAD_DIM)
        )
        key_low = rotate(projected[1], cosine_table, sine_table, 1.0).astype(jnp.bfloat16)
        value_low = projected[2].astype(jnp.bfloat16)
        all_keys, all_values = (
            lax.all_gather(key_low, "ctx", axis=0, tiled=True),
            lax.all_gather(value_low, "ctx", axis=0, tiled=True),
        )
        key_heads = all_keys.reshape(length, HEADS, HEAD_DIM)
        value_heads = all_values.reshape(length, HEADS, HEAD_DIM)
        scores = masked_scores(query_heads, key_heads, query_index, key_index, prefix_len)
        row_max = jnp.max(scores, axis=-1, keepdims=True)
        log_total = row_max + jnp.log(jnp.sum(jnp.exp(scores - row_max), axis=-1, keepdims=True))
        probs_low = jnp.exp(scores - log_total).astype(jnp.bfloat16)
        heads_low = (
            jnp.einsum("hqk,khd->qhd", probs_low, value_heads, preferred_element_type=jnp.float32)
            .reshape(row_count, model_width)
            .astype(jnp.bfloat16)
        )
        hidden = inputs[3] + jnp.dot(heads_low, out_full, preferred_element_type=jnp.float32)
        normed_mlp = layer_norm(hidden, gain_full[3]).astype(jnp.bfloat16)
        upper = jnp.dot(normed_mlp, up_full, preferred_element_type=jnp.float32)
        activated = gelu_exact(upper).astype(jnp.bfloat16)
        layer_out = hidden + jnp.dot(activated, down_full, preferred_element_type=jnp.float32)
        normed_mix = rms_norm(layer_out, gain_full[4]).astype(jnp.bfloat16)
        mix_hidden = jnp.dot(normed_mix, first_full, preferred_element_type=jnp.float32)
        mix_active = gelu_exact(mix_hidden)
        coeff = jnp.dot(mix_active, mixer_second, precision=highest) + mixer_bias
        coeff_grid = coeff.reshape(row_count, 4, -1)
        outputs_all = jnp.concatenate([past_outputs.astype(jnp.float32), layer_out[None]], axis=0)
        next_block = jnp.einsum("tsj,jtd->std", coeff_grid, outputs_all, precision=highest)
        difference = next_block - target
        loss_part = jnp.sum(jnp.sum(difference * difference, axis=(0, 2)) * valid_row) / (
            4.0 * model_width * token_total
        )
        grad_next = factor * valid_row[None, :, None] * difference
        grad_coeff = jnp.einsum("std,jtd->tsj", grad_next, outputs_all, precision=highest).reshape(
            row_count, -1
        )
        grad_outputs = jnp.einsum("tsj,std->jtd", coeff_grid, grad_next, precision=highest)
        grad_past = grad_outputs[:-1].astype(jnp.bfloat16)
        grad_second = jnp.dot(mix_active.T, grad_coeff, precision=highest)
        grad_bias = jnp.sum(grad_coeff, axis=0)
        grad_active = jnp.dot(grad_coeff, mixer_second.T, precision=highest)
        gelu_mix_back = jax.vjp(gelu_exact, mix_hidden)[1]
        grad_mix = gelu_mix_back(grad_active)[0].astype(jnp.bfloat16)
        grad_first = jnp.einsum(
            "td,tm->dm", normed_mix, grad_mix, preferred_element_type=jnp.float32
        )
        grad_normed_mix = jnp.einsum(
            "tm,dm->td", grad_mix, first_full, preferred_element_type=jnp.float32
        )
        rms_back = jax.vjp(rms_norm, layer_out, gain_full[4])[1]
        grad_layer_mix, grad_gain_mix = rms_back(grad_normed_mix)
        grad_layer = grad_outputs[-1] + grad_layer_mix
        grad_branch = grad_layer.astype(jnp.bfloat16)
        grad_down = jnp.einsum(
            "tf,td->fd", activated, grad_branch, preferred_element_type=jnp.float32
        )
        grad_active_up = jnp.einsum(
            "td,fd->tf", grad_branch, down_full, preferred_element_type=jnp.float32
        )
        gelu_up_back = jax.vjp(gelu_exact, upper)[1]
        grad_upper = gelu_up_back(grad_active_up)[0].astype(jnp.bfloat16)
        grad_up = jnp.einsum(
            "td,tf->df", normed_mlp, grad_upper, preferred_element_type=jnp.float32
        )
        grad_normed_mlp = jnp.einsum(
            "tf,df->td", grad_upper, up_full, preferred_element_type=jnp.float32
        )
        down_shard, first_shard, up_shard = (
            lax.psum_scatter(grad_down, ("dp", "ctx"), scatter_dimension=0, tiled=True),
            lax.psum_scatter(grad_first, ("dp", "ctx"), scatter_dimension=0, tiled=True),
            lax.psum_scatter(grad_up, ("dp", "ctx"), scatter_dimension=0, tiled=True),
        )
        down_next = kept_down + down_shard
        norm_mlp_back = jax.vjp(layer_norm, hidden, gain_full[3])[1]
        grad_hidden_mlp, grad_gain_mlp = norm_mlp_back(grad_normed_mlp)
        grad_hidden = grad_layer + grad_hidden_mlp
        grad_attn = grad_hidden.astype(jnp.bfloat16)
        grad_attention = jnp.einsum(
            "td,te->de", heads_low, grad_attn, preferred_element_type=jnp.float32
        )
        grad_heads = jnp.einsum(
            "te,de->td", grad_attn, out_full, preferred_element_type=jnp.float32
        ).astype(jnp.bfloat16)
        grad_head_grid = grad_heads.reshape(row_count, HEADS, HEAD_DIM)
        scores_again = masked_scores(query_heads, key_heads, query_index, key_index, prefix_len)
        probs_exact = jnp.exp(scores_again - log_total)
        probs_again = probs_exact.astype(jnp.bfloat16)
        grad_probs = jnp.einsum(
            "qhd,khd->hqk", grad_head_grid, value_heads, preferred_element_type=jnp.float32
        )
        row_inner = jnp.sum(probs_exact * grad_probs, axis=-1, keepdims=True)
        grad_scores = (probs_exact * (grad_probs - row_inner)).astype(jnp.bfloat16)
        grad_queries = (
            jnp.einsum(
                "hqk,khd->qhd", grad_scores, key_heads, preferred_element_type=jnp.float32
            ).reshape(row_count, model_width)
            * score_scale
        )
        grad_key_part = (
            jnp.einsum("hqk,qhd->khd", grad_scores, query_heads, preferred_element_type=jnp.float32)
            * score_scale
        )
        grad_value_part = jnp.einsum(
            "hqk,qhd->khd", probs_again, grad_head_grid, preferred_element_type=jnp.float32
        )
        key_grads = lax.psum_scatter(
            jnp.concatenate(
                [
                    grad_key_part.reshape(row_count * lax.axis_size("ctx"), -1),
                    grad_value_part.reshape(row_count * lax.axis_size("ctx"), -1),
                ],
                axis=-1,
            ).astype(jnp.bfloat16),
            "ctx",
            scatter_dimension=0,
            tiled=True,
        ).astype(jnp.float32)
        grad_query_low = rotate(grad_queries, cosine_table, sine_table, -1.0).astype(jnp.bfloat16)
        grad_key_low = rotate(key_grads[:, :model_width], cosine_table, sine_table, -1.0).astype(
            jnp.bfloat16
        )
        grad_value_low = key_grads[:, model_width:].astype(jnp.bfloat16)
        grad_projected = jnp.stack([grad_query_low, grad_key_low, grad_value_low])
        grad_proj = jnp.einsum(
            "std,ste->sde", normed_low, grad_projected, preferred_element_type=jnp.float32
        )
        grad_normed = jnp.einsum(
            "ste,sde->std", grad_projected, proj_full, preferred_element_type=jnp.float32
        )
        norm_three_back = jax.vjp(layer_norm, inputs[:3], gain_three)[1]
        grad_inputs_three, grad_gain_three = norm_three_back(grad_normed)
        grad_gain_all = jnp.concatenate(
            [grad_gain_three.reshape(3, -1), grad_gain_mlp[None], grad_gain_mix[None]], axis=0
        )
        proj_shard, attention_shard, gain_shard = (
            lax.psum_scatter(grad_proj, ("dp", "ctx"), scatter_dimension=1, tiled=True),
            lax.psum_scatter(grad_attention, ("dp", "ctx"), scatter_dimension=0, tiled=True),
            lax.psum_scatter(grad_gain_all, ("dp", "ctx"), scatter_dimension=1, tiled=True),
        )
        grad_block = jnp.concatenate([grad_inputs_three, grad_hidden[None]], axis=0).astype(
            jnp.bfloat16
        )
        new_totals = (
            kept_projections + proj_shard,
            kept_attention + attention_shard,
            kept_gains + gain_shard,
            kept_up + up_shard,
            down_next,
            kept_first + first_shard,
            kept_second + grad_second,
            kept_bias + grad_bias,
            kept_loss + loss_part,
        )
        return (new_totals, (next_block.astype(jnp.bfloat16), grad_block, grad_past))

    down_start = jnp.zeros(down_weight.shape, jnp.float32)
    start_totals = (
        jnp.zeros(projections.shape, jnp.float32),
        jnp.zeros(attention_out.shape, jnp.float32),
        jnp.zeros(gains.shape, jnp.float32),
        jnp.zeros(up_weight.shape, jnp.float32),
        down_start,
        jnp.zeros(mixer_first.shape, jnp.float32),
        jnp.zeros(mixer_second.shape, jnp.float32),
        jnp.zeros(mixer_bias.shape, jnp.float32),
        jnp.zeros((), jnp.float32),
    )
    final_totals, stacked = lax.scan(
        one_batch, start_totals, jnp.arange(micro_count, dtype=jnp.int32)
    )
    (
        sum_projections,
        sum_attention,
        sum_gains,
        sum_up,
        sum_down,
        sum_first,
        sum_second,
        sum_bias,
        sum_loss,
    ) = final_totals
    grad_second_all, grad_bias_all, loss_all = lax.psum(
        (sum_second, sum_bias, sum_loss), ("dp", "ctx")
    )
    next_streams = jnp.moveaxis(stacked[0], 0, 1)
    grad_streams = jnp.moveaxis(stacked[1], 0, 1)
    grad_history = jnp.moveaxis(stacked[2], 0, 1)
    return (
        next_streams,
        loss_all,
        grad_streams,
        grad_history,
        sum_projections,
        sum_attention,
        sum_up,
        sum_down,
        sum_first,
        grad_second_all,
        grad_bias_all,
        sum_gains,
    )


def fits(mesh):
    return mesh.shape["ctx"] == 4 and mesh.shape["dp"] == 8


def solution(mesh):
    specs = dict(
        in_specs=(
            P(None, "dp", "ctx", None),
            P(None, "dp", "ctx", None),
            P(None, "dp", "ctx", None),
            P("dp"),
            P("dp", "ctx"),
            P(),
            P(None, ("dp", "ctx"), None),
            P(("dp", "ctx"), None),
            P(("dp", "ctx"), None),
            P(("dp", "ctx"), None),
            P(("dp", "ctx"), None),
            P(),
            P(),
            P(None, ("dp", "ctx")),
        ),
        out_specs=(
            P(None, "dp", "ctx", None),
            P(),
            P(None, "dp", "ctx", None),
            P(None, "dp", "ctx", None),
            P(None, ("dp", "ctx"), None),
            P(("dp", "ctx"), None),
            P(("dp", "ctx"), None),
            P(("dp", "ctx"), None),
            P(("dp", "ctx"), None),
            P(),
            P(),
            P(None, ("dp", "ctx")),
        ),
        check_vma=False,
    )

    def chosen(*arrays):
        fast = fits(mesh) and arrays[0].shape[1] == 2 * mesh.shape["dp"]
        return jax.shard_map(local_fast if fast else local_plain, mesh=mesh, **specs)(*arrays)

    return chosen
```

```python
import functools
import math

import jax
import jax.numpy as jnp
from jax import lax
from jax.experimental import pallas as pl
from jax.experimental.pallas import tpu as pltpu
from jax.sharding import PartitionSpec as P

HEADS = 16
HEAD_DIM = 64
ROT = 16
AXES = ("dp", "ctx")

highest = lax.Precision.HIGHEST
epsilon = 1e-05
f32 = jnp.float32
bf16 = jnp.bfloat16
VMEM_BYTES = 60 * 1024 * 1024


def dot_nn(a, b, precision=None):
    return lax.dot_general(
        a, b, (((1,), (0,)), ((), ())), precision=precision, preferred_element_type=f32
    )


def dot_nt(a, b, precision=None):
    return lax.dot_general(
        a, b, (((1,), (1,)), ((), ())), precision=precision, preferred_element_type=f32
    )


def dot_tn(a, b, precision=None):
    return lax.dot_general(
        a, b, (((0,), (0,)), ((), ())), precision=precision, preferred_element_type=f32
    )


def normal_cdf(v):
    z = jnp.abs(v) * math.sqrt(0.5)
    t = 1.0 / (1.0 + 0.39 * z)
    bell = jnp.exp(-0.5 * v * v)
    poly = -0.22760540438261295
    for c in (
        0.8869388009365644,
        -0.6358388689155755,
        0.649907738051149,
        0.09125094908545259,
        0.23534677935551734,
    ):
        poly = poly * t + c
    half_tail = (0.5 * poly) * t * bell
    return jnp.where(v < 0.0, half_tail, 1.0 - half_tail), bell


def gelu_pair(v):
    cdf, bell = normal_cdf(v)
    return v * cdf, cdf + v * bell * (1.0 / math.sqrt(2.0 * math.pi))


def vmem(block=None, index_map=None):
    if block is None:
        return pl.BlockSpec(memory_space=pltpu.VMEM)
    return pl.BlockSpec(block, index_map)


def params(**kw):
    return pltpu.CompilerParams(vmem_limit_bytes=VMEM_BYTES, **kw)


Z_ORDER = (0, 2, 1, 3)


UP_BITS = (8, 16)
DOWN_BITS = (16, 8)


def gathered_from(me, place, outer):
    distance = 4 * (place // 16) + outer[0] * (place // 8 % 2) + outer[1] * (place // 4 % 2)
    return jnp.bitwise_xor(me, distance + Z_ORDER[place % 4])


def place_rows(me, ref, outer, out_ref):
    rows = ref.shape[-2]
    for place in range(ref.shape[0]):
        device = gathered_from(me, place, outer)
        out_ref[pl.ds(pl.multiple_of(device * rows, rows), rows), :] = ref[place]


def take_rows(me, from_ref, outer, refs):
    rows = refs[0].shape[-2]
    each_has = refs[0].shape[0]
    for place in range(each_has * len(refs)):
        device = gathered_from(me, place, outer)
        refs[place // each_has][place % each_has] = from_ref[
            pl.ds(pl.multiple_of(device * rows, rows), rows), :
        ]


def place_tile(me, all_up_ref, some_down_ref, up_ref, down_ref):
    place_rows(me, all_up_ref, UP_BITS, up_ref)
    rows = some_down_ref.shape[1]
    for q, z in enumerate(Z_ORDER):
        at = pl.multiple_of(jnp.bitwise_xor(lax.rem(me, 4), z) * rows, rows)
        down_ref[pl.ds(at, rows), :] = some_down_ref[q]


def turn(x, cosine, sine_up, sine_down):
    return (
        x * cosine + pltpu.roll(x, ROT // 2, 1) * sine_up + pltpu.roll(x, 128 - ROT // 2, 1) * sine_down
    )


def allowed_limit(base, rows, prefix, axis):
    shape = (rows, 1) if axis == 0 else (1, rows)
    position = base + lax.broadcasted_iota(jnp.int32, shape, axis)
    return jnp.maximum(position, prefix - 1)


def flip(bit, by):
    return bit + by - 2 * bit * by


class Place:
    def __init__(self):
        self.group = lax.axis_index("dp")
        self.z = lax.axis_index("ctx")
        self.core = lax.rem(self.group, 2)
        self.x = lax.rem(lax.div(self.group, 2), 2)
        self.y = lax.div(self.group, 4)
        self.z_low = lax.rem(self.z, 2)
        self.z_high = lax.div(self.z, 2)

    def across(self, axis):
        if axis == "core":
            return (self.group + 1 - 2 * self.core, self.z)
        if axis == "x":
            return (self.group + 2 - 4 * self.x, self.z)
        if axis == "y":
            return (self.group + 4 - 8 * self.y, self.z)
        if axis == "zl":
            return (self.group, self.z + 1 - 2 * self.z_low)
        return (self.group, self.z + 2 - 4 * self.z_high)

    def device(self, y, x, core, z):
        pair = flip(self.y, y) * 4 + flip(self.x, x) * 2 + flip(self.core, core)
        return pair * 4 + flip(self.z_high, z // 2) * 2 + flip(self.z_low, z % 2)

    def code(self, k):
        return flip(self.z_high, lax.div(k, 2)), flip(self.z_low, lax.rem(k, 2))

    def block(self, k):
        return flip(self.z_low, lax.div(k, 2)) * 2 + flip(self.core, lax.rem(k, 2))

    def out_to(self, k):
        seq, half = self.code(k)
        return (self.group - self.core + half, 2 * self.core + seq)

    def back_to(self, k):
        return (self.group - self.core + self.z_high, self.block(k))

    def is_self(self, device):
        return jnp.logical_and(device[0] == self.group, device[1] == self.z)

    def meet(self, names):
        barrier = pltpu.get_barrier_semaphore()
        others = [self.across(name) for name in names]
        for step in range(1, 8):
            place = self.core * 4 + self.z + step
            others.append(
                (self.group - self.core + lax.rem(lax.div(place, 4), 2), lax.rem(place, 4))
            )
        for other in others:
            pl.semaphore_signal(barrier, inc=1, device_id=other, device_id_type=pl.DeviceIdType.MESH)
        pl.semaphore_wait(barrier, len(others))


class Sends:
    def __init__(self, here, send_sems, recv_sems):
        self.here, self.send_sems, self.recv_sems = here, send_sems, recv_sems
        self.used, self.open = 0, []

    def make(self, n, source, target, device):
        return pltpu.make_async_remote_copy(
            src_ref=source,
            dst_ref=target,
            send_sem=self.send_sems.at[n],
            recv_sem=self.recv_sems.at[n],
            device_id=device,
            device_id_type=pl.DeviceIdType.MESH,
        )

    def start(self, source, target, device):
        copy = self.make(self.used, source, target, device)
        self.used += 1
        copy.start()
        self.open.append(copy)
        return copy

    def four(self, source, target, device):
        base = self.used
        self.used += 4

        def copy(k):
            return self.make(base + k, source(k), target(k), device(k))

        def start(k):
            stays = self.here.is_self(device(k))

            @pl.when(stays)
            def _():
                pltpu.make_async_copy(source(k), target(k), self.recv_sems.at[base + k]).start()

            @pl.when(jnp.logical_not(stays))
            def _():
                copy(k).start()

        def sent(k):
            @pl.when(jnp.logical_not(self.here.is_self(device(k))))
            def _():
                copy(k).wait_send()

        def came(k):
            copy(k).wait_recv()

        return start, sent, came

    def finish(self):
        for copy in self.open:
            copy.wait_send()


def each(n, body):
    def step(i, _):
        body(i)
        return 0

    lax.fori_loop(0, n, step, 0)


class Gathers:
    def __init__(self, here, sends, refs):
        self.here, self.sends, self.refs = here, sends, refs
        self.coming = {name: [] for name in refs}

    def settle(self, name, first=0, count=1 << 20):
        left = []
        for at, n, copy in self.coming[name]:
            if at < first + count and first < at + n:
                copy.wait_recv()
            else:
                left.append((at, n, copy))
        self.coming[name] = left

    def move(self, name, axis, first, count, to):
        self.settle(name, first, count)
        ref = self.refs[name]
        copy = self.sends.start(
            ref.at[pl.ds(first, count)], ref.at[pl.ds(to, count)], self.here.across(axis)
        )
        self.coming[name].append((to, count, copy))


def key_positions(length, blocks, axis):
    shape = (length, 1) if axis == 0 else (1, length)
    i = lax.broadcasted_iota(jnp.int32, shape, axis)
    piece = length // (2 * blocks)
    return (
        lax.rem(lax.div(i, piece), blocks) * (2 * piece)
        + lax.div(i, length // 2) * piece
        + lax.rem(i, piece)
    )


FRONT_PLAN = (
    ("start", "zl"),
    ("move", "proj", "zh", 0, 1, 1),
    ("move", "proj", "zl", 0, 1, 2),
    ("add",),
    ("start", "zh"),
    ("move", "up", "zh", 0, 1, 1),
    ("move", "up", "zl", 0, 1, 2),
    ("move", "down", "zh", 0, 1, 1),
    ("move", "down", "zl", 0, 1, 2),
    ("add",),
    ("start", "x"),
    ("move", "proj", "y", 0, 1, 4),
    ("move", "proj", "x", 0, 1, 8),
    ("move", "up", "y", 0, 1, 4),
    ("move", "down", "x", 0, 1, 4),
    ("move", "up", "x", 0, 1, 8),
    ("move", "down", "y", 0, 1, 8),
    ("move", "proj", "zl", 1, 1, 3),
    ("move", "up", "zl", 1, 1, 3),
    ("move", "down", "zl", 1, 1, 3),
    ("rows", 1),
    ("add",),
    ("start", "y"),
    ("move", "proj", "y", 1, 1, 5),
    ("move", "proj", "x", 1, 1, 9),
    ("add",),
    ("start", "core"),
    ("move", "proj", "x", 4, 1, 12),
    ("add",),
    ("rows", 2),
    ("move", "up", "y", 1, 1, 5),
    ("move", "down", "x", 1, 1, 5),
    ("move", "up", "x", 1, 1, 9),
    ("move", "down", "y", 1, 1, 9),
    ("rows", 0),
    ("move", "proj", "y", 2, 2, 6),
    ("move", "proj", "x", 2, 2, 10),
    ("move", "proj", "x", 5, 1, 13),
    ("move", "up", "x", 4, 1, 12),
    ("move", "down", "y", 4, 1, 12),
    ("move", "up", "y", 2, 2, 6),
    ("move", "down", "x", 2, 2, 6),
    ("norm", 1),
    ("move", "proj", "x", 6, 2, 14),
    ("move", "up", "x", 2, 2, 10),
    ("move", "down", "y", 2, 2, 10),
    ("move", "up", "x", 5, 1, 13),
    ("move", "down", "y", 5, 1, 13),
    ("norm", 2),
    ("move", "up", "x", 6, 2, 14),
    ("move", "down", "y", 6, 2, 14),
    ("move", "up", "core", 0, 8, 16),
    ("move", "down", "core", 0, 8, 16),
    ("assemble",),
    ("project", 1),
    ("project", 2),
    ("norm", 0),
    ("project", 0),
    ("move", "up", "core", 8, 4, 24),
    ("move", "down", "core", 8, 4, 24),
    ("attend",),
    ("move", "up", "core", 12, 4, 28),
    ("move", "down", "core", 12, 4, 28),
)


def front_body(
    prefix_in, streams_ref, proj_in, up_in, down_in, out_in, gains_in, first_in, valid_in, cos_ref, rise_ref, fall_ref,
    received_out, normed_out, weight_out, far_out, up_ref, down_ref, small_ref, first_ref, prefix_ref,
    q_out, k_out, v_out, heads_out, lse_ref, got_ref,
    received_ref, normed_ref, proj_ref, weight_ref, q_ref, k_ref, v_ref, heads_ref,
    small_got, first_got, prefix_own, prefix_got, local_sems, send_sems, recv_sems,
):
    here = Place()
    sends = Sends(here, send_sems, recv_sems)
    gathers = Gathers(here, sends, {"proj": proj_ref, "up": up_ref, "down": down_ref})
    features = proj_ref.shape[-1]
    units = down_in.shape[0]
    kept = []

    def keep(source, target):
        copy = pltpu.make_async_copy(source, target, local_sems.at[len(kept)])
        kept.append(copy)
        copy.start()
        return copy

    def columns(which):
        return proj_in.at[:, :, pl.ds(pl.multiple_of(which * features, features), features)]

    shard = gains_in.shape[1]
    lanes = small_ref.shape[1]
    column = lax.broadcasted_iota(jnp.int32, (shard, lanes), 1)
    row = lax.broadcasted_iota(jnp.int32, (shard, lanes), 0)
    chosen = (column == row + here.device(0, 0, 0, 0) * shard).astype(bf16)
    count = jnp.sum(valid_in[...].astype(f32))
    small_ref[...] = jnp.zeros_like(small_ref)
    small_ref[0:5, :] = dot_nn(gains_in[...], chosen)
    small_ref[7:8, :] = jnp.full((1, lanes), 1.0, f32) * count
    first_ref[...] = jnp.zeros_like(first_ref)
    first_ref[0 : first_in.shape[1], :] = dot_tn(first_in[...], chosen).astype(bf16)
    second_row = lax.broadcasted_iota(jnp.int32, prefix_own.shape, 0) == 1
    prefix_own[...] = jnp.where(second_row, prefix_in[1], prefix_in[0])
    here.meet(("x", "y"))
    small_steps = []

    def small_start(axis):
        n = len(small_steps)
        device = here.across(axis)
        small_steps.append(
            (
                sends.start(small_ref, small_got.at[n], device),
                sends.start(first_ref, first_got.at[n], device),
            )
        )

    def small_end():
        n = len(small_steps) - 1
        for copy in small_steps[n]:
            copy.wait()
        sends.open = [c for c in sends.open if not any(c is s for s in small_steps[n])]
        small_ref[...] += small_got[n]
        first_ref[...] += first_got[n]

    def stream(s):
        def source(k):
            seq, half = here.code(k)
            return streams_ref.at[s, 2 * seq + half]

        steps = sends.four(source, lambda k: received_ref.at[s, k], here.out_to)
        each(4, steps[0])
        return steps

    chunk = 32

    def norm(s, steps):
        gain = small_ref[s : s + 1, :].astype(f32)

        def step(k):
            steps[2](k)
            block = here.block(k)

            def body(i, _):
                at = pl.ds(pl.multiple_of(i * chunk, chunk), chunk)
                x = received_ref[s, k, at, :].astype(f32)
                x = x - jnp.mean(x, axis=-1, keepdims=True)
                scale = lax.rsqrt(jnp.mean(x * x, axis=-1, keepdims=True) + epsilon)
                normed_ref[s, here.core, block, at, :] = (x * scale * gain).astype(bf16)
                return 0

            lax.fori_loop(0, received_ref.shape[2] // chunk, body, 0, unroll=2)

        each(4, step)
        keep(received_ref.at[s], received_out.at[s])
        keep(normed_ref.at[s, here.core], normed_out.at[s, here.core])
        return sends.start(
            normed_ref.at[s, here.core], normed_ref.at[s, here.core], here.across("core")
        )

    prefix_send = sends.start(prefix_own, prefix_got, here.across("core"))
    gathers.coming["proj"].append(
        (0, 1, sends.start(columns(1 - here.core), proj_ref.at[0, 1], here.across("core")))
    )
    own = [
        keep(columns(here.core), proj_ref.at[0, 0]),
        keep(up_in, up_ref.at[0]),
        keep(down_in, down_ref.at[0, pl.ds(0, units)]),
        keep(out_in, down_ref.at[0, pl.ds(units, out_in.shape[0])]),
    ]
    for copy in own:
        copy.wait()
    prefix_send.wait_recv()
    prefixes = jnp.where(here.z_high == here.core, prefix_own[...], prefix_got[...])
    prefix_ref[...] = jnp.broadcast_to(
        jnp.where(here.z_low == 0, prefixes[0:1], prefixes[1:2]), prefix_ref.shape
    )
    def assemble(s):
        rows = proj_ref.shape[-2]
        for x in range(2):
            for y in range(2):
                for q, z in enumerate(Z_ORDER):
                    for core in range(2):
                        device = here.device(y, x, core, z)
                        at = pl.ds(pl.multiple_of(device * rows, rows), rows)
                        weight_ref[s, at, :] = proj_ref[(x * 2 + y) * 4 + q, core, s]


    _, blocks, piece, width = q_ref.shape
    half_rows = blocks * piece
    length = 2 * half_rows

    def project(s, out_ref):
        def step(half):
            y = dot_nn(normed_ref[s, half].reshape(half_rows, -1), weight_ref[s])
            if s < 2:
                tables = [r[half].reshape(half_rows, 128) for r in (cos_ref, rise_ref, fall_ref)]
                y = jnp.concatenate(
                    [turn(y[:, i : i + 128], *tables) for i in range(0, width, 128)], axis=1
                )
            y = y.astype(bf16)
            if s == 0:
                y = y * jnp.asarray(HEAD_DIM**-0.5, bf16)
            out_ref[half] = y.reshape(blocks, piece, width)

        each(2, step)

    rows = 2 * piece
    lane = lax.broadcasted_iota(jnp.int32, (rows, 128), 1)
    key_index = key_positions(length, blocks, 1)
    heads_steps = sends.four(
        lambda k: heads_ref.at[here.block(k)], lambda k: got_ref.at[k], here.back_to
    )

    def block_body(k):
        block = here.block(k)
        allowed = key_index <= allowed_limit(block * rows, rows, prefix_ref[0:1, 0:1], 0)
        lse_all = jnp.zeros((rows, 128), f32)
        for pair in range(width // 128):
            at = slice(pair * 128, pair * 128 + 128)
            queries = q_ref[:, block, :, at].reshape(rows, 128)
            keys = k_ref[:, :, :, at].reshape(length, 128)
            values = v_ref[:, :, :, at].reshape(length, 128)
            results = []
            for h in range(2):
                chosen = (lane < 64) if h == 0 else (lane >= 64)
                scores = dot_nt(jnp.where(chosen, queries, jnp.zeros_like(queries)), keys)
                scores = jnp.where(allowed, scores, -1e30)
                top = jnp.max(scores, axis=-1, keepdims=True)
                weights = jnp.exp(scores - top)
                total = jnp.sum(weights, axis=-1, keepdims=True)
                results.append(dot_nn(weights.astype(bf16), values) / total)
                lse_all = jnp.where(lane == pair * 2 + h, top + jnp.log(total), lse_all)
            heads_ref[block, :, at] = jnp.where(lane < 64, results[0], results[1]).astype(bf16)
        lse_ref[block] = lse_all.T[0:8]
        heads_steps[0](k)


    rows_steps, others, far = {}, {}, []
    for step in FRONT_PLAN:
        kind = step[0]
        if kind == "start":
            small_start(step[1])
        elif kind == "add":
            small_end()
        elif kind == "rows":
            rows_steps[step[1]] = stream(step[1])
        elif kind == "move":
            gathers.move(*step[1:])
        elif kind == "norm":
            others[step[1]] = norm(step[1], rows_steps[step[1]])
        elif kind == "assemble":
            gathers.settle("proj")
            each(3, assemble)
            far.append(sends.start(weight_ref, far_out, here.across("core")))
            keep(weight_ref, weight_out)
        elif kind == "project":
            s = step[1]
            others[s].wait_recv()
            keep(normed_ref.at[s, 1 - here.core], normed_out.at[s, 1 - here.core])
            ref, out = ((q_ref, q_out), (k_ref, k_out), (v_ref, v_out))[s]
            project(s, ref)
            keep(ref, out)
        else:
            each(4, block_body)
            keep(heads_ref, heads_out)
    each(4, heads_steps[2])
    for name in ("up", "down"):
        gathers.settle(name)
    far[0].wait_recv()
    for steps in list(rows_steps.values()) + [heads_steps]:
        each(4, steps[1])
    sends.finish()
    for copy in kept[len(own) :]:
        copy.wait()


def mlp_forward_body(
    ids, heads_ref, res_ref, gain_ref, all_up_ref, some_down_ref, gathered_out_ref,
    hidden_ref, normed_ref, active_ref, slope_ref, layer_ref,
    out_w_ref, up_ref, down_ref,
):
    step = pl.program_id(0)
    seqs, rows, width = res_ref.shape[1:]
    me = ids[4]

    @pl.when(step == 0)
    def _():
        place_rows(me, gathered_out_ref, DOWN_BITS, out_w_ref)
        hidden_ref[...] = res_ref[0].astype(f32)
        for k in range(heads_ref.shape[0]):
            code = jnp.bitwise_xor(ids[0], k)
            features = heads_ref.shape[-1]
            at = pl.ds(pl.multiple_of(lax.rem(code, 2) * features, features), features)
            hidden_ref[lax.div(code, 2)] += dot_nn(heads_ref[k], out_w_ref[at, :])
        gain = gain_ref[3:4, :].astype(f32)
        for j in range(seqs):
            x = hidden_ref[j]
            layer_ref[j] = x
            x = x - jnp.mean(x, axis=-1, keepdims=True)
            scale = lax.rsqrt(jnp.mean(x * x, axis=-1, keepdims=True) + epsilon)
            normed_ref[j] = (x * scale * gain).astype(bf16)

    place_tile(me, all_up_ref, some_down_ref, up_ref, down_ref)
    upper = dot_nn(normed_ref[...].reshape(seqs * rows, width), up_ref[...])
    active, slope = gelu_pair(upper)
    active = active.astype(bf16)
    active_ref[...] = active
    slope_ref[...] = slope.astype(bf16)
    layer_ref[...] += dot_nn(active, down_ref[...]).reshape(seqs, rows, width)


def mixer_body(
    scal_ref, layer_ref, hist_ref, teacher_ref, valid_in, gain_ref, first_ref, second_in, bias_in,
    next_ref, ghist_ref, glayer_ref, gfirst_ref, gsecond_ref, stats_ref, ggain_ref,
    coef_ref, part_ref, gnext_ref, valid_ref, second_ref, bias_ref,
):
    step = pl.program_id(0)
    past, rows, width = hist_ref.shape
    streams = teacher_ref.shape[0]
    outs = past + 1
    span = first_ref.shape[0]

    @pl.when(step == 0)
    def _():
        gfirst_ref[...] = jnp.zeros_like(gfirst_ref)
        gsecond_ref[...] = jnp.zeros_like(gsecond_ref)
        stats_ref[...] = jnp.zeros_like(stats_ref)
        ggain_ref[...] = jnp.zeros_like(ggain_ref)
        second_ref[...] = jnp.zeros_like(second_ref)
        second_ref[0 : second_in.shape[0], 0 : second_in.shape[1]] = second_in[...]
        bias_ref[...] = jnp.zeros_like(bias_ref)
        bias_ref[:, 0 : bias_in.shape[1]] = bias_in[...]

    factor = scal_ref[0] * 2.0 / (4.0 * width * gain_ref[7:8, 0:128])
    diagonal = lax.broadcasted_iota(jnp.int32, (rows, rows), 0) == lax.broadcasted_iota(
        jnp.int32, (rows, rows), 1
    )
    valid_row = jnp.broadcast_to(valid_in[0].astype(f32), (rows, rows))
    valid_ref[...] = jnp.sum(jnp.where(diagonal, valid_row, 0.0), axis=1, keepdims=True)
    x = layer_ref[...]
    scale = lax.rsqrt(jnp.mean(x * x, axis=-1, keepdims=True) + epsilon)
    gain = gain_ref[4:5, :].astype(f32)
    normed = (x * scale * gain).astype(bf16)
    mix_hidden = dot_nt(normed, first_ref[...])
    mix_active, mix_slope = gelu_pair(mix_hidden)
    coeff = dot_nn(mix_active, second_ref[...], highest) + bias_ref[...]
    for c in range(streams * outs):
        coef_ref[c] = jnp.broadcast_to(coeff[:, c : c + 1], (rows, 128))
    part_ref[...] = jnp.zeros_like(part_ref)

    chunk = 16
    lanes = 512

    def rows_body(i, loss_rows):
        at = pl.ds(pl.multiple_of(i * chunk, chunk), chunk)
        valid = jnp.broadcast_to(valid_ref[at, :], (chunk, 128))

        def read(j, lane_at):
            return layer_ref[at, lane_at] if j == past else hist_ref[j, at, lane_at].astype(f32)

        for l0 in range(0, width, 256):
            lane_at = slice(l0, l0 + 256)
            sums = [jnp.zeros((chunk, 256), f32) for _ in range(streams)]
            for j in range(outs):
                value = read(j, lane_at)
                for s in range(streams):
                    c = coef_ref[s * outs + j, at, :]
                    sums[s] = sums[s] + jnp.concatenate([c, c], axis=1) * value
            both = jnp.concatenate([valid, valid], axis=1)
            for s in range(streams):
                next_ref[s, at, lane_at] = sums[s].astype(bf16)
                difference = sums[s] - teacher_ref[s, at, lane_at].astype(f32)
                weighted = both * difference
                gnext_ref[s, at, lane_at] = jnp.concatenate([factor, factor], axis=1) * weighted
                square = weighted * difference
                loss_rows = loss_rows + square[:, :128] + square[:, 128:]
        for l0 in range(0, width, lanes):
            lane_at = slice(l0, l0 + lanes)
            for j in range(outs):
                value = read(j, lane_at)
                total = jnp.zeros((chunk, lanes), f32)
                for s in range(streams):
                    grad = gnext_ref[s, at, lane_at]
                    c = coef_ref[s * outs + j, at, :]
                    total = total + jnp.concatenate([c] * (lanes // 128), axis=1) * grad
                    product = grad * value
                    folded = product[:, :128]
                    for q in range(128, lanes, 128):
                        folded = folded + product[:, q : q + 128]
                    part_ref[s * outs + j, at, :] += folded
                if j == past:
                    glayer_ref[at, lane_at] = total
                else:
                    ghist_ref[j, at, lane_at] = total.astype(bf16)
        return loss_rows

    loss_rows = lax.fori_loop(0, rows // chunk, rows_body, jnp.zeros((chunk, 128), f32))
    lane = lax.broadcasted_iota(jnp.int32, (rows, span), 1)
    grad_coeff = jnp.zeros((rows, span), f32)
    for c in range(streams * outs):
        grad_coeff = jnp.where(lane == c, jnp.sum(part_ref[c], axis=-1, keepdims=True), grad_coeff)
    gsecond_ref[...] += dot_tn(mix_active, grad_coeff, highest)
    stats_ref[0:1, :] += jnp.sum(grad_coeff, axis=0, keepdims=True)
    stats_ref[1:2, :] += jnp.broadcast_to(jnp.sum(loss_rows), (1, span))
    grad_active = dot_nt(grad_coeff, second_ref[...], highest)
    grad_mix = (grad_active * mix_slope).astype(bf16)
    gfirst_ref[...] += dot_tn(grad_mix, normed)
    grad_normed = dot_nn(grad_mix, first_ref[...])
    x = layer_ref[...]
    ggain_ref[...] += jnp.sum(grad_normed * (x * scale), axis=0, keepdims=True)
    inner = grad_normed * gain
    mean = jnp.mean(inner * x, axis=-1, keepdims=True)
    glayer_ref[...] += scale * inner - x * (scale * scale * scale * mean)


def norm_back(x, grad, gain):
    centered = x - jnp.mean(x, axis=-1, keepdims=True)
    scale = lax.rsqrt(jnp.mean(centered * centered, axis=-1, keepdims=True) + epsilon)
    unit = centered * scale
    grad_gain = jnp.sum(grad * unit, axis=0, keepdims=True)
    inner = grad * gain
    inner = (
        inner
        - jnp.mean(inner, axis=-1, keepdims=True)
        - unit * jnp.mean(inner * unit, axis=-1, keepdims=True)
    )
    return scale * inner, grad_gain


def mlp_backward_body(
    ids, glayer_ref, active_ref, slope_ref, normed_ref, all_up_ref, some_down_ref,
    hidden_ref, heads_ref, gain_ref, gathered_out_ref,
    gu0, gu1, gu2, gu3, gd0, gd1, gd2, gd3, gres_ref, g0, g1, g2, g3, go0, go1, go2, go3, ggain_ref,
    low_ref, normed_t_ref, up_ref, down_ref, tile_ref, sum_ref, out_w_ref, gout_ref,
):
    step = pl.program_id(0)
    seqs, rows, width = glayer_ref.shape
    tokens = seqs * rows
    me = ids[4]
    place = lax.rem(me, 4)

    @pl.when(step == 0)
    def _():
        low_ref[...] = glayer_ref[...].astype(bf16)
        sum_ref[...] = jnp.zeros_like(sum_ref)
        normed_t_ref[...] = normed_ref[...].reshape(tokens, width).T

    place_tile(me, all_up_ref, some_down_ref, up_ref, down_ref)
    grad = low_ref[...].reshape(tokens, width)
    grad_active = dot_nt(grad, down_ref[...])
    grad_upper = (grad_active * slope_ref[...].astype(f32)).astype(bf16)
    sum_ref[...] += dot_nt(grad_upper, up_ref[...]).reshape(seqs, rows, width)
    down_ref[...] = dot_tn(active_ref[...], grad).astype(bf16)
    for p, ref in enumerate((gd0, gd1, gd2, gd3)):

        @pl.when(lax.div(step, 2) == p)
        def _(ref=ref):
            block_rows = ref.shape[1]
            for q, z in enumerate(Z_ORDER):
                at = pl.multiple_of(jnp.bitwise_xor(place, z) * block_rows, block_rows)
                ref[q] = down_ref[pl.ds(at, block_rows), :]

    tile_ref[...] = dot_nn(normed_t_ref[...], grad_upper).astype(bf16)
    take_rows(me, tile_ref, UP_BITS, (gu0, gu1, gu2, gu3))

    @pl.when(step == pl.num_programs(0) - 1)
    def _():
        hidden_backward(
            ids, glayer_ref, sum_ref, hidden_ref, heads_ref, gain_ref, gathered_out_ref,
            gres_ref, g0, g1, g2, g3, go0, go1, go2, go3, ggain_ref, out_w_ref, gout_ref,
        )


def hidden_backward(
    ids, glayer_ref, sum_ref, hidden_ref, heads_ref, gain_ref, gathered_out_ref,
    gres_ref, g0, g1, g2, g3, go0, go1, go2, go3, ggain_ref,
    out_w_ref, gout_ref,
):
    seqs, rows, width = hidden_ref.shape
    me = ids[4]
    place_rows(me, gathered_out_ref, DOWN_BITS, out_w_ref)
    gain = gain_ref[3:4, :].astype(f32)
    ggain = jnp.zeros((1, width), f32)
    for j in range(seqs):
        back, part = norm_back(hidden_ref[j], sum_ref[j], gain)
        ggain = ggain + part
        gres_ref[j] = (glayer_ref[j] + back).astype(bf16)
    ggain_ref[...] = ggain
    gout_ref[...] = jnp.zeros_like(gout_ref)
    for k, out in enumerate((g0, g1, g2, g3)):
        code = jnp.bitwise_xor(ids[0], k)
        features = out.shape[-1]
        at = pl.ds(pl.multiple_of(lax.rem(code, 2) * features, features), features)
        low = gres_ref[lax.div(code, 2)]
        out[...] = dot_nt(low, out_w_ref[at, :]).astype(bf16)
        gout_ref[at, :] += dot_tn(heads_ref[k], low)
    out_w_ref[...] = gout_ref[...].astype(bf16)
    take_rows(me, out_w_ref, DOWN_BITS, (go0, go1, go2, go3))


def back_body(
    prefix_ref, q_in, k_in, v_in, heads_in, lse_ref, cos_ref, rise_ref, fall_ref,
    normed_in, received_in, weight_in, far_in, gain_ref, gfirst_in, gmlp_in, gmix_in, gsecond_in, stats_in, res_in,
    gh0, gh1, gh2, gh3, gu0, gu1, gu2, gu3, gd0, gd1, gd2, gd3, go0, go1, go2, go3,
    gstreams_ref, gproj_ref, gup_ref, gdown_ref, gout_ref, near_ref, tiny_ref, late_ref,
    q_ref, k_ref, v_ref, heads_ref, g_ref, d_ref, d_got, dk_ref, dv_ref, kt_ref,
    normed_ref, received_ref, weight_ref, gn_ref, b_ref, grad_ref,
    up_keep, down_keep, up_sum, up_a, up_b, up_c, up_d, down_sum, down_a, down_b, down_c, down_d,
    down_p, down_q, down_r, down_s,
    proj_sum, proj_a, proj_b, proj_c, proj_d, proj_e, early_ref, early_y, early_x, early_core, near_got, tiny_got, late_got,
    local_sems, send_sems, recv_sems,
):
    here = Place()
    sends = Sends(here, send_sems, recv_sems)
    used = []

    def load(source, target):
        copy = pltpu.make_async_copy(source, target, local_sems.at[len(used)])
        used.append(copy)
        copy.start()
        return copy

    def ready(source, target, axis):
        copy = sends.make(sends.used, source, target, here.across(axis))
        sends.used += 1
        sends.open.append(copy)
        return copy

    def send(source, target, axis):
        copy = ready(source, target, axis)
        copy.start()
        return copy

    def add(into, first, source, count, start=0):
        def body(i):
            into[first + i] = into[first + i] + source[start + i]

        each(count, body)

    span = gfirst_in.shape[0]
    early_ref[0:span, :] = gfirst_in[...]
    early_ref[span:, :] = jnp.zeros((8, early_ref.shape[1]), f32)
    early_ref[span : span + 1, :] = gmlp_in[...]
    early_ref[span + 1 : span + 2, :] = gmix_in[...]
    tiny_ref[0:span, :] = gsecond_in[...]
    tiny_ref[span:, :] = stats_in[...]
    here.meet(("x", "y"))

    def ring(*refs):
        stages = []

        def start(axis):
            n = len(stages)
            stages.append([send(value, got.at[n], axis) for value, got in refs])

        def end():
            n = len(stages) - 1
            for copy in stages[n]:
                copy.wait()
            sends.open = [c for c in sends.open if not any(c is s for s in stages[n])]
            for value, got in refs:
                value[...] += got[n]

        return start, end

    late_start, late_end = ring((late_ref, late_got))
    near_start, near_end = ring((near_ref, near_got))
    tiny_start, tiny_end = ring((tiny_ref, tiny_got))

    column = [0]
    halvings = []

    def early_start(axis):
        tiny_start(axis)
        got = {"y": early_y, "x": early_x, "core": early_core}.get(axis)
        if got is None:
            near_start(axis)
            return
        bit = {"y": here.y, "x": here.x, "core": here.core}[axis]
        size = got.shape[1]
        give = pl.multiple_of(column[0] + (1 - bit) * size, 128)
        column[0] = column[0] + bit * size
        halvings.append((send(early_ref.at[:, pl.ds(give, size)], got, axis), got))

    def early_end():
        tiny_end()
        if not halvings:
            near_end()
            return
        copy, got = halvings.pop()
        copy.wait()
        sends.open = [c for c in sends.open if c is not copy]
        at = pl.ds(pl.multiple_of(column[0], 128), got.shape[1])
        if got is early_core:
            near_ref[...] = early_ref[:, at] + got[...]
        else:
            early_ref[:, at] += got[...]

    early_start("y")
    gs = (gh0, gh1, gh2, gh3)
    base = sends.used
    sends.used += 4
    exchange = []
    for n, g in enumerate(gs):
        device = here.out_to(n)
        stays = here.is_self(device)
        copy = sends.make(base + n, g, g_ref.at[n], device)
        own = pltpu.make_async_copy(g, g_ref.at[n], recv_sems.at[base + n])

        @pl.when(stays)
        def _(own=own):
            own.start()

        @pl.when(jnp.logical_not(stays))
        def _(copy=copy):
            copy.start()

        exchange.append((copy, stays))
    units = gd0.shape[3]
    shard = go0.shape[3]
    cut = down_a.shape[-1]
    left, right = pl.ds(0, cut), pl.ds(cut, cut)

    def down_parts(ref):
        lead = (slice(None),) * (len(ref.shape) - 2)
        return ref.at[lead + (pl.ds(0, units),)], ref.at[lead + (pl.ds(units, shard),)]

    up_come, down_come = {}, {}
    for n, u, d, o in ((1, gu3, gd3, go3), (0, gu2, gd2, go2)):
        up_come[n] = [send(u, up_sum.at[pl.ds(8 * n, 8)], "core")]
        to_d, to_o = down_parts(down_sum.at[pl.ds(2 * n, 2)])
        down_come[n] = [send(d, to_d, "core"), send(o, to_o, "core")]
    attention_loads = [
        load(a, b)
        for a, b in ((q_in, q_ref), (k_in, k_ref), (v_in, v_ref), (heads_in, heads_ref))
    ]

    def load_stream(s, slot):
        return [
            load(normed_in.at[s], normed_ref.at[slot]),
            load(received_in.at[s], received_ref.at[slot]),
            load(weight_in.at[s], weight_ref.at[slot, 0]),
            load(far_in.at[s], weight_ref.at[slot, 1]),
        ]

    own_up = {1: gu1, 0: gu0}
    own_down = {1: (gd1, go1), 0: (gd0, go0)}

    def load_up(n, half):
        return [load(own_up[n].at[pl.ds(4 * half, 4)], up_keep)]

    def load_down(n, half):
        d, o = own_down[n]
        to_d, to_o = down_parts(down_keep)
        return [load(d.at[half], to_d), load(o.at[half], to_o)]

    def add_down(place, source, lanes, lows=(0, 1)):
        for low in lows:

            def body(high):
                down_sum[place, low, high, :, lanes] += source[low, high]

            each(2, body)

    order = ((1, 1), (1, 0), (0, 1), (0, 0))
    up_load, down_load = load_up(*order[0]), load_down(*order[0])
    up_hops, down_hops = {}, {}
    everything = pl.ds(0, 2 * cut)
    for i, (n, half) in enumerate(order):
        first = 8 * n + 4 * half
        for copy in up_come.pop(n, []):
            copy.wait_recv()
        for copy in up_load:
            copy.wait()
        add(up_sum, first, up_keep, 4)
        if n == 1:
            up_hops[half] = send(up_sum.at[pl.ds(first, 4)], up_a.at[pl.ds(4 * half, 4)], "x")
        if i < 3:
            up_load = load_up(*order[i + 1])
        for copy in down_come.pop(n, []):
            copy.wait_recv()
        for copy in down_load:
            copy.wait()
        add_down(2 * n + half, down_keep, everything)
        if n == 1:
            down_hops[half] = send(
                down_sum.at[2 + half, :, :, :, right], down_a.at[half], "y"
            )
        if i < 3:
            down_load = load_down(*order[i + 1])
        if i < 2:
            early_end()
            early_start(("x", "core")[i])
    early_end()
    early_start("zl")
    down_zl = {
        high: send(down_sum.at[:, 1, high, :, left], down_p.at[high], "zl") for high in (1, 0)
    }
    streams_loads = {2: load_stream(2, 0), 1: load_stream(1, 1)}
    res_copy = load(res_in, gstreams_ref.at[3])

    _, blocks, piece, width = q_ref.shape
    rows = 2 * piece
    half_rows = blocks * piece
    length = 2 * half_rows
    lane = lax.broadcasted_iota(jnp.int32, (rows, 128), 1)
    key_index = key_positions(length, blocks, 0)
    choose = (
        lax.div(lax.broadcasted_iota(jnp.int32, (8, 128), 1), 64)
        == lax.broadcasted_iota(jnp.int32, (8, 128), 0)
    ).astype(f32)

    def unturn(x, tables):
        return (
            x * tables[0]
            - pltpu.roll(x, ROT // 2, 1) * tables[1]
            - pltpu.roll(x, 128 - ROT // 2, 1) * tables[2]
        )

    rotary = (cos_ref, rise_ref, fall_ref)
    for copy in attention_loads:
        copy.wait()
    for copy, _ in exchange:
        copy.wait_recv()

    up_y = ready(up_sum.at[pl.ds(4, 4)], up_b, "y")
    down_x = ready(down_sum.at[1, :, :, :, right], down_b, "x")
    down_zh = ready(down_sum.at[:, 0, 1, :, left], down_q, "zh")

    def add_left(high, source):
        def body(place):
            down_sum[place, 0, high, :, left] += source[place]

        each(4, body)

    def hook_0():
        down_hops[1].wait_recv()
        add_down(1, down_a.at[1], right)
        down_x.start()
        up_hops[1].wait_recv()
        add(up_sum, 4, up_a, 4, 4)
        up_y.start()

    def hook_1():
        down_zl[1].wait_recv()
        add_left(1, down_p.at[1])
        down_zh.start()

    def hook_2():
        down_hops[0].wait_recv()
        add_down(0, down_a.at[0], right)

    hooks = (hook_0, hook_1, hook_2)

    def one_pair(pair):
        at = pl.ds(pl.multiple_of(pair * 128, 128), 128)
        dk_ref[...] = jnp.zeros_like(dk_ref)
        dv_ref[...] = jnp.zeros_like(dv_ref)
        keys = k_ref[:, :, :, at].reshape(length, 128)
        values = v_ref[:, :, :, at].reshape(length, 128)
        kt_ref[...] = keys.T

        def one_block(k):
            block = here.block(k)
            queries = q_ref[:, block, :, at].reshape(rows, 128)
            grads = g_ref[k, :, at]
            inner_rows = dot_nt(
                choose, grads.astype(f32) * heads_ref[block, :, at].astype(f32), highest
            )
            allowed = key_index <= allowed_limit(block * rows, rows, prefix_ref[0:1, 0:1], 1)
            dqt = []
            for h in range(2):
                chosen = (lane < 64) if h == 0 else (lane >= 64)
                q_h = jnp.where(chosen, queries, jnp.zeros_like(queries))
                g_h = jnp.where(chosen, grads, jnp.zeros_like(grads))
                scores = dot_nt(keys, q_h)
                probs = jnp.where(allowed, jnp.exp(scores - lse_ref[block, pl.ds(pair * 2 + h, 1), :]), 0.0)
                grad_probs = dot_nt(values, g_h)
                grad_scores = (probs * (grad_probs - inner_rows[h : h + 1, :])).astype(bf16)
                dv_ref[...] += dot_nn(probs.astype(bf16), g_h)
                dk_ref[...] += dot_nn(grad_scores, q_h)
                dqt.append(dot_nn(kt_ref[...], grad_scores)[h * 64 : h * 64 + 64, :])
            dq = jnp.concatenate(dqt, axis=0).T * (HEAD_DIM**-0.5)
            dq = unturn(dq, [r[:, block].reshape(rows, 128) for r in rotary])
            d_ref[0, :, block, :, at] = dq.astype(bf16).reshape(2, piece, 128)

        each(4, one_block)
        dk = unturn(dk_ref[...], [r[...].reshape(length, 128) for r in rotary])
        d_ref[1, :, :, :, at] = dk.astype(bf16).reshape(2, blocks, piece, 128)
        d_ref[2, :, :, :, at] = dv_ref[...].astype(bf16).reshape(2, blocks, piece, 128)
        for i, hook in enumerate(hooks):
            pl.when(pair == i)(hook)

    each(4, one_pair)

    far_half = 1 - here.core
    d_hops = {s: send(d_ref.at[s, far_half], d_got.at[s], "core") for s in (2, 1, 0)}
    early_end()
    early_start("zh")
    late_ref[...] = jnp.zeros_like(late_ref)
    back = {}

    def mine():
        return here.z_low * 2 + here.core

    def one_stream(s, slot):
        for copy in streams_loads[s]:
            copy.wait()
        d_hops[s].wait_recv()
        near = d_ref[s, here.core].reshape(half_rows, width)
        gn = dot_nt(near, weight_ref[slot, 0])
        gn = gn + dot_nt(d_got[s].reshape(half_rows, width), weight_ref[slot, 1])
        gn_ref[...] = gn.reshape(gn_ref.shape)
        gain = gain_ref[s : s + 1, :]

        def step(k):
            block = here.block(k)
            grad, part = norm_back(received_ref[slot, k].astype(f32), gn_ref[block], gain)
            b_ref[s, k] = grad.astype(bf16)
            late_ref[s : s + 1, :] += part

        each(4, step)

    def send_stream(s):
        steps = sends.four(
            lambda k: b_ref.at[s, k], lambda k: gstreams_ref.at[s, mine()], here.back_to
        )
        each(4, steps[0])
        back[s] = steps

    def project_back(s, slot):
        grad = dot_tn(
            normed_ref[slot, 0].reshape(half_rows, -1), d_ref[s, 0].reshape(half_rows, width)
        )
        grad = grad + dot_tn(
            normed_ref[slot, 1].reshape(half_rows, -1), d_ref[s, 1].reshape(half_rows, width)
        )
        grad_ref[...] = grad.astype(bf16)
        for x in range(2):
            for y in range(2):
                for q, z in enumerate(Z_ORDER):
                    for core in range(2):
                        at = pl.multiple_of(here.device(y, x, core, z) * shard, shard)
                        proj_sum[(x * 2 + y) * 4 + q, core, s] = grad_ref[pl.ds(at, shard), :]

    def settle_left():
        down_zl[0].wait_recv()
        add_left(0, down_p.at[0])

    def give_down(lanes, other):
        value = down_sum[0, 0, 0, :, lanes].astype(f32) + other[...].astype(f32)
        gdown_ref[:, lanes] = value[:units]
        gout_ref[:, lanes] = value[units:]

    one_stream(2, 0)
    send_stream(2)
    project_back(2, 0)
    streams_loads[0] = load_stream(0, 0)
    up_hops[0].wait_recv()
    add(up_sum, 0, up_a, 4)
    settle_left()
    one_stream(1, 1)
    early_end()
    up_y.wait_recv()
    add(up_sum, 0, up_b, 4)
    up_zl = send(up_sum.at[pl.ds(2, 2)], up_c, "zl")
    send_stream(1)
    project_back(1, 1)
    one_stream(0, 0)
    project_back(0, 0)
    lanes_of = {"x": pl.ds(0, width // 2), "y": pl.ds(width // 2, width // 2)}
    far_of = {"x": (8, 4), "y": (4, 8)}
    proj_hops = {}

    def proj_send(first, target, start, axis, side):
        lanes = lanes_of[side]
        return send(
            proj_sum.at[pl.ds(first, 4), :, :, :, lanes],
            target.at[pl.ds(start, 4), :, :, :, lanes],
            axis,
        )

    def proj_add(first, source, start, side):
        lanes = lanes_of[side]

        def body(i):
            proj_sum[first + i, :, :, :, lanes] += source[start + i, :, :, :, lanes]

        each(4, body)

    for half in (1, 0):
        for side in ("x", "y"):
            far, other = far_of[side]
            proj_hops[side, half] = proj_send(far + other * half, proj_a, 4 * half, side, side)
    late_start("core")
    down_x.wait_recv()
    add_down(0, down_b, right)
    down_low = send(down_sum.at[0, 1, :, :, right], down_c, "zl")
    late_end()
    late_start("y")
    down_zh.wait_recv()
    add_left(0, down_q)
    left_y = send(down_sum.at[pl.ds(2, 2), 0, 0, :, left], down_r, "y")
    late_end()
    late_start("x")
    up_zl.wait_recv()
    add(up_sum, 0, up_c, 2)
    up_zh = send(up_sum.at[pl.ds(1, 1)], up_d, "zh")
    send_stream(0)
    left_y.wait_recv()
    for place in range(2):
        down_sum[place, 0, 0, :, left] += down_r[place]
    left_x = send(down_sum.at[1, 0, 0, :, left], down_s, "x")
    proj_next = {}
    for side, axis in (("x", "y"), ("y", "x")):
        other = far_of[side][1]
        proj_hops[side, 1].wait_recv()
        proj_add(other, proj_a, 4, side)
        proj_next[side] = proj_send(other, proj_b, 0, axis, side)
    late_end()
    late_start("zl")
    for side in ("x", "y"):
        proj_hops[side, 0].wait_recv()
        proj_add(0, proj_a, 0, side)
    for side in ("x", "y"):
        proj_next[side].wait_recv()
        proj_add(0, proj_b, 0, side)
    proj_zl = send(proj_sum.at[pl.ds(2, 2)], proj_c, "zl")
    left_x.wait_recv()
    give_down(left, down_s)
    down_low.wait_recv()
    for high in range(2):
        down_sum[0, 0, high, :, right] += down_c[high]
    down_high = send(down_sum.at[0, 0, 1, :, right], down_d, "zh")
    up_zh.wait_recv()
    gup_ref[...] = up_sum[0].astype(f32) + up_d[0].astype(f32)
    late_end()
    late_start("zh")
    proj_zl.wait_recv()
    add(proj_sum, 0, proj_c, 2)
    proj_zh = send(proj_sum.at[pl.ds(1, 1)], proj_d, "zh")
    down_high.wait_recv()
    give_down(right, down_d)
    late_end()
    proj_zh.wait_recv()
    add(proj_sum, 0, proj_d, 1)
    proj_core = send(proj_sum.at[0, 1], proj_e, "core")
    for which, source in ((here.core, proj_sum.at[0, 0]), (1 - here.core, proj_e)):
        if source is proj_e:
            proj_core.wait_recv()
        at = pl.ds(pl.multiple_of(which * width, width), width)
        gproj_ref[:, :, at] = source[...].astype(f32)
    for s in range(3):
        each(4, back[s][2])
        each(4, back[s][1])
    for copy, stays in exchange:

        @pl.when(jnp.logical_not(stays))
        def _(copy=copy):
            copy.wait_send()

    res_copy.wait()
    sends.finish()


def finish_body(
    me_ref, streams_ref, proj_ref, up_ref, down_ref, out_ref, early_ref, tiny_ref, late_ref, small_ref,
    streams_out, proj_out, up_out, down_out, out_out, first_out, second_out, bias_out, gains_out, loss_out,
):
    streams_out[...] = streams_ref[...]

    @pl.when(pl.program_id(0) == 0)
    def _():
        for source, target in (
            (proj_ref, proj_out),
            (up_ref, up_out),
            (down_ref, down_out),
            (out_ref, out_out),
        ):
            target[...] = source[...]
        shard, mixw = first_out.shape
        width = late_ref.shape[1]
        near = early_ref.shape[1]
        span = tiny_ref.shape[1]

        def chosen(size, first):
            column = lax.broadcasted_iota(jnp.int32, (shard, size), 1)
            row = lax.broadcasted_iota(jnp.int32, (shard, size), 0)
            return (column == row + first).astype(f32)

        mine = chosen(near, lax.rem(me_ref[0] * shard, near))
        first_out[...] = dot_nt(mine, early_ref[...], highest)[:, 0:mixw]
        gains_out[3:5, :] = dot_nt(early_ref[span : span + 8, :], mine, highest)[0:2]
        gains_out[0:3, :] = dot_nt(late_ref[...], chosen(width, me_ref[0] * shard), highest)[0:3]
        second_out[...] = tiny_ref[0:mixw, 0:mixw]
        bias_out[...] = tiny_ref[span : span + 1, 0:mixw]
        loss_out[...] = tiny_ref[span + 1 : span + 2, 0:1] / (4.0 * width * small_ref[7:8, 0:1])


def rotary_lanes(length, piece):
    lane = jnp.arange(128, dtype=jnp.int32) % HEAD_DIM
    step = (lane % (ROT // 2)).astype(f32)
    inverse = jnp.exp(step * (-2.0 * math.log(10000.0) / ROT))
    angles = jnp.arange(length, dtype=jnp.int32).astype(f32)[:, None] * inverse[None, :]
    cosine = jnp.where(lane < ROT, jnp.cos(angles), 1.0)
    sine = jnp.sin(angles)
    up = jnp.where((lane >= ROT // 2) & (lane < ROT), sine, 0.0)
    down = jnp.where(lane < ROT // 2, -sine, 0.0)
    return [
        t.reshape(-1, 2, piece, 128).transpose(1, 0, 2, 3) for t in (cosine, up, down)
    ]


def local_fast(
    streams, history, teacher, prefix, valid_mask, loss_scale, projections, attention_out,
    up_weight, down_weight, mixer_first, mixer_second, mixer_bias, gains,
):
    lines = lax.axis_size("ctx")
    count = lax.axis_size("dp") * lines
    place = lax.axis_index("ctx")
    group = lax.axis_index("dp")
    me = group * lines + place
    half = group % 2
    mine = 2 * (place % 2) + half
    seqs, rows, width = streams.shape[1:]
    tokens = seqs * rows
    piece = rows // 2
    length = rows * lines
    features = width // 2
    hidden_units = down_weight.shape[0] * count
    past = history.shape[0]
    count_of_streams = teacher.shape[0]
    mixw = mixer_bias.shape[0]
    span = 64

    ids = jnp.stack([place, half, mine, mine, me]).astype(jnp.int32)
    shard = width // count
    unit_shard = hidden_units // count

    smem = pl.BlockSpec(memory_space=pltpu.SMEM)
    anywhere = pl.BlockSpec(memory_space=pl.ANY)
    proj_shape = (count // 2, 2, 3, shard, features)
    tables = rotary_lanes(length, piece)
    row_shape = (3, 4, piece, width)
    normed_shape = (3, 2, lines, piece, width)
    wide_shape = (2, lines, piece, features)
    heads_shape = (lines, rows, features)

    def array(shape, dtype=bf16):
        return jax.ShapeDtypeStruct(shape, dtype)

    (
        received, normed, proj, proj_other, up_all, down_all, small, first_t, prefix_rows,
        queries, keys, values, heads_seq, lse, heads,
    ) = pl.pallas_call(
        front_body,
        in_specs=[smem, anywhere] + [vmem()] * 10,
        out_specs=[anywhere] * 6 + [vmem()] * 3 + [anywhere] * 4 + [vmem(), anywhere],
        out_shape=[
            array(row_shape),
            array(normed_shape),
            array((3, width, features)),
            array((3, width, features)),
            array((count, shard, hidden_units)),
            array((count, unit_shard + shard, width)),
            array((8, width), f32),
            array((span, width)),
            array((8, 128), jnp.int32),
            array(wide_shape),
            array(wide_shape),
            array(wide_shape),
            array(heads_shape),
            array((lines, 8, rows), f32),
            array((4, rows, features)),
        ],
        scratch_shapes=[
            pltpu.VMEM(row_shape, bf16),
            pltpu.VMEM(normed_shape, bf16),
            pltpu.VMEM(proj_shape, bf16),
            pltpu.VMEM((3, width, features), bf16),
            pltpu.VMEM(wide_shape, bf16),
            pltpu.VMEM(wide_shape, bf16),
            pltpu.VMEM(wide_shape, bf16),
            pltpu.VMEM(heads_shape, bf16),
            pltpu.VMEM((5, 8, width), f32),
            pltpu.VMEM((5, span, width), bf16),
            pltpu.VMEM((8, 128), jnp.int32),
            pltpu.VMEM((8, 128), jnp.int32),
            pltpu.SemaphoreType.DMA((24,)),
            pltpu.SemaphoreType.DMA((112,)),
            pltpu.SemaphoreType.DMA((112,)),
        ],
        compiler_params=params(collective_id=0, has_side_effects=True),
        name="front",
    )(
        prefix,
        streams.reshape(streams.shape[0], 2 * seqs, piece, width),
        projections, up_weight, down_weight, attention_out, gains, mixer_first, valid_mask, *tables,
    )
    gain_full = small
    tile = 512
    tiles = hidden_units // tile
    token_shape = (seqs, rows, width)

    def fixed(shape, index=None):
        index = index or (0,) * len(shape)
        return pl.BlockSpec(shape, lambda i, *_: index)

    def up_column(i, ids):
        distance = lax.rem(lax.div(i, 2), 2) * 4 + lax.rem(i, 2) * 2 + lax.div(i, 4)
        return (0, 0, jnp.bitwise_xor(lax.div(ids[4], 4), distance))

    def down_block(p):
        return lambda i, *_: (jnp.clip(i - 2 * p, 0, 1), 0, 0)

    weight_specs = [
        pl.BlockSpec((count, shard, tile), up_column),
        pl.BlockSpec((4, unit_shard, width), lambda i, *_: (i, 0, 0)),
    ]
    out_weight_spec = pl.BlockSpec(
        (count, shard, width), lambda i, *_: (0, unit_shard // shard, 0)
    )
    tile_specs = [pl.BlockSpec((8, shard, tile), up_column)] * 4
    tile_specs += [pl.BlockSpec((4, unit_shard, width), down_block(p)) for p in range(4)]

    hidden, normed_mlp, active, slope, layer_out = pl.pallas_call(
        mlp_forward_body,
        grid_spec=pltpu.PrefetchScalarGridSpec(
            num_scalar_prefetch=1,
            grid=(tiles,),
            in_specs=[
                fixed((4, rows, features)),
                fixed((1,) + token_shape, (3, 0, 0, 0)),
                fixed((8, width)),
            ]
            + weight_specs
            + [out_weight_spec],
            out_specs=[
                fixed(token_shape),
                fixed(token_shape),
                pl.BlockSpec((tokens, tile), lambda i, *_: (0, i)),
                pl.BlockSpec((tokens, tile), lambda i, *_: (0, i)),
                fixed(token_shape),
            ],
            scratch_shapes=[
                pltpu.VMEM((width, width), bf16),
                pltpu.VMEM((width, tile), bf16),
                pltpu.VMEM((tile, width), bf16),
            ],
        ),
        out_shape=[
            jax.ShapeDtypeStruct(token_shape, f32),
            jax.ShapeDtypeStruct(token_shape, bf16),
            jax.ShapeDtypeStruct((tokens, hidden_units), bf16),
            jax.ShapeDtypeStruct((tokens, hidden_units), bf16),
            jax.ShapeDtypeStruct(token_shape, f32),
        ],
        compiler_params=params(),
        name="mlp_forward",
    )(ids, heads, streams, gain_full, up_all, down_all, down_all)

    block = 128
    next_streams, grad_history, grad_layer, g_first, g_second, stats, g_gain_mix = pl.pallas_call(
        mixer_body,
        grid=(tokens // block,),
        in_specs=[
            smem,
            pl.BlockSpec((block, width), lambda i: (i, 0)),
            pl.BlockSpec((past, block, width), lambda i: (0, i, 0)),
            pl.BlockSpec((count_of_streams, block, width), lambda i: (0, i, 0)),
            pl.BlockSpec((1, 1, block), lambda i: (i, 0, 0)),
            fixed((8, width)),
            fixed((span, width)),
            fixed((mixw, mixw)),
            fixed((1, mixw)),
        ],
        out_specs=[
            pl.BlockSpec((count_of_streams, block, width), lambda i: (0, i, 0)),
            pl.BlockSpec((past, block, width), lambda i: (0, i, 0)),
            pl.BlockSpec((block, width), lambda i: (i, 0)),
            fixed((span, width)),
            fixed((span, span)),
            fixed((8, span)),
            fixed((1, width)),
        ],
        out_shape=[
            jax.ShapeDtypeStruct((count_of_streams, tokens, width), bf16),
            jax.ShapeDtypeStruct((past, tokens, width), bf16),
            jax.ShapeDtypeStruct((tokens, width), f32),
            jax.ShapeDtypeStruct((span, width), f32),
            jax.ShapeDtypeStruct((span, span), f32),
            jax.ShapeDtypeStruct((8, span), f32),
            jax.ShapeDtypeStruct((1, width), f32),
        ],
        scratch_shapes=[
            pltpu.VMEM((mixw, block, 128), f32),
            pltpu.VMEM((mixw, block, 128), f32),
            pltpu.VMEM((count_of_streams, block, width), f32),
            pltpu.VMEM((block, 1), f32),
            pltpu.VMEM((span, span), f32),
            pltpu.VMEM((1, span), f32),
        ],
        compiler_params=params(),
        name="mixer",
    )(
        loss_scale,
        layer_out.reshape(tokens, width),
        history.reshape(past, tokens, width),
        teacher.reshape(count_of_streams, tokens, width),
        valid_mask.reshape(-1, 1, block),
        gain_full,
        first_t,
        mixer_second,
        mixer_bias.reshape(1, mixw),
    )

    def once(shape, index=None):
        index = index or (0,) * len(shape)
        return pl.BlockSpec(shape, lambda i, *_: index, pipeline_mode=pl.Buffered(1))

    results = pl.pallas_call(
        mlp_backward_body,
        grid_spec=pltpu.PrefetchScalarGridSpec(
            num_scalar_prefetch=1,
            grid=(tiles,),
            in_specs=[
                once(token_shape),
                pl.BlockSpec((tokens, tile), lambda i, *_: (0, i)),
                pl.BlockSpec((tokens, tile), lambda i, *_: (0, i)),
                once(token_shape),
            ]
            + weight_specs
            + [
                once(token_shape),
                once((4, rows, features)),
                fixed((8, width)),
                once((count, shard, width), (0, unit_shard // shard, 0)),
            ],
            out_specs=tile_specs
            + [fixed(token_shape)]
            + [fixed((rows, features))] * 4
            + [fixed((8, shard, width))] * 4
            + [fixed((1, width))],
            scratch_shapes=[
                pltpu.VMEM(token_shape, bf16),
                pltpu.VMEM((width, tokens), bf16),
                pltpu.VMEM((width, tile), bf16),
                pltpu.VMEM((tile, width), bf16),
                pltpu.VMEM((width, tile), bf16),
                pltpu.VMEM(token_shape, f32),
                pltpu.VMEM((width, width), bf16),
                pltpu.VMEM((width, width), f32),
            ],
        ),
        out_shape=[jax.ShapeDtypeStruct((8, shard, hidden_units), bf16)] * 4
        + [jax.ShapeDtypeStruct((8, unit_shard, width), bf16)] * 4
        + [jax.ShapeDtypeStruct(token_shape, bf16)]
        + [jax.ShapeDtypeStruct((rows, features), bf16)] * 4
        + [jax.ShapeDtypeStruct((8, shard, width), bf16)] * 4
        + [jax.ShapeDtypeStruct((1, width), f32)],
        compiler_params=pltpu.CompilerParams(vmem_limit_bytes=63 * 1024 * 1024),
        name="mlp_backward",
    )(
        ids, grad_layer.reshape(token_shape), active, slope, normed_mlp, up_all, down_all,
        hidden, heads, gain_full, down_all,
    )
    g_ups, g_downs = results[:4], results[4:8]
    g_res, gh0, gh1, gh2, gh3, go0, go1, go2, go3, g_gain_mlp = results[8:]

    down_block_shape = (unit_shard + shard, width)
    down_half = (unit_shard + shard, width // 2)
    slot_shape = (2, lines, piece, width)

    def buffer(shape, dtype=bf16):
        return pltpu.VMEM(shape, dtype)

    grad_streams, grad_projections, sum_up, sum_down, sum_out, early, tiny, late = pl.pallas_call(
        back_body,
        in_specs=[vmem()]
        + [anywhere] * 4
        + [vmem()] * 4
        + [anywhere] * 4
        + [vmem()] * 6
        + [anywhere] * 17,
        out_specs=[anywhere] + [vmem()] * 7,
        out_shape=[
            array((streams.shape[0], 2 * seqs, piece, width)),
            array((3, shard, width), f32),
            array((shard, hidden_units), f32),
            array((unit_shard, width), f32),
            array((shard, width), f32),
            array((span + 8, width // 8), f32),
            array((span + 8, span), f32),
            array((8, width), f32),
        ],
        scratch_shapes=[
            buffer(wide_shape),
            buffer(wide_shape),
            buffer(wide_shape),
            buffer(heads_shape),
            buffer((4, rows, features)),
            buffer((3,) + wide_shape),
            buffer((3,) + wide_shape[1:]),
            buffer((length, 128), f32),
            buffer((length, 128), f32),
            buffer((128, length)),
            buffer((2,) + slot_shape),
            buffer((2,) + row_shape[1:]),
            buffer((2, 2, width, features)),
            buffer((lines, piece, width), f32),
            buffer(row_shape),
            buffer((width, features)),
            buffer((4, shard, hidden_units)),
            buffer((2, 2) + down_block_shape),
            buffer((16, shard, hidden_units)),
            buffer((8, shard, hidden_units)),
            buffer((4, shard, hidden_units)),
            buffer((2, shard, hidden_units)),
            buffer((1, shard, hidden_units)),
            buffer((4, 2, 2) + down_block_shape),
            buffer((2, 2, 2) + down_half),
            buffer((2, 2) + down_half),
            buffer((2,) + down_half),
            buffer(down_half),
            buffer((2, 4) + down_half),
            buffer((4,) + down_half),
            buffer((2,) + down_half),
            buffer(down_half),
            buffer(proj_shape),
            buffer((8,) + proj_shape[1:]),
            buffer((4,) + proj_shape[1:]),
            buffer((2,) + proj_shape[1:]),
            buffer((1,) + proj_shape[1:]),
            buffer(proj_shape[2:]),
            buffer((span + 8, width), f32),
            buffer((span + 8, width // 2), f32),
            buffer((span + 8, width // 4), f32),
            buffer((span + 8, width // 8), f32),
            buffer((2, span + 8, width // 8), f32),
            buffer((5, span + 8, span), f32),
            buffer((5, 8, width), f32),
            pltpu.SemaphoreType.DMA((40,)),
            pltpu.SemaphoreType.DMA((64,)),
            pltpu.SemaphoreType.DMA((64,)),
        ],
        compiler_params=pltpu.CompilerParams(
            vmem_limit_bytes=63 * 1024 * 1024, collective_id=1, has_side_effects=True
        ),
        name="back",
    )(
        prefix_rows,
        queries, keys, values, heads_seq,
        lse,
        *tables,
        normed, received, proj, proj_other, gain_full, g_first, g_gain_mlp, g_gain_mix, g_second, stats,
        g_res.reshape(2 * seqs, piece, width),
        gh0, gh1, gh2, gh3, *g_ups,
        *[g.reshape(2, 2, 2, -1, width) for g in (*g_downs, go0, go1, go2, go3)],
    )
    quarters = 2 * seqs
    stream_block = pl.BlockSpec((1, quarters, piece, width), lambda i: (i, 0, 0, 0))
    whole_shapes = [
        ((3, shard, width), f32),
        ((shard, hidden_units), f32),
        ((unit_shard, width), f32),
        ((shard, width), f32),
    ]
    small_shapes = [((shard, mixw), f32), ((mixw, mixw), f32), ((1, mixw), f32), ((5, shard), f32), ((1, 1), f32)]
    (
        grad_streams, grad_projections, sum_up, sum_down, sum_out,
        grad_first, grad_second, grad_bias, grad_gains, mean_loss,
    ) = pl.pallas_call(
        finish_body,
        grid=(streams.shape[0],),
        in_specs=[smem, stream_block]
        + [fixed(s) for s, _ in whole_shapes]
        + [
            fixed((span + 8, width // 8)),
            fixed((span + 8, span)),
            fixed((8, width)),
            fixed((8, width)),
        ],
        out_specs=[stream_block] + [fixed(s) for s, _ in whole_shapes + small_shapes],
        out_shape=[array((streams.shape[0], quarters, piece, width))]
        + [array(*s) for s in whole_shapes + small_shapes],
        compiler_params=params(),
        name="finish",
    )(
        me.reshape(1).astype(jnp.int32),
        grad_streams, grad_projections, sum_up, sum_down, sum_out, early, tiny, late, small,
    )
    return (
        next_streams.reshape(teacher.shape),
        mean_loss.reshape(()),
        grad_streams.reshape(streams.shape),
        grad_history.reshape(history.shape),
        grad_projections,
        sum_out,
        sum_up,
        sum_down,
        grad_first,
        grad_second,
        grad_bias.reshape(mixw),
        grad_gains,
    )


def layer_norm(values, gain_row):
    centered = values - jnp.mean(values, axis=-1, keepdims=True)
    return (
        centered
        * lax.rsqrt(jnp.mean(centered * centered, axis=-1, keepdims=True) + epsilon)
        * gain_row
    )


def rms_norm(values, gain_row):
    return (
        values * lax.rsqrt(jnp.mean(values * values, axis=-1, keepdims=True) + epsilon) * gain_row
    )


def gelu_exact(values):
    return jax.nn.gelu(values, approximate=False)


def rotary_tables(positions):
    frequency_steps = jnp.arange(ROT // 2).astype(positions.dtype)
    inverse = jnp.exp(frequency_steps * (-2.0 * math.log(10000.0) / ROT))
    angles = positions[:, None] * inverse[None, :]
    return (jnp.cos(angles)[:, None, :], jnp.sin(angles)[:, None, :])


def rotate(values, cosine_table, sine_table, direction):
    row_count = values.shape[0]
    shaped = values.reshape(row_count, HEADS, HEAD_DIM)
    half_rot = ROT // 2
    first_half = shaped[:, :, :half_rot]
    second_half = shaped[:, :, half_rot:ROT]
    remainder = shaped[:, :, ROT:]
    turned_first = first_half * cosine_table - direction * second_half * sine_table
    turned_second = second_half * cosine_table + direction * first_half * sine_table
    return jnp.concatenate([turned_first, turned_second, remainder], axis=-1).reshape(row_count, -1)


def masked_scores(query_heads, key_heads, query_index, key_index, prefix_len):
    scores = jnp.einsum(
        "qhd,khd->hqk", query_heads, key_heads, preferred_element_type=jnp.float32
    ) * HEAD_DIM ** (-0.5)
    allowed = (key_index[None, :] <= query_index[:, None]) | (key_index[None, :] < prefix_len)
    return jnp.where(allowed[None], scores, -1e30)


def local_plain(
    streams,
    history,
    teacher,
    prefix,
    valid_mask,
    loss_scale,
    projections,
    attention_out,
    up_weight,
    down_weight,
    mixer_first,
    mixer_second,
    mixer_bias,
    gains,
):
    micro_count = streams.shape[1]
    row_count = streams.shape[2]
    model_width = streams.shape[3]
    length = row_count * lax.axis_size("ctx")
    query_index = lax.axis_index("ctx") * row_count + jnp.arange(row_count, dtype=jnp.int32)
    key_index = jnp.arange(length, dtype=jnp.int32)
    cosine_table, sine_table = rotary_tables(query_index.astype(jnp.float32))
    score_scale = HEAD_DIM ** (-0.5)
    valid_float = valid_mask.astype(jnp.float32)
    token_total = lax.psum(jnp.sum(valid_float), ("dp", "ctx"))
    factor = loss_scale[0] * 2.0 / (4.0 * model_width * token_total)

    def one_batch(totals, number):
        (
            kept_projections,
            kept_attention,
            kept_gains,
            kept_up,
            kept_down,
            kept_first,
            kept_second,
            kept_bias,
            kept_loss,
        ) = totals
        stream_block = lax.dynamic_index_in_dim(streams, number, 1, keepdims=False)
        past_outputs = lax.dynamic_index_in_dim(history, number, 1, keepdims=False)
        target = lax.dynamic_index_in_dim(teacher, number, 1, keepdims=False).astype(jnp.float32)
        prefix_len = lax.dynamic_index_in_dim(prefix, number, 0, keepdims=False)
        valid_row = lax.dynamic_index_in_dim(valid_float, number, 0, keepdims=False)
        proj_full, out_full, gain_low, up_full, down_full, first_full = (
            lax.all_gather(projections, ("dp", "ctx"), axis=1, tiled=True),
            lax.all_gather(attention_out, ("dp", "ctx"), axis=0, tiled=True),
            lax.all_gather(gains, ("dp", "ctx"), axis=1, tiled=True),
            lax.all_gather(up_weight, ("dp", "ctx"), axis=0, tiled=True),
            lax.all_gather(down_weight, ("dp", "ctx"), axis=0, tiled=True),
            lax.all_gather(mixer_first, ("dp", "ctx"), axis=0, tiled=True),
        )
        gain_full = gain_low.astype(jnp.float32)
        inputs = stream_block.astype(jnp.float32)
        gain_three = gain_full[:3, None, :]
        normed_low = layer_norm(inputs[:3], gain_three).astype(jnp.bfloat16)
        projected = jnp.einsum(
            "std,sde->ste", normed_low, proj_full, preferred_element_type=jnp.float32
        )
        query_heads = (
            rotate(projected[0], cosine_table, sine_table, 1.0)
            .astype(jnp.bfloat16)
            .reshape(row_count, HEADS, HEAD_DIM)
        )
        key_low = rotate(projected[1], cosine_table, sine_table, 1.0).astype(jnp.bfloat16)
        value_low = projected[2].astype(jnp.bfloat16)
        all_keys, all_values = (
            lax.all_gather(key_low, "ctx", axis=0, tiled=True),
            lax.all_gather(value_low, "ctx", axis=0, tiled=True),
        )
        key_heads = all_keys.reshape(length, HEADS, HEAD_DIM)
        value_heads = all_values.reshape(length, HEADS, HEAD_DIM)
        scores = masked_scores(query_heads, key_heads, query_index, key_index, prefix_len)
        row_max = jnp.max(scores, axis=-1, keepdims=True)
        log_total = row_max + jnp.log(jnp.sum(jnp.exp(scores - row_max), axis=-1, keepdims=True))
        probs_low = jnp.exp(scores - log_total).astype(jnp.bfloat16)
        heads_low = (
            jnp.einsum("hqk,khd->qhd", probs_low, value_heads, preferred_element_type=jnp.float32)
            .reshape(row_count, model_width)
            .astype(jnp.bfloat16)
        )
        hidden = inputs[3] + jnp.dot(heads_low, out_full, preferred_element_type=jnp.float32)
        normed_mlp = layer_norm(hidden, gain_full[3]).astype(jnp.bfloat16)
        upper = jnp.dot(normed_mlp, up_full, preferred_element_type=jnp.float32)
        activated = gelu_exact(upper).astype(jnp.bfloat16)
        layer_out = hidden + jnp.dot(activated, down_full, preferred_element_type=jnp.float32)
        normed_mix = rms_norm(layer_out, gain_full[4]).astype(jnp.bfloat16)
        mix_hidden = jnp.dot(normed_mix, first_full, preferred_element_type=jnp.float32)
        mix_active = gelu_exact(mix_hidden)
        coeff = jnp.dot(mix_active, mixer_second, precision=highest) + mixer_bias
        coeff_grid = coeff.reshape(row_count, 4, -1)
        outputs_all = jnp.concatenate([past_outputs.astype(jnp.float32), layer_out[None]], axis=0)
        next_block = jnp.einsum("tsj,jtd->std", coeff_grid, outputs_all, precision=highest)
        difference = next_block - target
        loss_part = jnp.sum(jnp.sum(difference * difference, axis=(0, 2)) * valid_row) / (
            4.0 * model_width * token_total
        )
        grad_next = factor * valid_row[None, :, None] * difference
        grad_coeff = jnp.einsum("std,jtd->tsj", grad_next, outputs_all, precision=highest).reshape(
            row_count, -1
        )
        grad_outputs = jnp.einsum("tsj,std->jtd", coeff_grid, grad_next, precision=highest)
        grad_past = grad_outputs[:-1].astype(jnp.bfloat16)
        grad_second = jnp.dot(mix_active.T, grad_coeff, precision=highest)
        grad_bias = jnp.sum(grad_coeff, axis=0)
        grad_active = jnp.dot(grad_coeff, mixer_second.T, precision=highest)
        gelu_mix_back = jax.vjp(gelu_exact, mix_hidden)[1]
        grad_mix = gelu_mix_back(grad_active)[0].astype(jnp.bfloat16)
        grad_first = jnp.einsum(
            "td,tm->dm", normed_mix, grad_mix, preferred_element_type=jnp.float32
        )
        grad_normed_mix = jnp.einsum(
            "tm,dm->td", grad_mix, first_full, preferred_element_type=jnp.float32
        )
        rms_back = jax.vjp(rms_norm, layer_out, gain_full[4])[1]
        grad_layer_mix, grad_gain_mix = rms_back(grad_normed_mix)
        grad_layer = grad_outputs[-1] + grad_layer_mix
        grad_branch = grad_layer.astype(jnp.bfloat16)
        grad_down = jnp.einsum(
            "tf,td->fd", activated, grad_branch, preferred_element_type=jnp.float32
        )
        grad_active_up = jnp.einsum(
            "td,fd->tf", grad_branch, down_full, preferred_element_type=jnp.float32
        )
        gelu_up_back = jax.vjp(gelu_exact, upper)[1]
        grad_upper = gelu_up_back(grad_active_up)[0].astype(jnp.bfloat16)
        grad_up = jnp.einsum(
            "td,tf->df", normed_mlp, grad_upper, preferred_element_type=jnp.float32
        )
        grad_normed_mlp = jnp.einsum(
            "tf,df->td", grad_upper, up_full, preferred_element_type=jnp.float32
        )
        down_shard, first_shard, up_shard = (
            lax.psum_scatter(grad_down, ("dp", "ctx"), scatter_dimension=0, tiled=True),
            lax.psum_scatter(grad_first, ("dp", "ctx"), scatter_dimension=0, tiled=True),
            lax.psum_scatter(grad_up, ("dp", "ctx"), scatter_dimension=0, tiled=True),
        )
        down_next = kept_down + down_shard
        norm_mlp_back = jax.vjp(layer_norm, hidden, gain_full[3])[1]
        grad_hidden_mlp, grad_gain_mlp = norm_mlp_back(grad_normed_mlp)
        grad_hidden = grad_layer + grad_hidden_mlp
        grad_attn = grad_hidden.astype(jnp.bfloat16)
        grad_attention = jnp.einsum(
            "td,te->de", heads_low, grad_attn, preferred_element_type=jnp.float32
        )
        grad_heads = jnp.einsum(
            "te,de->td", grad_attn, out_full, preferred_element_type=jnp.float32
        ).astype(jnp.bfloat16)
        grad_head_grid = grad_heads.reshape(row_count, HEADS, HEAD_DIM)
        scores_again = masked_scores(query_heads, key_heads, query_index, key_index, prefix_len)
        probs_exact = jnp.exp(scores_again - log_total)
        probs_again = probs_exact.astype(jnp.bfloat16)
        grad_probs = jnp.einsum(
            "qhd,khd->hqk", grad_head_grid, value_heads, preferred_element_type=jnp.float32
        )
        row_inner = jnp.sum(probs_exact * grad_probs, axis=-1, keepdims=True)
        grad_scores = (probs_exact * (grad_probs - row_inner)).astype(jnp.bfloat16)
        grad_queries = (
            jnp.einsum(
                "hqk,khd->qhd", grad_scores, key_heads, preferred_element_type=jnp.float32
            ).reshape(row_count, model_width)
            * score_scale
        )
        grad_key_part = (
            jnp.einsum("hqk,qhd->khd", grad_scores, query_heads, preferred_element_type=jnp.float32)
            * score_scale
        )
        grad_value_part = jnp.einsum(
            "hqk,qhd->khd", probs_again, grad_head_grid, preferred_element_type=jnp.float32
        )
        key_grads = lax.psum_scatter(
            jnp.concatenate(
                [
                    grad_key_part.reshape(row_count * lax.axis_size("ctx"), -1),
                    grad_value_part.reshape(row_count * lax.axis_size("ctx"), -1),
                ],
                axis=-1,
            ).astype(jnp.bfloat16),
            "ctx",
            scatter_dimension=0,
            tiled=True,
        ).astype(jnp.float32)
        grad_query_low = rotate(grad_queries, cosine_table, sine_table, -1.0).astype(jnp.bfloat16)
        grad_key_low = rotate(key_grads[:, :model_width], cosine_table, sine_table, -1.0).astype(
            jnp.bfloat16
        )
        grad_value_low = key_grads[:, model_width:].astype(jnp.bfloat16)
        grad_projected = jnp.stack([grad_query_low, grad_key_low, grad_value_low])
        grad_proj = jnp.einsum(
            "std,ste->sde", normed_low, grad_projected, preferred_element_type=jnp.float32
        )
        grad_normed = jnp.einsum(
            "ste,sde->std", grad_projected, proj_full, preferred_element_type=jnp.float32
        )
        norm_three_back = jax.vjp(layer_norm, inputs[:3], gain_three)[1]
        grad_inputs_three, grad_gain_three = norm_three_back(grad_normed)
        grad_gain_all = jnp.concatenate(
            [grad_gain_three.reshape(3, -1), grad_gain_mlp[None], grad_gain_mix[None]], axis=0
        )
        proj_shard, attention_shard, gain_shard = (
            lax.psum_scatter(grad_proj, ("dp", "ctx"), scatter_dimension=1, tiled=True),
            lax.psum_scatter(grad_attention, ("dp", "ctx"), scatter_dimension=0, tiled=True),
            lax.psum_scatter(grad_gain_all, ("dp", "ctx"), scatter_dimension=1, tiled=True),
        )
        grad_block = jnp.concatenate([grad_inputs_three, grad_hidden[None]], axis=0).astype(
            jnp.bfloat16
        )
        new_totals = (
            kept_projections + proj_shard,
            kept_attention + attention_shard,
            kept_gains + gain_shard,
            kept_up + up_shard,
            down_next,
            kept_first + first_shard,
            kept_second + grad_second,
            kept_bias + grad_bias,
            kept_loss + loss_part,
        )
        return (new_totals, (next_block.astype(jnp.bfloat16), grad_block, grad_past))

    down_start = jnp.zeros(down_weight.shape, jnp.float32)
    start_totals = (
        jnp.zeros(projections.shape, jnp.float32),
        jnp.zeros(attention_out.shape, jnp.float32),
        jnp.zeros(gains.shape, jnp.float32),
        jnp.zeros(up_weight.shape, jnp.float32),
        down_start,
        jnp.zeros(mixer_first.shape, jnp.float32),
        jnp.zeros(mixer_second.shape, jnp.float32),
        jnp.zeros(mixer_bias.shape, jnp.float32),
        jnp.zeros((), jnp.float32),
    )
    final_totals, stacked = lax.scan(
        one_batch, start_totals, jnp.arange(micro_count, dtype=jnp.int32)
    )
    (
        sum_projections,
        sum_attention,
        sum_gains,
        sum_up,
        sum_down,
        sum_first,
        sum_second,
        sum_bias,
        sum_loss,
    ) = final_totals
    grad_second_all, grad_bias_all, loss_all = lax.psum(
        (sum_second, sum_bias, sum_loss), ("dp", "ctx")
    )
    next_streams = jnp.moveaxis(stacked[0], 0, 1)
    grad_streams = jnp.moveaxis(stacked[1], 0, 1)
    grad_history = jnp.moveaxis(stacked[2], 0, 1)
    return (
        next_streams,
        loss_all,
        grad_streams,
        grad_history,
        sum_projections,
        sum_attention,
        sum_up,
        sum_down,
        sum_first,
        grad_second_all,
        grad_bias_all,
        sum_gains,
    )


def fits(mesh):
    return mesh.shape["ctx"] == 4 and mesh.shape["dp"] == 8


def solution(mesh):
    specs = dict(
        in_specs=(
            P(None, "dp", "ctx", None),
            P(None, "dp", "ctx", None),
            P(None, "dp", "ctx", None),
            P("dp"),
            P("dp", "ctx"),
            P(),
            P(None, ("dp", "ctx"), None),
            P(("dp", "ctx"), None),
            P(("dp", "ctx"), None),
            P(("dp", "ctx"), None),
            P(("dp", "ctx"), None),
            P(),
            P(),
            P(None, ("dp", "ctx")),
        ),
        out_specs=(
            P(None, "dp", "ctx", None),
            P(),
            P(None, "dp", "ctx", None),
            P(None, "dp", "ctx", None),
            P(None, ("dp", "ctx"), None),
            P(("dp", "ctx"), None),
            P(("dp", "ctx"), None),
            P(("dp", "ctx"), None),
            P(("dp", "ctx"), None),
            P(),
            P(),
            P(None, ("dp", "ctx")),
        ),
        check_vma=False,
    )

    def chosen(*arrays):
        fast = fits(mesh) and arrays[0].shape[1] == 2 * mesh.shape["dp"]
        return jax.shard_map(local_fast if fast else local_plain, mesh=mesh, **specs)(*arrays)

    return chosen
```
